32 devices in a mesh: dp: 8 (over y, x, core), seq: 4 (over z).
Axes of the slice: x: 2, y: 2, z: 4, core: 2. Of those that a mesh axis runs over, the one named last changes fastest.
Arguments:
- embeddings: bfloat16 [2, 8, 2048, 768], P(None, 'dp', 'seq'), may hold values from -6 to 6
- lengths: int32 [2, 8], P(None, 'dp'), may hold values from 512 to 2048, as said below
- cotangent: bfloat16 [2, 8, 1024, 768], P(None, 'dp', 'seq'), may hold values from -6 to 6
- conv_weight: bfloat16 [5, 768], P(None, ('dp', 'seq')), may hold values from -2.5 to 2.5
- scorer: bfloat16 [768], P(('dp', 'seq')), may hold values from -0.4375 to 0.4375
- gain_attn: bfloat16 [768], P(('dp', 'seq')), may hold values from 0.5 to 1.5
- w_query: bfloat16 [768, 768], P(('dp', 'seq')), may hold values from -0.109375 to 0.109375
- w_key: bfloat16 [768, 768], P(('dp', 'seq')), may hold values from -0.109375 to 0.109375
- w_value: bfloat16 [768, 768], P(('dp', 'seq')), may hold values from -0.21875 to 0.21875
- w_out: bfloat16 [768, 768], P(('dp', 'seq')), may hold values from -0.875 to 0.875
- rel_bias: bfloat16 [32, 12], replicated, may hold values from -4 to 4
- gain_ffn: bfloat16 [768], P(('dp', 'seq')), may hold values from 0.5 to 1.5
- w_gate: bfloat16 [768, 2048], P(('dp', 'seq')), may hold values from -0.21875 to 0.21875
- w_up: bfloat16 [768, 2048], P(('dp', 'seq')), may hold values from -0.21875 to 0.21875
- w_down: bfloat16 [2048, 768], P(('dp', 'seq')), may hold values from -0.125 to 0.125
Outputs:
- blocks: bfloat16 [2, 8, 1024, 768], P(None, 'dp', 'seq')
- embed_grad: float32 [2, 8, 2048, 768], P(None, 'dp', 'seq')
- conv_grad: float32 [5, 768], P(None, ('dp', 'seq'))
- scorer_grad: float32 [768], P(('dp', 'seq'))
- gain_attn_grad: float32 [768], P(('dp', 'seq'))
- query_grad: float32 [768, 768], P(('dp', 'seq'))
- key_grad: float32 [768, 768], P(('dp', 'seq'))
- value_grad: float32 [768, 768], P(('dp', 'seq'))
- out_grad: float32 [768, 768], P(('dp', 'seq'))
- rel_bias_grad: float32 [32, 12], replicated
- gain_ffn_grad: float32 [768], P(('dp', 'seq'))
- gate_grad: float32 [768, 2048], P(('dp', 'seq'))
- up_grad: float32 [768, 2048], P(('dp', 'seq'))
- down_grad: float32 [2048, 768], P(('dp', 'seq'))
The draws below stay inside these ranges and needn't reach their ends.
Inputs may be any that keep to these rules, and one draw needn't show every extreme that they name: `lengths`: each sequence's live bytes; in every draw one sequence has exactly 2048 and one exactly 512.
All inputs are finite; a program needn't handle non-finite values.
Results may differ from the reference program's by a relative error of at most 0.02.
Values may be sent and summed in bfloat16 or wider, within the bound.
No kernel may reach another device: no remote copies, remote signals or barrier semaphores. Data moves between devices by JAX's collectives and lax.ppermute only.
A program may use at most 256 MiB of HBM per device.

```python
import jax
import jax.numpy as jnp
from jax import lax

D = 768
FF = 2048
HEADS = 12
HEAD = 64
BUCKETS = 32
KERNEL = 5
SEQ_BYTES = 2048
MICRO = 2
SEQ_TOTAL = 8
SEQ_TOKENS = 1024


def draw_lengths(key, part):
    length_draw = jax.random.randint(key, (MICRO, SEQ_TOTAL), SEQ_BYTES // 4, SEQ_BYTES + 1, dtype=jnp.int32)
    length_draw = length_draw.at[0, 0].set(SEQ_BYTES)
    return length_draw.at[MICRO - 1, SEQ_TOTAL - 1].set(SEQ_BYTES // 4)


def level_of(key, dims, cuts, least, high):
    def one(position, blocks):
        steps = jax.random.uniform(jax.random.fold_in(jax.random.fold_in(key, 6), position), (blocks,), jnp.float32, least / len(cuts), high / len(cuts))
        return jnp.repeat(jnp.exp(steps), dims[position] // blocks).reshape((-1,) + (1,) * (len(dims) - position - 1))

    loudness = one(*cuts[0])
    for cut in cuts[1:]:
        loudness = loudness * one(*cut)
    return loudness


def normal_values(own_key, shape, spread, reach, shards=(), held_as=jnp.bfloat16):
    entries = spread * jax.random.normal(own_key, shape, jnp.float32)
    if shards:
        entries = entries * level_of(own_key, shape, shards, -0.22, 0.18)
    return jnp.clip(entries, -reach, reach).astype(held_as)


def setup_inputs(seed: int = 0) -> dict:
    key_of = jax.random.split(jax.random.key(seed), 16)
    return {
        "embeddings": normal_values(key_of[0], (MICRO, SEQ_TOTAL, SEQ_BYTES, D), 1.0, 6.0, ((1, 8), (2, 4))),
        "lengths": draw_lengths(jax.random.fold_in(key_of[15], 71), 0),
        "cotangent": normal_values(key_of[2], (MICRO, SEQ_TOTAL, SEQ_TOKENS, D), 1.0, 6.0, ((1, 8), (2, 4))),
        "conv_weight": normal_values(key_of[3], (KERNEL, D), KERNEL ** -0.5, 2.5, ((1, 32),)),
        "scorer": normal_values(key_of[4], (D,), (D // 4) ** -0.5, 0.4375, ((0, 32),)),
        "gain_attn": jnp.clip(1.0 + 0.1 * jax.random.normal(key_of[5], (D,), jnp.float32), 0.5, 1.5).astype(jnp.bfloat16),
        "w_query": normal_values(key_of[6], (D, D), (4 * D) ** -0.5, 0.109375, ((0, 32),)),
        "w_key": normal_values(key_of[7], (D, D), (4 * D) ** -0.5, 0.109375, ((0, 32),)),
        "w_value": normal_values(key_of[8], (D, D), D ** -0.5, 0.21875, ((0, 32),)),
        "w_out": normal_values(key_of[9], (D, D), (D // 16) ** -0.5, 0.875, ((0, 32),)),
        "rel_bias": normal_values(key_of[10], (BUCKETS, HEADS), 1.0, 4.0),
        "gain_ffn": jnp.clip(1.0 + 0.1 * jax.random.normal(key_of[11], (D,), jnp.float32), 0.5, 1.5).astype(jnp.bfloat16),
        "w_gate": normal_values(key_of[12], (D, FF), D ** -0.5, 0.21875, ((0, 32),)),
        "w_up": normal_values(key_of[13], (D, FF), D ** -0.5, 0.21875, ((0, 32),)),
        "w_down": normal_values(key_of[14], (FF, D), FF ** -0.5, 0.125, ((0, 32),)),
    }


@jax.custom_vjp
def low(v):
    return lax.optimization_barrier(v.astype(jnp.bfloat16)).astype(jnp.float32)

@jax.custom_vjp
def low_back(v):
    return v

def low_keep(v):
    return (low(v), None)

def low_pass(kept, grad):
    return (grad,)

def back_keep(v):
    return (v, None)

def back_low(kept, grad):
    return (low(grad),)
low.defvjp(low_keep, low_pass)
low_back.defvjp(back_keep, back_low)
norm_eps = 1e-06
highest = lax.Precision.HIGHEST
cut_points = (12, 16, 23, 32, 46, 64, 91)

def bucket_of(offset):
    distance = jnp.abs(offset)
    far_bucket = 8 + sum(((distance >= cut_point).astype(jnp.int32) for cut_point in cut_points))
    return jnp.where(distance < 8, distance, far_bucket) + jnp.where(offset > 0, 16, 0)

def rms_scale(values, gain_vec):
    return values * lax.rsqrt(lax.optimization_barrier(jnp.mean(values * values, axis=-1, keepdims=True)) + norm_eps) * gain_vec

def block_mean(center, block_size):
    shape_now = center.shape
    grouped = center.reshape(shape_now[:-2] + (shape_now[-2] // block_size, block_size, shape_now[-1]))
    averaged = lax.optimization_barrier(jnp.mean(grouped, axis=-2, keepdims=True))
    return jnp.broadcast_to(averaged, grouped.shape).reshape(shape_now)

def triple_mean(conv_wide, positions):
    num_cells = positions.shape[0]
    window = [conv_wide[..., offset_cell:offset_cell + num_cells, :] for offset_cell in range(5)]
    leading = window[2] + window[3] + window[4]
    central = window[1] + window[2] + window[3]
    trailing = window[0] + window[1] + window[2]
    remainder = (positions % 3)[:, None]
    return jnp.where(remainder == 0, leading, jnp.where(remainder == 1, central, trailing)) / 3.0

def gbst_forward(wide_bytes, conv_weight, scorer, positions_wide, lengths):
    half_kernel = KERNEL // 2
    rim_width = half_kernel + 2
    num_cells = wide_bytes.shape[-2] - 2 * rim_width
    conv_len = num_cells + 4
    byte_live = ((positions_wide >= 0) & (positions_wide < lengths[..., None])).astype(jnp.float32)[..., None]
    masked = wide_bytes * byte_live
    conv_wide = sum((conv_weight[tap_index] * masked[..., tap_index:tap_index + conv_len, :] for tap_index in range(KERNEL)))
    conv_wide = conv_wide * byte_live[..., half_kernel:half_kernel + conv_len, :]
    center = conv_wide[..., 2:2 + num_cells, :]
    center_pos = positions_wide[rim_width:rim_width + num_cells]
    stacked = jnp.stack([center, block_mean(center, 2), triple_mean(conv_wide, center_pos), block_mean(center, 4)], axis=0)
    size_logits = jnp.einsum('s...d,d->s...', stacked, scorer, precision=highest)
    size_weights = jax.nn.softmax(size_logits, axis=0)
    mixture = lax.optimization_barrier(jnp.sum(size_weights[..., None] * stacked, axis=0))
    shape_now = mixture.shape
    return lax.optimization_barrier(jnp.mean(mixture.reshape(shape_now[:-2] + (shape_now[-2] // 2, 2, shape_now[-1])), axis=-2))

def layer_forward(weights, embedded, lengths):
    conv_weight, scorer, gain_attn, w_query, w_key, w_value, w_out, rel_bias, gain_ffn, w_gate, w_up, w_down = weights
    rim_width = KERNEL // 2 + 2
    wide_bytes = jnp.pad(embedded, ((rim_width, rim_width), (0, 0)))
    positions_wide = jnp.arange(-rim_width, SEQ_BYTES + rim_width, dtype=jnp.int32)
    hidden_in = gbst_forward(wide_bytes, conv_weight, scorer, positions_wide, lengths)
    normed = low(rms_scale(hidden_in, gain_attn))
    queries = low(low_back(jnp.dot(normed, w_query, precision=highest))).reshape(SEQ_TOKENS, HEADS, HEAD)
    keys_all = low(low_back(jnp.dot(normed, w_key, precision=highest))).reshape(SEQ_TOKENS, HEADS, HEAD)
    values_all = low(low_back(jnp.dot(normed, w_value, precision=highest))).reshape(SEQ_TOKENS, HEADS, HEAD)
    token_pos = jnp.arange(SEQ_TOKENS, dtype=jnp.int32)
    buckets = bucket_of(token_pos[None, :] - token_pos[:, None])
    pair_bias = jnp.transpose(rel_bias[buckets], (2, 0, 1))
    key_live = 2 * token_pos < lengths
    raw_scores = jnp.einsum('thd,uhd->htu', queries, keys_all, precision=highest) + pair_bias
    scores = low_back(jnp.where(key_live[None, None, :], raw_scores, -1000000000.0))
    attn_probs = low(jax.nn.softmax(scores, axis=-1))
    attended = low(low_back(jnp.einsum('htu,uhd->thd', attn_probs, values_all, precision=highest))).reshape(SEQ_TOKENS, D)
    after_attn = hidden_in + low_back(jnp.dot(attended, w_out, precision=highest))
    normed_ffn = low(rms_scale(after_attn, gain_ffn))
    gate_value = low_back(jnp.dot(normed_ffn, w_gate, precision=highest))
    up_value = low_back(jnp.dot(normed_ffn, w_up, precision=highest))
    inner_act = low(jax.nn.gelu(gate_value, approximate=True) * up_value)
    return after_attn + low_back(jnp.dot(inner_act, w_down, precision=highest))

def reference(embeddings, lengths, cotangent, conv_weight, scorer, gain_attn, w_query, w_key, w_value, w_out, rel_bias, gain_ffn, w_gate, w_up, w_down):
    weights = tuple((weight_arg.astype(jnp.float32) for weight_arg in (conv_weight, scorer, gain_attn, w_query, w_key, w_value, w_out, rel_bias, gain_ffn, w_gate, w_up, w_down)))
    flat_embed = embeddings.reshape(MICRO * SEQ_TOTAL, SEQ_BYTES, D).astype(jnp.float32)
    flat_length = lengths.reshape(MICRO * SEQ_TOTAL).astype(jnp.int32)
    flat_seed = cotangent.reshape(MICRO * SEQ_TOTAL, SEQ_TOKENS, D).astype(jnp.float32)

    def one_sequence(totals, inputs):
        embedded, seq_length, seed_grad = inputs

        def apply_layer(weights_now, embedded_now):
            return layer_forward(weights_now, embedded_now, seq_length)
        output, pullback = jax.vjp(apply_layer, weights, embedded)
        grad_weights, grad_embed = pullback(seed_grad)
        totals = jax.tree.map(jnp.add, totals, grad_weights)
        return (totals, (output.astype(jnp.bfloat16), grad_embed))
    zero_grads = jax.tree.map(jnp.zeros_like, weights)
    totals, (outputs, grad_embeds) = lax.scan(one_sequence, zero_grads, (flat_embed, flat_length, flat_seed))
    blocks = outputs.reshape(MICRO, SEQ_TOTAL, SEQ_TOKENS, D)
    embed_grad = grad_embeds.reshape(MICRO, SEQ_TOTAL, SEQ_BYTES, D)
    return (blocks, embed_grad, totals[0], totals[1], totals[2], totals[3], totals[4], totals[5], totals[6], totals[7], totals[8], totals[9], totals[10], totals[11])
```

```python
import jax
import jax.numpy as jnp
from jax import lax
from jax.experimental import pallas as pl
from jax.experimental.pallas import tpu as pltpu
from jax.sharding import PartitionSpec as P

HEADS = 12
HEAD = 64
BUCKETS = 32
KERNEL = 5


norm_eps = 1e-06
highest = lax.Precision.HIGHEST
cut_points = (12, 16, 23, 32, 46, 64, 91)


def neighbour_edges(x, width):
    devices, length = (lax.axis_size("seq"), x.shape[1])
    up = [(i, i + 1) for i in range(devices - 1)]
    down = [(j, i) for i, j in up]
    before = lax.ppermute(x[:, length - width :], "seq", up)
    after = lax.ppermute(x[:, :width], "seq", down)
    return before, after


def bucket_of(offset):
    distance = jnp.abs(offset)
    far_bucket = 8 + sum(((distance >= cut_point).astype(jnp.int32) for cut_point in cut_points))
    return jnp.where(distance < 8, distance, far_bucket) + jnp.where(offset > 0, 16, 0)


def rms_scale(values, gain_vec):
    return (
        values * lax.rsqrt(jnp.mean(values * values, axis=-1, keepdims=True) + norm_eps) * gain_vec
    )


def gelu_gate(gate_in, up_in):
    return jax.nn.gelu(gate_in, approximate=True) * up_in


EDGE = 8
LANES = 128


def shifted(x, step):
    return pltpu.roll(x, (-step) % x.shape[0], 0)


def byte_facts(token_start, length, rows):
    token = token_start - EDGE + lax.broadcasted_iota(jnp.int32, (rows, LANES), 0)
    first = 2 * token
    even_live = jnp.where((first >= 0) & (first < length), 1.0, 0.0)
    odd_live = jnp.where((first + 1 >= 0) & (first + 1 < length), 1.0, 0.0)
    remainder = lax.rem(first + 6 * EDGE, 3)
    odd_token = lax.rem(token + 2 * EDGE, 2) == 1
    return even_live, odd_live, remainder, odd_token


def pooled_scalars(six, remainder, odd_token):
    even_b, odd_b, even, odd, even_a, odd_a = six
    pair = even + odd
    quad = pair + jnp.where(odd_token, even_b + odd_b, even_a + odd_a)
    shared = pair + jnp.where(remainder == 0, even_a, odd_b)
    split = remainder == 2
    triple_even = jnp.where(split, even_b + odd_b + even, shared)
    triple_odd = jnp.where(split, odd + even_a + odd_a, shared)
    third = 1.0 / 3.0
    return (
        (even, 0.5 * pair, third * triple_even, 0.25 * quad),
        (odd, 0.5 * pair, third * triple_odd, 0.25 * quad),
    )


def spread_scalars(even, odd, remainder, odd_token):
    third = 1.0 / 3.0
    pair = 0.5 * (even[1] + odd[1])
    quad = 0.25 * (even[3] + odd[3])
    both = third * (even[2] + odd[2])
    only_even = third * even[2]
    only_odd = third * odd[2]
    split = remainder == 2
    zero = jnp.zeros_like(pair)
    quad_b = jnp.where(odd_token, quad, zero)
    quad_a = jnp.where(odd_token, zero, quad)
    even_here = even[0] + pair + quad + jnp.where(split, only_even, both)
    odd_here = odd[0] + pair + quad + jnp.where(split, only_odd, both)
    even_b = quad_b + jnp.where(split, only_even, zero)
    odd_b = quad_b + jnp.where(split, only_even, jnp.where(remainder == 1, both, zero))
    even_a = quad_a + jnp.where(split, only_odd, jnp.where(remainder == 0, both, zero))
    odd_a = quad_a + jnp.where(split, only_odd, zero)
    return even_b, odd_b, even_here, odd_here, even_a, odd_a


def softmax_of(logits):
    top = jnp.maximum(jnp.maximum(logits[0], logits[1]), jnp.maximum(logits[2], logits[3]))
    parts = [jnp.exp(logit - top) for logit in logits]
    total = (parts[0] + parts[1]) + (parts[2] + parts[3])
    return [part / total for part in parts]


def lane_sum(x):
    return jnp.broadcast_to(jnp.sum(x, axis=1, keepdims=True), x.shape)


def byte_windows(ref, rows, lanes):
    return [ref[EDGE + step : EDGE + step + rows, lanes] for step in (-1, 0, 1)]


def load_bytes(before_ref, body_ref, after_ref, wide_ref):
    edge = 2 * EDGE
    size = body_ref.shape[1]
    for number in range(body_ref.shape[2] // LANES):
        lanes = slice(number * LANES, (number + 1) * LANES)
        wide_ref[number, :edge] = before_ref[0, :, lanes].astype(jnp.float32)
        wide_ref[number, edge : edge + size] = body_ref[0, :, lanes].astype(jnp.float32)
        wide_ref[number, edge + size :] = after_ref[0, :, lanes].astype(jnp.float32)


def conv_chunk(wide_ref, xe_ref, xo_ref, ce_ref, co_ref, vec_ref, facts, number):
    lanes = chunk_lanes(number)
    rows = facts[0].shape[0]
    main = slice(EDGE, EDGE + rows)
    xe_ref[main, lanes] = wide_ref[number, pl.ds(0, rows, stride=2)] * facts[0]
    xo_ref[main, lanes] = wide_ref[number, pl.ds(1, rows, stride=2)] * facts[1]
    even_b, even, even_a = byte_windows(xe_ref, rows, lanes)
    odd_b, odd, odd_a = byte_windows(xo_ref, rows, lanes)
    taps = [vec_ref[j : j + 1, lanes] for j in range(KERNEL)]
    conv_even = (
        taps[0] * even_b + taps[1] * odd_b + taps[2] * even + taps[3] * odd + taps[4] * even_a
    )
    conv_odd = (
        taps[0] * odd_b + taps[1] * even + taps[2] * odd + taps[3] * even_a + taps[4] * odd_a
    )
    ce_ref[main, lanes] = conv_even * facts[0]
    co_ref[main, lanes] = conv_odd * facts[1]


def clear_edges(refs, rows):
    for ref in refs:
        zeros = jnp.zeros((EDGE, ref.shape[1]), jnp.float32)
        ref[:EDGE] = zeros
        ref[EDGE + rows :] = zeros


def chunk_lanes(number):
    return pl.ds(pl.multiple_of(number * LANES, LANES), LANES)


def size_weights(logit_ref, remainder, odd_token):
    even = lane_sum(logit_ref[0])
    odd = lane_sum(logit_ref[1])
    six = (shifted(even, -1), shifted(odd, -1), even, odd, shifted(even, 1), shifted(odd, 1))
    logits_even, logits_odd = pooled_scalars(six, remainder, odd_token)
    return softmax_of(logits_even), softmax_of(logits_odd)


def pool_forward_kernel(
    info_ref,
    before_ref,
    body_ref,
    after_ref,
    vec_ref,
    out_ref,
    wide_ref,
    xe_ref,
    xo_ref,
    ce_ref,
    co_ref,
    logit_ref,
    coef_ref,
    square_ref,
):
    piece = pl.program_id(0)
    width = body_ref.shape[2]
    tokens = body_ref.shape[1] // 2
    rows = tokens + 2 * EDGE
    chunks = width // LANES
    facts = byte_facts(info_ref[0], info_ref[1 + piece], rows)
    load_bytes(before_ref, body_ref, after_ref, wide_ref)
    clear_edges((xe_ref, xo_ref, ce_ref, co_ref), rows)
    logit_ref[...] = jnp.zeros_like(logit_ref)
    main = slice(EDGE, EDGE + rows)

    def first_pass(number, carry):
        lanes = chunk_lanes(number)
        conv_chunk(wide_ref, xe_ref, xo_ref, ce_ref, co_ref, vec_ref, facts, number)
        scorer = vec_ref[KERNEL : KERNEL + 1, lanes]
        logit_ref[0] = logit_ref[0] + ce_ref[main, lanes] * scorer
        logit_ref[1] = logit_ref[1] + co_ref[main, lanes] * scorer
        return carry

    lax.fori_loop(0, chunks, first_pass, 0)
    remainder, odd_token = facts[2:]
    even, odd = size_weights(logit_ref, remainder, odd_token)
    spread = spread_scalars(even, odd, remainder, odd_token)
    for k in range(6):
        coef_ref[k] = 0.5 * spread[k][EDGE : EDGE + tokens]
    square_ref[...] = jnp.zeros_like(square_ref)

    def second_pass(number, carry):
        lanes = chunk_lanes(number)
        total = None
        for step in range(3):
            start = 2 * EDGE + step - 1
            for parity, ref in ((0, ce_ref), (1, co_ref)):
                term = coef_ref[2 * step + parity] * ref[start : start + tokens, lanes]
                total = term if total is None else total + term
        xe_ref[:tokens, lanes] = total
        square_ref[...] = square_ref[...] + total * total
        return carry

    lax.fori_loop(0, chunks, second_pass, 0)
    scale = lax.rsqrt(lane_sum(square_ref[...]) * (1.0 / width) + norm_eps)
    square_ref[...] = scale

    def third_pass(number, carry):
        lanes = chunk_lanes(number)
        gain = vec_ref[KERNEL + 1 : KERNEL + 2, lanes]
        out_ref[0, :tokens, lanes] = (
            xe_ref[:tokens, lanes] * square_ref[...] * gain
        ).astype(jnp.bfloat16)
        return carry

    lax.fori_loop(0, chunks, third_pass, 0)
    row = jnp.transpose(scale)[: 2 * EDGE]
    top = row.astype(jnp.bfloat16).astype(jnp.float32)
    line = lax.broadcasted_iota(jnp.int32, row.shape, 0)
    tail = jnp.where(line == 0, top, jnp.where(line == 1, row - top, 0.0)).astype(jnp.bfloat16)
    rest = jnp.zeros((2 * EDGE, width - tokens), jnp.bfloat16)
    out_ref[0, tokens:] = jnp.concatenate([tail, rest], axis=1)


def pool_forward(info, before, body, after, vectors):
    count, size, width = body.shape
    tokens = size // 2
    rows = tokens + 2 * EDGE
    assert tokens % LANES == 0 and tokens < width
    wide = pltpu.VMEM((width // LANES, size + 4 * EDGE, LANES), jnp.float32)
    tall = pltpu.VMEM((rows + 2 * EDGE, width), jnp.float32)
    edge = pl.BlockSpec((1, 2 * EDGE, width), lambda p, _: (p, 0, 0))
    return pl.pallas_call(
        pool_forward_kernel,
        name="pool_forward",
        grid_spec=pltpu.PrefetchScalarGridSpec(
            num_scalar_prefetch=1,
            grid=(count,),
            in_specs=[
                edge,
                pl.BlockSpec((1, size, width), lambda p, _: (p, 0, 0)),
                edge,
                pl.BlockSpec((8, width), lambda p, _: (0, 0)),
            ],
            out_specs=pl.BlockSpec((1, tokens + 2 * EDGE, width), lambda p, _: (p, 0, 0)),
            scratch_shapes=[
                wide,
                tall,
                tall,
                tall,
                tall,
                pltpu.VMEM((2, rows, LANES), jnp.float32),
                pltpu.VMEM((6, tokens, LANES), jnp.float32),
                pltpu.VMEM((tokens, LANES), jnp.float32),
            ],
        ),
        out_shape=jax.ShapeDtypeStruct((count, tokens + 2 * EDGE, width), jnp.bfloat16),
        compiler_params=pltpu.CompilerParams(vmem_limit_bytes=48 << 20),
    )(info, before, body, after, vectors)


def pool_backward_kernel(
    info_ref,
    before_ref,
    body_ref,
    after_ref,
    grad_before_ref,
    grad_ref,
    grad_after_ref,
    vec_ref,
    embed_ref,
    small_ref,
    wide_ref,
    xe_ref,
    xo_ref,
    ce_ref,
    co_ref,
    dh_ref,
    de_ref,
    do_ref,
    logit_ref,
    dots_ref,
    coef_ref,
    pair_ref,
):
    piece = pl.program_id(0)
    width = body_ref.shape[2]
    tokens = body_ref.shape[1] // 2
    rows = tokens + 2 * EDGE
    chunks = width // LANES
    f32 = jnp.float32
    facts = byte_facts(info_ref[0], info_ref[1 + piece], rows)
    load_bytes(before_ref, body_ref, after_ref, wide_ref)
    clear_edges((xe_ref, xo_ref, ce_ref, co_ref, dh_ref, de_ref, do_ref), rows)
    dh_ref[EDGE : 2 * EDGE] = grad_before_ref[0].astype(f32)
    dh_ref[2 * EDGE : 2 * EDGE + tokens] = grad_ref[0].astype(f32)
    dh_ref[2 * EDGE + tokens : 3 * EDGE + tokens] = grad_after_ref[0].astype(f32)
    logit_ref[...] = jnp.zeros_like(logit_ref)
    dots_ref[...] = jnp.zeros_like(dots_ref)
    main = slice(EDGE, EDGE + rows)

    def first_pass(number, carry):
        lanes = chunk_lanes(number)
        conv_chunk(wide_ref, xe_ref, xo_ref, ce_ref, co_ref, vec_ref, facts, number)
        scorer = vec_ref[KERNEL : KERNEL + 1, lanes]
        logit_ref[0] = logit_ref[0] + ce_ref[main, lanes] * scorer
        logit_ref[1] = logit_ref[1] + co_ref[main, lanes] * scorer
        grad = dh_ref[main, lanes]
        for step in range(3):
            start = EDGE + step - 1
            for parity, ref in ((0, ce_ref), (1, co_ref)):
                k = 2 * step + parity
                dots_ref[k] = dots_ref[k] + grad * ref[start : start + rows, lanes]
        return carry

    lax.fori_loop(0, chunks, first_pass, 0)
    remainder, odd_token = facts[2:]
    even, odd = size_weights(logit_ref, remainder, odd_token)
    six = [0.5 * lane_sum(dots_ref[k]) for k in range(6)]
    grads_even, grads_odd = pooled_scalars(six, remainder, odd_token)

    def logit_grads(weights, grads):
        mean = (weights[0] * grads[0] + weights[1] * grads[1]) + (
            weights[2] * grads[2] + weights[3] * grads[3]
        )
        return [weight * (grad - mean) for weight, grad in zip(weights, grads)]

    spread = spread_scalars(even, odd, remainder, odd_token)
    steer = spread_scalars(
        logit_grads(even, grads_even), logit_grads(odd, grads_odd), remainder, odd_token
    )
    for k in range(6):
        step = k // 2 - 1
        coef_ref[k] = 0.5 * shifted(spread[k], -step)
    coef_ref[6] = steer[2] + shifted(steer[4], -1) + shifted(steer[0], 1)
    coef_ref[7] = steer[3] + shifted(steer[5], -1) + shifted(steer[1], 1)

    def second_pass(number, carry):
        lanes = chunk_lanes(number)
        scorer = vec_ref[KERNEL : KERNEL + 1, lanes]
        grad_b, grad, grad_a = byte_windows(dh_ref, rows, lanes)
        for parity, live, ref in ((0, facts[0], de_ref), (1, facts[1], do_ref)):
            total = (
                coef_ref[parity] * grad_a
                + coef_ref[2 + parity] * grad
                + coef_ref[4 + parity] * grad_b
                + coef_ref[6 + parity] * scorer
            )
            ref[main, lanes] = total * live
        own = slice(2 * EDGE, 2 * EDGE + tokens)
        before = slice(2 * EDGE - 1, 2 * EDGE - 1 + tokens)
        after = slice(2 * EDGE + 1, 2 * EDGE + 1 + tokens)
        taps = [vec_ref[j : j + 1, lanes] for j in range(KERNEL)]
        even_b, even, even_a = [de_ref[part, lanes] for part in (before, own, after)]
        odd_b, odd, odd_a = [do_ref[part, lanes] for part in (before, own, after)]
        inner = slice(EDGE, EDGE + tokens)
        pair_ref[pl.ds(0, tokens, stride=2)] = facts[0][inner] * (
            taps[0] * even_a + taps[1] * odd + taps[2] * even + taps[3] * odd_b + taps[4] * even_b
        )
        pair_ref[pl.ds(1, tokens, stride=2)] = facts[1][inner] * (
            taps[0] * odd_a + taps[1] * even_a + taps[2] * odd + taps[3] * even + taps[4] * odd_b
        )
        embed_ref[0, :, lanes] = pair_ref[...]
        x_even = [xe_ref[part, lanes] for part in (before, own, after)]
        x_odd = [xo_ref[part, lanes] for part in (before, own, after)]
        terms = [
            even * x_even[0] + odd * x_odd[0],
            even * x_odd[0] + odd * x_even[1],
            even * x_even[1] + odd * x_odd[1],
            even * x_odd[1] + odd * x_even[2],
            even * x_even[2] + odd * x_odd[2],
            coef_ref[6, inner] * ce_ref[own, lanes] + coef_ref[7, inner] * co_ref[own, lanes],
        ]
        sums = [jnp.sum(term, axis=0, keepdims=True) for term in terms]
        sums = sums + [jnp.zeros_like(sums[0])] * (8 - len(sums))
        small_ref[0, :, lanes] = jnp.concatenate(sums, axis=0)
        return carry

    lax.fori_loop(0, chunks, second_pass, 0)


def pool_backward(info, before, body, after, grad_before, grad, grad_after, vectors):
    count, size, width = body.shape
    tokens = size // 2
    rows = tokens + 2 * EDGE
    wide = pltpu.VMEM((width // LANES, size + 4 * EDGE, LANES), jnp.float32)
    tall = pltpu.VMEM((rows + 2 * EDGE, width), jnp.float32)
    edge = pl.BlockSpec((1, 2 * EDGE, width), lambda p, _: (p, 0, 0))
    grad_edge = pl.BlockSpec((1, EDGE, width), lambda p, _: (p, 0, 0))
    return pl.pallas_call(
        pool_backward_kernel,
        name="pool_backward",
        grid_spec=pltpu.PrefetchScalarGridSpec(
            num_scalar_prefetch=1,
            grid=(count,),
            in_specs=[
                edge,
                pl.BlockSpec((1, size, width), lambda p, _: (p, 0, 0)),
                edge,
                grad_edge,
                pl.BlockSpec((1, tokens, width), lambda p, _: (p, 0, 0)),
                grad_edge,
                pl.BlockSpec((8, width), lambda p, _: (0, 0)),
            ],
            out_specs=[
                pl.BlockSpec((1, size, width), lambda p, _: (p, 0, 0)),
                pl.BlockSpec((1, 8, width), lambda p, _: (p, 0, 0)),
            ],
            scratch_shapes=[wide]
            + [tall] * 7
            + [
                pltpu.VMEM((2, rows, LANES), jnp.float32),
                pltpu.VMEM((6, rows, LANES), jnp.float32),
                pltpu.VMEM((8, rows, LANES), jnp.float32),
                pltpu.VMEM((size, LANES), jnp.float32),
            ],
        ),
        out_shape=[
            jax.ShapeDtypeStruct((count, size, width), jnp.float32),
            jax.ShapeDtypeStruct((count, 8, width), jnp.float32),
        ],
        compiler_params=pltpu.CompilerParams(vmem_limit_bytes=56 << 20),
    )(info, before, body, after, grad_before, grad, grad_after, vectors)


def bits_of(axis):
    size = lax.axis_size(axis)
    count = size.bit_length() - 1
    assert 1 << count == size
    return count


def stage_orders():
    dp_bits, seq_bits = (bits_of("dp"), bits_of("seq"))
    along_seq = [("seq", bit) for bit in reversed(range(seq_bits))]
    across = [("dp", bit) for bit in range(1, dp_bits)]
    cores = [("dp", 0)]
    return (along_seq + across[::-1] + cores, along_seq + across + cores)


def place_of(axis, bit):
    dp_bits, seq_bits = (bits_of("dp"), bits_of("seq"))
    return dp_bits - 1 - bit if axis == "dp" else dp_bits + seq_bits - 1 - bit


def swap_bit(x, axis, bit):
    size = lax.axis_size(axis)
    return lax.ppermute(x, axis, [(i, i ^ (1 << bit)) for i in range(size)])


def own_bit(axis, bit):
    return (lax.axis_index(axis) >> bit) & 1


def gather_all(x, order):
    held = []
    whole = x
    for axis, bit in order:
        place = place_of(axis, bit)
        dim = sum(other < place for other in held)
        arrived = swap_bit(whole, axis, bit)
        upper = own_bit(axis, bit) == 1
        whole = jnp.stack(
            [jnp.where(upper, arrived, whole), jnp.where(upper, whole, arrived)], axis=dim
        )
        held.append(place)
    return whole.reshape((1 << len(order),) + x.shape)


def scatter_sum(blocks, order):
    shape = blocks.shape[1:]
    part = blocks.reshape((2,) * len(order) + shape)
    held = list(range(len(order)))
    for number, (axis, bit) in enumerate(order[::-1]):
        place = place_of(axis, bit)
        dim = held.index(place)
        held.remove(place)
        mine = own_bit(axis, bit)
        leaving = lax.dynamic_index_in_dim(part, 1 - mine, dim, keepdims=False)
        staying = lax.dynamic_index_in_dim(part, mine, dim, keepdims=False)
        arrived = swap_bit(leaving.astype(jnp.bfloat16), axis, bit)
        part = staying.astype(jnp.float32) + arrived.astype(jnp.float32)
        if number < len(order) - 1:
            part = part.astype(jnp.bfloat16)
    return part


def sum_all(x, order):
    for axis, bit in order[::-1]:
        x = x + swap_bit(x, axis, bit)
    return x


def to_chips(pieces):
    count = pieces.shape[0]
    dp_size, seq_size = (lax.axis_size("dp"), lax.axis_size("seq"))
    seq_index = lax.axis_index("seq")
    arrived = []
    for phase in range(count):
        pairs = chip_pairs(dp_size, seq_size, count, phase)
        leaving = lax.dynamic_index_in_dim(pieces, (seq_index + phase) % count, 0, keepdims=False)
        arrived.append(lax.ppermute(leaving, ("dp", "seq"), pairs))
    stacked = jnp.stack(arrived)
    number = seq_index % count
    return jnp.concatenate(
        [
            lax.dynamic_index_in_dim(stacked, (number - r) % count, 0, keepdims=False)
            for r in range(count)
        ],
        axis=0,
    )


def from_chips(tokens, count):
    dp_size, seq_size = (lax.axis_size("dp"), lax.axis_size("seq"))
    seq_index = lax.axis_index("seq")
    number = seq_index % count
    split = tokens.reshape((count, tokens.shape[0] // count) + tokens.shape[1:])
    arrived = []
    for phase in range(count):
        pairs = [(j, i) for i, j in chip_pairs(dp_size, seq_size, count, phase)]
        leaving = lax.dynamic_index_in_dim(split, (number - phase) % count, 0, keepdims=False)
        arrived.append(lax.ppermute(leaving, ("dp", "seq"), pairs))
    stacked = jnp.stack(arrived)
    return jnp.stack(
        [
            lax.dynamic_index_in_dim(stacked, (j - seq_index) % count, 0, keepdims=False)
            for j in range(count)
        ]
    )


def chip_pairs(dp_size, seq_size, count, phase):
    pairs = []
    for dp in range(dp_size):
        for seq in range(seq_size):
            core_to = seq // count
            seq_to = dp % 2 * count + (seq + phase) % count
            pairs.append((dp * seq_size + seq, (dp // 2 * 2 + core_to) * seq_size + seq_to))
    return pairs


TILE = 128
AUG = 16


def mm(a, b):
    return jnp.dot(a, b, preferred_element_type=jnp.float32)


def mm_nt(a, b):
    return lax.dot_general(a, b, (((1,), (1,)), ((), ())), preferred_element_type=jnp.float32)


def mm_tn(a, b):
    return lax.dot_general(a, b, (((0,), (0,)), ((), ())), preferred_element_type=jnp.float32)


def one_head(pair_rows, a):
    zeros = jnp.zeros((HEAD, pair_rows.shape[1]), pair_rows.dtype)
    half = pair_rows[a * HEAD : (a + 1) * HEAD]
    return jnp.concatenate([half, zeros] if a == 0 else [zeros, half], axis=0)


def near_rows(first_tile, i, d):
    return pl.ds(pl.multiple_of((first_tile + (i + d)) * TILE, TILE), TILE)


def split_rows(base, row):
    low, f32 = (jnp.bfloat16, jnp.float32)
    top = row.astype(low).astype(f32)
    middle = (row - top).astype(low).astype(f32)
    bottom = row - top - middle
    line = lax.broadcasted_iota(jnp.int32, base.shape, 0)
    return jnp.where(
        line == 9, -top, jnp.where(line == 10, -middle, jnp.where(line == 11, -bottom, base))
    ).astype(low)


def attn_forward_kernel(
    first_ref, q_ref, k_ref, ka_ref, v_ref, far_ref, bias_ref, out_ref, lse_ref, s_ref
):
    keys = k_ref.shape[0]
    tokens = q_ref.shape[1]
    lhs = jnp.concatenate([k_ref[...], ka_ref[...]], axis=1)
    pad = jnp.zeros((TILE - AUG, tokens), jnp.bfloat16)
    first = first_ref[0]
    for a in range(2):
        rhs = jnp.concatenate([one_head(q_ref[...], a), far_ref[a], pad], axis=0)
        s_ref[TILE : TILE + keys] = mm(lhs, rhs)
        for i in range(tokens // TILE):
            for d in range(3):
                rows = near_rows(first, i, d)
                lanes = slice(i * TILE, (i + 1) * TILE)
                s_ref[rows, lanes] = s_ref[rows, lanes] + bias_ref[a, d]
        s = s_ref[TILE : TILE + keys]
        row_max = jnp.max(s, axis=0, keepdims=True)
        probs = jnp.exp(s - row_max).astype(jnp.bfloat16)
        v_rows = jnp.concatenate(
            [v_ref[a * HEAD : (a + 1) * HEAD], jnp.ones((AUG, keys), jnp.bfloat16)], axis=0
        )
        both = mm(v_rows, probs)
        total = both[HEAD : HEAD + 1]
        out_ref[a * HEAD : (a + 1) * HEAD] = (both[:HEAD] / total).astype(jnp.bfloat16)
        lse_ref[0, a : a + 1] = row_max + jnp.log(total)


def attn_forward(first, q_t, keys, key_aug, v_t, far, bias):
    width, tokens = q_t.shape
    key_count = keys.shape[0]
    pairs = width // TILE
    return pl.pallas_call(
        attn_forward_kernel,
        name="attn_forward",
        grid_spec=pltpu.PrefetchScalarGridSpec(
            num_scalar_prefetch=1,
            grid=(pairs,),
            in_specs=[
                pl.BlockSpec((TILE, tokens), lambda h, _: (h, 0)),
                pl.BlockSpec((key_count, TILE), lambda h, _: (0, h)),
                pl.BlockSpec((key_count, TILE), lambda h, _: (0, 0)),
                pl.BlockSpec((TILE, key_count), lambda h, _: (h, 0)),
                pl.BlockSpec((2, AUG, tokens), lambda h, _: (h, 0, 0)),
                pl.BlockSpec((2, 3, TILE, TILE), lambda h, _: (h, 0, 0, 0)),
            ],
            out_specs=[
                pl.BlockSpec((TILE, tokens), lambda h, _: (h, 0)),
                pl.BlockSpec((1, 2, tokens), lambda h, _: (h, 0, 0)),
            ],
            scratch_shapes=[pltpu.VMEM((key_count + 2 * TILE, tokens), jnp.float32)],
        ),
        out_shape=[
            jax.ShapeDtypeStruct((width, tokens), jnp.bfloat16),
            jax.ShapeDtypeStruct((pairs, 2, tokens), jnp.float32),
        ],
        compiler_params=pltpu.CompilerParams(vmem_limit_bytes=48 << 20),
    )(first, q_t, keys, key_aug, v_t, far, bias)


def attn_backward_kernel(
    first_ref,
    q_ref,
    do_ref,
    out_ref,
    lse_ref,
    k_ref,
    v_ref,
    kt_ref,
    ka_ref,
    block_ref,
    far_ref,
    bias_ref,
    dq_ref,
    dk_ref,
    dv_ref,
    near_ref,
    sums_ref,
    s_ref,
    ds_ref,
    p_ref,
):
    keys = k_ref.shape[0]
    tokens = q_ref.shape[1]
    f32, low = (jnp.float32, jnp.bfloat16)
    first = first_ref[0]
    main = slice(TILE, TILE + keys)
    k_lhs = jnp.concatenate([k_ref[...], ka_ref[...]], axis=1)
    v_lhs = jnp.concatenate([v_ref[...], ka_ref[...]], axis=1)
    pad = jnp.zeros((TILE - AUG, tokens), low)
    edge = jnp.zeros((TILE, tokens), low)
    q_heads = [one_head(q_ref[...], a) for a in range(2)]
    do_heads = [one_head(do_ref[...], a) for a in range(2)]
    for a in range(2):
        head = slice(a * HEAD, (a + 1) * HEAD)
        aug = split_rows(far_ref[a].astype(f32), lse_ref[0, a : a + 1])
        s_ref[main] = mm(k_lhs, jnp.concatenate([q_heads[a], aug, pad], axis=0))
        for i in range(tokens // TILE):
            for d in range(3):
                rows = near_rows(first, i, d)
                lanes = slice(i * TILE, (i + 1) * TILE)
                s_ref[rows, lanes] = s_ref[rows, lanes] + bias_ref[a, d]
        probs = jnp.exp(s_ref[main])
        p_ref[a] = probs.astype(low)
        row_dot = jnp.sum(
            do_ref[head].astype(f32) * out_ref[head].astype(f32), axis=0, keepdims=True
        )
        aug = split_rows(jnp.zeros((AUG, tokens), f32), row_dot)
        grad_probs = mm(v_lhs, jnp.concatenate([do_heads[a], aug, pad], axis=0))
        ds_ref[a, main] = (probs * grad_probs).astype(low)
        ds_ref[a, :TILE] = edge
        ds_ref[a, TILE + keys :] = edge
        left = jnp.concatenate([kt_ref[head], block_ref[...]], axis=0)
        both = mm(left, ds_ref[a, main])
        dq_ref[head] = both[:HEAD].astype(low)
        sums_ref[0, a] = both[HEAD:]
        for d in range(3):
            total = None
            for i in range(tokens // TILE):
                rows = near_rows(first, i, d)
                term = ds_ref[a, rows, i * TILE : (i + 1) * TILE].astype(f32)
                total = term if total is None else total + term
            near_ref[a, d] = total
    dk_ref[...] = mm_nt(
        jnp.concatenate([ds_ref[0, main], ds_ref[1, main]], axis=1),
        jnp.concatenate(q_heads, axis=1),
    ).astype(low)
    dv_ref[...] = mm_nt(
        jnp.concatenate([p_ref[0], p_ref[1]], axis=1), jnp.concatenate(do_heads, axis=1)
    ).astype(low)


def attn_backward(first, q_t, do_t, out_t, lse, keys, values, k_t, key_aug, block_rows, far, bias):
    width, tokens = q_t.shape
    key_count = keys.shape[0]
    pairs = width // TILE
    across = pl.BlockSpec((TILE, tokens), lambda h, _: (h, 0))
    along = pl.BlockSpec((key_count, TILE), lambda h, _: (0, h))
    return pl.pallas_call(
        attn_backward_kernel,
        name="attn_backward",
        grid_spec=pltpu.PrefetchScalarGridSpec(
            num_scalar_prefetch=1,
            grid=(pairs,),
            in_specs=[
                across,
                across,
                across,
                pl.BlockSpec((1, 2, tokens), lambda h, _: (h, 0, 0)),
                along,
                along,
                pl.BlockSpec((TILE, key_count), lambda h, _: (h, 0)),
                pl.BlockSpec((key_count, TILE), lambda h, _: (0, 0)),
                pl.BlockSpec((AUG, key_count), lambda h, _: (0, 0)),
                pl.BlockSpec((2, AUG, tokens), lambda h, _: (h, 0, 0)),
                pl.BlockSpec((2, 3, TILE, TILE), lambda h, _: (h, 0, 0, 0)),
            ],
            out_specs=[
                across,
                along,
                along,
                pl.BlockSpec((2, 3, TILE, TILE), lambda h, _: (h, 0, 0, 0)),
                pl.BlockSpec((1, 2, AUG, tokens), lambda h, _: (h, 0, 0, 0)),
            ],
            scratch_shapes=[
                pltpu.VMEM((key_count + 2 * TILE, tokens), jnp.float32),
                pltpu.VMEM((2, key_count + 2 * TILE, tokens), jnp.bfloat16),
                pltpu.VMEM((2, key_count, tokens), jnp.bfloat16),
            ],
        ),
        out_shape=[
            jax.ShapeDtypeStruct((width, tokens), jnp.bfloat16),
            jax.ShapeDtypeStruct((key_count, width), jnp.bfloat16),
            jax.ShapeDtypeStruct((key_count, width), jnp.bfloat16),
            jax.ShapeDtypeStruct((2 * pairs, 3, TILE, TILE), jnp.float32),
            jax.ShapeDtypeStruct((pairs, 2, AUG, tokens), jnp.float32),
        ],
        compiler_params=pltpu.CompilerParams(vmem_limit_bytes=56 << 20),
    )(first, q_t, do_t, out_t, lse, keys, values, k_t, key_aug, block_rows, far, bias)


def attn_tables(first, tokens, key_count, length, rel_bias):
    low, f32 = (jnp.bfloat16, jnp.float32)
    blocks = key_count // TILE
    assert blocks <= 8
    key_pos = jnp.arange(key_count, dtype=jnp.int32)
    column = jnp.arange(TILE, dtype=jnp.int32)[None, :]
    key_aug = jnp.where(column == (key_pos // TILE)[:, None], 1.0, 0.0)
    dead = jnp.where(2 * key_pos < length, 0.0, -1000000000.0)[:, None]
    key_aug = jnp.where(column == 8, dead, key_aug)
    key_aug = jnp.where((column >= 9) & (column < 12), 1.0, key_aug).astype(low)
    line = jnp.arange(AUG, dtype=jnp.int32)
    block_rows = jnp.where(line[:, None] == (key_pos // TILE)[None, :], 1.0, 0.0).astype(low)
    tile = first + jnp.arange(tokens, dtype=jnp.int32) // TILE
    apart = (line[:, None] - tile[None, :])[None]
    rel_t = rel_bias.astype(f32).T
    before = rel_t[:, BUCKETS // 2 - 1][:, None, None]
    after = rel_t[:, BUCKETS - 1][:, None, None]
    far = jnp.where(apart <= -2, before, jnp.where(apart >= 2, after, 0.0))
    in_use = (line < blocks)[None, :, None]
    far = jnp.where(in_use, far, jnp.where((line == 8)[None, :, None], 1.0, 0.0)).astype(low)
    bias = jnp.einsum("djib,bh->hdji", near_onehot(), rel_bias.astype(f32), precision=highest)
    return key_aug, block_rows, far, bias


def near_onehot():
    step = jnp.arange(TILE, dtype=jnp.int32)
    offset = (
        TILE * (jnp.arange(3, dtype=jnp.int32) - 1)[:, None, None]
        + step[None, :, None]
        - step[None, None, :]
    )
    return (bucket_of(offset)[..., None] == jnp.arange(BUCKETS, dtype=jnp.int32)).astype(
        jnp.float32
    )


def bias_gradient(first, near, sums):
    pairs, _, _, tokens = sums.shape
    close = jnp.einsum("hdji,djib->bh", near, near_onehot(), precision=highest)
    line = jnp.arange(AUG, dtype=jnp.int32)[:, None]
    tile = first + jnp.arange(tokens, dtype=jnp.int32)[None, :] // TILE
    apart = line - tile
    sums = sums.reshape(2 * pairs, AUG, tokens)
    before = jnp.sum(jnp.where(apart <= -2, sums, 0.0), axis=(1, 2))
    after = jnp.sum(jnp.where(apart >= 2, sums, 0.0), axis=(1, 2))
    bucket = jnp.arange(BUCKETS, dtype=jnp.int32)[:, None]
    return (
        close
        + jnp.where(bucket == BUCKETS // 2 - 1, before[None, :], 0.0)
        + jnp.where(bucket == BUCKETS - 1, after[None, :], 0.0)
    )


def shards(
    embeddings,
    lengths,
    cotangent,
    conv_weight,
    scorer,
    gain_attn,
    w_query,
    w_key,
    w_value,
    w_out,
    rel_bias,
    gain_ffn,
    w_gate,
    w_up,
    w_down,
):
    num_micro, num_seqs, local_bytes, model_width = embeddings.shape
    piece_tokens = local_bytes // 2
    count = num_micro * num_seqs
    seq_count = lax.axis_size("seq")
    assert seq_count == 2 * count
    seq_index = lax.axis_index("seq")
    core = lax.axis_index("dp") % 2
    device = lax.axis_index("dp") * seq_count + seq_index
    local_tokens = count * piece_tokens
    key_count = 2 * local_tokens
    low, f32 = (jnp.bfloat16, jnp.float32)
    order_a, order_b = stage_orders()
    rows = w_query.shape[0]
    vec_rows = KERNEL + 3

    vectors = jnp.concatenate(
        [conv_weight, scorer[None], gain_attn[None], gain_ffn[None]], axis=0
    )
    vectors = gather_all(vectors, order_a)
    vectors = jnp.swapaxes(vectors, 0, 1).reshape(vec_rows, model_width).astype(f32)
    gain_one, gain_two = (vectors[KERNEL + 1], vectors[KERNEL + 2])

    pieces = embeddings.reshape(count, local_bytes, model_width)
    piece_lengths = lengths.reshape(count)
    bytes_before, bytes_after = neighbour_edges(pieces, 2 * EDGE)
    token_start = seq_index * piece_tokens
    info = jnp.concatenate([token_start.reshape(1).astype(jnp.int32), piece_lengths])
    both_lengths = swap_bit(piece_lengths, "dp", 0)
    both_lengths = jnp.where(
        core == seq_index // count, piece_lengths, both_lengths
    )
    seq_length = lax.dynamic_index_in_dim(both_lengths, seq_index % count, 0, keepdims=False)

    sent = pool_forward(info, bytes_before, pieces, bytes_after, vectors)
    arrived = to_chips(sent).reshape(count, piece_tokens + 2 * EDGE, model_width)
    normed_low = arrived[:, :piece_tokens].reshape(local_tokens, model_width)
    scale = arrived[:, piece_tokens : piece_tokens + 2, :piece_tokens].astype(f32)
    scale = jnp.sum(scale, axis=1).reshape(local_tokens, 1)
    unit = normed_low.astype(f32) / gain_one
    hidden_in = unit / scale
    seed_low = to_chips(cotangent.reshape(count, piece_tokens, model_width))
    seed_grad = seed_low.astype(f32)

    first = gather_all(jnp.concatenate([w_query, w_key], axis=1), order_a)
    second = gather_all(jnp.concatenate([w_value, w_out], axis=1), order_b)
    gate_full = gather_all(w_gate, order_a).reshape(model_width, -1)
    up_full = gather_all(w_up, order_b).reshape(model_width, -1)
    down_full = gather_all(w_down, order_a).reshape(-1, model_width)
    first = first.reshape(model_width, 2 * model_width)
    second = second.reshape(model_width, 2 * model_width)
    query_full, key_full = (first[:, :model_width], first[:, model_width:])
    value_full, out_full = (second[:, :model_width], second[:, model_width:])

    normed_other = swap_bit(normed_low, "dp", 0)
    normed_all = jnp.concatenate(
        [
            jnp.where(core == 0, normed_low, normed_other),
            jnp.where(core == 0, normed_other, normed_low),
        ],
        axis=0,
    )

    first_tile = core * (local_tokens // TILE)
    key_aug, block_rows, far, bias = attn_tables(
        first_tile, local_tokens, key_count, seq_length, rel_bias
    )
    first_ref = first_tile.astype(jnp.int32).reshape(1)

    def project_t(weight, tokens):
        return lax.dot_general(
            weight, tokens, (((0,), (1,)), ((), ())), preferred_element_type=f32
        ).astype(low)

    q_t = project_t(query_full, normed_low)
    k_t = project_t(key_full, normed_all)
    v_t = project_t(value_full, normed_all)
    keys_all = mm(normed_all, key_full).astype(low)
    values_all = mm(normed_all, value_full).astype(low)
    attended_t, lse = attn_forward(first_ref, q_t, keys_all, key_aug, v_t, far, bias)
    after_attn = hidden_in + mm_tn(attended_t, out_full)
    normed_ffn, ffn_pull = jax.vjp(rms_scale, after_attn, gain_two)
    normed_ffn_low = normed_ffn.astype(low)
    gate_value = mm(normed_ffn_low, gate_full)
    up_value = mm(normed_ffn_low, up_full)
    inner_act, gelu_pull = jax.vjp(gelu_gate, gate_value, up_value)
    inner_low = inner_act.astype(low)
    block_out = (after_attn + mm(inner_low, down_full)).astype(low)
    blocks_out = from_chips(block_out, count).reshape(
        num_micro, num_seqs, piece_tokens, model_width
    )

    down_grad = mm_tn(inner_low, seed_low).astype(low)
    down_grad = scatter_sum(down_grad.reshape(-1, w_down.shape[0], model_width), order_b)
    grad_inner = mm_nt(seed_low, down_full)
    grad_gate, grad_up = gelu_pull(grad_inner)
    grad_gate_low = grad_gate.astype(low)
    grad_up_low = grad_up.astype(low)
    gate_grad = mm_tn(normed_ffn_low, grad_gate_low).astype(low)
    gate_grad = scatter_sum(gate_grad.reshape(-1, rows, w_gate.shape[1]), order_a)
    up_grad = mm_tn(normed_ffn_low, grad_up_low).astype(low)
    up_grad = scatter_sum(up_grad.reshape(-1, rows, w_up.shape[1]), order_b)
    grad_normed_ffn = mm_nt(grad_gate_low, gate_full) + mm_nt(grad_up_low, up_full)
    grad_after, gain_ffn_grad = ffn_pull(grad_normed_ffn)
    grad_after = seed_grad + grad_after
    grad_after_low = grad_after.astype(low)
    out_grad = mm(attended_t, grad_after_low).astype(low)
    out_grad = scatter_sum(out_grad.reshape(-1, rows, model_width), order_a)
    grad_attended_t = mm_nt(out_full, grad_after_low).astype(low)
    grad_queries_t, key_terms, value_terms, near, sums = attn_backward(
        first_ref,
        q_t,
        grad_attended_t,
        attended_t,
        lse,
        keys_all,
        values_all,
        k_t,
        key_aug,
        block_rows,
        far,
        bias,
    )
    shared = mm_nt(key_terms, key_full) + mm_nt(value_terms, value_full)
    shared = shared.reshape(2, local_tokens, model_width)
    leaving = lax.dynamic_index_in_dim(shared, 1 - core, 0, keepdims=False).astype(low)
    staying = lax.dynamic_index_in_dim(shared, core, 0, keepdims=False)
    grad_normed = lax.dot_general(
        grad_queries_t, query_full, (((0,), (1,)), ((), ())), preferred_element_type=f32
    ) + staying + swap_bit(leaving, "dp", 0).astype(f32)
    query_grad = lax.dot_general(
        normed_low, grad_queries_t, (((0,), (1,)), ((), ())), preferred_element_type=f32
    ).astype(low)
    query_grad = scatter_sum(query_grad.reshape(-1, rows, model_width), order_b)
    key_grad = mm_tn(normed_all, key_terms).astype(low)
    key_grad = scatter_sum(key_grad.reshape(-1, rows, model_width), order_a)
    value_grad = mm_tn(normed_all, value_terms).astype(low)
    value_grad = scatter_sum(value_grad.reshape(-1, rows, model_width), order_b)
    gained = grad_normed * gain_one
    gain_attn_grad = jnp.sum(grad_normed * unit, axis=0)
    grad_hidden = grad_after + scale * (
        gained - unit * jnp.mean(gained * unit, axis=-1, keepdims=True)
    )
    grad_pieces = from_chips(grad_hidden.astype(low), count)
    grad_before, grad_after_edge = neighbour_edges(grad_pieces, EDGE)
    embed_grad, pool_small = pool_backward(
        info, bytes_before, pieces, bytes_after, grad_before, grad_pieces, grad_after_edge, vectors
    )
    embed_out = embed_grad.reshape(num_micro, num_seqs, local_bytes, model_width)
    pool_small = jnp.sum(pool_small, axis=0)[: KERNEL + 1]
    bias_terms = bias_gradient(first_tile, near, sums)
    bias_row = jnp.pad(bias_terms.reshape(-1), (0, model_width - bias_terms.size))
    small = jnp.concatenate(
        [pool_small, gain_attn_grad[None], gain_ffn_grad[None], bias_row[None]],
        axis=0,
    )
    small = sum_all(small, order_a)
    bias_total = small[vec_rows, : bias_terms.size].reshape(bias_terms.shape)
    own = lax.dynamic_slice_in_dim(small[:vec_rows], device * rows, rows, axis=1)
    return (
        blocks_out,
        embed_out,
        own[:KERNEL],
        own[KERNEL],
        own[KERNEL + 1],
        query_grad,
        key_grad,
        value_grad,
        out_grad,
        bias_total,
        own[KERNEL + 2],
        gate_grad,
        up_grad,
        down_grad,
    )


def solution(mesh):
    return jax.shard_map(
        shards,
        mesh=mesh,
        in_specs=(
            P(None, "dp", "seq", None),
            P(None, "dp"),
            P(None, "dp", "seq", None),
            P(None, ("dp", "seq")),
            P(("dp", "seq")),
            P(("dp", "seq")),
            P(("dp", "seq"), None),
            P(("dp", "seq"), None),
            P(("dp", "seq"), None),
            P(("dp", "seq"), None),
            P(),
            P(("dp", "seq")),
            P(("dp", "seq"), None),
            P(("dp", "seq"), None),
            P(("dp", "seq"), None),
        ),
        out_specs=(
            P(None, "dp", "seq", None),
            P(None, "dp", "seq", None),
            P(None, ("dp", "seq")),
            P(("dp", "seq")),
            P(("dp", "seq")),
            P(("dp", "seq"), None),
            P(("dp", "seq"), None),
            P(("dp", "seq"), None),
            P(("dp", "seq"), None),
            P(),
            P(("dp", "seq")),
            P(("dp", "seq"), None),
            P(("dp", "seq"), None),
            P(("dp", "seq"), None),
        ),
        check_vma=False,
    )
```

```python
import functools

import jax
import jax.numpy as jnp
from jax import lax
from jax.experimental import pallas as pl
from jax.experimental.pallas import tpu as pltpu
from jax.sharding import PartitionSpec as P

HEADS = 12
HEAD = 64
BUCKETS = 32
KERNEL = 5


norm_eps = 1e-06
highest = lax.Precision.HIGHEST
cut_points = (12, 16, 23, 32, 46, 64, 91)


def neighbour_edges(x, width):
    devices, length = (lax.axis_size("seq"), x.shape[1])
    up = [(i, i + 1) for i in range(devices - 1)]
    down = [(j, i) for i, j in up]
    before = lax.ppermute(x[:, length - width :], "seq", up)
    after = lax.ppermute(x[:, :width], "seq", down)
    return before, after


def bucket_of(offset):
    distance = jnp.abs(offset)
    far_bucket = 8 + sum(((distance >= cut_point).astype(jnp.int32) for cut_point in cut_points))
    return jnp.where(distance < 8, distance, far_bucket) + jnp.where(offset > 0, 16, 0)


EDGE = 8
LANES = 128


def shifted(x, step):
    return pltpu.roll(x, (-step) % x.shape[0], 0)


def byte_facts(token_start, length, rows):
    token = token_start - EDGE + lax.broadcasted_iota(jnp.int32, (rows, LANES), 0)
    first = 2 * token
    even_live = jnp.where((first >= 0) & (first < length), 1.0, 0.0)
    odd_live = jnp.where((first + 1 >= 0) & (first + 1 < length), 1.0, 0.0)
    remainder = lax.rem(first + 6 * EDGE, 3)
    odd_token = lax.rem(token + 2 * EDGE, 2) == 1
    return even_live, odd_live, remainder, odd_token


def pooled_scalars(six, remainder, odd_token):
    even_b, odd_b, even, odd, even_a, odd_a = six
    pair = even + odd
    quad = pair + jnp.where(odd_token, even_b + odd_b, even_a + odd_a)
    shared = pair + jnp.where(remainder == 0, even_a, odd_b)
    split = remainder == 2
    triple_even = jnp.where(split, even_b + odd_b + even, shared)
    triple_odd = jnp.where(split, odd + even_a + odd_a, shared)
    third = 1.0 / 3.0
    return (
        (even, 0.5 * pair, third * triple_even, 0.25 * quad),
        (odd, 0.5 * pair, third * triple_odd, 0.25 * quad),
    )


def spread_scalars(even, odd, remainder, odd_token):
    third = 1.0 / 3.0
    pair = 0.5 * (even[1] + odd[1])
    quad = 0.25 * (even[3] + odd[3])
    both = third * (even[2] + odd[2])
    only_even = third * even[2]
    only_odd = third * odd[2]
    split = remainder == 2
    zero = jnp.zeros_like(pair)
    quad_b = jnp.where(odd_token, quad, zero)
    quad_a = jnp.where(odd_token, zero, quad)
    even_here = even[0] + pair + quad + jnp.where(split, only_even, both)
    odd_here = odd[0] + pair + quad + jnp.where(split, only_odd, both)
    even_b = quad_b + jnp.where(split, only_even, zero)
    odd_b = quad_b + jnp.where(split, only_even, jnp.where(remainder == 1, both, zero))
    even_a = quad_a + jnp.where(split, only_odd, jnp.where(remainder == 0, both, zero))
    odd_a = quad_a + jnp.where(split, only_odd, zero)
    return even_b, odd_b, even_here, odd_here, even_a, odd_a


def softmax_of(logits):
    top = jnp.maximum(jnp.maximum(logits[0], logits[1]), jnp.maximum(logits[2], logits[3]))
    parts = [jnp.exp(logit - top) for logit in logits]
    total = (parts[0] + parts[1]) + (parts[2] + parts[3])
    return [part / total for part in parts]


def lane_sum(x):
    return jnp.broadcast_to(jnp.sum(x, axis=1, keepdims=True), x.shape)


def byte_windows(ref, rows, lanes):
    return [ref[EDGE + step : EDGE + step + rows, lanes] for step in (-1, 0, 1)]


def load_bytes(before_ref, body_ref, after_ref, wide_ref):
    edge = 2 * EDGE
    size = body_ref.shape[1]
    for number in range(body_ref.shape[2] // LANES):
        lanes = slice(number * LANES, (number + 1) * LANES)
        wide_ref[number, :edge] = before_ref[0, :, lanes].astype(jnp.float32)
        wide_ref[number, edge : edge + size] = body_ref[0, :, lanes].astype(jnp.float32)
        wide_ref[number, edge + size :] = after_ref[0, :, lanes].astype(jnp.float32)


def conv_chunk(wide_ref, xe_ref, xo_ref, ce_ref, co_ref, vec_ref, facts, number):
    lanes = chunk_lanes(number)
    rows = facts[0].shape[0]
    main = slice(EDGE, EDGE + rows)
    xe_ref[main, lanes] = wide_ref[number, pl.ds(0, rows, stride=2)] * facts[0]
    xo_ref[main, lanes] = wide_ref[number, pl.ds(1, rows, stride=2)] * facts[1]
    even_b, even, even_a = byte_windows(xe_ref, rows, lanes)
    odd_b, odd, odd_a = byte_windows(xo_ref, rows, lanes)
    taps = [vec_ref[j : j + 1, lanes] for j in range(KERNEL)]
    conv_even = (
        taps[0] * even_b + taps[1] * odd_b + taps[2] * even + taps[3] * odd + taps[4] * even_a
    )
    conv_odd = (
        taps[0] * odd_b + taps[1] * even + taps[2] * odd + taps[3] * even_a + taps[4] * odd_a
    )
    ce_ref[main, lanes] = conv_even * facts[0]
    co_ref[main, lanes] = conv_odd * facts[1]


def clear_edges(refs, rows):
    for ref in refs:
        zeros = jnp.zeros((EDGE, ref.shape[1]), jnp.float32)
        ref[:EDGE] = zeros
        ref[EDGE + rows :] = zeros


def chunk_lanes(number):
    return pl.ds(pl.multiple_of(number * LANES, LANES), LANES)


def size_weights(logit_ref, remainder, odd_token):
    even = lane_sum(logit_ref[0])
    odd = lane_sum(logit_ref[1])
    six = (shifted(even, -1), shifted(odd, -1), even, odd, shifted(even, 1), shifted(odd, 1))
    logits_even, logits_odd = pooled_scalars(six, remainder, odd_token)
    return softmax_of(logits_even), softmax_of(logits_odd)


def pool_forward_kernel(
    info_ref,
    before_ref,
    body_ref,
    after_ref,
    vec_ref,
    out_ref,
    wide_ref,
    xe_ref,
    xo_ref,
    ce_ref,
    co_ref,
    logit_ref,
    coef_ref,
    square_ref,
):
    piece = pl.program_id(0)
    width = body_ref.shape[2]
    tokens = body_ref.shape[1] // 2
    rows = tokens + 2 * EDGE
    chunks = width // LANES
    facts = byte_facts(info_ref[0], info_ref[1 + piece], rows)
    load_bytes(before_ref, body_ref, after_ref, wide_ref)
    clear_edges((xe_ref, xo_ref, ce_ref, co_ref), rows)
    logit_ref[...] = jnp.zeros_like(logit_ref)
    main = slice(EDGE, EDGE + rows)

    def first_pass(number, carry):
        lanes = chunk_lanes(number)
        conv_chunk(wide_ref, xe_ref, xo_ref, ce_ref, co_ref, vec_ref, facts, number)
        scorer = vec_ref[KERNEL : KERNEL + 1, lanes]
        logit_ref[0] = logit_ref[0] + ce_ref[main, lanes] * scorer
        logit_ref[1] = logit_ref[1] + co_ref[main, lanes] * scorer
        return carry

    lax.fori_loop(0, chunks, first_pass, 0)
    remainder, odd_token = facts[2:]
    even, odd = size_weights(logit_ref, remainder, odd_token)
    spread = spread_scalars(even, odd, remainder, odd_token)
    for k in range(6):
        coef_ref[k] = 0.5 * spread[k][EDGE : EDGE + tokens]
    square_ref[...] = jnp.zeros_like(square_ref)

    def second_pass(number, carry):
        lanes = chunk_lanes(number)
        total = None
        for step in range(3):
            start = 2 * EDGE + step - 1
            for parity, ref in ((0, ce_ref), (1, co_ref)):
                term = coef_ref[2 * step + parity] * ref[start : start + tokens, lanes]
                total = term if total is None else total + term
        xe_ref[:tokens, lanes] = total
        square_ref[...] = square_ref[...] + total * total
        return carry

    lax.fori_loop(0, chunks, second_pass, 0)
    scale = lax.rsqrt(lane_sum(square_ref[...]) * (1.0 / width) + norm_eps)
    square_ref[...] = scale

    def third_pass(number, carry):
        lanes = chunk_lanes(number)
        gain = vec_ref[KERNEL + 1 : KERNEL + 2, lanes]
        out_ref[0, :tokens, lanes] = (
            xe_ref[:tokens, lanes] * square_ref[...] * gain
        ).astype(jnp.bfloat16)
        return carry

    lax.fori_loop(0, chunks, third_pass, 0)
    row = jnp.transpose(scale)[: 2 * EDGE]
    top = row.astype(jnp.bfloat16).astype(jnp.float32)
    line = lax.broadcasted_iota(jnp.int32, row.shape, 0)
    tail = jnp.where(line == 0, top, jnp.where(line == 1, row - top, 0.0)).astype(jnp.bfloat16)
    rest = jnp.zeros((2 * EDGE, width - tokens), jnp.bfloat16)
    out_ref[0, tokens:] = jnp.concatenate([tail, rest], axis=1)


def pool_forward(info, before, body, after, vectors):
    count, size, width = body.shape
    tokens = size // 2
    rows = tokens + 2 * EDGE
    assert tokens % LANES == 0 and tokens < width
    wide = pltpu.VMEM((width // LANES, size + 4 * EDGE, LANES), jnp.float32)
    tall = pltpu.VMEM((rows + 2 * EDGE, width), jnp.float32)
    edge = pl.BlockSpec((1, 2 * EDGE, width), lambda p, _: (p, 0, 0))
    return pl.pallas_call(
        pool_forward_kernel,
        name="pool_forward",
        cost_estimate=pl.CostEstimate(
            flops=count * (4 << 30), bytes_accessed=1 << 20, transcendentals=0
        ),
        grid_spec=pltpu.PrefetchScalarGridSpec(
            num_scalar_prefetch=1,
            grid=(count,),
            in_specs=[
                edge,
                pl.BlockSpec((1, size, width), lambda p, _: (p, 0, 0)),
                edge,
                pl.BlockSpec((8, width), lambda p, _: (0, 0)),
            ],
            out_specs=pl.BlockSpec((1, tokens + 2 * EDGE, width), lambda p, _: (p, 0, 0)),
            scratch_shapes=[
                wide,
                tall,
                tall,
                tall,
                tall,
                pltpu.VMEM((2, rows, LANES), jnp.float32),
                pltpu.VMEM((6, tokens, LANES), jnp.float32),
                pltpu.VMEM((tokens, LANES), jnp.float32),
            ],
        ),
        out_shape=jax.ShapeDtypeStruct((count, tokens + 2 * EDGE, width), jnp.bfloat16),
        compiler_params=pltpu.CompilerParams(vmem_limit_bytes=48 << 20),
    )(info, before, body, after, vectors)


def pool_backward_kernel(
    info_ref,
    before_ref,
    body_ref,
    after_ref,
    grad_before_ref,
    grad_ref,
    grad_after_ref,
    vec_ref,
    embed_ref,
    small_ref,
    wide_ref,
    xe_ref,
    xo_ref,
    ce_ref,
    co_ref,
    dh_ref,
    de_ref,
    do_ref,
    logit_ref,
    dots_ref,
    coef_ref,
    pair_ref,
):
    piece = pl.program_id(0)
    width = body_ref.shape[2]
    tokens = body_ref.shape[1] // 2
    rows = tokens + 2 * EDGE
    chunks = width // LANES
    f32 = jnp.float32
    facts = byte_facts(info_ref[0], info_ref[1 + piece], rows)
    load_bytes(before_ref, body_ref, after_ref, wide_ref)
    clear_edges((xe_ref, xo_ref, ce_ref, co_ref, dh_ref, de_ref, do_ref), rows)
    dh_ref[EDGE : 2 * EDGE] = grad_before_ref[0].astype(f32)
    dh_ref[2 * EDGE : 2 * EDGE + tokens] = grad_ref[0].astype(f32)
    dh_ref[2 * EDGE + tokens : 3 * EDGE + tokens] = grad_after_ref[0].astype(f32)
    logit_ref[...] = jnp.zeros_like(logit_ref)
    dots_ref[...] = jnp.zeros_like(dots_ref)
    main = slice(EDGE, EDGE + rows)

    def first_pass(number, carry):
        lanes = chunk_lanes(number)
        conv_chunk(wide_ref, xe_ref, xo_ref, ce_ref, co_ref, vec_ref, facts, number)
        scorer = vec_ref[KERNEL : KERNEL + 1, lanes]
        logit_ref[0] = logit_ref[0] + ce_ref[main, lanes] * scorer
        logit_ref[1] = logit_ref[1] + co_ref[main, lanes] * scorer
        grad = dh_ref[main, lanes]
        for step in range(3):
            start = EDGE + step - 1
            for parity, ref in ((0, ce_ref), (1, co_ref)):
                k = 2 * step + parity
                dots_ref[k] = dots_ref[k] + grad * ref[start : start + rows, lanes]
        return carry

    lax.fori_loop(0, chunks, first_pass, 0)
    remainder, odd_token = facts[2:]
    even, odd = size_weights(logit_ref, remainder, odd_token)
    six = [0.5 * lane_sum(dots_ref[k]) for k in range(6)]
    grads_even, grads_odd = pooled_scalars(six, remainder, odd_token)

    def logit_grads(weights, grads):
        mean = (weights[0] * grads[0] + weights[1] * grads[1]) + (
            weights[2] * grads[2] + weights[3] * grads[3]
        )
        return [weight * (grad - mean) for weight, grad in zip(weights, grads)]

    spread = spread_scalars(even, odd, remainder, odd_token)
    steer = spread_scalars(
        logit_grads(even, grads_even), logit_grads(odd, grads_odd), remainder, odd_token
    )
    for k in range(6):
        step = k // 2 - 1
        coef_ref[k] = 0.5 * shifted(spread[k], -step)
    coef_ref[6] = steer[2] + shifted(steer[4], -1) + shifted(steer[0], 1)
    coef_ref[7] = steer[3] + shifted(steer[5], -1) + shifted(steer[1], 1)

    def second_pass(number, carry):
        lanes = chunk_lanes(number)
        scorer = vec_ref[KERNEL : KERNEL + 1, lanes]
        grad_b, grad, grad_a = byte_windows(dh_ref, rows, lanes)
        for parity, live, ref in ((0, facts[0], de_ref), (1, facts[1], do_ref)):
            total = (
                coef_ref[parity] * grad_a
                + coef_ref[2 + parity] * grad
                + coef_ref[4 + parity] * grad_b
                + coef_ref[6 + parity] * scorer
            )
            ref[main, lanes] = total * live
        own = slice(2 * EDGE, 2 * EDGE + tokens)
        before = slice(2 * EDGE - 1, 2 * EDGE - 1 + tokens)
        after = slice(2 * EDGE + 1, 2 * EDGE + 1 + tokens)
        taps = [vec_ref[j : j + 1, lanes] for j in range(KERNEL)]
        even_b, even, even_a = [de_ref[part, lanes] for part in (before, own, after)]
        odd_b, odd, odd_a = [do_ref[part, lanes] for part in (before, own, after)]
        inner = slice(EDGE, EDGE + tokens)
        pair_ref[pl.ds(0, tokens, stride=2)] = facts[0][inner] * (
            taps[0] * even_a + taps[1] * odd + taps[2] * even + taps[3] * odd_b + taps[4] * even_b
        )
        pair_ref[pl.ds(1, tokens, stride=2)] = facts[1][inner] * (
            taps[0] * odd_a + taps[1] * even_a + taps[2] * odd + taps[3] * even + taps[4] * odd_b
        )
        embed_ref[0, :, lanes] = pair_ref[...]
        x_even = [xe_ref[part, lanes] for part in (before, own, after)]
        x_odd = [xo_ref[part, lanes] for part in (before, own, after)]
        terms = [
            even * x_even[0] + odd * x_odd[0],
            even * x_odd[0] + odd * x_even[1],
            even * x_even[1] + odd * x_odd[1],
            even * x_odd[1] + odd * x_even[2],
            even * x_even[2] + odd * x_odd[2],
            coef_ref[6, inner] * ce_ref[own, lanes] + coef_ref[7, inner] * co_ref[own, lanes],
        ]
        sums = [jnp.sum(term, axis=0, keepdims=True) for term in terms]
        sums = sums + [jnp.zeros_like(sums[0])] * (8 - len(sums))
        small_ref[0, :, lanes] = jnp.concatenate(sums, axis=0)
        return carry

    lax.fori_loop(0, chunks, second_pass, 0)


def pool_backward(info, before, body, after, grad_before, grad, grad_after, vectors):
    count, size, width = body.shape
    tokens = size // 2
    rows = tokens + 2 * EDGE
    wide = pltpu.VMEM((width // LANES, size + 4 * EDGE, LANES), jnp.float32)
    tall = pltpu.VMEM((rows + 2 * EDGE, width), jnp.float32)
    edge = pl.BlockSpec((1, 2 * EDGE, width), lambda p, _: (p, 0, 0))
    grad_edge = pl.BlockSpec((1, EDGE, width), lambda p, _: (p, 0, 0))
    return pl.pallas_call(
        pool_backward_kernel,
        name="pool_backward",
        cost_estimate=pl.CostEstimate(
            flops=count * (10 << 30), bytes_accessed=1 << 20, transcendentals=0
        ),
        grid_spec=pltpu.PrefetchScalarGridSpec(
            num_scalar_prefetch=1,
            grid=(count,),
            in_specs=[
                edge,
                pl.BlockSpec((1, size, width), lambda p, _: (p, 0, 0)),
                edge,
                grad_edge,
                pl.BlockSpec((1, tokens, width), lambda p, _: (p, 0, 0)),
                grad_edge,
                pl.BlockSpec((8, width), lambda p, _: (0, 0)),
            ],
            out_specs=[
                pl.BlockSpec((1, size, width), lambda p, _: (p, 0, 0)),
                pl.BlockSpec((1, 8, width), lambda p, _: (p, 0, 0)),
            ],
            scratch_shapes=[wide]
            + [tall] * 7
            + [
                pltpu.VMEM((2, rows, LANES), jnp.float32),
                pltpu.VMEM((6, rows, LANES), jnp.float32),
                pltpu.VMEM((8, rows, LANES), jnp.float32),
                pltpu.VMEM((size, LANES), jnp.float32),
            ],
        ),
        out_shape=[
            jax.ShapeDtypeStruct((count, size, width), jnp.float32),
            jax.ShapeDtypeStruct((count, 8, width), jnp.float32),
        ],
        compiler_params=pltpu.CompilerParams(vmem_limit_bytes=56 << 20),
    )(info, before, body, after, grad_before, grad, grad_after, vectors)


def bits_of(axis):
    size = lax.axis_size(axis)
    count = size.bit_length() - 1
    assert 1 << count == size
    return count


def stage_phases():
    dp_bits, seq_bits = (bits_of("dp"), bits_of("seq"))
    along = [("seq", bit) for bit in reversed(range(seq_bits))]
    low_half = [("dp", bit) for bit in range(1, 1 + (dp_bits - 1) // 2)]
    high_half = [("dp", bit) for bit in range(1 + (dp_bits - 1) // 2, dp_bits)]
    ends = ([along[:1], along[1:]], [[("dp", 0)]])
    return (ends[0] + [high_half, low_half] + ends[1], ends[0] + [low_half, high_half] + ends[1])


def place_of(axis, bit):
    dp_bits, seq_bits = (bits_of("dp"), bits_of("seq"))
    return dp_bits - 1 - bit if axis == "dp" else dp_bits + seq_bits - 1 - bit


def swap_bit(x, axis, bit):
    size = lax.axis_size(axis)
    return lax.ppermute(x, axis, [(i, i ^ (1 << bit)) for i in range(size)])


def own_bit(axis, bit):
    return (lax.axis_index(axis) >> bit) & 1


class Chain:
    def __init__(self):
        self.noted = None

    def after(self, *values):
        if self.noted is not None:
            values = lax.optimization_barrier(values + (self.noted,))[:-1]
        return values if len(values) > 1 else values[0]

    def note(self, value):
        self.noted = value
        return value


class Gathering:
    def __init__(self, chain, block, phases, held=()):
        self.chain, self.whole, self.held = (chain, block, list(held))
        self.phases = [list(phase) for phase in phases]
        self.start()

    def start(self):
        if self.phases:
            self.arrived = swap_bit(self.whole, *self.phases[0][0])

    def finish(self):
        for axis, bit in self.phases.pop(0):
            if self.arrived is None:
                self.arrived = swap_bit(self.whole, axis, bit)
            place = place_of(axis, bit)
            dim = sum(other < place for other in self.held)
            arrived, whole = self.chain.after(self.arrived, self.whole)
            upper = own_bit(axis, bit) == 1
            self.whole = self.chain.note(
                jnp.stack(
                    [jnp.where(upper, arrived, whole), jnp.where(upper, whole, arrived)], axis=dim
                )
            )
            self.held.append(place)
            self.arrived = None
        self.start()
        return self.whole


class Reduction:
    def __init__(self, chain, leaving, staying, rows, phases):
        self.chain = chain
        self.steps = [step for phase in phases[::-1] for step in phase[::-1]]
        self.counts = [len(phase) for phase in phases[::-1]]
        self.held = list(range(len(self.steps)))
        axis, bit = self.steps.pop(0)
        assert (axis, bit) == ("dp", 0)
        self.held.remove(place_of(axis, bit))
        shape = leaving.shape[:1] + (2,) * len(self.steps) + (rows, leaving.shape[-1])
        self.staying = staying.reshape(shape)
        self.arriving = swap_bit(leaving, axis, bit).reshape(shape)

    def halves(self, x):
        axis, bit = self.steps[0]
        dim = 1 + self.held.index(place_of(axis, bit))
        own = own_bit(axis, bit)
        return [
            lax.dynamic_index_in_dim(x, which, dim, keepdims=False) for which in (1 - own, own)
        ]

    def finish(self):
        f32 = jnp.float32
        for _ in range(self.counts.pop(0)):
            arrived, staying = self.chain.after(self.arriving, self.staying)
            if not self.steps:
                self.chain.note(arrived)
                return staying.astype(f32) + arrived.astype(f32)
            parts = zip(self.halves(staying), self.halves(arrived))
            leaving, staying = [
                (x.astype(f32) + y.astype(f32)).astype(jnp.bfloat16) for x, y in parts
            ]
            self.chain.note(leaving)
            self.staying = staying
            axis, bit = self.steps.pop(0)
            self.held.remove(place_of(axis, bit))
            self.arriving = swap_bit(leaving, axis, bit)


def group_masks(group):
    axis = group[0][0]
    size = lax.axis_size(axis)
    masks = [0]
    for _, bit in group:
        masks = masks + [mask | 1 << bit for mask in masks]
    return [(axis, [(i, i ^ mask) for i in range(size)]) for mask in masks[1:]]


def exchange(x, group):
    return [x] + [lax.ppermute(x, axis, pairs) for axis, pairs in group_masks(group)]


def tree_sum(values):
    while len(values) > 1:
        values = [a + b for a, b in zip(values[::2], values[1::2])]
    return values[0]


def exchange_groups():
    groups = [[("dp", 0)]]
    for axis, first in (("dp", 1), ("seq", 0)):
        left = [(axis, bit) for bit in range(first, bits_of(axis))]
        groups += [left[i : i + 2] for i in range(0, len(left), 2)]
    return groups


def pack_kernel(*refs):
    ins, out_refs = (refs[:-2], refs[-2:])
    for out_ref, part in ((out_refs[0], ins[:4]), (out_refs[1], ins[4:])):
        place = 0
        for ref in part:
            width = ref.shape[1]
            out_ref[:, place : place + width] = ref[...]
            place += width


def pack_weights(w_query, w_key, w_value, w_out, w_gate, w_up):
    rows = w_query.shape[0]
    parts = (w_query, w_key, w_value, w_out, w_gate, w_up)
    widths = (4 * w_query.shape[1], 2 * w_gate.shape[1])
    return pl.pallas_call(
        pack_kernel,
        name="pack_weights",
        out_shape=[jax.ShapeDtypeStruct((rows, width), w_query.dtype) for width in widths],
    )(*parts)


def to_chips(pieces):
    count = pieces.shape[0]
    dp_size, seq_size = (lax.axis_size("dp"), lax.axis_size("seq"))
    seq_index = lax.axis_index("seq")
    arrived = []
    for phase in range(count):
        pairs = chip_pairs(dp_size, seq_size, count, phase)
        leaving = lax.dynamic_index_in_dim(pieces, (seq_index + phase) % count, 0, keepdims=False)
        arrived.append(lax.ppermute(leaving, ("dp", "seq"), pairs))
    return arrived


def in_token_order(arrived):
    count = len(arrived)
    number = lax.axis_index("seq") % count
    stacked = jnp.stack(arrived)
    return jnp.stack(
        [
            lax.dynamic_index_in_dim(stacked, (number - r) % count, 0, keepdims=False)
            for r in range(count)
        ]
    )


def from_chips(tokens, count):
    dp_size, seq_size = (lax.axis_size("dp"), lax.axis_size("seq"))
    number = lax.axis_index("seq") % count
    split = tokens.reshape((count, tokens.shape[0] // count) + tokens.shape[1:])
    arrived = []
    for phase in range(count):
        pairs = [(j, i) for i, j in chip_pairs(dp_size, seq_size, count, phase)]
        leaving = lax.dynamic_index_in_dim(split, (number - phase) % count, 0, keepdims=False)
        arrived.append(lax.ppermute(leaving, ("dp", "seq"), pairs))
    return arrived


def in_piece_order(arrived):
    count = len(arrived)
    seq_index = lax.axis_index("seq")
    stacked = jnp.stack(arrived)
    return jnp.stack(
        [
            lax.dynamic_index_in_dim(stacked, (j - seq_index) % count, 0, keepdims=False)
            for j in range(count)
        ]
    )


def chip_pairs(dp_size, seq_size, count, phase):
    pairs = []
    for dp in range(dp_size):
        for seq in range(seq_size):
            core_to = seq // count
            seq_to = dp % 2 * count + (seq + phase) % count
            pairs.append((dp * seq_size + seq, (dp // 2 * 2 + core_to) * seq_size + seq_to))
    return pairs


TILE = 128
AUG = 16


def mm(a, b):
    return jnp.dot(a, b, preferred_element_type=jnp.float32)


def mm_nt(a, b):
    return lax.dot_general(a, b, (((1,), (1,)), ((), ())), preferred_element_type=jnp.float32)


def mm_tn(a, b):
    return lax.dot_general(a, b, (((0,), (0,)), ((), ())), preferred_element_type=jnp.float32)


def one_head(pair_rows, a):
    zeros = jnp.zeros((HEAD, pair_rows.shape[1]), pair_rows.dtype)
    half = pair_rows[a * HEAD : (a + 1) * HEAD]
    return jnp.concatenate([half, zeros] if a == 0 else [zeros, half], axis=0)


def near_rows(first_tile, i, d):
    return pl.ds(pl.multiple_of((first_tile + (i + d)) * TILE, TILE), TILE)


def split_rows(base, row):
    low, f32 = (jnp.bfloat16, jnp.float32)
    top = row.astype(low).astype(f32)
    middle = (row - top).astype(low).astype(f32)
    bottom = row - top - middle
    line = lax.broadcasted_iota(jnp.int32, base.shape, 0)
    return jnp.where(
        line == 9, -top, jnp.where(line == 10, -middle, jnp.where(line == 11, -bottom, base))
    ).astype(low)


def attn_forward_kernel(
    skipped, first_ref, q_ref, k_ref, ka_ref, v_ref, far_ref, bias_ref, *rest
):
    out_ref, lse_ref, s_ref = rest[skipped:]
    keys = k_ref.shape[0]
    tokens = q_ref.shape[1]
    lhs = jnp.concatenate([k_ref[...], ka_ref[...]], axis=1)
    pad = jnp.zeros((TILE - AUG, tokens), jnp.bfloat16)
    first = first_ref[0]
    for a in range(2):
        rhs = jnp.concatenate([one_head(q_ref[...], a), far_ref[a], pad], axis=0)
        s_ref[TILE : TILE + keys] = mm(lhs, rhs)
        for i in range(tokens // TILE):
            for d in range(3):
                rows = near_rows(first, i, d)
                lanes = slice(i * TILE, (i + 1) * TILE)
                s_ref[rows, lanes] = s_ref[rows, lanes] + bias_ref[a, d]
        s = s_ref[TILE : TILE + keys]
        row_max = jnp.max(s, axis=0, keepdims=True)
        probs = jnp.exp(s - row_max).astype(jnp.bfloat16)
        v_rows = jnp.concatenate(
            [v_ref[a * HEAD : (a + 1) * HEAD], jnp.ones((AUG, keys), jnp.bfloat16)], axis=0
        )
        both = mm(v_rows, probs)
        total = both[HEAD : HEAD + 1]
        out_ref[a * HEAD : (a + 1) * HEAD] = (both[:HEAD] / total).astype(jnp.bfloat16)
        lse_ref[0, a : a + 1] = row_max + jnp.log(total)


def attn_forward(first, q_t, keys, key_aug, v_t, far, bias, pair_range, earlier):
    width, tokens = q_t.shape
    key_count = keys.shape[0]
    pairs = width // TILE
    base, stop = pair_range
    return pl.pallas_call(
        functools.partial(attn_forward_kernel, len(earlier)),
        name="attn_forward",
        cost_estimate=pl.CostEstimate(
            flops=(stop - base) * (5 << 29), bytes_accessed=1 << 20, transcendentals=0
        ),
        grid_spec=pltpu.PrefetchScalarGridSpec(
            num_scalar_prefetch=1,
            grid=(stop - base,),
            in_specs=[
                pl.BlockSpec((TILE, tokens), lambda h, _: (h + base, 0)),
                pl.BlockSpec((key_count, TILE), lambda h, _: (0, h + base)),
                pl.BlockSpec((key_count, TILE), lambda h, _: (0, 0)),
                pl.BlockSpec((TILE, key_count), lambda h, _: (h + base, 0)),
                pl.BlockSpec((2, AUG, tokens), lambda h, _: (h + base, 0, 0)),
                pl.BlockSpec((2, 3, TILE, TILE), lambda h, _: (h + base, 0, 0, 0)),
            ]
            + [pl.BlockSpec(memory_space=pl.ANY)] * len(earlier),
            out_specs=[
                pl.BlockSpec((TILE, tokens), lambda h, _: (h + base, 0)),
                pl.BlockSpec((1, 2, tokens), lambda h, _: (h + base, 0, 0)),
            ],
            scratch_shapes=[pltpu.VMEM((key_count + 2 * TILE, tokens), jnp.float32)],
        ),
        out_shape=[
            jax.ShapeDtypeStruct((width, tokens), jnp.bfloat16),
            jax.ShapeDtypeStruct((pairs, 2, tokens), jnp.float32),
        ],
        input_output_aliases={7 + i: i for i in range(len(earlier))},
        compiler_params=pltpu.CompilerParams(vmem_limit_bytes=48 << 20),
    )(first, q_t, keys, key_aug, v_t, far, bias, *earlier)


def attn_backward_kernel(
    skipped,
    first_ref,
    q_ref,
    do_ref,
    out_ref,
    lse_ref,
    k_ref,
    v_ref,
    kt_ref,
    ka_ref,
    block_ref,
    far_ref,
    bias_ref,
    *rest,
):
    dq_ref, dk_ref, dv_ref, near_ref, sums_ref, s_ref, ds_ref, p_ref = rest[skipped:]
    keys = k_ref.shape[0]
    tokens = q_ref.shape[1]
    f32, low = (jnp.float32, jnp.bfloat16)
    first = first_ref[0]
    main = slice(TILE, TILE + keys)
    k_lhs = jnp.concatenate([k_ref[...], ka_ref[...]], axis=1)
    v_lhs = jnp.concatenate([v_ref[...], ka_ref[...]], axis=1)
    pad = jnp.zeros((TILE - AUG, tokens), low)
    edge = jnp.zeros((TILE, tokens), low)
    q_heads = [one_head(q_ref[...], a) for a in range(2)]
    do_heads = [one_head(do_ref[...], a) for a in range(2)]
    for a in range(2):
        head = slice(a * HEAD, (a + 1) * HEAD)
        aug = split_rows(far_ref[a].astype(f32), lse_ref[0, a : a + 1])
        s_ref[main] = mm(k_lhs, jnp.concatenate([q_heads[a], aug, pad], axis=0))
        for i in range(tokens // TILE):
            for d in range(3):
                rows = near_rows(first, i, d)
                lanes = slice(i * TILE, (i + 1) * TILE)
                s_ref[rows, lanes] = s_ref[rows, lanes] + bias_ref[a, d]
        probs = jnp.exp(s_ref[main])
        p_ref[a] = probs.astype(low)
        row_dot = jnp.sum(
            do_ref[head].astype(f32) * out_ref[head].astype(f32), axis=0, keepdims=True
        )
        aug = split_rows(jnp.zeros((AUG, tokens), f32), row_dot)
        grad_probs = mm(v_lhs, jnp.concatenate([do_heads[a], aug, pad], axis=0))
        ds_ref[a, main] = (probs * grad_probs).astype(low)
        ds_ref[a, :TILE] = edge
        ds_ref[a, TILE + keys :] = edge
        left = jnp.concatenate([kt_ref[head], block_ref[...]], axis=0)
        both = mm(left, ds_ref[a, main])
        dq_ref[head] = both[:HEAD].astype(low)
        sums_ref[0, a] = both[HEAD:]
        for d in range(3):
            total = None
            for i in range(tokens // TILE):
                rows = near_rows(first, i, d)
                term = ds_ref[a, rows, i * TILE : (i + 1) * TILE].astype(f32)
                total = term if total is None else total + term
            near_ref[a, d] = total
    dk_ref[...] = mm_nt(
        jnp.concatenate([ds_ref[0, main], ds_ref[1, main]], axis=1),
        jnp.concatenate(q_heads, axis=1),
    ).astype(low)
    dv_ref[...] = mm_nt(
        jnp.concatenate([p_ref[0], p_ref[1]], axis=1), jnp.concatenate(do_heads, axis=1)
    ).astype(low)


def attn_backward(
    first,
    q_t,
    do_t,
    out_t,
    lse,
    keys,
    values,
    k_t,
    key_aug,
    block_rows,
    far,
    bias,
    pair_range,
    earlier,
):
    width, tokens = q_t.shape
    key_count = keys.shape[0]
    pairs = width // TILE
    base, stop = pair_range
    across = pl.BlockSpec((TILE, tokens), lambda h, _: (h + base, 0))
    along = pl.BlockSpec((key_count, TILE), lambda h, _: (0, h + base))
    return pl.pallas_call(
        functools.partial(attn_backward_kernel, len(earlier)),
        name="attn_backward",
        cost_estimate=pl.CostEstimate(
            flops=(stop - base) * (9 << 29), bytes_accessed=1 << 20, transcendentals=0
        ),
        grid_spec=pltpu.PrefetchScalarGridSpec(
            num_scalar_prefetch=1,
            grid=(stop - base,),
            in_specs=[
                across,
                across,
                across,
                pl.BlockSpec((1, 2, tokens), lambda h, _: (h + base, 0, 0)),
                along,
                along,
                pl.BlockSpec((TILE, key_count), lambda h, _: (h + base, 0)),
                pl.BlockSpec((key_count, TILE), lambda h, _: (0, 0)),
                pl.BlockSpec((AUG, key_count), lambda h, _: (0, 0)),
                pl.BlockSpec((2, AUG, tokens), lambda h, _: (h + base, 0, 0)),
                pl.BlockSpec((2, 3, TILE, TILE), lambda h, _: (h + base, 0, 0, 0)),
            ]
            + [pl.BlockSpec(memory_space=pl.ANY)] * len(earlier),
            out_specs=[
                across,
                along,
                along,
                pl.BlockSpec((2, 3, TILE, TILE), lambda h, _: (h + base, 0, 0, 0)),
                pl.BlockSpec((1, 2, AUG, tokens), lambda h, _: (h + base, 0, 0, 0)),
            ],
            scratch_shapes=[
                pltpu.VMEM((key_count + 2 * TILE, tokens), jnp.float32),
                pltpu.VMEM((2, key_count + 2 * TILE, tokens), jnp.bfloat16),
                pltpu.VMEM((2, key_count, tokens), jnp.bfloat16),
            ],
        ),
        out_shape=[
            jax.ShapeDtypeStruct((width, tokens), jnp.bfloat16),
            jax.ShapeDtypeStruct((key_count, width), jnp.bfloat16),
            jax.ShapeDtypeStruct((key_count, width), jnp.bfloat16),
            jax.ShapeDtypeStruct((2 * pairs, 3, TILE, TILE), jnp.float32),
            jax.ShapeDtypeStruct((pairs, 2, AUG, tokens), jnp.float32),
        ],
        input_output_aliases={12 + i: i for i in range(len(earlier))},
        compiler_params=pltpu.CompilerParams(vmem_limit_bytes=56 << 20),
    )(
        first,
        q_t,
        do_t,
        out_t,
        lse,
        keys,
        values,
        k_t,
        key_aug,
        block_rows,
        far,
        bias,
        *earlier,
    )


def attn_tables(first, tokens, key_count, length, rel_bias):
    low, f32 = (jnp.bfloat16, jnp.float32)
    blocks = key_count // TILE
    assert blocks <= 8
    key_pos = jnp.arange(key_count, dtype=jnp.int32)
    column = jnp.arange(TILE, dtype=jnp.int32)[None, :]
    key_aug = jnp.where(column == (key_pos // TILE)[:, None], 1.0, 0.0)
    dead = jnp.where(2 * key_pos < length, 0.0, -1000000000.0)[:, None]
    key_aug = jnp.where(column == 8, dead, key_aug)
    key_aug = jnp.where((column >= 9) & (column < 12), 1.0, key_aug).astype(low)
    line = jnp.arange(AUG, dtype=jnp.int32)
    block_rows = jnp.where(line[:, None] == (key_pos // TILE)[None, :], 1.0, 0.0).astype(low)
    tile = first + jnp.arange(tokens, dtype=jnp.int32) // TILE
    apart = (line[:, None] - tile[None, :])[None]
    rel_t = rel_bias.astype(f32).T
    before = rel_t[:, BUCKETS // 2 - 1][:, None, None]
    after = rel_t[:, BUCKETS - 1][:, None, None]
    far = jnp.where(apart <= -2, before, jnp.where(apart >= 2, after, 0.0))
    in_use = (line < blocks)[None, :, None]
    far = jnp.where(in_use, far, jnp.where((line == 8)[None, :, None], 1.0, 0.0)).astype(low)
    return key_aug, block_rows, far


def near_bias_kernel(rel_ref, out_ref):
    width = 4 * TILE
    heads = rel_ref.shape[0]
    lane = lax.broadcasted_iota(jnp.int32, (BUCKETS, width), 1)
    bucket = bucket_of(2 * TILE - 1 - lane)
    line = lax.broadcasted_iota(jnp.int32, (BUCKETS, width), 0)
    table = mm(rel_ref[...], jnp.where(bucket == line, 1.0, 0.0).astype(jnp.bfloat16))
    for h in range(heads):
        rows = jnp.broadcast_to(table[h : h + 1], (TILE, width))
        rows = pltpu.roll(rows, 3 * TILE + 1, 1, stride=1, stride_axis=0)
        for d in range(3):
            out_ref[h, d] = rows[:, (2 - d) * TILE : (3 - d) * TILE]


def near_bias(rel_t):
    return pl.pallas_call(
        near_bias_kernel,
        name="near_bias",
        cost_estimate=pl.CostEstimate(
            flops=3 << 30, bytes_accessed=1 << 20, transcendentals=0
        ),
        out_shape=jax.ShapeDtypeStruct((rel_t.shape[0], 3, TILE, TILE), jnp.float32),
    )(rel_t)


def bias_gradient_kernel(first_ref, near_ref, sums_ref, out_ref, line_ref):
    width = 4 * TILE
    heads = near_ref.shape[0]
    tokens = sums_ref.shape[3]
    f32 = jnp.float32
    line = lax.broadcasted_iota(jnp.int32, (AUG, tokens), 0)
    tile = first_ref[0] + lax.broadcasted_iota(jnp.int32, (AUG, tokens), 1) // TILE
    apart = line - tile
    column = lax.broadcasted_iota(jnp.int32, (1, BUCKETS), 1)
    far_rows = []
    for h in range(heads):
        tiles = [near_ref[h, 2 - k] for k in range(3)]
        rows = jnp.concatenate(tiles + [jnp.zeros((TILE, TILE), f32)], axis=1)
        eight = rows[:8]
        for start in range(8, TILE, 8):
            eight = eight + pltpu.roll(rows[start : start + 8], width - start, 1)
        total = eight[:1]
        for step in range(1, 8):
            total = total + pltpu.roll(eight[step : step + 1], width - step, 1)
        line_ref[h : h + 1] = total
        sums = sums_ref[h // 2, h % 2]
        before = jnp.sum(jnp.where(apart <= -2, sums, 0.0), axis=1, keepdims=True)
        after = jnp.sum(jnp.where(apart >= 2, sums, 0.0), axis=1, keepdims=True)
        before = jnp.sum(before, axis=0, keepdims=True)
        after = jnp.sum(after, axis=0, keepdims=True)
        far_rows.append(
            jnp.where(column == BUCKETS // 2 - 1, before, 0.0)
            + jnp.where(column == BUCKETS - 1, after, 0.0)
        )
    lane = lax.broadcasted_iota(jnp.int32, (BUCKETS, width), 1)
    offset = jnp.where(lane < 3 * TILE, TILE - lane, 5 * TILE - lane)
    bucket = bucket_of(offset)
    pick = jnp.where(bucket == lax.broadcasted_iota(jnp.int32, (BUCKETS, width), 0), 1.0, 0.0)
    close = lax.dot_general(
        line_ref[...], pick, (((1,), (1,)), ((), ())), precision=highest, preferred_element_type=f32
    )
    out_ref[...] = close + jnp.concatenate(far_rows, axis=0)


def bias_gradient(first_ref, near, sums):
    heads = near.shape[0]
    return pl.pallas_call(
        bias_gradient_kernel,
        name="bias_gradient",
        cost_estimate=pl.CostEstimate(
            flops=4 << 30, bytes_accessed=1 << 20, transcendentals=0
        ),
        in_specs=[
            pl.BlockSpec(memory_space=pltpu.SMEM),
            pl.BlockSpec(memory_space=pltpu.VMEM),
            pl.BlockSpec(memory_space=pltpu.VMEM),
        ],
        out_shape=jax.ShapeDtypeStruct((heads, BUCKETS), jnp.float32),
        scratch_shapes=[pltpu.VMEM((heads, 4 * TILE), jnp.float32)],
    )(first_ref, near, sums)


def part_rows(blocks, mine, size):
    width = blocks.shape[-1]
    split = blocks.reshape(blocks.shape[0] // (2 * size), 2, size, width)
    other, own = (split[:, 0], split[:, 1])
    first = mine == 1
    return jnp.where(first, other, own), jnp.where(first, own, other)


def ffn_kernel(
    sub,
    core_ref,
    after_ref,
    gain_ref,
    seed_ref,
    gate_ref,
    up_ref,
    down_ref,
    block_ref,
    grad_ref,
    gain_grad_ref,
    wide_leave_ref,
    wide_stay_ref,
    down_leave_ref,
    down_stay_ref,
    unit_ref,
    normed_ref,
    normed_t_ref,
    out_ref,
    back_ref,
):
    f32, low = (jnp.float32, jnp.bfloat16)
    step = pl.program_id(0)
    core = core_ref[0]

    @pl.when(step == 0)
    def _():
        after = after_ref[...]
        scale = lax.rsqrt(jnp.mean(after * after, axis=1, keepdims=True) + norm_eps)
        normed = (after * scale * gain_ref[...]).astype(low)
        unit_ref[...] = jnp.broadcast_to(scale, unit_ref.shape)
        normed_ref[...] = normed
        normed_t_ref[...] = jnp.transpose(normed)
        out_ref[...] = after
        back_ref[...] = jnp.zeros_like(back_ref)

    normed = normed_ref[...]
    seed = seed_ref[...]
    gate = mm(normed, gate_ref[...])
    up = mm(normed, up_ref[...])
    cube = 0.044715 * gate * gate
    bend = jnp.tanh(0.7978845608028654 * (gate + cube * gate))
    half = 0.5 * (1.0 + bend)
    act = gate * half
    slope = half + (0.5 * 0.7978845608028654) * gate * (1.0 - bend * bend) * (1.0 + 3.0 * cube)
    inner = (act * up).astype(low)
    out_ref[...] += mm(inner, down_ref[...])
    grad_inner = mm_nt(seed, down_ref[...])
    grad_gate = (grad_inner * up * slope).astype(low)
    grad_up = (grad_inner * act).astype(low)
    back_ref[...] += mm_nt(grad_gate, gate_ref[...]) + mm_nt(grad_up, up_ref[...])
    rows = wide_leave_ref.shape[2]
    for number, grad in enumerate((grad_gate, grad_up)):
        leave, stay = part_rows(mm(normed_t_ref[...], grad), core, rows)
        wide_leave_ref[number] = leave.astype(low)
        wide_stay_ref[number] = stay.astype(low)
    leave, stay = part_rows(mm_tn(inner, seed), core, sub)
    down_leave_ref[...] = leave.astype(low)
    down_stay_ref[...] = stay.astype(low)

    @pl.when(step == pl.num_programs(0) - 1)
    def _():
        block_ref[...] = out_ref[...].astype(low)
        back = back_ref[...]
        scale = unit_ref[:, :1]
        unit = after_ref[...] * scale
        gained = back * gain_ref[...]
        mean = jnp.mean(gained * unit, axis=1, keepdims=True)
        grad_ref[...] = seed_ref[...].astype(f32) + scale * (gained - unit * mean)
        gain_grad_ref[...] = jnp.sum(back * unit, axis=0, keepdims=True)


def feed_forward(core, after_attn, gain, seed, gate, up, down, rows, sub):
    tokens, width = after_attn.shape
    ff = gate.shape[1]
    step = 512
    chips = width // (2 * rows)
    f32, low = (jnp.float32, jnp.bfloat16)
    full = pl.BlockSpec((tokens, width), lambda i, _: (0, 0))
    line = pl.BlockSpec((1, width), lambda i, _: (0, 0))
    columns = pl.BlockSpec((width, step), lambda i, _: (0, i))
    wide = pl.BlockSpec((2, chips, rows, step), lambda i, _: (0, 0, 0, i))
    tall = pl.BlockSpec((step // (2 * sub), sub, width), lambda i, _: (i, 0, 0))
    return pl.pallas_call(
        functools.partial(ffn_kernel, sub),
        name="feed_forward",
        cost_estimate=pl.CostEstimate(
            flops=ff * (12 << 20), bytes_accessed=1 << 20, transcendentals=0
        ),
        grid_spec=pltpu.PrefetchScalarGridSpec(
            num_scalar_prefetch=1,
            grid=(ff // step,),
            in_specs=[
                full,
                line,
                full,
                columns,
                columns,
                pl.BlockSpec((step, width), lambda i, _: (i, 0)),
            ],
            out_specs=[full, full, line, wide, wide, tall, tall],
            scratch_shapes=[
                pltpu.VMEM((tokens, LANES), f32),
                pltpu.VMEM((tokens, width), low),
                pltpu.VMEM((width, tokens), low),
                pltpu.VMEM((tokens, width), f32),
                pltpu.VMEM((tokens, width), f32),
            ],
        ),
        out_shape=[
            jax.ShapeDtypeStruct((tokens, width), low),
            jax.ShapeDtypeStruct((tokens, width), f32),
            jax.ShapeDtypeStruct((1, width), f32),
            jax.ShapeDtypeStruct((2, chips, rows, ff), low),
            jax.ShapeDtypeStruct((2, chips, rows, ff), low),
            jax.ShapeDtypeStruct((ff // (2 * sub), sub, width), low),
            jax.ShapeDtypeStruct((ff // (2 * sub), sub, width), low),
        ],
        compiler_params=pltpu.CompilerParams(vmem_limit_bytes=58 << 20),
    )(core, after_attn, gain, seed, gate, up, down)


def square_gradient_kernel(
    core_ref,
    normed_ref,
    att_ref,
    dq_ref,
    dk_ref,
    dv_ref,
    do_ref,
    qk_leave_ref,
    qk_stay_ref,
    vo_leave_ref,
    vo_stay_ref,
    normed_t_ref,
):
    core = core_ref[0]
    tokens = att_ref.shape[1]

    @pl.when(pl.program_id(0) == 0)
    def _():
        normed_t_ref[...] = jnp.transpose(normed_ref[...])

    normed_t = normed_t_ref[...]
    own = normed_t_ref[:, pl.ds(pl.multiple_of(core * tokens, tokens), tokens)]
    grads = (
        (qk_leave_ref, qk_stay_ref, 0, mm_nt(own, dq_ref[...])),
        (qk_leave_ref, qk_stay_ref, 1, mm(normed_t, dk_ref[...])),
        (vo_leave_ref, vo_stay_ref, 0, mm(normed_t, dv_ref[...])),
        (vo_leave_ref, vo_stay_ref, 1, mm(att_ref[...], do_ref[...])),
    )
    for leave_ref, stay_ref, number, grad in grads:
        leave, stay = part_rows(grad, core, leave_ref.shape[2])
        leave_ref[number] = leave.astype(jnp.bfloat16)
        stay_ref[number] = stay.astype(jnp.bfloat16)


def square_gradients(core, normed_all, attended_t, grad_q_t, grad_k, grad_v, grad_out, rows):
    keys, width = normed_all.shape
    tokens = attended_t.shape[1]
    step = 256
    chips = width // (2 * rows)
    low = jnp.bfloat16
    block = pl.BlockSpec((2, chips, rows, step), lambda i, _: (0, 0, 0, i))
    shape = jax.ShapeDtypeStruct((2, chips, rows, width), low)
    return pl.pallas_call(
        square_gradient_kernel,
        name="square_gradients",
        cost_estimate=pl.CostEstimate(
            flops=8 << 30, bytes_accessed=1 << 20, transcendentals=0
        ),
        grid_spec=pltpu.PrefetchScalarGridSpec(
            num_scalar_prefetch=1,
            grid=(width // step,),
            in_specs=[
                pl.BlockSpec((keys, width), lambda i, _: (0, 0)),
                pl.BlockSpec((width, tokens), lambda i, _: (0, 0)),
                pl.BlockSpec((step, tokens), lambda i, _: (i, 0)),
                pl.BlockSpec((keys, step), lambda i, _: (0, i)),
                pl.BlockSpec((keys, step), lambda i, _: (0, i)),
                pl.BlockSpec((tokens, step), lambda i, _: (0, i)),
            ],
            out_specs=[block] * 4,
            scratch_shapes=[pltpu.VMEM((width, keys), low)],
        ),
        out_shape=[shape] * 4,
        compiler_params=pltpu.CompilerParams(vmem_limit_bytes=48 << 20),
    )(core, normed_all, attended_t, grad_q_t, grad_k, grad_v, grad_out)


def shards(
    embeddings,
    lengths,
    cotangent,
    conv_weight,
    scorer,
    gain_attn,
    w_query,
    w_key,
    w_value,
    w_out,
    rel_bias,
    gain_ffn,
    w_gate,
    w_up,
    w_down,
):
    num_micro, num_seqs, local_bytes, model_width = embeddings.shape
    piece_tokens = local_bytes // 2
    count = num_micro * num_seqs
    seq_count = lax.axis_size("seq")
    assert seq_count == 2 * count
    seq_index = lax.axis_index("seq")
    core = lax.axis_index("dp") % 2
    device = lax.axis_index("dp") * seq_count + seq_index
    local_tokens = count * piece_tokens
    key_count = 2 * local_tokens
    low, f32 = (jnp.bfloat16, jnp.float32)
    phases_a, phases_b = stage_phases()
    along, across_a, across_b = (phases_a[:2], phases_a[2:], phases_b[2:])
    rows = w_query.shape[0]
    vec_rows = KERNEL + 3
    half = 2 * model_width
    ff = w_gate.shape[1]
    chain = Chain()

    groups = exchange_groups()
    pieces = embeddings.reshape(count, local_bytes, model_width)
    piece_lengths = lengths.reshape(count)
    square, wide = pack_weights(w_query, w_key, w_value, w_out, w_gate, w_up)
    vectors = jnp.concatenate(
        [conv_weight, scorer[None], gain_attn[None], gain_ffn[None]], axis=0
    )
    vectors = exchange(vectors, groups[0])
    square = Gathering(chain, square, along)
    bytes_before, bytes_after = neighbour_edges(pieces, 2 * EDGE)
    for group in groups[1:]:
        vectors = chain.note(jnp.concatenate(chain.after(*vectors), axis=1))
        vectors = exchange(vectors, group)
        if group is groups[1]:
            square.finish()
            wide = Gathering(chain, chain.after(wide), along)
    vectors = chain.note(jnp.concatenate(chain.after(*vectors), axis=1))
    steps = [step for group in groups for step in group]
    source = jnp.arange(model_width, dtype=jnp.int32)
    partner = device ^ sum(
        ((source // rows >> number) & 1) * (1 << bit if axis == "seq" else seq_count << bit)
        for number, (axis, bit) in enumerate(steps)
    )
    target = partner * rows + source % rows
    place = target[:, None] == jnp.arange(model_width, dtype=jnp.int32)[None, :]
    vectors = chain.note(mm(vectors, place.astype(low)))
    gain_one, gain_two = (vectors[KERNEL + 1], vectors[KERNEL + 2])
    token_start = seq_index * piece_tokens
    info = jnp.concatenate([token_start.reshape(1).astype(jnp.int32), piece_lengths])
    square.finish()
    first = Gathering(chain, square.whole[..., :half], across_a, square.held)
    second = Gathering(chain, square.whole[..., half:], across_b, square.held)
    sent = chain.note(
        pool_forward(info, bytes_before, chain.after(pieces), bytes_after, vectors)
    )
    arrived = to_chips(sent)
    other_lengths = swap_bit(chain.after(piece_lengths), "dp", 0)
    chain_lengths = jnp.where(core == seq_index // count, piece_lengths, other_lengths)
    seq_length = lax.dynamic_index_in_dim(chain_lengths, seq_index % count, 0, keepdims=False)
    first_tile = core * (local_tokens // TILE)
    first_ref = first_tile.astype(jnp.int32).reshape(1)
    wide.finish()
    first.finish()
    second.finish()
    seq_length, rel_late = chain.after(seq_length, rel_bias)
    key_aug, block_rows, far = attn_tables(
        first_tile, local_tokens, key_count, seq_length, rel_late
    )
    bias = chain.note(near_bias(rel_late.T))
    wide.finish()
    gate_full = Gathering(chain, wide.whole[..., :ff], across_a, wide.held)
    up_full = Gathering(chain, wide.whole[..., ff:], across_b, wide.held)
    arrived = in_token_order(chain.after(*arrived))
    normed_low = chain.note(arrived[:, :piece_tokens].reshape(local_tokens, model_width))
    normed_other = swap_bit(normed_low, "dp", 0)
    tall = Gathering(chain, chain.after(w_down), phases_b)
    scale = arrived[:, piece_tokens : piece_tokens + 2, :piece_tokens].astype(f32)
    scale = jnp.sum(scale, axis=1).reshape(local_tokens, 1)
    unit = normed_low.astype(f32) / gain_one
    hidden_in = unit / scale
    first.finish()
    second.finish()
    tall.finish()
    normed_other = chain.after(normed_other)
    normed_all = chain.note(
        jnp.concatenate(
            [
                jnp.where(core == 0, normed_low, normed_other),
                jnp.where(core == 0, normed_other, normed_low),
            ],
            axis=0,
        )
    )
    first = first.finish().reshape(model_width, half)
    second = second.finish().reshape(model_width, half)
    query_full, key_full = (first[:, :model_width], first[:, model_width:])
    value_full, out_full = (second[:, :model_width], second[:, model_width:])

    def project_t(weight, tokens):
        return lax.dot_general(
            weight, tokens, (((0,), (1,)), ((), ())), preferred_element_type=f32
        ).astype(low)

    tall.finish()
    q_t = project_t(query_full, chain.after(normed_low))
    v_t = project_t(value_full, normed_all)
    keys_all = chain.note(mm(normed_all, key_full).astype(low))
    gate_full.finish()
    up_full.finish()
    tall.finish()
    seed_pieces = cotangent.reshape(count, piece_tokens, model_width)
    pairs = model_width // TILE
    fwd_out = ()
    for part in range(2):
        fwd_out = attn_forward(
            first_ref,
            chain.after(q_t),
            keys_all,
            key_aug,
            v_t,
            far,
            bias,
            (part * pairs // 2, (part + 1) * pairs // 2),
            tuple(fwd_out),
        )
        chain.note(fwd_out[0])
        if part == 0:
            seed_arrived = to_chips(chain.after(seed_pieces))
    attended_t, lse = fwd_out
    gate_full.finish()
    up_full.finish()
    after_attn = chain.note(hidden_in + mm_tn(chain.after(attended_t), out_full))
    tall.finish()
    k_t = chain.note(project_t(key_full, chain.after(normed_all)))
    values_all = chain.note(mm(chain.after(normed_all), value_full).astype(low))
    gate_full = gate_full.finish().reshape(model_width, ff)
    up_full = up_full.finish().reshape(model_width, ff)
    seed_low = in_token_order(chain.after(*seed_arrived)).reshape(local_tokens, model_width)
    chain.note(seed_low)
    down_full = tall.finish().reshape(ff, model_width)

    core_ref = core.astype(jnp.int32).reshape(1)
    block_out, grad_after, gain_ffn_grad, wide_leave, wide_stay, down_leave, down_stay = (
        feed_forward(
            core_ref,
            chain.after(after_attn),
            gain_two[None],
            seed_low,
            gate_full,
            up_full,
            down_full,
            rows * seq_count,
            w_down.shape[0] * seq_count,
        )
    )
    chain.note(block_out)
    down_sum = Reduction(chain, down_leave[None], down_stay[None], w_down.shape[0], phases_b)
    wide_sum = Reduction(chain, wide_leave, wide_stay, rows, phases_a)
    blocks_arrived = from_chips(block_out, count)
    grad_after_low = grad_after.astype(low)
    grad_attended_t = chain.note(mm_nt(out_full, chain.after(grad_after_low)).astype(low))
    down_sum.finish()
    wide_sum.finish()
    bwd_out = ()
    for part in range(2):
        bwd_out = attn_backward(
            first_ref,
            q_t,
            chain.after(grad_attended_t),
            attended_t,
            lse,
            keys_all,
            values_all,
            k_t,
            key_aug,
            block_rows,
            far,
            bias,
            (part * pairs // 2, (part + 1) * pairs // 2),
            tuple(bwd_out),
        )
        chain.note(bwd_out[0])
        if part == 0:
            down_sum.finish()
            blocks_arrived = chain.after(*blocks_arrived)
            chain.note(blocks_arrived[0])
            blocks_out = in_piece_order(blocks_arrived)
    grad_queries_t, key_terms, value_terms, near, sums = bwd_out
    shared = mm_nt(chain.after(key_terms), key_full) + mm_nt(value_terms, value_full)
    shared = chain.note(shared.reshape(2, local_tokens, model_width))
    leaving = lax.dynamic_index_in_dim(shared, 1 - core, 0, keepdims=False).astype(low)
    staying = lax.dynamic_index_in_dim(shared, core, 0, keepdims=False)
    arrived = swap_bit(leaving, "dp", 0)
    down_sum.finish()
    wide_sum.finish()
    arrived = chain.after(arrived)
    grad_normed = lax.dot_general(
        grad_queries_t, query_full, (((0,), (1,)), ((), ())), preferred_element_type=f32
    ) + (staying + arrived.astype(f32))
    gained = grad_normed * gain_one
    grad_hidden = grad_after + scale * (
        gained - unit * jnp.mean(gained * unit, axis=-1, keepdims=True)
    )
    arrived = from_chips(chain.note(grad_hidden.astype(low)), count)
    first_leave, first_stay, second_leave, second_stay = square_gradients(
        core_ref,
        normed_all,
        attended_t,
        grad_queries_t,
        chain.after(key_terms),
        value_terms,
        grad_after_low,
        rows * seq_count,
    )
    chain.note(first_leave)
    second_sum = Reduction(chain, second_leave, second_stay, rows, phases_b)
    first_sum = Reduction(chain, first_leave, first_stay, rows, phases_a)
    second_sum.finish()
    first_sum.finish()
    down_sum.finish()
    bias_terms = chain.note(bias_gradient(first_ref, chain.after(near), sums))
    gain_attn_grad = chain.note(jnp.sum(chain.after(grad_normed) * unit, axis=0))
    grad_pieces = chain.note(in_piece_order(chain.after(*arrived)))
    grad_before, grad_after_edge = neighbour_edges(grad_pieces, EDGE)
    wide_sum.finish()
    down_grad = down_sum.finish()[0]
    second_sum.finish()
    first_sum.finish()
    embed_grad, pool_small = pool_backward(
        info,
        bytes_before,
        pieces,
        bytes_after,
        grad_before,
        chain.after(grad_pieces),
        grad_after_edge,
        vectors,
    )
    chain.note(pool_small)
    embed_out = embed_grad.reshape(num_micro, num_seqs, local_bytes, model_width)
    pool_small = jnp.sum(pool_small, axis=0)[: KERNEL + 1]
    bias_row = jnp.pad(bias_terms.reshape(-1), (0, model_width - bias_terms.size))
    small = jnp.concatenate(
        [pool_small, gain_attn_grad[None], gain_ffn_grad, bias_row[None]],
        axis=0,
    )
    small = exchange(chain.note(small), groups[0])
    second_sum.finish()
    first_sum.finish()
    wide_sum.finish()
    for group in groups[1:]:
        small = exchange(chain.note(tree_sum(chain.after(*small))), group)
        if group is groups[1]:
            second_sum.finish()
            first_sum.finish()
    wide_grad = wide_sum.finish()
    small = chain.note(tree_sum(chain.after(*small)))
    gate_grad, up_grad = (wide_grad[0], wide_grad[1])
    blocks_out = blocks_out.reshape(num_micro, num_seqs, piece_tokens, model_width)
    second_grad = second_sum.finish()
    first_grad = first_sum.finish()
    query_grad, key_grad = (first_grad[0], first_grad[1])
    value_grad, out_grad = (second_grad[0], second_grad[1])
    bias_total = small[vec_rows, : bias_terms.size].reshape(bias_terms.shape).T
    own = lax.dynamic_slice_in_dim(small[:vec_rows], device * rows, rows, axis=1)
    return (
        blocks_out,
        embed_out,
        own[:KERNEL],
        own[KERNEL],
        own[KERNEL + 1],
        query_grad,
        key_grad,
        value_grad,
        out_grad,
        bias_total,
        own[KERNEL + 2],
        gate_grad,
        up_grad,
        down_grad,
    )


def solution(mesh):
    return jax.shard_map(
        shards,
        mesh=mesh,
        in_specs=(
            P(None, "dp", "seq", None),
            P(None, "dp"),
            P(None, "dp", "seq", None),
            P(None, ("dp", "seq")),
            P(("dp", "seq")),
            P(("dp", "seq")),
            P(("dp", "seq"), None),
            P(("dp", "seq"), None),
            P(("dp", "seq"), None),
            P(("dp", "seq"), None),
            P(),
            P(("dp", "seq")),
            P(("dp", "seq"), None),
            P(("dp", "seq"), None),
            P(("dp", "seq"), None),
        ),
        out_specs=(
            P(None, "dp", "seq", None),
            P(None, "dp", "seq", None),
            P(None, ("dp", "seq")),
            P(("dp", "seq")),
            P(("dp", "seq")),
            P(("dp", "seq"), None),
            P(("dp", "seq"), None),
            P(("dp", "seq"), None),
            P(("dp", "seq"), None),
            P(),
            P(("dp", "seq")),
            P(("dp", "seq"), None),
            P(("dp", "seq"), None),
            P(("dp", "seq"), None),
        ),
        check_vma=False,
    )
```

```python
import functools

import jax
import jax.numpy as jnp
from jax import lax
from jax.experimental import pallas as pl
from jax.experimental.layout import Layout, with_layout_constraint
from jax.experimental.pallas import tpu as pltpu
from jax.sharding import PartitionSpec as P

HEADS = 12
HEAD = 64
BUCKETS = 32
KERNEL = 5


norm_eps = 1e-06
highest = lax.Precision.HIGHEST
cut_points = (12, 16, 23, 32, 46, 64, 91)


def neighbour_edges(x, width):
    devices, length = (lax.axis_size("seq"), x.shape[1])
    up = [(i, i + 1) for i in range(devices - 1)]
    down = [(j, i) for i, j in up]
    before = lax.ppermute(x[:, length - width :], "seq", up)
    after = lax.ppermute(x[:, :width], "seq", down)
    return before, after


def bucket_of(offset):
    distance = jnp.abs(offset)
    far_bucket = 8 + sum(((distance >= cut_point).astype(jnp.int32) for cut_point in cut_points))
    return jnp.where(distance < 8, distance, far_bucket) + jnp.where(offset > 0, 16, 0)


EDGE = 8
LANES = 128


def shifted(x, step):
    return pltpu.roll(x, (-step) % x.shape[0], 0)


def byte_facts(token_start, length, rows):
    token = token_start - EDGE + lax.broadcasted_iota(jnp.int32, (rows, LANES), 0)
    first = 2 * token
    even_live = jnp.where((first >= 0) & (first < length), 1.0, 0.0)
    odd_live = jnp.where((first + 1 >= 0) & (first + 1 < length), 1.0, 0.0)
    remainder = lax.rem(first + 6 * EDGE, 3)
    odd_token = lax.rem(token + 2 * EDGE, 2) == 1
    return even_live, odd_live, remainder, odd_token


def pooled_scalars(six, remainder, odd_token):
    even_b, odd_b, even, odd, even_a, odd_a = six
    pair = even + odd
    quad = pair + jnp.where(odd_token, even_b + odd_b, even_a + odd_a)
    shared = pair + jnp.where(remainder == 0, even_a, odd_b)
    split = remainder == 2
    triple_even = jnp.where(split, even_b + odd_b + even, shared)
    triple_odd = jnp.where(split, odd + even_a + odd_a, shared)
    third = 1.0 / 3.0
    return (
        (even, 0.5 * pair, third * triple_even, 0.25 * quad),
        (odd, 0.5 * pair, third * triple_odd, 0.25 * quad),
    )


def spread_scalars(even, odd, remainder, odd_token):
    third = 1.0 / 3.0
    pair = 0.5 * (even[1] + odd[1])
    quad = 0.25 * (even[3] + odd[3])
    both = third * (even[2] + odd[2])
    only_even = third * even[2]
    only_odd = third * odd[2]
    split = remainder == 2
    zero = jnp.zeros_like(pair)
    quad_b = jnp.where(odd_token, quad, zero)
    quad_a = jnp.where(odd_token, zero, quad)
    even_here = even[0] + pair + quad + jnp.where(split, only_even, both)
    odd_here = odd[0] + pair + quad + jnp.where(split, only_odd, both)
    even_b = quad_b + jnp.where(split, only_even, zero)
    odd_b = quad_b + jnp.where(split, only_even, jnp.where(remainder == 1, both, zero))
    even_a = quad_a + jnp.where(split, only_odd, jnp.where(remainder == 0, both, zero))
    odd_a = quad_a + jnp.where(split, only_odd, zero)
    return even_b, odd_b, even_here, odd_here, even_a, odd_a


def softmax_of(logits):
    top = jnp.maximum(jnp.maximum(logits[0], logits[1]), jnp.maximum(logits[2], logits[3]))
    parts = [jnp.exp(logit - top) for logit in logits]
    total = (parts[0] + parts[1]) + (parts[2] + parts[3])
    return [part / total for part in parts]


def lane_sum(x):
    return jnp.broadcast_to(jnp.sum(x, axis=1, keepdims=True), x.shape)


def byte_windows(ref, rows, lanes):
    return [ref[EDGE + step : EDGE + step + rows, lanes] for step in (-1, 0, 1)]


def load_bytes(before_ref, body_ref, after_ref, wide_ref):
    edge = 2 * EDGE
    size = body_ref.shape[1]
    for number in range(body_ref.shape[2] // LANES):
        lanes = slice(number * LANES, (number + 1) * LANES)
        wide_ref[number, :edge] = before_ref[0, :, lanes].astype(jnp.float32)
        wide_ref[number, edge : edge + size] = body_ref[0, :, lanes].astype(jnp.float32)
        wide_ref[number, edge + size :] = after_ref[0, :, lanes].astype(jnp.float32)


def conv_chunk(wide_ref, xe_ref, xo_ref, ce_ref, co_ref, vec_ref, facts, number):
    lanes = chunk_lanes(number)
    rows = facts[0].shape[0]
    main = slice(EDGE, EDGE + rows)
    xe_ref[main, lanes] = wide_ref[number, pl.ds(0, rows, stride=2)] * facts[0]
    xo_ref[main, lanes] = wide_ref[number, pl.ds(1, rows, stride=2)] * facts[1]
    even_b, even, even_a = byte_windows(xe_ref, rows, lanes)
    odd_b, odd, odd_a = byte_windows(xo_ref, rows, lanes)
    taps = [vec_ref[j : j + 1, lanes] for j in range(KERNEL)]
    conv_even = (
        taps[0] * even_b + taps[1] * odd_b + taps[2] * even + taps[3] * odd + taps[4] * even_a
    )
    conv_odd = (
        taps[0] * odd_b + taps[1] * even + taps[2] * odd + taps[3] * even_a + taps[4] * odd_a
    )
    ce_ref[main, lanes] = conv_even * facts[0]
    co_ref[main, lanes] = conv_odd * facts[1]


def clear_edges(refs, rows):
    for ref in refs:
        zeros = jnp.zeros((EDGE, ref.shape[1]), jnp.float32)
        ref[:EDGE] = zeros
        ref[EDGE + rows :] = zeros


def chunk_lanes(number):
    return pl.ds(pl.multiple_of(number * LANES, LANES), LANES)


def size_weights(logit_ref, remainder, odd_token):
    even = lane_sum(logit_ref[0])
    odd = lane_sum(logit_ref[1])
    six = (shifted(even, -1), shifted(odd, -1), even, odd, shifted(even, 1), shifted(odd, 1))
    logits_even, logits_odd = pooled_scalars(six, remainder, odd_token)
    return softmax_of(logits_even), softmax_of(logits_odd)


def pool_forward_kernel(
    info_ref,
    before_ref,
    body_ref,
    after_ref,
    vec_ref,
    out_ref,
    wide_ref,
    xe_ref,
    xo_ref,
    ce_ref,
    co_ref,
    logit_ref,
    coef_ref,
    square_ref,
):
    piece = pl.program_id(0)
    width = body_ref.shape[2]
    tokens = body_ref.shape[1] // 2
    rows = tokens + 2 * EDGE
    chunks = width // LANES
    facts = byte_facts(info_ref[0], info_ref[1 + piece], rows)
    load_bytes(before_ref, body_ref, after_ref, wide_ref)
    clear_edges((xe_ref, xo_ref, ce_ref, co_ref), rows)
    logit_ref[...] = jnp.zeros_like(logit_ref)
    main = slice(EDGE, EDGE + rows)

    def first_pass(number, carry):
        lanes = chunk_lanes(number)
        conv_chunk(wide_ref, xe_ref, xo_ref, ce_ref, co_ref, vec_ref, facts, number)
        scorer = vec_ref[KERNEL : KERNEL + 1, lanes]
        logit_ref[0] = logit_ref[0] + ce_ref[main, lanes] * scorer
        logit_ref[1] = logit_ref[1] + co_ref[main, lanes] * scorer
        return carry

    lax.fori_loop(0, chunks, first_pass, 0)
    remainder, odd_token = facts[2:]
    even, odd = size_weights(logit_ref, remainder, odd_token)
    spread = spread_scalars(even, odd, remainder, odd_token)
    for k in range(6):
        coef_ref[k] = 0.5 * spread[k][EDGE : EDGE + tokens]
    square_ref[...] = jnp.zeros_like(square_ref)

    def second_pass(number, carry):
        lanes = chunk_lanes(number)
        total = None
        for step in range(3):
            start = 2 * EDGE + step - 1
            for parity, ref in ((0, ce_ref), (1, co_ref)):
                term = coef_ref[2 * step + parity] * ref[start : start + tokens, lanes]
                total = term if total is None else total + term
        xe_ref[:tokens, lanes] = total
        square_ref[...] = square_ref[...] + total * total
        return carry

    lax.fori_loop(0, chunks, second_pass, 0)
    scale = lax.rsqrt(lane_sum(square_ref[...]) * (1.0 / width) + norm_eps)
    square_ref[...] = scale

    def third_pass(number, carry):
        lanes = chunk_lanes(number)
        gain = vec_ref[KERNEL + 1 : KERNEL + 2, lanes]
        out_ref[0, :tokens, lanes] = (
            xe_ref[:tokens, lanes] * square_ref[...] * gain
        ).astype(jnp.bfloat16)
        return carry

    lax.fori_loop(0, chunks, third_pass, 0)
    row = jnp.transpose(scale)[: 2 * EDGE]
    top = row.astype(jnp.bfloat16).astype(jnp.float32)
    line = lax.broadcasted_iota(jnp.int32, row.shape, 0)
    tail = jnp.where(line == 0, top, jnp.where(line == 1, row - top, 0.0)).astype(jnp.bfloat16)
    rest = jnp.zeros((2 * EDGE, width - tokens), jnp.bfloat16)
    out_ref[0, tokens:] = jnp.concatenate([tail, rest], axis=1)


def pool_forward(info, before, body, after, vectors):
    count, size, width = body.shape
    tokens = size // 2
    rows = tokens + 2 * EDGE
    assert tokens % LANES == 0 and tokens < width
    wide = pltpu.VMEM((width // LANES, size + 4 * EDGE, LANES), jnp.float32)
    tall = pltpu.VMEM((rows + 2 * EDGE, width), jnp.float32)
    edge = pl.BlockSpec((1, 2 * EDGE, width), lambda p, _: (p, 0, 0))
    return pl.pallas_call(
        pool_forward_kernel,
        name="pool_forward",
        grid_spec=pltpu.PrefetchScalarGridSpec(
            num_scalar_prefetch=1,
            grid=(count,),
            in_specs=[
                edge,
                pl.BlockSpec((1, size, width), lambda p, _: (p, 0, 0)),
                edge,
                pl.BlockSpec((8, width), lambda p, _: (0, 0)),
            ],
            out_specs=pl.BlockSpec((1, tokens + 2 * EDGE, width), lambda p, _: (p, 0, 0)),
            scratch_shapes=[
                wide,
                tall,
                tall,
                tall,
                tall,
                pltpu.VMEM((2, rows, LANES), jnp.float32),
                pltpu.VMEM((6, tokens, LANES), jnp.float32),
                pltpu.VMEM((tokens, LANES), jnp.float32),
            ],
        ),
        out_shape=jax.ShapeDtypeStruct((count, tokens + 2 * EDGE, width), jnp.bfloat16),
        compiler_params=pltpu.CompilerParams(vmem_limit_bytes=48 << 20),
    )(info, before, body, after, vectors)


def pool_backward_kernel(
    base,
    skipped,
    info_ref,
    before_ref,
    body_ref,
    after_ref,
    grad_before_ref,
    grad_ref,
    grad_after_ref,
    vec_ref,
    *rest,
):
    (
        embed_ref,
        small_ref,
        wide_ref,
        xe_ref,
        xo_ref,
        ce_ref,
        co_ref,
        dh_ref,
        de_ref,
        do_ref,
        logit_ref,
        dots_ref,
        coef_ref,
        pair_ref,
    ) = rest[skipped:]
    piece = pl.program_id(0) + base
    width = body_ref.shape[2]
    tokens = body_ref.shape[1] // 2
    rows = tokens + 2 * EDGE
    chunks = width // LANES
    f32 = jnp.float32
    facts = byte_facts(info_ref[0], info_ref[1 + piece], rows)
    load_bytes(before_ref, body_ref, after_ref, wide_ref)
    clear_edges((xe_ref, xo_ref, ce_ref, co_ref, dh_ref, de_ref, do_ref), rows)
    dh_ref[EDGE : 2 * EDGE] = grad_before_ref[0].astype(f32)
    dh_ref[2 * EDGE : 2 * EDGE + tokens] = grad_ref[0].astype(f32)
    dh_ref[2 * EDGE + tokens : 3 * EDGE + tokens] = grad_after_ref[0].astype(f32)
    logit_ref[...] = jnp.zeros_like(logit_ref)
    dots_ref[...] = jnp.zeros_like(dots_ref)
    main = slice(EDGE, EDGE + rows)

    def first_pass(number, carry):
        lanes = chunk_lanes(number)
        conv_chunk(wide_ref, xe_ref, xo_ref, ce_ref, co_ref, vec_ref, facts, number)
        scorer = vec_ref[KERNEL : KERNEL + 1, lanes]
        logit_ref[0] = logit_ref[0] + ce_ref[main, lanes] * scorer
        logit_ref[1] = logit_ref[1] + co_ref[main, lanes] * scorer
        grad = dh_ref[main, lanes]
        for step in range(3):
            start = EDGE + step - 1
            for parity, ref in ((0, ce_ref), (1, co_ref)):
                k = 2 * step + parity
                dots_ref[k] = dots_ref[k] + grad * ref[start : start + rows, lanes]
        return carry

    lax.fori_loop(0, chunks, first_pass, 0)
    remainder, odd_token = facts[2:]
    even, odd = size_weights(logit_ref, remainder, odd_token)
    six = [0.5 * lane_sum(dots_ref[k]) for k in range(6)]
    grads_even, grads_odd = pooled_scalars(six, remainder, odd_token)

    def logit_grads(weights, grads):
        mean = (weights[0] * grads[0] + weights[1] * grads[1]) + (
            weights[2] * grads[2] + weights[3] * grads[3]
        )
        return [weight * (grad - mean) for weight, grad in zip(weights, grads)]

    spread = spread_scalars(even, odd, remainder, odd_token)
    steer = spread_scalars(
        logit_grads(even, grads_even), logit_grads(odd, grads_odd), remainder, odd_token
    )
    for k in range(6):
        step = k // 2 - 1
        coef_ref[k] = 0.5 * shifted(spread[k], -step)
    coef_ref[6] = steer[2] + shifted(steer[4], -1) + shifted(steer[0], 1)
    coef_ref[7] = steer[3] + shifted(steer[5], -1) + shifted(steer[1], 1)

    def second_pass(number, carry):
        lanes = chunk_lanes(number)
        scorer = vec_ref[KERNEL : KERNEL + 1, lanes]
        grad_b, grad, grad_a = byte_windows(dh_ref, rows, lanes)
        for parity, live, ref in ((0, facts[0], de_ref), (1, facts[1], do_ref)):
            total = (
                coef_ref[parity] * grad_a
                + coef_ref[2 + parity] * grad
                + coef_ref[4 + parity] * grad_b
                + coef_ref[6 + parity] * scorer
            )
            ref[main, lanes] = total * live
        own = slice(2 * EDGE, 2 * EDGE + tokens)
        before = slice(2 * EDGE - 1, 2 * EDGE - 1 + tokens)
        after = slice(2 * EDGE + 1, 2 * EDGE + 1 + tokens)
        taps = [vec_ref[j : j + 1, lanes] for j in range(KERNEL)]
        even_b, even, even_a = [de_ref[part, lanes] for part in (before, own, after)]
        odd_b, odd, odd_a = [do_ref[part, lanes] for part in (before, own, after)]
        inner = slice(EDGE, EDGE + tokens)
        pair_ref[pl.ds(0, tokens, stride=2)] = facts[0][inner] * (
            taps[0] * even_a + taps[1] * odd + taps[2] * even + taps[3] * odd_b + taps[4] * even_b
        )
        pair_ref[pl.ds(1, tokens, stride=2)] = facts[1][inner] * (
            taps[0] * odd_a + taps[1] * even_a + taps[2] * odd + taps[3] * even + taps[4] * odd_b
        )
        embed_ref[0, :, lanes] = pair_ref[...]
        x_even = [xe_ref[part, lanes] for part in (before, own, after)]
        x_odd = [xo_ref[part, lanes] for part in (before, own, after)]
        terms = [
            even * x_even[0] + odd * x_odd[0],
            even * x_odd[0] + odd * x_even[1],
            even * x_even[1] + odd * x_odd[1],
            even * x_odd[1] + odd * x_even[2],
            even * x_even[2] + odd * x_odd[2],
            coef_ref[6, inner] * ce_ref[own, lanes] + coef_ref[7, inner] * co_ref[own, lanes],
        ]
        sums = [jnp.sum(term, axis=0, keepdims=True) for term in terms]
        sums = sums + [jnp.zeros_like(sums[0])] * (8 - len(sums))
        small_ref[0, :, lanes] = jnp.concatenate(sums, axis=0)
        return carry

    lax.fori_loop(0, chunks, second_pass, 0)


def pool_backward(
    info, before, body, after, grad_before, grad, grad_after, vectors, base, stop, earlier
):
    count, size, width = body.shape
    tokens = size // 2
    rows = tokens + 2 * EDGE
    wide = pltpu.VMEM((width // LANES, size + 4 * EDGE, LANES), jnp.float32)
    tall = pltpu.VMEM((rows + 2 * EDGE, width), jnp.float32)
    edge = pl.BlockSpec((1, 2 * EDGE, width), lambda p, _: (p + base, 0, 0))
    grad_edge = pl.BlockSpec((1, EDGE, width), lambda p, _: (p + base, 0, 0))
    return pl.pallas_call(
        functools.partial(pool_backward_kernel, base, len(earlier)),
        name="pool_backward",
        grid_spec=pltpu.PrefetchScalarGridSpec(
            num_scalar_prefetch=1,
            grid=(stop - base,),
            in_specs=[
                edge,
                pl.BlockSpec((1, size, width), lambda p, _: (p + base, 0, 0)),
                edge,
                grad_edge,
                pl.BlockSpec((1, tokens, width), lambda p, _: (p + base, 0, 0)),
                grad_edge,
                pl.BlockSpec((8, width), lambda p, _: (0, 0)),
            ]
            + [pl.BlockSpec(memory_space=pl.ANY)] * len(earlier),
            out_specs=[
                pl.BlockSpec((1, size, width), lambda p, _: (p + base, 0, 0)),
                pl.BlockSpec((1, 8, width), lambda p, _: (p + base, 0, 0)),
            ],
            scratch_shapes=[wide]
            + [tall] * 7
            + [
                pltpu.VMEM((2, rows, LANES), jnp.float32),
                pltpu.VMEM((6, rows, LANES), jnp.float32),
                pltpu.VMEM((8, rows, LANES), jnp.float32),
                pltpu.VMEM((size, LANES), jnp.float32),
            ],
        ),
        out_shape=[
            jax.ShapeDtypeStruct((count, size, width), jnp.float32),
            jax.ShapeDtypeStruct((count, 8, width), jnp.float32),
        ],
        input_output_aliases={8 + i: i for i in range(len(earlier))},
        compiler_params=pltpu.CompilerParams(vmem_limit_bytes=56 << 20),
    )(info, before, body, after, grad_before, grad, grad_after, vectors, *earlier)


def bits_of(axis):
    size = lax.axis_size(axis)
    count = size.bit_length() - 1
    assert 1 << count == size
    return count


def stage_phases():
    dp_bits, seq_bits = (bits_of("dp"), bits_of("seq"))
    along = [("seq", bit) for bit in reversed(range(seq_bits))]
    low_half = [("dp", bit) for bit in range(1, 1 + (dp_bits - 1) // 2)]
    high_half = [("dp", bit) for bit in range(1 + (dp_bits - 1) // 2, dp_bits)]
    ends = ([along[:1], along[1:]], [[("dp", 0)]])
    return (ends[0] + [high_half, low_half] + ends[1], ends[0] + [low_half, high_half] + ends[1])


def place_of(axis, bit):
    dp_bits, seq_bits = (bits_of("dp"), bits_of("seq"))
    return dp_bits - 1 - bit if axis == "dp" else dp_bits + seq_bits - 1 - bit


def swap_bit(x, axis, bit):
    size = lax.axis_size(axis)
    return lax.ppermute(x, axis, [(i, i ^ (1 << bit)) for i in range(size)])


def own_bit(axis, bit):
    return (lax.axis_index(axis) >> bit) & 1


def in_order(x):
    return with_layout_constraint(x, Layout(major_to_minor=tuple(range(x.ndim))))


class Chain:
    def __init__(self):
        self.noted = None

    def after(self, *values):
        if self.noted is not None:
            values = lax.optimization_barrier(values + (self.noted,))[:-1]
        return values if len(values) > 1 else values[0]

    def note(self, value):
        self.noted = value
        return value


class Gathering:
    def __init__(self, chain, block, phases, held=()):
        self.chain, self.whole, self.held = (chain, block, list(held))
        self.phases = [list(phase) for phase in phases]
        self.start()

    def start(self):
        if self.phases:
            self.arrived = swap_bit(self.whole, *self.phases[0][0])

    def finish(self):
        for axis, bit in self.phases.pop(0):
            if self.arrived is None:
                self.arrived = swap_bit(self.whole, axis, bit)
            place = place_of(axis, bit)
            dim = sum(other < place for other in self.held)
            arrived, whole = self.chain.after(self.arrived, self.whole)
            upper = own_bit(axis, bit) == 1
            self.whole = self.chain.note(
                in_order(
                    jnp.stack(
                        [jnp.where(upper, arrived, whole), jnp.where(upper, whole, arrived)],
                        axis=dim,
                    )
                )
            )
            self.held.append(place)
            self.arrived = None
        self.start()
        return self.whole


    def last(self):
        assert len(self.phases) == 1
        return self.whole, self.arrived


class Reduction:
    def __init__(self, chain, staying, arriving, rows, phases):
        self.chain = chain
        phases = phases[::-1]
        assert phases[0] == [("dp", 0)]
        self.steps = [step for phase in phases[1:] for step in phase[::-1]]
        self.counts = [len(phase) for phase in phases]
        self.held = list(range(1 + len(self.steps)))
        self.held.remove(place_of("dp", 0))
        shape = staying.shape[:1] + (2,) * len(self.steps) + (rows, staying.shape[-1])
        self.staying = staying.reshape(shape)
        self.arriving = arriving.reshape(shape)

    def halves(self, x):
        axis, bit = self.steps[0]
        dim = 1 + self.held.index(place_of(axis, bit))
        own = own_bit(axis, bit)
        return [
            lax.dynamic_index_in_dim(x, which, dim, keepdims=False) for which in (1 - own, own)
        ]

    def finish(self):
        f32 = jnp.float32
        for _ in range(self.counts.pop(0)):
            arrived, staying = self.chain.after(self.arriving, self.staying)
            if not self.steps:
                self.chain.note(arrived)
                return staying.astype(f32) + arrived.astype(f32)
            parts = zip(self.halves(staying), self.halves(arrived))
            leaving, staying = [
                (x.astype(f32) + y.astype(f32)).astype(jnp.bfloat16) for x, y in parts
            ]
            self.chain.note(leaving)
            self.staying = staying
            axis, bit = self.steps.pop(0)
            self.held.remove(place_of(axis, bit))
            self.arriving = swap_bit(leaving, axis, bit)


def group_masks(group):
    axis = group[0][0]
    size = lax.axis_size(axis)
    masks = [0]
    for _, bit in group:
        masks = masks + [mask | 1 << bit for mask in masks]
    return [(axis, [(i, i ^ mask) for i in range(size)]) for mask in masks[1:]]


def exchange(x, group):
    return [x] + [lax.ppermute(x, axis, pairs) for axis, pairs in group_masks(group)]


def tree_sum(values):
    while len(values) > 1:
        values = [a + b for a, b in zip(values[::2], values[1::2])]
    return values[0]


def exchange_groups():
    groups = [[("dp", 0)]]
    for axis, first in (("dp", 1), ("seq", 0)):
        left = [(axis, bit) for bit in range(first, bits_of(axis))]
        groups += [left[i : i + 2] for i in range(0, len(left), 2)]
    return groups


def fold_rows(x, rows):
    width, third, side = (x.shape[1], rows // 3, x.shape[1] // 3)
    rest = x[2 * rows :]
    corner = jnp.concatenate([rest[:third, 2 * side :], rest[third:, 2 * side :]], axis=1)
    tail = jnp.concatenate([rest[:, : 2 * side], corner], axis=0)
    return jnp.concatenate([x[:rows], x[rows : 2 * rows], tail], axis=1)


def unfold_rows(x, width):
    rows, third, side = (x.shape[0], x.shape[0] // 3, width // 3)
    tail = x[:, 2 * width :]
    corner = tail[2 * third :]
    right = jnp.concatenate([corner[:, :side], corner[:, side:]], axis=0)
    rest = jnp.concatenate([tail[: 2 * third], right], axis=1)
    return jnp.concatenate([x[:, :width], x[:, width : 2 * width], rest], axis=0)


def each_block(fold, x, size, *rest):
    parts = [fold(x[i : i + size], *rest) for i in range(0, x.shape[0], size)]
    return parts[0] if len(parts) == 1 else jnp.concatenate(parts, axis=0)


def pack_kernel(*refs):
    *square, gate_ref, up_ref, down_ref, square_ref, wide_ref = refs
    rows, ff = gate_ref.shape
    place = 0
    for ref in square:
        width = ref.shape[1]
        square_ref[:, place : place + width] = ref[...]
        place += width
    half = ff // 2
    down = down_ref[...]
    if down.shape[0] != rows:
        down = fold_rows(down.astype(jnp.float32), rows).astype(jnp.bfloat16)
    wide_ref[:, :ff] = gate_ref[...]
    wide_ref[:, ff : ff + half] = down[:, :half]
    wide_ref[:, ff + half : 2 * ff + half] = up_ref[...]
    wide_ref[:, 2 * ff + half :] = down[:, half:]


def pack_weights(w_query, w_key, w_value, w_out, w_gate, w_up, w_down):
    rows = w_query.shape[0]
    parts = (w_query, w_key, w_value, w_out, w_gate, w_up, w_down)
    widths = (4 * w_query.shape[1], 3 * w_gate.shape[1])
    return pl.pallas_call(
        pack_kernel,
        name="pack_weights",
        out_shape=[jax.ShapeDtypeStruct((rows, width), w_query.dtype) for width in widths],
    )(*parts)


def to_chips(pieces):
    count = pieces.shape[0]
    dp_size, seq_size = (lax.axis_size("dp"), lax.axis_size("seq"))
    seq_index = lax.axis_index("seq")
    arrived = []
    for phase in range(count):
        pairs = chip_pairs(dp_size, seq_size, count, phase)
        leaving = lax.dynamic_index_in_dim(pieces, (seq_index + phase) % count, 0, keepdims=False)
        arrived.append(lax.ppermute(leaving, ("dp", "seq"), pairs))
    return arrived


def in_token_order(arrived):
    count = len(arrived)
    number = lax.axis_index("seq") % count
    stacked = jnp.stack(arrived)
    return jnp.stack(
        [
            lax.dynamic_index_in_dim(stacked, (number - r) % count, 0, keepdims=False)
            for r in range(count)
        ]
    )


def from_chips(tokens, count):
    dp_size, seq_size = (lax.axis_size("dp"), lax.axis_size("seq"))
    number = lax.axis_index("seq") % count
    split = tokens.reshape((count, tokens.shape[0] // count) + tokens.shape[1:])
    arrived = []
    for phase in range(count):
        pairs = [(j, i) for i, j in chip_pairs(dp_size, seq_size, count, phase)]
        leaving = lax.dynamic_index_in_dim(split, (number - phase) % count, 0, keepdims=False)
        arrived.append(lax.ppermute(leaving, ("dp", "seq"), pairs))
    return arrived


def in_piece_order(arrived):
    count = len(arrived)
    seq_index = lax.axis_index("seq")
    stacked = jnp.stack(arrived)
    return jnp.stack(
        [
            lax.dynamic_index_in_dim(stacked, (j - seq_index) % count, 0, keepdims=False)
            for j in range(count)
        ]
    )


def chip_pairs(dp_size, seq_size, count, phase):
    pairs = []
    for dp in range(dp_size):
        for seq in range(seq_size):
            core_to = seq // count
            seq_to = dp % 2 * count + (seq + phase) % count
            pairs.append((dp * seq_size + seq, (dp // 2 * 2 + core_to) * seq_size + seq_to))
    return pairs


TILE = 128
AUG = 16


def mm(a, b):
    return jnp.dot(a, b, preferred_element_type=jnp.float32)


def mm_nt(a, b):
    return lax.dot_general(a, b, (((1,), (1,)), ((), ())), preferred_element_type=jnp.float32)


def mm_tn(a, b):
    return lax.dot_general(a, b, (((0,), (0,)), ((), ())), preferred_element_type=jnp.float32)


def one_head(pair_rows, a):
    zeros = jnp.zeros((HEAD, pair_rows.shape[1]), pair_rows.dtype)
    half = pair_rows[a * HEAD : (a + 1) * HEAD]
    return jnp.concatenate([half, zeros] if a == 0 else [zeros, half], axis=0)


def near_rows(first_tile, i, d):
    return pl.ds(pl.multiple_of((first_tile + (i + d)) * TILE, TILE), TILE)


def split_rows(base, row):
    low, f32 = (jnp.bfloat16, jnp.float32)
    top = row.astype(low).astype(f32)
    middle = (row - top).astype(low).astype(f32)
    bottom = row - top - middle
    line = lax.broadcasted_iota(jnp.int32, base.shape, 0)
    return jnp.where(
        line == 9, -top, jnp.where(line == 10, -middle, jnp.where(line == 11, -bottom, base))
    ).astype(low)


def attn_forward_kernel(
    first_ref, q_ref, k_ref, ka_ref, v_ref, far_ref, bias_ref, out_ref, lse_ref, s_ref
):
    keys = k_ref.shape[0]
    tokens = q_ref.shape[1]
    lhs = jnp.concatenate([k_ref[...], ka_ref[...]], axis=1)
    pad = jnp.zeros((TILE - AUG, tokens), jnp.bfloat16)
    first = first_ref[0]
    for a in range(2):
        rhs = jnp.concatenate([one_head(q_ref[...], a), far_ref[a], pad], axis=0)
        s_ref[TILE : TILE + keys] = mm(lhs, rhs)
        for i in range(tokens // TILE):
            for d in range(3):
                rows = near_rows(first, i, d)
                lanes = slice(i * TILE, (i + 1) * TILE)
                s_ref[rows, lanes] = s_ref[rows, lanes] + bias_ref[a, d]
        s = s_ref[TILE : TILE + keys]
        row_max = jnp.max(s, axis=0, keepdims=True)
        probs = jnp.exp(s - row_max).astype(jnp.bfloat16)
        v_rows = jnp.concatenate(
            [v_ref[a * HEAD : (a + 1) * HEAD], jnp.ones((AUG, keys), jnp.bfloat16)], axis=0
        )
        both = mm(v_rows, probs)
        total = both[HEAD : HEAD + 1]
        out_ref[a * HEAD : (a + 1) * HEAD] = (both[:HEAD] / total).astype(jnp.bfloat16)
        lse_ref[0, a : a + 1] = row_max + jnp.log(total)


def attn_forward(first, q_t, keys, key_aug, v_t, far, bias):
    width, tokens = q_t.shape
    key_count = keys.shape[0]
    pairs = width // TILE
    return pl.pallas_call(
        attn_forward_kernel,
        name="attn_forward",
        grid_spec=pltpu.PrefetchScalarGridSpec(
            num_scalar_prefetch=1,
            grid=(pairs,),
            in_specs=[
                pl.BlockSpec((TILE, tokens), lambda h, _: (h, 0)),
                pl.BlockSpec((key_count, TILE), lambda h, _: (0, h)),
                pl.BlockSpec((key_count, TILE), lambda h, _: (0, 0)),
                pl.BlockSpec((TILE, key_count), lambda h, _: (h, 0)),
                pl.BlockSpec((2, AUG, tokens), lambda h, _: (h, 0, 0)),
                pl.BlockSpec((2, 3, TILE, TILE), lambda h, _: (h, 0, 0, 0)),
            ],
            out_specs=[
                pl.BlockSpec((TILE, tokens), lambda h, _: (h, 0)),
                pl.BlockSpec((1, 2, tokens), lambda h, _: (h, 0, 0)),
            ],
            scratch_shapes=[pltpu.VMEM((key_count + 2 * TILE, tokens), jnp.float32)],
        ),
        out_shape=[
            jax.ShapeDtypeStruct((width, tokens), jnp.bfloat16),
            jax.ShapeDtypeStruct((pairs, 2, tokens), jnp.float32),
        ],
        compiler_params=pltpu.CompilerParams(vmem_limit_bytes=48 << 20),
    )(first, q_t, keys, key_aug, v_t, far, bias)


def attn_backward_kernel(
    first_ref,
    q_ref,
    do_ref,
    out_ref,
    lse_ref,
    k_ref,
    v_ref,
    kt_ref,
    ka_ref,
    block_ref,
    far_ref,
    bias_ref,
    wq_ref,
    wk_ref,
    wv_ref,
    dq_ref,
    dk_ref,
    dv_ref,
    near_ref,
    sums_ref,
    leave_ref,
    stay_ref,
    s_ref,
    ds_ref,
    p_ref,
    dq_all_ref,
    dk_all_ref,
    dv_all_ref,
):
    keys = k_ref.shape[0]
    tokens = q_ref.shape[1]
    f32, low = (jnp.float32, jnp.bfloat16)
    first = first_ref[0]
    main = slice(TILE, TILE + keys)
    k_lhs = jnp.concatenate([k_ref[...], ka_ref[...]], axis=1)
    v_lhs = jnp.concatenate([v_ref[...], ka_ref[...]], axis=1)
    pad = jnp.zeros((TILE - AUG, tokens), low)
    edge = jnp.zeros((TILE, tokens), low)
    q_heads = [one_head(q_ref[...], a) for a in range(2)]
    do_heads = [one_head(do_ref[...], a) for a in range(2)]
    for a in range(2):
        head = slice(a * HEAD, (a + 1) * HEAD)
        aug = split_rows(far_ref[a].astype(f32), lse_ref[0, a : a + 1])
        s_ref[main] = mm(k_lhs, jnp.concatenate([q_heads[a], aug, pad], axis=0))
        for i in range(tokens // TILE):
            for d in range(3):
                rows = near_rows(first, i, d)
                lanes = slice(i * TILE, (i + 1) * TILE)
                s_ref[rows, lanes] = s_ref[rows, lanes] + bias_ref[a, d]
        probs = jnp.exp(s_ref[main])
        p_ref[a] = probs.astype(low)
        row_dot = jnp.sum(
            do_ref[head].astype(f32) * out_ref[head].astype(f32), axis=0, keepdims=True
        )
        aug = split_rows(jnp.zeros((AUG, tokens), f32), row_dot)
        grad_probs = mm(v_lhs, jnp.concatenate([do_heads[a], aug, pad], axis=0))
        ds_ref[a, main] = (probs * grad_probs).astype(low)
        ds_ref[a, :TILE] = edge
        ds_ref[a, TILE + keys :] = edge
        left = jnp.concatenate([kt_ref[head], block_ref[...]], axis=0)
        both = mm(left, ds_ref[a, main])
        dq_ref[head] = both[:HEAD].astype(low)
        sums_ref[0, a] = both[HEAD:]
        for d in range(3):
            total = None
            for i in range(tokens // TILE):
                rows = near_rows(first, i, d)
                term = ds_ref[a, rows, i * TILE : (i + 1) * TILE].astype(f32)
                total = term if total is None else total + term
            near_ref[a, d] = total
    dk_ref[...] = mm_nt(
        jnp.concatenate([ds_ref[0, main], ds_ref[1, main]], axis=1),
        jnp.concatenate(q_heads, axis=1),
    ).astype(low)
    dv_ref[...] = mm_nt(
        jnp.concatenate([p_ref[0], p_ref[1]], axis=1), jnp.concatenate(do_heads, axis=1)
    ).astype(low)
    pair = pl.program_id(0)
    place = pl.ds(pl.multiple_of(pair * TILE, TILE), TILE)
    dq_all_ref[place] = dq_ref[...]
    dk_all_ref[:, place] = dk_ref[...]
    dv_all_ref[:, place] = dv_ref[...]

    @pl.when(pair == pl.num_programs(0) - 1)
    def _():
        core = jnp.where(first == 0, 0, 1)

        def shared(number):
            rows = pl.ds(pl.multiple_of(number * tokens, tokens), tokens)
            return mm_nt(dk_all_ref[rows], wk_ref[...]) + mm_nt(dv_all_ref[rows], wv_ref[...])

        leave_ref[...] = shared(1 - core).astype(low)
        stay_ref[...] = shared(core) + lax.dot_general(
            dq_all_ref[...], wq_ref[...], (((0,), (1,)), ((), ())), preferred_element_type=f32
        )


def attn_backward(
    first,
    q_t,
    do_t,
    out_t,
    lse,
    keys,
    values,
    k_t,
    key_aug,
    block_rows,
    far,
    bias,
    w_query,
    w_key,
    w_value,
):
    width, tokens = q_t.shape
    key_count = keys.shape[0]
    pairs = width // TILE
    weight = pl.BlockSpec((width, width), lambda h, _: (0, 0), pipeline_mode=pl.Buffered(1))
    whole = pl.BlockSpec((tokens, width), lambda h, _: (0, 0))
    across = pl.BlockSpec((TILE, tokens), lambda h, _: (h, 0))
    along = pl.BlockSpec((key_count, TILE), lambda h, _: (0, h))
    return pl.pallas_call(
        attn_backward_kernel,
        name="attn_backward",
        grid_spec=pltpu.PrefetchScalarGridSpec(
            num_scalar_prefetch=1,
            grid=(pairs,),
            in_specs=[
                across,
                across,
                across,
                pl.BlockSpec((1, 2, tokens), lambda h, _: (h, 0, 0)),
                along,
                along,
                pl.BlockSpec((TILE, key_count), lambda h, _: (h, 0)),
                pl.BlockSpec((key_count, TILE), lambda h, _: (0, 0)),
                pl.BlockSpec((AUG, key_count), lambda h, _: (0, 0)),
                pl.BlockSpec((2, AUG, tokens), lambda h, _: (h, 0, 0)),
                pl.BlockSpec((2, 3, TILE, TILE), lambda h, _: (h, 0, 0, 0)),
                weight,
                weight,
                weight,
            ],
            out_specs=[
                across,
                along,
                along,
                pl.BlockSpec((2, 3, TILE, TILE), lambda h, _: (h, 0, 0, 0)),
                pl.BlockSpec((1, 2, AUG, tokens), lambda h, _: (h, 0, 0, 0)),
                whole,
                whole,
            ],
            scratch_shapes=[
                pltpu.VMEM((key_count + 2 * TILE, tokens), jnp.float32),
                pltpu.VMEM((2, key_count + 2 * TILE, tokens), jnp.bfloat16),
                pltpu.VMEM((2, key_count, tokens), jnp.bfloat16),
                pltpu.VMEM((width, tokens), jnp.bfloat16),
                pltpu.VMEM((key_count, width), jnp.bfloat16),
                pltpu.VMEM((key_count, width), jnp.bfloat16),
            ],
        ),
        out_shape=[
            jax.ShapeDtypeStruct((width, tokens), jnp.bfloat16),
            jax.ShapeDtypeStruct((key_count, width), jnp.bfloat16),
            jax.ShapeDtypeStruct((key_count, width), jnp.bfloat16),
            jax.ShapeDtypeStruct((2 * pairs, 3, TILE, TILE), jnp.float32),
            jax.ShapeDtypeStruct((pairs, 2, AUG, tokens), jnp.float32),
            jax.ShapeDtypeStruct((tokens, width), jnp.bfloat16),
            jax.ShapeDtypeStruct((tokens, width), jnp.float32),
        ],
        compiler_params=pltpu.CompilerParams(vmem_limit_bytes=56 << 20),
    )(
        first,
        q_t,
        do_t,
        out_t,
        lse,
        keys,
        values,
        k_t,
        key_aug,
        block_rows,
        far,
        bias,
        w_query,
        w_key,
        w_value,
    )


def attn_tables(first, tokens, key_count, length, rel_bias):
    low, f32 = (jnp.bfloat16, jnp.float32)
    blocks = key_count // TILE
    assert blocks <= 8
    key_pos = jnp.arange(key_count, dtype=jnp.int32)
    column = jnp.arange(TILE, dtype=jnp.int32)[None, :]
    key_aug = jnp.where(column == (key_pos // TILE)[:, None], 1.0, 0.0)
    dead = jnp.where(2 * key_pos < length, 0.0, -1000000000.0)[:, None]
    key_aug = jnp.where(column == 8, dead, key_aug)
    key_aug = jnp.where((column >= 9) & (column < 12), 1.0, key_aug).astype(low)
    line = jnp.arange(AUG, dtype=jnp.int32)
    block_rows = jnp.where(line[:, None] == (key_pos // TILE)[None, :], 1.0, 0.0).astype(low)
    tile = first + jnp.arange(tokens, dtype=jnp.int32) // TILE
    apart = (line[:, None] - tile[None, :])[None]
    rel_t = rel_bias.astype(f32).T
    before = rel_t[:, BUCKETS // 2 - 1][:, None, None]
    after = rel_t[:, BUCKETS - 1][:, None, None]
    far = jnp.where(apart <= -2, before, jnp.where(apart >= 2, after, 0.0))
    in_use = (line < blocks)[None, :, None]
    far = jnp.where(in_use, far, jnp.where((line == 8)[None, :, None], 1.0, 0.0)).astype(low)
    return key_aug, block_rows, far


def near_bias_kernel(rel_ref, out_ref):
    width = 4 * TILE
    heads = rel_ref.shape[0]
    lane = lax.broadcasted_iota(jnp.int32, (BUCKETS, width), 1)
    bucket = bucket_of(2 * TILE - 1 - lane)
    line = lax.broadcasted_iota(jnp.int32, (BUCKETS, width), 0)
    table = mm(rel_ref[...], jnp.where(bucket == line, 1.0, 0.0).astype(jnp.bfloat16))
    for h in range(heads):
        rows = jnp.broadcast_to(table[h : h + 1], (TILE, width))
        rows = pltpu.roll(rows, 3 * TILE + 1, 1, stride=1, stride_axis=0)
        for d in range(3):
            out_ref[h, d] = rows[:, (2 - d) * TILE : (3 - d) * TILE]


def near_bias(rel_t):
    return pl.pallas_call(
        near_bias_kernel,
        name="near_bias",
        out_shape=jax.ShapeDtypeStruct((rel_t.shape[0], 3, TILE, TILE), jnp.float32),
    )(rel_t)


def bias_gradient_kernel(first_ref, near_ref, sums_ref, out_ref, line_ref):
    width = 4 * TILE
    heads = near_ref.shape[0]
    tokens = sums_ref.shape[3]
    f32 = jnp.float32
    line = lax.broadcasted_iota(jnp.int32, (AUG, tokens), 0)
    tile = first_ref[0] + lax.broadcasted_iota(jnp.int32, (AUG, tokens), 1) // TILE
    apart = line - tile
    column = lax.broadcasted_iota(jnp.int32, (1, BUCKETS), 1)
    far_rows = []
    for h in range(heads):
        tiles = [near_ref[h, 2 - k] for k in range(3)]
        rows = jnp.concatenate(tiles + [jnp.zeros((TILE, TILE), f32)], axis=1)
        eight = rows[:8]
        for start in range(8, TILE, 8):
            eight = eight + pltpu.roll(rows[start : start + 8], width - start, 1)
        total = eight[:1]
        for step in range(1, 8):
            total = total + pltpu.roll(eight[step : step + 1], width - step, 1)
        line_ref[h : h + 1] = total
        sums = sums_ref[h // 2, h % 2]
        before = jnp.sum(jnp.where(apart <= -2, sums, 0.0), axis=1, keepdims=True)
        after = jnp.sum(jnp.where(apart >= 2, sums, 0.0), axis=1, keepdims=True)
        before = jnp.sum(before, axis=0, keepdims=True)
        after = jnp.sum(after, axis=0, keepdims=True)
        far_rows.append(
            jnp.where(column == BUCKETS // 2 - 1, before, 0.0)
            + jnp.where(column == BUCKETS - 1, after, 0.0)
        )
    lane = lax.broadcasted_iota(jnp.int32, (BUCKETS, width), 1)
    offset = jnp.where(lane < 3 * TILE, TILE - lane, 5 * TILE - lane)
    bucket = bucket_of(offset)
    pick = jnp.where(bucket == lax.broadcasted_iota(jnp.int32, (BUCKETS, width), 0), 1.0, 0.0)
    close = lax.dot_general(
        line_ref[...], pick, (((1,), (1,)), ((), ())), precision=highest, preferred_element_type=f32
    )
    out_ref[...] = close + jnp.concatenate(far_rows, axis=0)


def bias_gradient(first_ref, near, sums):
    heads = near.shape[0]
    return pl.pallas_call(
        bias_gradient_kernel,
        name="bias_gradient",
        in_specs=[
            pl.BlockSpec(memory_space=pltpu.SMEM),
            pl.BlockSpec(memory_space=pltpu.VMEM),
            pl.BlockSpec(memory_space=pltpu.VMEM),
        ],
        out_shape=jax.ShapeDtypeStruct((heads, BUCKETS), jnp.float32),
        scratch_shapes=[pltpu.VMEM((heads, 4 * TILE), jnp.float32)],
    )(first_ref, near, sums)


def part_rows(blocks, mine, size):
    width = blocks.shape[-1]
    split = blocks.reshape(blocks.shape[0] // (2 * size), 2, size, width)
    other, own = (split[:, 0], split[:, 1])
    first = mine == 1
    return jnp.where(first, other, own), jnp.where(first, own, other)


def join_rows(own, other, core):
    kind = own.dtype
    chips, size, width = own.shape
    if size % 16:
        own, other = (own.astype(jnp.float32), other.astype(jnp.float32))
    first = core == 0
    blocks = jnp.stack([jnp.where(first, own, other), jnp.where(first, other, own)], axis=1)
    return blocks.reshape(2 * chips * size, width).astype(kind)


def ffn_kernel(
    rows,
    sub,
    folded,
    core_ref,
    hidden_ref,
    att_ref,
    w_out_ref,
    gain_ref,
    seed_ref,
    gate_own_ref,
    gate_other_ref,
    up_own_ref,
    up_other_ref,
    *rest,
):
    f32, low = (jnp.float32, jnp.bfloat16)
    count = 4 if folded else 2
    down_refs, rest = (rest[:count], rest[count:])
    block_ref, grad_ref, grad_low_ref, grad_att_ref, gain_grad_ref = rest[:5]
    leave_refs, stay_refs = (rest[5:7], rest[7:9])
    rest = rest[9:]
    if not folded:
        down_leave_ref, down_stay_ref = rest[:2]
        rest = rest[2:]
    after_ref, unit_ref, normed_ref, normed_t_ref, out_ref, back_ref = rest
    number = pl.program_id(0)
    core = core_ref[0]
    step = gate_own_ref.shape[2]
    chips, size, packed = leave_refs[0].shape
    half_ff = packed // 3
    ff = 2 * half_ff
    width = hidden_ref.shape[1]

    @pl.when(number == 0)
    def _():
        after = hidden_ref[...] + mm_tn(att_ref[...], w_out_ref[...])
        scale = lax.rsqrt(jnp.mean(after * after, axis=1, keepdims=True) + norm_eps)
        normed = (after * scale * gain_ref[...]).astype(low)
        after_ref[...] = after
        unit_ref[...] = jnp.broadcast_to(scale, unit_ref.shape)
        normed_ref[...] = normed
        normed_t_ref[...] = jnp.transpose(normed)
        out_ref[...] = after
        back_ref[...] = jnp.zeros_like(back_ref)

    normed = normed_ref[...]
    seed = seed_ref[...]
    w_gate = join_rows(gate_own_ref[...], gate_other_ref[...], core)
    w_up = join_rows(up_own_ref[...], up_other_ref[...], core)
    if folded:
        own, other = [
            jnp.concatenate([down_refs[i][0], down_refs[i + 2][0]], axis=1).astype(f32)
            for i in range(2)
        ]
        own, other = [
            each_block(unfold_rows, x, rows, width).astype(low)[None] for x in (own, other)
        ]
        w_down = join_rows(own, other, core)
    else:
        w_down = join_rows(down_refs[0][...], down_refs[1][...], core)
    gate = mm(normed, w_gate)
    up = mm(normed, w_up)
    cube = 0.044715 * gate * gate
    bend = jnp.tanh(0.7978845608028654 * (gate + cube * gate))
    half = 0.5 * (1.0 + bend)
    act = gate * half
    slope = half + (0.5 * 0.7978845608028654) * gate * (1.0 - bend * bend) * (1.0 + 3.0 * cube)
    inner = (act * up).astype(low)
    out_ref[...] += mm(inner, w_down)
    grad_inner = mm_nt(seed, w_down)
    grad_gate = (grad_inner * up * slope).astype(low)
    grad_up = (grad_inner * act).astype(low)
    back_ref[...] += mm_nt(grad_gate, w_gate) + mm_nt(grad_up, w_up)
    lanes = pl.ds(pl.multiple_of(number * step, step), step)
    for side, grad in enumerate((grad_gate, grad_up)):
        leave, stay = part_rows(mm(normed_t_ref[...], grad), core, size)
        leave_refs[side][:, :, lanes] = leave.astype(low)
        stay_refs[side][:, :, lanes] = stay.astype(low)
    leave, stay = part_rows(mm_tn(inner, seed), core, sub)
    if folded:
        for refs, part in ((leave_refs, leave), (stay_refs, stay)):
            part = each_block(fold_rows, part[0], 8 * rows // 3, rows).astype(low)
            refs[0][number, :, ff:] = part[:, :half_ff]
            refs[1][number, :, ff:] = part[:, half_ff:]
    else:
        down_leave_ref[...] = leave.astype(low)
        down_stay_ref[...] = stay.astype(low)

    @pl.when(number == pl.num_programs(0) - 1)
    def _():
        block_ref[...] = out_ref[...].astype(low)
        back = back_ref[...]
        scale = unit_ref[:, :1]
        unit = after_ref[...] * scale
        gained = back * gain_ref[...]
        mean = jnp.mean(gained * unit, axis=1, keepdims=True)
        grad = seed_ref[...].astype(f32) + scale * (gained - unit * mean)
        grad_ref[...] = grad
        grad_low_ref[...] = grad.astype(low)
        grad_att_ref[...] = mm_nt(w_out_ref[...], grad.astype(low)).astype(low)
        gain_grad_ref[...] = jnp.sum(back * unit, axis=0, keepdims=True)


def feed_forward(core, hidden, attended_t, w_out, gain, seed, first, second, rows, down_rows):
    tokens, width = hidden.shape
    step = 512
    f32, low = (jnp.float32, jnp.bfloat16)
    ff = 2 * first[0].shape[-1] // 3
    half_ff = ff // 2
    size = rows * lax.axis_size("seq")
    sub = down_rows * lax.axis_size("seq")
    chips = width // (2 * size)
    folded = down_rows != rows and 2 * sub == step
    first, second = [[x.reshape(chips, size, ff + half_ff) for x in pair] for pair in (first, second)]
    once = dict(pipeline_mode=pl.Buffered(1))
    full = pl.BlockSpec((tokens, width), lambda i, _: (0, 0))
    full_once = pl.BlockSpec((tokens, width), lambda i, _: (0, 0), **once)
    line = pl.BlockSpec((1, width), lambda i, _: (0, 0))
    across = pl.BlockSpec((width, tokens), lambda i, _: (0, 0))
    across_once = pl.BlockSpec((width, tokens), lambda i, _: (0, 0), **once)
    columns = pl.BlockSpec((chips, size, step), lambda i, _: (0, 0, i))
    tall = pl.BlockSpec((step // (2 * sub), sub, width), lambda i, _: (i, 0, 0))
    packed = pl.BlockSpec((chips, size, ff + half_ff), lambda i, _: (0, 0, 0))
    if folded:
        down = [first[0], first[1], second[0], second[1]]
        down_specs = [pl.BlockSpec((1, size, half_ff), lambda i, _: (i, 0, 2))] * 4
    else:
        down = [
            jnp.concatenate([x[..., ff:], y[..., ff:]], axis=-1).reshape(-1, sub, width)
            for x, y in zip(first, second)
        ]
        down_specs = [tall, tall]
    packed_shape = jax.ShapeDtypeStruct((chips, size, ff + half_ff), low)
    tall_shape = jax.ShapeDtypeStruct((ff // (2 * sub), sub, width), low)
    extra = 0 if folded else 2
    out = pl.pallas_call(
        functools.partial(ffn_kernel, rows, sub, folded),
        name="feed_forward",
        grid_spec=pltpu.PrefetchScalarGridSpec(
            num_scalar_prefetch=1,
            grid=(ff // step,),
            in_specs=[
                full_once,
                across_once,
                pl.BlockSpec((width, width), lambda i, _: (0, 0), **once),
                line,
                full_once,
                columns,
                columns,
                columns,
                columns,
            ]
            + down_specs,
            out_specs=[full, full, full, across, line] + [packed] * 4 + [tall] * extra,
            scratch_shapes=[
                pltpu.VMEM((tokens, width), f32),
                pltpu.VMEM((tokens, LANES), f32),
                pltpu.VMEM((tokens, width), low),
                pltpu.VMEM((width, tokens), low),
                pltpu.VMEM((tokens, width), f32),
                pltpu.VMEM((tokens, width), f32),
            ],
        ),
        out_shape=[
            jax.ShapeDtypeStruct((tokens, width), low),
            jax.ShapeDtypeStruct((tokens, width), f32),
            jax.ShapeDtypeStruct((tokens, width), low),
            jax.ShapeDtypeStruct((width, tokens), low),
            jax.ShapeDtypeStruct((1, width), f32),
        ]
        + [packed_shape] * 4
        + [tall_shape] * extra,
        compiler_params=pltpu.CompilerParams(vmem_limit_bytes=61 << 20),
    )(core, hidden, attended_t, w_out, gain, seed, *first, *second, *down)
    if folded:
        return out
    out = list(out)
    for part in range(2):
        rest = out[9 + part].reshape(chips, size, ff)
        for side in range(2):
            number = 5 + 2 * part + side
            half = rest[..., side * half_ff : (side + 1) * half_ff]
            out[number] = out[number].at[:, :, ff:].set(half)
    return out[:9]


def square_gradient_kernel(
    core_ref,
    normed_ref,
    att_ref,
    dq_ref,
    dk_ref,
    dv_ref,
    do_ref,
    qk_leave_ref,
    vo_leave_ref,
    qk_stay_ref,
    vo_stay_ref,
    normed_t_ref,
):
    core = core_ref[0]
    tokens = att_ref.shape[1]

    @pl.when(pl.program_id(0) == 0)
    def _():
        normed_t_ref[...] = jnp.transpose(normed_ref[...])

    normed_t = normed_t_ref[...]
    own = normed_t_ref[:, pl.ds(pl.multiple_of(core * tokens, tokens), tokens)]
    grads = (
        mm_nt(own, dq_ref[...]),
        mm(normed_t, dk_ref[...]),
        mm(normed_t, dv_ref[...]),
        mm(att_ref[...], do_ref[...]),
    )
    for number, grad in enumerate(grads):
        leave_ref, stay_ref = (
            (qk_leave_ref, qk_stay_ref) if number < 2 else (vo_leave_ref, vo_stay_ref)
        )
        leave, stay = part_rows(grad, core, leave_ref.shape[2])
        leave_ref[number % 2] = leave.astype(jnp.bfloat16)
        stay_ref[number % 2] = stay.astype(jnp.bfloat16)


def square_gradients(core, normed_all, attended_t, grad_q_t, grad_k, grad_v, grad_out, rows):
    keys, width = normed_all.shape
    tokens = attended_t.shape[1]
    step = 256
    chips = width // (2 * rows)
    low = jnp.bfloat16
    block = pl.BlockSpec((2, chips, rows, step), lambda i, _: (0, 0, 0, i))
    shape = jax.ShapeDtypeStruct((2, chips, rows, width), low)
    return pl.pallas_call(
        square_gradient_kernel,
        name="square_gradients",
        grid_spec=pltpu.PrefetchScalarGridSpec(
            num_scalar_prefetch=1,
            grid=(width // step,),
            in_specs=[
                pl.BlockSpec((keys, width), lambda i, _: (0, 0)),
                pl.BlockSpec((width, tokens), lambda i, _: (0, 0)),
                pl.BlockSpec((step, tokens), lambda i, _: (i, 0)),
                pl.BlockSpec((keys, step), lambda i, _: (0, i)),
                pl.BlockSpec((keys, step), lambda i, _: (0, i)),
                pl.BlockSpec((tokens, step), lambda i, _: (0, i)),
            ],
            out_specs=[block] * 4,
            scratch_shapes=[pltpu.VMEM((width, keys), low)],
        ),
        out_shape=[shape] * 4,
        compiler_params=pltpu.CompilerParams(vmem_limit_bytes=48 << 20),
    )(core, normed_all, attended_t, grad_q_t, grad_k, grad_v, grad_out)


def shards(
    embeddings,
    lengths,
    cotangent,
    conv_weight,
    scorer,
    gain_attn,
    w_query,
    w_key,
    w_value,
    w_out,
    rel_bias,
    gain_ffn,
    w_gate,
    w_up,
    w_down,
):
    num_micro, num_seqs, local_bytes, model_width = embeddings.shape
    piece_tokens = local_bytes // 2
    count = num_micro * num_seqs
    seq_count = lax.axis_size("seq")
    assert seq_count == 2 * count
    seq_index = lax.axis_index("seq")
    core = lax.axis_index("dp") % 2
    device = lax.axis_index("dp") * seq_count + seq_index
    local_tokens = count * piece_tokens
    key_count = 2 * local_tokens
    low, f32 = (jnp.bfloat16, jnp.float32)
    phases_a, phases_b = stage_phases()
    along, across_a, across_b = (phases_a[:2], phases_a[2:], phases_b[2:])
    rows = w_query.shape[0]
    vec_rows = KERNEL + 3
    half = 2 * model_width
    ff = w_gate.shape[1]
    chain = Chain()

    groups = exchange_groups()
    lines = [[step] for group in groups for step in group]
    pieces = embeddings.reshape(count, local_bytes, model_width)
    piece_lengths = lengths.reshape(count)
    down_rows = w_down.shape[0]
    folded = rows % 24 == 0 and 2 * down_rows * seq_count == 512 and 3 * ff == 8 * model_width
    down_block = w_down if folded else w_down.reshape(rows, ff)
    square, wide = pack_weights(w_query, w_key, w_value, w_out, w_gate, w_up, down_block)
    digits = jnp.concatenate([piece_lengths // 64, piece_lengths % 64]).astype(low)
    vectors = jnp.concatenate(
        [
            conv_weight,
            scorer[None],
            gain_attn[None],
            gain_ffn[None],
            jnp.broadcast_to(digits[:, None], (2 * count, rows)),
        ],
        axis=0,
    )
    vectors = exchange(vectors, lines[0])
    digits = vectors[1][vec_rows:, 0].astype(jnp.int32)
    other_lengths = 64 * digits[:count] + digits[count:]
    vectors = [vector[:vec_rows] for vector in vectors]
    square = Gathering(chain, square, along)
    bytes_before, bytes_after = neighbour_edges(pieces, 2 * EDGE)
    for number, group in enumerate(lines[1:]):
        vectors = chain.note(jnp.concatenate(chain.after(*vectors), axis=1))
        vectors = exchange(vectors, group)
        if number == 1:
            square.finish()
            wide = Gathering(chain, chain.after(wide), along)
    vectors = chain.note(jnp.concatenate(chain.after(*vectors), axis=1))
    steps = [step for group in groups for step in group]
    source = jnp.arange(model_width, dtype=jnp.int32)
    partner = device ^ sum(
        ((source // rows >> number) & 1) * (1 << bit if axis == "seq" else seq_count << bit)
        for number, (axis, bit) in enumerate(steps)
    )
    target = partner * rows + source % rows
    place = target[:, None] == jnp.arange(model_width, dtype=jnp.int32)[None, :]
    vectors = chain.note(mm(vectors, place.astype(low)))
    gain_one, gain_two = (vectors[KERNEL + 1], vectors[KERNEL + 2])
    token_start = seq_index * piece_tokens
    info = jnp.concatenate([token_start.reshape(1).astype(jnp.int32), piece_lengths])
    square.finish()
    first = Gathering(chain, chain.note(square.whole[..., :half]), across_a, square.held)
    second = Gathering(chain, chain.note(square.whole[..., half:]), across_b, square.held)
    sent = chain.note(
        pool_forward(info, bytes_before, chain.after(pieces), bytes_after, vectors)
    )
    arrived = to_chips(sent)
    chain_lengths = jnp.where(core == seq_index // count, piece_lengths, other_lengths)
    seq_length = lax.dynamic_index_in_dim(chain_lengths, seq_index % count, 0, keepdims=False)
    first_tile = core * (local_tokens // TILE)
    first_ref = first_tile.astype(jnp.int32).reshape(1)
    wide.finish()
    first.finish()
    second.finish()
    seq_length, rel_late = chain.after(seq_length, rel_bias)
    key_aug, block_rows, far = attn_tables(
        first_tile, local_tokens, key_count, seq_length, rel_late
    )
    bias = chain.note(near_bias(rel_late.T))
    wide.finish()
    ff_side = 3 * ff // 2
    gate_full = Gathering(chain, chain.note(wide.whole[..., :ff_side]), across_a, wide.held)
    up_full = Gathering(chain, chain.note(wide.whole[..., ff_side:]), across_b, wide.held)
    arrived = in_token_order(chain.after(*arrived))
    normed_low = chain.note(arrived[:, :piece_tokens].reshape(local_tokens, model_width))
    normed_other = swap_bit(normed_low, "dp", 0)
    scale = arrived[:, piece_tokens : piece_tokens + 2, :piece_tokens].astype(f32)
    scale = jnp.sum(scale, axis=1).reshape(local_tokens, 1)
    unit = normed_low.astype(f32) / gain_one
    hidden_in = unit / scale
    first.finish()
    second.finish()
    normed_other = chain.after(normed_other)
    normed_all = chain.note(
        jnp.concatenate(
            [
                jnp.where(core == 0, normed_low, normed_other),
                jnp.where(core == 0, normed_other, normed_low),
            ],
            axis=0,
        )
    )
    first = first.finish().reshape(model_width, half)
    second = second.finish().reshape(model_width, half)
    query_full, key_full = (first[:, :model_width], first[:, model_width:])
    value_full, out_full = (second[:, :model_width], second[:, model_width:])

    def project_t(weight, tokens):
        return lax.dot_general(
            weight, tokens, (((0,), (1,)), ((), ())), preferred_element_type=f32
        ).astype(low)

    q_t = project_t(query_full, chain.after(normed_low))
    v_t = project_t(value_full, normed_all)
    keys_all = chain.note(mm(normed_all, key_full).astype(low))
    gate_full.finish()
    up_full.finish()
    seed_pieces = cotangent.reshape(count, piece_tokens, model_width)
    seed_arrived = to_chips(chain.after(seed_pieces))
    attended_t, lse = attn_forward(
        first_ref, chain.after(q_t), keys_all, key_aug, v_t, far, bias
    )
    chain.note(attended_t)
    seed_low = in_token_order(chain.after(*seed_arrived)).reshape(local_tokens, model_width)
    chain.note(seed_low)
    gate_full.finish()
    up_full.finish()
    k_t = chain.note(project_t(key_full, chain.after(normed_all)))
    halves = [gather.last() for gather in (gate_full, up_full)]
    waiting = chain.after(*[half[1] for half in halves])
    halves = [(half[0], other) for half, other in zip(halves, waiting)]

    core_ref = core.astype(jnp.int32).reshape(1)
    (
        block_out,
        grad_after,
        grad_after_low,
        grad_attended_t,
        gain_ffn_grad,
        gate_leave,
        up_leave,
        gate_stay,
        up_stay,
    ) = feed_forward(
        core_ref,
        hidden_in,
        attended_t,
        out_full,
        gain_two[None],
        seed_low,
        *halves,
        rows,
        down_rows,
    )
    chain.note(grad_after_low)
    gate_arrived = swap_bit(gate_leave, "dp", 0)
    up_arrived = swap_bit(up_leave, "dp", 0)
    values_all = chain.note(mm(chain.after(normed_all), value_full).astype(low))
    gate_sum = Reduction(chain, gate_stay[None], gate_arrived[None], rows, phases_a)
    up_sum = Reduction(chain, up_stay[None], up_arrived[None], rows, phases_b)
    gate_sum.finish()
    up_sum.finish()
    grad_queries_t, key_terms, value_terms, near, sums, leaving, staying = attn_backward(
        first_ref,
        q_t,
        chain.after(grad_attended_t),
        attended_t,
        lse,
        keys_all,
        values_all,
        k_t,
        key_aug,
        block_rows,
        far,
        bias,
        query_full,
        key_full,
        value_full,
    )
    arrived = swap_bit(chain.note(leaving), "dp", 0)
    blocks_arrived = from_chips(block_out, count)
    first_leave, second_leave, first_stay, second_stay = square_gradients(
        core_ref,
        normed_all,
        attended_t,
        grad_queries_t,
        chain.after(key_terms),
        value_terms,
        grad_after_low,
        rows * seq_count,
    )
    chain.note(first_leave)
    blocks_arrived = chain.after(*blocks_arrived)
    chain.note(blocks_arrived[0])
    blocks_out = in_piece_order(blocks_arrived)
    gate_sum.finish()
    up_sum.finish()
    first_arrived = swap_bit(chain.after(first_leave), "dp", 0)
    second_arrived = swap_bit(chain.after(second_leave), "dp", 0)
    grad_normed = staying + chain.after(arrived).astype(f32)
    gained = grad_normed * gain_one
    grad_hidden = grad_after + scale * (
        gained - unit * jnp.mean(gained * unit, axis=-1, keepdims=True)
    )
    arrived = from_chips(chain.note(grad_hidden.astype(low)), count)
    bias_terms = chain.note(bias_gradient(first_ref, chain.after(near), sums))
    first_sum = Reduction(chain, first_stay, first_arrived, rows, phases_a)
    second_sum = Reduction(chain, second_stay, second_arrived, rows, phases_b)
    gate_sum.finish()
    up_sum.finish()
    grad_pieces = chain.note(in_piece_order(chain.after(*arrived)))
    grad_before, grad_after_edge = neighbour_edges(grad_pieces, EDGE)
    first_sum.finish()
    second_sum.finish()
    gain_attn_grad = chain.note(jnp.sum(chain.after(grad_normed) * unit, axis=0))
    gate_sum.finish()
    up_sum.finish()
    pooled = ()
    for part in range(2):
        pooled = pool_backward(
            info,
            bytes_before,
            pieces,
            bytes_after,
            grad_before,
            chain.after(grad_pieces),
            grad_after_edge,
            vectors,
            part * count // 2,
            (part + 1) * count // 2,
            tuple(pooled),
        )
        chain.note(pooled[1])
        if part == 0:
            gate_side = gate_sum.finish()[0]
            up_side = up_sum.finish()[0]
        first_sum.finish()
        second_sum.finish()
    embed_grad, pool_small = pooled
    embed_out = embed_grad.reshape(num_micro, num_seqs, local_bytes, model_width)
    pool_small = jnp.sum(pool_small, axis=0)[: KERNEL + 1]
    bias_row = jnp.pad(bias_terms.reshape(-1), (0, model_width - bias_terms.size))
    small = jnp.concatenate(
        [pool_small, gain_attn_grad[None], gain_ffn_grad, bias_row[None]],
        axis=0,
    )
    small = exchange(chain.note(small), groups[0])
    for group in groups[1:]:
        small = exchange(chain.note(tree_sum(chain.after(*small))), group)
        if group is groups[1]:
            first_sum.finish()
            second_sum.finish()
    small = chain.note(tree_sum(chain.after(*small)))
    gate_grad, up_grad = (gate_side[:, :ff], up_side[:, :ff])
    down_grad = jnp.concatenate([gate_side[:, ff:], up_side[:, ff:]], axis=1)
    down_grad = (
        unfold_rows(down_grad, model_width) if folded else down_grad.reshape(down_rows, model_width)
    )
    blocks_out = blocks_out.reshape(num_micro, num_seqs, piece_tokens, model_width)
    second_grad = second_sum.finish()
    first_grad = first_sum.finish()
    query_grad, key_grad = (first_grad[0], first_grad[1])
    value_grad, out_grad = (second_grad[0], second_grad[1])
    bias_total = small[vec_rows, : bias_terms.size].reshape(bias_terms.shape).T
    own = lax.dynamic_slice_in_dim(small[:vec_rows], device * rows, rows, axis=1)
    return (
        blocks_out,
        embed_out,
        own[:KERNEL],
        own[KERNEL],
        own[KERNEL + 1],
        query_grad,
        key_grad,
        value_grad,
        out_grad,
        bias_total,
        own[KERNEL + 2],
        gate_grad,
        up_grad,
        down_grad,
    )


def solution(mesh):
    return jax.shard_map(
        shards,
        mesh=mesh,
        in_specs=(
            P(None, "dp", "seq", None),
            P(None, "dp"),
            P(None, "dp", "seq", None),
            P(None, ("dp", "seq")),
            P(("dp", "seq")),
            P(("dp", "seq")),
            P(("dp", "seq"), None),
            P(("dp", "seq"), None),
            P(("dp", "seq"), None),
            P(("dp", "seq"), None),
            P(),
            P(("dp", "seq")),
            P(("dp", "seq"), None),
            P(("dp", "seq"), None),
            P(("dp", "seq"), None),
        ),
        out_specs=(
            P(None, "dp", "seq", None),
            P(None, "dp", "seq", None),
            P(None, ("dp", "seq")),
            P(("dp", "seq")),
            P(("dp", "seq")),
            P(("dp", "seq"), None),
            P(("dp", "seq"), None),
            P(("dp", "seq"), None),
            P(("dp", "seq"), None),
            P(),
            P(("dp", "seq")),
            P(("dp", "seq"), None),
            P(("dp", "seq"), None),
            P(("dp", "seq"), None),
        ),
        check_vma=False,
    )
```

```python
import functools

import jax
import jax.numpy as jnp
from jax import lax
from jax.experimental import pallas as pl
from jax.experimental.layout import Layout, with_layout_constraint
from jax.experimental.pallas import tpu as pltpu
from jax.sharding import PartitionSpec as P

HEADS = 12
HEAD = 64
BUCKETS = 32
KERNEL = 5


norm_eps = 1e-06
highest = lax.Precision.HIGHEST
cut_points = (12, 16, 23, 32, 46, 64, 91)


def neighbour_edges(x, width):
    devices, length = (lax.axis_size("seq"), x.shape[1])
    up = [(i, i + 1) for i in range(devices - 1)]
    down = [(j, i) for i, j in up]
    before = lax.ppermute(x[:, length - width :], "seq", up)
    after = lax.ppermute(x[:, :width], "seq", down)
    return before, after


def bucket_of(offset):
    distance = jnp.abs(offset)
    far_bucket = 8 + sum(((distance >= cut_point).astype(jnp.int32) for cut_point in cut_points))
    return jnp.where(distance < 8, distance, far_bucket) + jnp.where(offset > 0, 16, 0)


EDGE = 8
LANES = 128


def shifted(x, step):
    return pltpu.roll(x, (-step) % x.shape[0], 0)


def byte_facts(token_start, length, rows):
    token = token_start - EDGE + lax.broadcasted_iota(jnp.int32, (rows, LANES), 0)
    first = 2 * token
    even_live = jnp.where((first >= 0) & (first < length), 1.0, 0.0)
    odd_live = jnp.where((first + 1 >= 0) & (first + 1 < length), 1.0, 0.0)
    remainder = lax.rem(first + 6 * EDGE, 3)
    odd_token = lax.rem(token + 2 * EDGE, 2) == 1
    return even_live, odd_live, remainder, odd_token


def pooled_scalars(six, remainder, odd_token):
    even_b, odd_b, even, odd, even_a, odd_a = six
    pair = even + odd
    quad = pair + jnp.where(odd_token, even_b + odd_b, even_a + odd_a)
    shared = pair + jnp.where(remainder == 0, even_a, odd_b)
    split = remainder == 2
    triple_even = jnp.where(split, even_b + odd_b + even, shared)
    triple_odd = jnp.where(split, odd + even_a + odd_a, shared)
    third = 1.0 / 3.0
    return (
        (even, 0.5 * pair, third * triple_even, 0.25 * quad),
        (odd, 0.5 * pair, third * triple_odd, 0.25 * quad),
    )


def spread_scalars(even, odd, remainder, odd_token):
    third = 1.0 / 3.0
    pair = 0.5 * (even[1] + odd[1])
    quad = 0.25 * (even[3] + odd[3])
    both = third * (even[2] + odd[2])
    only_even = third * even[2]
    only_odd = third * odd[2]
    split = remainder == 2
    zero = jnp.zeros_like(pair)
    quad_b = jnp.where(odd_token, quad, zero)
    quad_a = jnp.where(odd_token, zero, quad)
    even_here = even[0] + pair + quad + jnp.where(split, only_even, both)
    odd_here = odd[0] + pair + quad + jnp.where(split, only_odd, both)
    even_b = quad_b + jnp.where(split, only_even, zero)
    odd_b = quad_b + jnp.where(split, only_even, jnp.where(remainder == 1, both, zero))
    even_a = quad_a + jnp.where(split, only_odd, jnp.where(remainder == 0, both, zero))
    odd_a = quad_a + jnp.where(split, only_odd, zero)
    return even_b, odd_b, even_here, odd_here, even_a, odd_a


def softmax_of(logits):
    top = jnp.maximum(jnp.maximum(logits[0], logits[1]), jnp.maximum(logits[2], logits[3]))
    parts = [jnp.exp(logit - top) for logit in logits]
    total = (parts[0] + parts[1]) + (parts[2] + parts[3])
    return [part / total for part in parts]


def lane_sum(x):
    return jnp.broadcast_to(jnp.sum(x, axis=1, keepdims=True), x.shape)


def byte_windows(ref, rows, lanes):
    return [ref[EDGE + step : EDGE + step + rows, lanes] for step in (-1, 0, 1)]


def load_bytes(before_ref, body_ref, after_ref, wide_ref):
    edge = 2 * EDGE
    size = body_ref.shape[1]
    for number in range(body_ref.shape[2] // LANES):
        lanes = slice(number * LANES, (number + 1) * LANES)
        wide_ref[number, :edge] = before_ref[0, :, lanes].astype(jnp.float32)
        wide_ref[number, edge : edge + size] = body_ref[0, :, lanes].astype(jnp.float32)
        wide_ref[number, edge + size :] = after_ref[0, :, lanes].astype(jnp.float32)


def conv_chunk(wide_ref, xe_ref, xo_ref, ce_ref, co_ref, vec_ref, facts, number):
    lanes = chunk_lanes(number)
    rows = facts[0].shape[0]
    main = slice(EDGE, EDGE + rows)
    xe_ref[main, lanes] = wide_ref[number, pl.ds(0, rows, stride=2)] * facts[0]
    xo_ref[main, lanes] = wide_ref[number, pl.ds(1, rows, stride=2)] * facts[1]
    even_b, even, even_a = byte_windows(xe_ref, rows, lanes)
    odd_b, odd, odd_a = byte_windows(xo_ref, rows, lanes)
    taps = [vec_ref[j : j + 1, lanes] for j in range(KERNEL)]
    conv_even = (
        taps[0] * even_b + taps[1] * odd_b + taps[2] * even + taps[3] * odd + taps[4] * even_a
    )
    conv_odd = (
        taps[0] * odd_b + taps[1] * even + taps[2] * odd + taps[3] * even_a + taps[4] * odd_a
    )
    ce_ref[main, lanes] = conv_even * facts[0]
    co_ref[main, lanes] = conv_odd * facts[1]


def clear_edges(refs, rows):
    for ref in refs:
        zeros = jnp.zeros((EDGE, ref.shape[1]), jnp.float32)
        ref[:EDGE] = zeros
        ref[EDGE + rows :] = zeros


def chunk_lanes(number):
    return pl.ds(pl.multiple_of(number * LANES, LANES), LANES)


def size_weights(logit_ref, remainder, odd_token):
    even = lane_sum(logit_ref[0])
    odd = lane_sum(logit_ref[1])
    six = (shifted(even, -1), shifted(odd, -1), even, odd, shifted(even, 1), shifted(odd, 1))
    logits_even, logits_odd = pooled_scalars(six, remainder, odd_token)
    return softmax_of(logits_even), softmax_of(logits_odd)


def pool_forward_kernel(
    info_ref,
    before_ref,
    body_ref,
    after_ref,
    vec_ref,
    out_ref,
    wide_ref,
    xe_ref,
    xo_ref,
    ce_ref,
    co_ref,
    logit_ref,
    coef_ref,
    square_ref,
):
    piece = pl.program_id(0)
    width = body_ref.shape[2]
    tokens = body_ref.shape[1] // 2
    rows = tokens + 2 * EDGE
    chunks = width // LANES
    facts = byte_facts(info_ref[0], info_ref[1 + piece], rows)
    load_bytes(before_ref, body_ref, after_ref, wide_ref)
    clear_edges((xe_ref, xo_ref, ce_ref, co_ref), rows)
    logit_ref[...] = jnp.zeros_like(logit_ref)
    main = slice(EDGE, EDGE + rows)

    def first_pass(number, carry):
        lanes = chunk_lanes(number)
        conv_chunk(wide_ref, xe_ref, xo_ref, ce_ref, co_ref, vec_ref, facts, number)
        scorer = vec_ref[KERNEL : KERNEL + 1, lanes]
        logit_ref[0] = logit_ref[0] + ce_ref[main, lanes] * scorer
        logit_ref[1] = logit_ref[1] + co_ref[main, lanes] * scorer
        return carry

    lax.fori_loop(0, chunks, first_pass, 0)
    remainder, odd_token = facts[2:]
    even, odd = size_weights(logit_ref, remainder, odd_token)
    spread = spread_scalars(even, odd, remainder, odd_token)
    for k in range(6):
        coef_ref[k] = 0.5 * spread[k][EDGE : EDGE + tokens]
    square_ref[...] = jnp.zeros_like(square_ref)

    def second_pass(number, carry):
        lanes = chunk_lanes(number)
        total = None
        for step in range(3):
            start = 2 * EDGE + step - 1
            for parity, ref in ((0, ce_ref), (1, co_ref)):
                term = coef_ref[2 * step + parity] * ref[start : start + tokens, lanes]
                total = term if total is None else total + term
        xe_ref[:tokens, lanes] = total
        square_ref[...] = square_ref[...] + total * total
        return carry

    lax.fori_loop(0, chunks, second_pass, 0)
    scale = lax.rsqrt(lane_sum(square_ref[...]) * (1.0 / width) + norm_eps)
    square_ref[...] = scale

    def third_pass(number, carry):
        lanes = chunk_lanes(number)
        gain = vec_ref[KERNEL + 1 : KERNEL + 2, lanes]
        out_ref[0, :tokens, lanes] = (
            xe_ref[:tokens, lanes] * square_ref[...] * gain
        ).astype(jnp.bfloat16)
        return carry

    lax.fori_loop(0, chunks, third_pass, 0)
    row = jnp.transpose(scale)[: 2 * EDGE]
    top = row.astype(jnp.bfloat16).astype(jnp.float32)
    line = lax.broadcasted_iota(jnp.int32, row.shape, 0)
    tail = jnp.where(line == 0, top, jnp.where(line == 1, row - top, 0.0)).astype(jnp.bfloat16)
    rest = jnp.zeros((2 * EDGE, width - tokens), jnp.bfloat16)
    out_ref[0, tokens:] = jnp.concatenate([tail, rest], axis=1)


def pool_forward(info, before, body, after, vectors):
    count, size, width = body.shape
    tokens = size // 2
    rows = tokens + 2 * EDGE
    assert tokens % LANES == 0 and tokens < width
    wide = pltpu.VMEM((width // LANES, size + 4 * EDGE, LANES), jnp.float32)
    tall = pltpu.VMEM((rows + 2 * EDGE, width), jnp.float32)
    edge = pl.BlockSpec((1, 2 * EDGE, width), lambda p, _: (p, 0, 0))
    return pl.pallas_call(
        pool_forward_kernel,
        name="pool_forward",
        grid_spec=pltpu.PrefetchScalarGridSpec(
            num_scalar_prefetch=1,
            grid=(count,),
            in_specs=[
                edge,
                pl.BlockSpec((1, size, width), lambda p, _: (p, 0, 0)),
                edge,
                pl.BlockSpec((8, width), lambda p, _: (0, 0)),
            ],
            out_specs=pl.BlockSpec((1, tokens + 2 * EDGE, width), lambda p, _: (p, 0, 0)),
            scratch_shapes=[
                wide,
                tall,
                tall,
                tall,
                tall,
                pltpu.VMEM((2, rows, LANES), jnp.float32),
                pltpu.VMEM((6, tokens, LANES), jnp.float32),
                pltpu.VMEM((tokens, LANES), jnp.float32),
            ],
        ),
        out_shape=jax.ShapeDtypeStruct((count, tokens + 2 * EDGE, width), jnp.bfloat16),
        compiler_params=pltpu.CompilerParams(vmem_limit_bytes=14 << 20),
    )(info, before, body, after, vectors)


def pool_backward_kernel(
    base,
    skipped,
    info_ref,
    before_ref,
    body_ref,
    after_ref,
    grad_before_ref,
    grad_ref,
    grad_after_ref,
    vec_ref,
    *rest,
):
    (
        embed_ref,
        small_ref,
        wide_ref,
        xe_ref,
        xo_ref,
        ce_ref,
        co_ref,
        dh_ref,
        de_ref,
        do_ref,
        logit_ref,
        dots_ref,
        coef_ref,
        pair_ref,
    ) = rest[skipped:]
    piece = pl.program_id(0) + base
    width = body_ref.shape[2]
    tokens = body_ref.shape[1] // 2
    rows = tokens + 2 * EDGE
    chunks = width // LANES
    f32 = jnp.float32
    facts = byte_facts(info_ref[0], info_ref[1 + piece], rows)
    load_bytes(before_ref, body_ref, after_ref, wide_ref)
    clear_edges((xe_ref, xo_ref, ce_ref, co_ref, dh_ref, de_ref, do_ref), rows)
    dh_ref[EDGE : 2 * EDGE] = grad_before_ref[0].astype(f32)
    dh_ref[2 * EDGE : 2 * EDGE + tokens] = grad_ref[0].astype(f32)
    dh_ref[2 * EDGE + tokens : 3 * EDGE + tokens] = grad_after_ref[0].astype(f32)
    logit_ref[...] = jnp.zeros_like(logit_ref)
    dots_ref[...] = jnp.zeros_like(dots_ref)
    main = slice(EDGE, EDGE + rows)

    def first_pass(number, carry):
        lanes = chunk_lanes(number)
        conv_chunk(wide_ref, xe_ref, xo_ref, ce_ref, co_ref, vec_ref, facts, number)
        scorer = vec_ref[KERNEL : KERNEL + 1, lanes]
        logit_ref[0] = logit_ref[0] + ce_ref[main, lanes] * scorer
        logit_ref[1] = logit_ref[1] + co_ref[main, lanes] * scorer
        grad = dh_ref[main, lanes]
        for step in range(3):
            start = EDGE + step - 1
            for parity, ref in ((0, ce_ref), (1, co_ref)):
                k = 2 * step + parity
                dots_ref[k] = dots_ref[k] + grad * ref[start : start + rows, lanes]
        return carry

    lax.fori_loop(0, chunks, first_pass, 0)
    remainder, odd_token = facts[2:]
    even, odd = size_weights(logit_ref, remainder, odd_token)
    six = [0.5 * lane_sum(dots_ref[k]) for k in range(6)]
    grads_even, grads_odd = pooled_scalars(six, remainder, odd_token)

    def logit_grads(weights, grads):
        mean = (weights[0] * grads[0] + weights[1] * grads[1]) + (
            weights[2] * grads[2] + weights[3] * grads[3]
        )
        return [weight * (grad - mean) for weight, grad in zip(weights, grads)]

    spread = spread_scalars(even, odd, remainder, odd_token)
    steer = spread_scalars(
        logit_grads(even, grads_even), logit_grads(odd, grads_odd), remainder, odd_token
    )
    for k in range(6):
        step = k // 2 - 1
        coef_ref[k] = 0.5 * shifted(spread[k], -step)
    coef_ref[6] = steer[2] + shifted(steer[4], -1) + shifted(steer[0], 1)
    coef_ref[7] = steer[3] + shifted(steer[5], -1) + shifted(steer[1], 1)

    def second_pass(number, carry):
        lanes = chunk_lanes(number)
        scorer = vec_ref[KERNEL : KERNEL + 1, lanes]
        grad_b, grad, grad_a = byte_windows(dh_ref, rows, lanes)
        for parity, live, ref in ((0, facts[0], de_ref), (1, facts[1], do_ref)):
            total = (
                coef_ref[parity] * grad_a
                + coef_ref[2 + parity] * grad
                + coef_ref[4 + parity] * grad_b
                + coef_ref[6 + parity] * scorer
            )
            ref[main, lanes] = total * live
        own = slice(2 * EDGE, 2 * EDGE + tokens)
        before = slice(2 * EDGE - 1, 2 * EDGE - 1 + tokens)
        after = slice(2 * EDGE + 1, 2 * EDGE + 1 + tokens)
        taps = [vec_ref[j : j + 1, lanes] for j in range(KERNEL)]
        even_b, even, even_a = [de_ref[part, lanes] for part in (before, own, after)]
        odd_b, odd, odd_a = [do_ref[part, lanes] for part in (before, own, after)]
        inner = slice(EDGE, EDGE + tokens)
        pair_ref[pl.ds(0, tokens, stride=2)] = facts[0][inner] * (
            taps[0] * even_a + taps[1] * odd + taps[2] * even + taps[3] * odd_b + taps[4] * even_b
        )
        pair_ref[pl.ds(1, tokens, stride=2)] = facts[1][inner] * (
            taps[0] * odd_a + taps[1] * even_a + taps[2] * odd + taps[3] * even + taps[4] * odd_b
        )
        embed_ref[0, :, lanes] = pair_ref[...]
        x_even = [xe_ref[part, lanes] for part in (before, own, after)]
        x_odd = [xo_ref[part, lanes] for part in (before, own, after)]
        terms = [
            even * x_even[0] + odd * x_odd[0],
            even * x_odd[0] + odd * x_even[1],
            even * x_even[1] + odd * x_odd[1],
            even * x_odd[1] + odd * x_even[2],
            even * x_even[2] + odd * x_odd[2],
            coef_ref[6, inner] * ce_ref[own, lanes] + coef_ref[7, inner] * co_ref[own, lanes],
        ]
        sums = [jnp.sum(term, axis=0, keepdims=True) for term in terms]
        sums = sums + [jnp.zeros_like(sums[0])] * (8 - len(sums))
        small_ref[0, :, lanes] = jnp.concatenate(sums, axis=0)
        return carry

    lax.fori_loop(0, chunks, second_pass, 0)


def pool_backward(
    info, before, body, after, grad_before, grad, grad_after, vectors, base, stop, earlier
):
    count, size, width = body.shape
    tokens = size // 2
    rows = tokens + 2 * EDGE
    wide = pltpu.VMEM((width // LANES, size + 4 * EDGE, LANES), jnp.float32)
    tall = pltpu.VMEM((rows + 2 * EDGE, width), jnp.float32)
    edge = pl.BlockSpec((1, 2 * EDGE, width), lambda p, _: (p + base, 0, 0))
    grad_edge = pl.BlockSpec((1, EDGE, width), lambda p, _: (p + base, 0, 0))
    return pl.pallas_call(
        functools.partial(pool_backward_kernel, base, len(earlier)),
        name="pool_backward",
        grid_spec=pltpu.PrefetchScalarGridSpec(
            num_scalar_prefetch=1,
            grid=(stop - base,),
            in_specs=[
                edge,
                pl.BlockSpec((1, size, width), lambda p, _: (p + base, 0, 0)),
                edge,
                grad_edge,
                pl.BlockSpec((1, tokens, width), lambda p, _: (p + base, 0, 0)),
                grad_edge,
                pl.BlockSpec((8, width), lambda p, _: (0, 0)),
            ]
            + [pl.BlockSpec(memory_space=pl.ANY)] * len(earlier),
            out_specs=[
                pl.BlockSpec((1, size, width), lambda p, _: (p + base, 0, 0)),
                pl.BlockSpec((1, 8, width), lambda p, _: (p + base, 0, 0)),
            ],
            scratch_shapes=[wide]
            + [tall] * 7
            + [
                pltpu.VMEM((2, rows, LANES), jnp.float32),
                pltpu.VMEM((6, rows, LANES), jnp.float32),
                pltpu.VMEM((8, rows, LANES), jnp.float32),
                pltpu.VMEM((size, LANES), jnp.float32),
            ],
        ),
        out_shape=[
            jax.ShapeDtypeStruct((count, size, width), jnp.float32),
            jax.ShapeDtypeStruct((count, 8, width), jnp.float32),
        ],
        input_output_aliases={8 + i: i for i in range(len(earlier))},
        compiler_params=pltpu.CompilerParams(vmem_limit_bytes=20 << 20),
    )(info, before, body, after, grad_before, grad, grad_after, vectors, *earlier)


def bits_of(axis):
    size = lax.axis_size(axis)
    count = size.bit_length() - 1
    assert 1 << count == size
    return count


def stage_phases():
    dp_bits, seq_bits = (bits_of("dp"), bits_of("seq"))
    along = [("seq", bit) for bit in reversed(range(seq_bits))]
    low_half = [("dp", bit) for bit in range(1, 1 + (dp_bits - 1) // 2)]
    high_half = [("dp", bit) for bit in range(1 + (dp_bits - 1) // 2, dp_bits)]
    ends = ([along[:1], along[1:]], [[("dp", 0)]])
    return (ends[0] + [high_half, low_half] + ends[1], ends[0] + [low_half, high_half] + ends[1])


def place_of(axis, bit):
    dp_bits, seq_bits = (bits_of("dp"), bits_of("seq"))
    return dp_bits - 1 - bit if axis == "dp" else dp_bits + seq_bits - 1 - bit


def swap_bit(x, axis, bit):
    size = lax.axis_size(axis)
    return lax.ppermute(x, axis, [(i, i ^ (1 << bit)) for i in range(size)])


def own_bit(axis, bit):
    return (lax.axis_index(axis) >> bit) & 1


def in_order(x):
    return with_layout_constraint(x, Layout(major_to_minor=tuple(range(x.ndim))))


class Chain:
    def __init__(self):
        self.noted = None

    def after(self, *values):
        if self.noted is not None:
            values = lax.optimization_barrier(values + (self.noted,))[:-1]
        return values if len(values) > 1 else values[0]

    def note(self, value):
        self.noted = value
        return value


class Gathering:
    def __init__(self, chain, block, phases, held=()):
        self.chain, self.whole, self.held = (chain, block, list(held))
        self.phases = [list(phase) for phase in phases]
        self.start()

    def start(self):
        if self.phases:
            self.arrived = swap_bit(self.whole, *self.phases[0][0])

    def finish(self):
        for axis, bit in self.phases.pop(0):
            if self.arrived is None:
                self.arrived = swap_bit(self.whole, axis, bit)
            place = place_of(axis, bit)
            dim = sum(other < place for other in self.held)
            arrived, whole = self.chain.after(self.arrived, self.whole)
            upper = own_bit(axis, bit) == 1
            self.whole = self.chain.note(
                in_order(
                    jnp.stack(
                        [jnp.where(upper, arrived, whole), jnp.where(upper, whole, arrived)],
                        axis=dim,
                    )
                )
            )
            self.held.append(place)
            self.arrived = None
        self.start()
        return self.whole


    def last(self):
        assert len(self.phases) == 1
        return self.whole, self.arrived


class Reduction:
    def __init__(self, chain, staying, arriving, rows, phases):
        self.chain = chain
        phases = phases[::-1]
        assert phases[0] == [("dp", 0)]
        self.steps = [step for phase in phases[1:] for step in phase[::-1]]
        self.counts = [len(phase) for phase in phases]
        self.held = list(range(1 + len(self.steps)))
        self.held.remove(place_of("dp", 0))
        shape = staying.shape[:1] + (2,) * len(self.steps) + (rows, staying.shape[-1])
        self.staying = staying.reshape(shape)
        self.arriving = arriving.reshape(shape)

    def halves(self, x):
        axis, bit = self.steps[0]
        dim = 1 + self.held.index(place_of(axis, bit))
        own = own_bit(axis, bit)
        return [
            lax.dynamic_index_in_dim(x, which, dim, keepdims=False) for which in (1 - own, own)
        ]

    def finish(self):
        f32 = jnp.float32
        for _ in range(self.counts.pop(0)):
            arrived, staying = self.chain.after(self.arriving, self.staying)
            if not self.steps:
                self.chain.note(arrived)
                return staying.astype(f32) + arrived.astype(f32)
            parts = zip(self.halves(staying), self.halves(arrived))
            leaving, staying = [
                (x.astype(f32) + y.astype(f32)).astype(jnp.bfloat16) for x, y in parts
            ]
            self.chain.note(leaving)
            self.staying = staying
            axis, bit = self.steps.pop(0)
            self.held.remove(place_of(axis, bit))
            self.arriving = swap_bit(leaving, axis, bit)


def group_masks(group):
    axis = group[0][0]
    size = lax.axis_size(axis)
    masks = [0]
    for _, bit in group:
        masks = masks + [mask | 1 << bit for mask in masks]
    return [(axis, [(i, i ^ mask) for i in range(size)]) for mask in masks[1:]]


def exchange(x, group):
    return [x] + [lax.ppermute(x, axis, pairs) for axis, pairs in group_masks(group)]


def tree_sum(values):
    while len(values) > 1:
        values = [a + b for a, b in zip(values[::2], values[1::2])]
    return values[0]


def exchange_groups():
    groups = [[("dp", 0)]]
    for axis, first in (("dp", 1), ("seq", 0)):
        left = [(axis, bit) for bit in range(first, bits_of(axis))]
        groups += [left[i : i + 2] for i in range(0, len(left), 2)]
    return groups


def fold_rows(x, rows):
    width, third, side = (x.shape[1], rows // 3, x.shape[1] // 3)
    rest = x[2 * rows :]
    corner = jnp.concatenate([rest[:third, 2 * side :], rest[third:, 2 * side :]], axis=1)
    tail = jnp.concatenate([rest[:, : 2 * side], corner], axis=0)
    return jnp.concatenate([x[:rows], x[rows : 2 * rows], tail], axis=1)


def unfold_rows(x, width):
    rows, third, side = (x.shape[0], x.shape[0] // 3, width // 3)
    tail = x[:, 2 * width :]
    corner = tail[2 * third :]
    right = jnp.concatenate([corner[:, :side], corner[:, side:]], axis=0)
    rest = jnp.concatenate([tail[: 2 * third], right], axis=1)
    return jnp.concatenate([x[:, :width], x[:, width : 2 * width], rest], axis=0)


def each_block(fold, x, size, *rest):
    parts = [fold(x[i : i + size], *rest) for i in range(0, x.shape[0], size)]
    return parts[0] if len(parts) == 1 else jnp.concatenate(parts, axis=0)


def pack_kernel(*refs):
    *square, gate_ref, up_ref, down_ref, square_ref, wide_ref = refs
    rows, ff = gate_ref.shape
    place = 0
    for ref in square:
        width = ref.shape[1]
        square_ref[:, place : place + width] = ref[...]
        place += width
    half = ff // 2
    down = down_ref[...]
    if down.shape[0] != rows:
        down = fold_rows(down.astype(jnp.float32), rows).astype(jnp.bfloat16)
    wide_ref[:, :ff] = gate_ref[...]
    wide_ref[:, ff : ff + half] = down[:, :half]
    wide_ref[:, ff + half : 2 * ff + half] = up_ref[...]
    wide_ref[:, 2 * ff + half :] = down[:, half:]


def pack_weights(w_query, w_key, w_value, w_out, w_gate, w_up, w_down):
    rows = w_query.shape[0]
    parts = (w_query, w_key, w_value, w_out, w_gate, w_up, w_down)
    widths = (4 * w_query.shape[1], 3 * w_gate.shape[1])
    return pl.pallas_call(
        pack_kernel,
        name="pack_weights",
        out_shape=[jax.ShapeDtypeStruct((rows, width), w_query.dtype) for width in widths],
    )(*parts)


def to_chips(pieces):
    count = pieces.shape[0]
    dp_size, seq_size = (lax.axis_size("dp"), lax.axis_size("seq"))
    seq_index = lax.axis_index("seq")
    arrived = []
    for phase in range(count):
        pairs = chip_pairs(dp_size, seq_size, count, phase)
        leaving = lax.dynamic_index_in_dim(pieces, (seq_index + phase) % count, 0, keepdims=False)
        arrived.append(lax.ppermute(leaving, ("dp", "seq"), pairs))
    return arrived


def in_token_order(arrived):
    count = len(arrived)
    number = lax.axis_index("seq") % count
    stacked = jnp.stack(arrived)
    return jnp.stack(
        [
            lax.dynamic_index_in_dim(stacked, (number - r) % count, 0, keepdims=False)
            for r in range(count)
        ]
    )


def from_chips(tokens, count):
    dp_size, seq_size = (lax.axis_size("dp"), lax.axis_size("seq"))
    number = lax.axis_index("seq") % count
    split = tokens.reshape((count, tokens.shape[0] // count) + tokens.shape[1:])
    arrived = []
    for phase in range(count):
        pairs = [(j, i) for i, j in chip_pairs(dp_size, seq_size, count, phase)]
        leaving = lax.dynamic_index_in_dim(split, (number - phase) % count, 0, keepdims=False)
        arrived.append(lax.ppermute(leaving, ("dp", "seq"), pairs))
    return arrived


def in_piece_order(arrived):
    count = len(arrived)
    seq_index = lax.axis_index("seq")
    stacked = jnp.stack(arrived)
    return jnp.stack(
        [
            lax.dynamic_index_in_dim(stacked, (j - seq_index) % count, 0, keepdims=False)
            for j in range(count)
        ]
    )


def chip_pairs(dp_size, seq_size, count, phase):
    pairs = []
    for dp in range(dp_size):
        for seq in range(seq_size):
            core_to = seq // count
            seq_to = dp % 2 * count + (seq + phase) % count
            pairs.append((dp * seq_size + seq, (dp // 2 * 2 + core_to) * seq_size + seq_to))
    return pairs


TILE = 128
AUG = 16


def mm(a, b):
    return jnp.dot(a, b, preferred_element_type=jnp.float32)


def mm_nt(a, b):
    return lax.dot_general(a, b, (((1,), (1,)), ((), ())), preferred_element_type=jnp.float32)


def mm_tn(a, b):
    return lax.dot_general(a, b, (((0,), (0,)), ((), ())), preferred_element_type=jnp.float32)


def one_head(pair_rows, a):
    zeros = jnp.zeros((HEAD, pair_rows.shape[1]), pair_rows.dtype)
    half = pair_rows[a * HEAD : (a + 1) * HEAD]
    return jnp.concatenate([half, zeros] if a == 0 else [zeros, half], axis=0)


def near_rows(first_tile, i, d):
    return pl.ds(pl.multiple_of((first_tile + (i + d)) * TILE, TILE), TILE)


def split_rows(base, row):
    low, f32 = (jnp.bfloat16, jnp.float32)
    top = row.astype(low).astype(f32)
    middle = (row - top).astype(low).astype(f32)
    bottom = row - top - middle
    line = lax.broadcasted_iota(jnp.int32, base.shape, 0)
    return jnp.where(
        line == 9, -top, jnp.where(line == 10, -middle, jnp.where(line == 11, -bottom, base))
    ).astype(low)


def attn_forward_kernel(
    first_ref, q_ref, k_ref, ka_ref, v_ref, far_ref, bias_ref, out_ref, lse_ref, s_ref
):
    keys = k_ref.shape[0]
    tokens = q_ref.shape[1]
    lhs = jnp.concatenate([k_ref[...], ka_ref[...]], axis=1)
    pad = jnp.zeros((TILE - AUG, tokens), jnp.bfloat16)
    first = first_ref[0]
    for a in range(2):
        rhs = jnp.concatenate([one_head(q_ref[...], a), far_ref[a], pad], axis=0)
        s_ref[TILE : TILE + keys] = mm(lhs, rhs)
        for i in range(tokens // TILE):
            for d in range(3):
                rows = near_rows(first, i, d)
                lanes = slice(i * TILE, (i + 1) * TILE)
                s_ref[rows, lanes] = s_ref[rows, lanes] + bias_ref[a, d]
        s = s_ref[TILE : TILE + keys]
        row_max = jnp.max(s, axis=0, keepdims=True)
        probs = jnp.exp(s - row_max).astype(jnp.bfloat16)
        v_rows = jnp.concatenate(
            [v_ref[a * HEAD : (a + 1) * HEAD], jnp.ones((AUG, keys), jnp.bfloat16)], axis=0
        )
        both = mm(v_rows, probs)
        total = both[HEAD : HEAD + 1]
        out_ref[a * HEAD : (a + 1) * HEAD] = (both[:HEAD] / total).astype(jnp.bfloat16)
        lse_ref[0, a : a + 1] = row_max + jnp.log(total)


def attn_forward(first, q_t, keys, key_aug, v_t, far, bias):
    width, tokens = q_t.shape
    key_count = keys.shape[0]
    pairs = width // TILE
    return pl.pallas_call(
        attn_forward_kernel,
        name="attn_forward",
        grid_spec=pltpu.PrefetchScalarGridSpec(
            num_scalar_prefetch=1,
            grid=(pairs,),
            in_specs=[
                pl.BlockSpec((TILE, tokens), lambda h, _: (h, 0)),
                pl.BlockSpec((key_count, TILE), lambda h, _: (0, h)),
                pl.BlockSpec((key_count, TILE), lambda h, _: (0, 0)),
                pl.BlockSpec((TILE, key_count), lambda h, _: (h, 0)),
                pl.BlockSpec((2, AUG, tokens), lambda h, _: (h, 0, 0)),
                pl.BlockSpec((2, 3, TILE, TILE), lambda h, _: (h, 0, 0, 0)),
            ],
            out_specs=[
                pl.BlockSpec((TILE, tokens), lambda h, _: (h, 0)),
                pl.BlockSpec((1, 2, tokens), lambda h, _: (h, 0, 0)),
            ],
            scratch_shapes=[pltpu.VMEM((key_count + 2 * TILE, tokens), jnp.float32)],
        ),
        out_shape=[
            jax.ShapeDtypeStruct((width, tokens), jnp.bfloat16),
            jax.ShapeDtypeStruct((pairs, 2, tokens), jnp.float32),
        ],
        compiler_params=pltpu.CompilerParams(vmem_limit_bytes=14 << 20),
    )(first, q_t, keys, key_aug, v_t, far, bias)


def attn_backward_kernel(
    first_ref,
    q_ref,
    do_ref,
    out_ref,
    lse_ref,
    k_ref,
    v_ref,
    kt_ref,
    ka_ref,
    block_ref,
    far_ref,
    bias_ref,
    wq_ref,
    wk_ref,
    wv_ref,
    dq_ref,
    dk_ref,
    dv_ref,
    near_ref,
    sums_ref,
    leave_ref,
    stay_ref,
    s_ref,
    ds_ref,
    p_ref,
    dq_all_ref,
    dk_all_ref,
    dv_all_ref,
):
    keys = k_ref.shape[0]
    tokens = q_ref.shape[1]
    f32, low = (jnp.float32, jnp.bfloat16)
    first = first_ref[0]
    main = slice(TILE, TILE + keys)
    k_lhs = jnp.concatenate([k_ref[...], ka_ref[...]], axis=1)
    v_lhs = jnp.concatenate([v_ref[...], ka_ref[...]], axis=1)
    pad = jnp.zeros((TILE - AUG, tokens), low)
    edge = jnp.zeros((TILE, tokens), low)
    q_heads = [one_head(q_ref[...], a) for a in range(2)]
    do_heads = [one_head(do_ref[...], a) for a in range(2)]
    for a in range(2):
        head = slice(a * HEAD, (a + 1) * HEAD)
        aug = split_rows(far_ref[a].astype(f32), lse_ref[0, a : a + 1])
        s_ref[main] = mm(k_lhs, jnp.concatenate([q_heads[a], aug, pad], axis=0))
        for i in range(tokens // TILE):
            for d in range(3):
                rows = near_rows(first, i, d)
                lanes = slice(i * TILE, (i + 1) * TILE)
                s_ref[rows, lanes] = s_ref[rows, lanes] + bias_ref[a, d]
        probs = jnp.exp(s_ref[main])
        p_ref[a] = probs.astype(low)
        row_dot = jnp.sum(
            do_ref[head].astype(f32) * out_ref[head].astype(f32), axis=0, keepdims=True
        )
        aug = split_rows(jnp.zeros((AUG, tokens), f32), row_dot)
        grad_probs = mm(v_lhs, jnp.concatenate([do_heads[a], aug, pad], axis=0))
        ds_ref[a, main] = (probs * grad_probs).astype(low)
        ds_ref[a, :TILE] = edge
        ds_ref[a, TILE + keys :] = edge
        left = jnp.concatenate([kt_ref[head], block_ref[...]], axis=0)
        both = mm(left, ds_ref[a, main])
        dq_ref[head] = both[:HEAD].astype(low)
        sums_ref[0, a] = both[HEAD:]
        for d in range(3):
            total = None
            for i in range(tokens // TILE):
                rows = near_rows(first, i, d)
                term = ds_ref[a, rows, i * TILE : (i + 1) * TILE].astype(f32)
                total = term if total is None else total + term
            near_ref[a, d] = total
    dk_ref[...] = mm_nt(
        jnp.concatenate([ds_ref[0, main], ds_ref[1, main]], axis=1),
        jnp.concatenate(q_heads, axis=1),
    ).astype(low)
    dv_ref[...] = mm_nt(
        jnp.concatenate([p_ref[0], p_ref[1]], axis=1), jnp.concatenate(do_heads, axis=1)
    ).astype(low)
    pair = pl.program_id(0)
    place = pl.ds(pl.multiple_of(pair * TILE, TILE), TILE)
    dq_all_ref[place] = dq_ref[...]
    dk_all_ref[:, place] = dk_ref[...]
    dv_all_ref[:, place] = dv_ref[...]

    @pl.when(pair == pl.num_programs(0) - 1)
    def _():
        core = jnp.where(first == 0, 0, 1)

        def shared(number):
            rows = pl.ds(pl.multiple_of(number * tokens, tokens), tokens)
            return mm_nt(dk_all_ref[rows], wk_ref[...]) + mm_nt(dv_all_ref[rows], wv_ref[...])

        leave_ref[...] = shared(1 - core).astype(low)
        stay_ref[...] = shared(core) + lax.dot_general(
            dq_all_ref[...], wq_ref[...], (((0,), (1,)), ((), ())), preferred_element_type=f32
        )


def attn_backward(
    first,
    q_t,
    do_t,
    out_t,
    lse,
    keys,
    values,
    k_t,
    key_aug,
    block_rows,
    far,
    bias,
    w_query,
    w_key,
    w_value,
):
    width, tokens = q_t.shape
    key_count = keys.shape[0]
    pairs = width // TILE
    weight = pl.BlockSpec((width, width), lambda h, _: (0, 0), pipeline_mode=pl.Buffered(1))
    whole = pl.BlockSpec((tokens, width), lambda h, _: (0, 0))
    across = pl.BlockSpec((TILE, tokens), lambda h, _: (h, 0))
    along = pl.BlockSpec((key_count, TILE), lambda h, _: (0, h))
    return pl.pallas_call(
        attn_backward_kernel,
        name="attn_backward",
        grid_spec=pltpu.PrefetchScalarGridSpec(
            num_scalar_prefetch=1,
            grid=(pairs,),
            in_specs=[
                across,
                across,
                across,
                pl.BlockSpec((1, 2, tokens), lambda h, _: (h, 0, 0)),
                along,
                along,
                pl.BlockSpec((TILE, key_count), lambda h, _: (h, 0)),
                pl.BlockSpec((key_count, TILE), lambda h, _: (0, 0)),
                pl.BlockSpec((AUG, key_count), lambda h, _: (0, 0)),
                pl.BlockSpec((2, AUG, tokens), lambda h, _: (h, 0, 0)),
                pl.BlockSpec((2, 3, TILE, TILE), lambda h, _: (h, 0, 0, 0)),
                weight,
                weight,
                weight,
            ],
            out_specs=[
                across,
                along,
                along,
                pl.BlockSpec((2, 3, TILE, TILE), lambda h, _: (h, 0, 0, 0)),
                pl.BlockSpec((1, 2, AUG, tokens), lambda h, _: (h, 0, 0, 0)),
                whole,
                whole,
            ],
            scratch_shapes=[
                pltpu.VMEM((key_count + 2 * TILE, tokens), jnp.float32),
                pltpu.VMEM((2, key_count + 2 * TILE, tokens), jnp.bfloat16),
                pltpu.VMEM((2, key_count, tokens), jnp.bfloat16),
                pltpu.VMEM((width, tokens), jnp.bfloat16),
                pltpu.VMEM((key_count, width), jnp.bfloat16),
                pltpu.VMEM((key_count, width), jnp.bfloat16),
            ],
        ),
        out_shape=[
            jax.ShapeDtypeStruct((width, tokens), jnp.bfloat16),
            jax.ShapeDtypeStruct((key_count, width), jnp.bfloat16),
            jax.ShapeDtypeStruct((key_count, width), jnp.bfloat16),
            jax.ShapeDtypeStruct((2 * pairs, 3, TILE, TILE), jnp.float32),
            jax.ShapeDtypeStruct((pairs, 2, AUG, tokens), jnp.float32),
            jax.ShapeDtypeStruct((tokens, width), jnp.bfloat16),
            jax.ShapeDtypeStruct((tokens, width), jnp.float32),
        ],
        compiler_params=pltpu.CompilerParams(vmem_limit_bytes=26 << 20),
    )(
        first,
        q_t,
        do_t,
        out_t,
        lse,
        keys,
        values,
        k_t,
        key_aug,
        block_rows,
        far,
        bias,
        w_query,
        w_key,
        w_value,
    )


def attn_tables(first, tokens, key_count, length, rel_bias):
    low, f32 = (jnp.bfloat16, jnp.float32)
    blocks = key_count // TILE
    assert blocks <= 8
    key_pos = jnp.arange(key_count, dtype=jnp.int32)
    column = jnp.arange(TILE, dtype=jnp.int32)[None, :]
    key_aug = jnp.where(column == (key_pos // TILE)[:, None], 1.0, 0.0)
    dead = jnp.where(2 * key_pos < length, 0.0, -1000000000.0)[:, None]
    key_aug = jnp.where(column == 8, dead, key_aug)
    key_aug = jnp.where((column >= 9) & (column < 12), 1.0, key_aug).astype(low)
    line = jnp.arange(AUG, dtype=jnp.int32)
    block_rows = jnp.where(line[:, None] == (key_pos // TILE)[None, :], 1.0, 0.0).astype(low)
    tile = first + jnp.arange(tokens, dtype=jnp.int32) // TILE
    apart = (line[:, None] - tile[None, :])[None]
    rel_t = rel_bias.astype(f32).T
    before = rel_t[:, BUCKETS // 2 - 1][:, None, None]
    after = rel_t[:, BUCKETS - 1][:, None, None]
    far = jnp.where(apart <= -2, before, jnp.where(apart >= 2, after, 0.0))
    in_use = (line < blocks)[None, :, None]
    far = jnp.where(in_use, far, jnp.where((line == 8)[None, :, None], 1.0, 0.0)).astype(low)
    return key_aug, block_rows, far


def near_bias_kernel(rel_ref, out_ref):
    width = 4 * TILE
    heads = rel_ref.shape[0]
    lane = lax.broadcasted_iota(jnp.int32, (BUCKETS, width), 1)
    bucket = bucket_of(2 * TILE - 1 - lane)
    line = lax.broadcasted_iota(jnp.int32, (BUCKETS, width), 0)
    table = mm(rel_ref[...], jnp.where(bucket == line, 1.0, 0.0).astype(jnp.bfloat16))
    for h in range(heads):
        rows = jnp.broadcast_to(table[h : h + 1], (TILE, width))
        rows = pltpu.roll(rows, 3 * TILE + 1, 1, stride=1, stride_axis=0)
        for d in range(3):
            out_ref[h, d] = rows[:, (2 - d) * TILE : (3 - d) * TILE]


def near_bias(rel_t):
    return pl.pallas_call(
        near_bias_kernel,
        name="near_bias",
        out_shape=jax.ShapeDtypeStruct((rel_t.shape[0], 3, TILE, TILE), jnp.float32),
    )(rel_t)


def bias_gradient_kernel(first_ref, near_ref, sums_ref, out_ref, line_ref):
    width = 4 * TILE
    heads = near_ref.shape[0]
    tokens = sums_ref.shape[3]
    f32 = jnp.float32
    line = lax.broadcasted_iota(jnp.int32, (AUG, tokens), 0)
    tile = first_ref[0] + lax.broadcasted_iota(jnp.int32, (AUG, tokens), 1) // TILE
    apart = line - tile
    column = lax.broadcasted_iota(jnp.int32, (1, BUCKETS), 1)
    far_rows = []
    for h in range(heads):
        tiles = [near_ref[h, 2 - k] for k in range(3)]
        rows = jnp.concatenate(tiles + [jnp.zeros((TILE, TILE), f32)], axis=1)
        eight = rows[:8]
        for start in range(8, TILE, 8):
            eight = eight + pltpu.roll(rows[start : start + 8], width - start, 1)
        total = eight[:1]
        for step in range(1, 8):
            total = total + pltpu.roll(eight[step : step + 1], width - step, 1)
        line_ref[h : h + 1] = total
        sums = sums_ref[h // 2, h % 2]
        before = jnp.sum(jnp.where(apart <= -2, sums, 0.0), axis=1, keepdims=True)
        after = jnp.sum(jnp.where(apart >= 2, sums, 0.0), axis=1, keepdims=True)
        before = jnp.sum(before, axis=0, keepdims=True)
        after = jnp.sum(after, axis=0, keepdims=True)
        far_rows.append(
            jnp.where(column == BUCKETS // 2 - 1, before, 0.0)
            + jnp.where(column == BUCKETS - 1, after, 0.0)
        )
    lane = lax.broadcasted_iota(jnp.int32, (BUCKETS, width), 1)
    offset = jnp.where(lane < 3 * TILE, TILE - lane, 5 * TILE - lane)
    bucket = bucket_of(offset)
    pick = jnp.where(bucket == lax.broadcasted_iota(jnp.int32, (BUCKETS, width), 0), 1.0, 0.0)
    close = lax.dot_general(
        line_ref[...], pick, (((1,), (1,)), ((), ())), precision=highest, preferred_element_type=f32
    )
    out_ref[...] = close + jnp.concatenate(far_rows, axis=0)


def bias_gradient(first_ref, near, sums):
    heads = near.shape[0]
    return pl.pallas_call(
        bias_gradient_kernel,
        name="bias_gradient",
        in_specs=[
            pl.BlockSpec(memory_space=pltpu.SMEM),
            pl.BlockSpec(memory_space=pltpu.VMEM),
            pl.BlockSpec(memory_space=pltpu.VMEM),
        ],
        out_shape=jax.ShapeDtypeStruct((heads, BUCKETS), jnp.float32),
        scratch_shapes=[pltpu.VMEM((heads, 4 * TILE), jnp.float32)],
    )(first_ref, near, sums)


def part_rows(blocks, mine, size):
    width = blocks.shape[-1]
    split = blocks.reshape(blocks.shape[0] // (2 * size), 2, size, width)
    other, own = (split[:, 0], split[:, 1])
    first = mine == 1
    return jnp.where(first, other, own), jnp.where(first, own, other)


def join_rows(own, other, core):
    kind = own.dtype
    chips, size, width = own.shape
    if size % 16:
        own, other = (own.astype(jnp.float32), other.astype(jnp.float32))
    first = core == 0
    blocks = jnp.stack([jnp.where(first, own, other), jnp.where(first, other, own)], axis=1)
    return blocks.reshape(2 * chips * size, width).astype(kind)


def ffn_kernel(
    rows,
    sub,
    folded,
    core_ref,
    hidden_ref,
    att_ref,
    w_out_ref,
    gain_ref,
    seed_ref,
    gate_own_ref,
    gate_other_ref,
    up_own_ref,
    up_other_ref,
    *rest,
):
    f32, low = (jnp.float32, jnp.bfloat16)
    count = 4 if folded else 2
    down_refs, rest = (rest[:count], rest[count:])
    block_ref, grad_ref, grad_low_ref, grad_att_ref, gain_grad_ref = rest[:5]
    out_refs = rest[5:9]
    rest = rest[9:]
    if not folded:
        down_leave_ref, down_stay_ref = rest[:2]
        rest = rest[2:]
    after_ref, unit_ref, normed_ref, normed_t_ref, out_ref, back_ref, *held_refs, sems = rest
    leave_refs, stay_refs = (held_refs[:2], held_refs[2:])
    number = pl.program_id(0)
    core = core_ref[0]
    step = gate_own_ref.shape[2]
    chips, size, packed = held_refs[0].shape
    half_ff = packed // 3
    ff = 2 * half_ff
    width = hidden_ref.shape[1]

    @pl.when(number == 0)
    def _():
        after = hidden_ref[...] + mm_tn(att_ref[...], w_out_ref[...])
        scale = lax.rsqrt(jnp.mean(after * after, axis=1, keepdims=True) + norm_eps)
        normed = (after * scale * gain_ref[...]).astype(low)
        after_ref[...] = after
        unit_ref[...] = jnp.broadcast_to(scale, unit_ref.shape)
        normed_ref[...] = normed
        normed_t_ref[...] = jnp.transpose(normed)
        out_ref[...] = after
        back_ref[...] = jnp.zeros_like(back_ref)

    normed = normed_ref[...]
    seed = seed_ref[...]
    w_gate = join_rows(gate_own_ref[...], gate_other_ref[...], core)
    w_up = join_rows(up_own_ref[...], up_other_ref[...], core)
    if folded:
        own, other = [
            jnp.concatenate([down_refs[i][0], down_refs[i + 2][0]], axis=1).astype(f32)
            for i in range(2)
        ]
        own, other = [
            each_block(unfold_rows, x, rows, width).astype(low)[None] for x in (own, other)
        ]
        w_down = join_rows(own, other, core)
    else:
        w_down = join_rows(down_refs[0][...], down_refs[1][...], core)
    gate = mm(normed, w_gate)
    up = mm(normed, w_up)
    cube = 0.044715 * gate * gate
    bend = jnp.tanh(0.7978845608028654 * (gate + cube * gate))
    half = 0.5 * (1.0 + bend)
    act = gate * half
    slope = half + (0.5 * 0.7978845608028654) * gate * (1.0 - bend * bend) * (1.0 + 3.0 * cube)
    inner = (act * up).astype(low)
    out_ref[...] += mm(inner, w_down)
    grad_inner = mm_nt(seed, w_down)
    grad_gate = (grad_inner * up * slope).astype(low)
    grad_up = (grad_inner * act).astype(low)
    back_ref[...] += mm_nt(grad_gate, w_gate) + mm_nt(grad_up, w_up)
    lanes = pl.ds(pl.multiple_of(number * step, step), step)
    for side, grad in enumerate((grad_gate, grad_up)):
        leave, stay = part_rows(mm(normed_t_ref[...], grad), core, size)
        leave_refs[side][:, :, lanes] = leave.astype(low)
        stay_refs[side][:, :, lanes] = stay.astype(low)
    leave, stay = part_rows(mm_tn(inner, seed), core, sub)
    if folded:
        for refs, part in ((leave_refs, leave), (stay_refs, stay)):
            part = each_block(fold_rows, part[0], 8 * rows // 3, rows).astype(low)
            refs[0][number, :, ff:] = part[:, :half_ff]
            refs[1][number, :, ff:] = part[:, half_ff:]
    else:
        down_leave_ref[...] = leave.astype(low)
        down_stay_ref[...] = stay.astype(low)

    def copies(at):
        lanes = pl.ds(pl.multiple_of(at * step, step), step)
        moves = []
        for i, (held_ref, moved_ref) in enumerate(zip(held_refs, out_refs)):
            moves.append(
                pltpu.make_async_copy(
                    held_ref.at[:, :, lanes], moved_ref.at[:, :, lanes], sems.at[at, i, 0]
                )
            )
            if folded:
                moves.append(
                    pltpu.make_async_copy(
                        held_ref.at[at, :, pl.ds(ff, half_ff)],
                        moved_ref.at[at, :, pl.ds(ff, half_ff)],
                        sems.at[at, i, 1],
                    )
                )
        return moves

    for move in copies(number):
        move.start()

    @pl.when(number == pl.num_programs(0) - 1)
    def _():
        block_ref[...] = out_ref[...].astype(low)
        back = back_ref[...]
        scale = unit_ref[:, :1]
        unit = after_ref[...] * scale
        gained = back * gain_ref[...]
        mean = jnp.mean(gained * unit, axis=1, keepdims=True)
        grad = seed_ref[...].astype(f32) + scale * (gained - unit * mean)
        grad_ref[...] = grad
        grad_low_ref[...] = grad.astype(low)
        grad_att_ref[...] = mm_nt(w_out_ref[...], grad.astype(low)).astype(low)
        gain_grad_ref[...] = jnp.sum(back * unit, axis=0, keepdims=True)
        for at in range(ff // step):
            for move in copies(at):
                move.wait()


def feed_forward(core, hidden, attended_t, w_out, gain, seed, first, second, rows, down_rows):
    tokens, width = hidden.shape
    step = 512
    f32, low = (jnp.float32, jnp.bfloat16)
    ff = 2 * first[0].shape[-1] // 3
    half_ff = ff // 2
    size = rows * lax.axis_size("seq")
    sub = down_rows * lax.axis_size("seq")
    chips = width // (2 * size)
    folded = down_rows != rows and 2 * sub == step
    first, second = [[x.reshape(chips, size, ff + half_ff) for x in pair] for pair in (first, second)]
    once = dict(pipeline_mode=pl.Buffered(1))
    full = pl.BlockSpec((tokens, width), lambda i, _: (0, 0))
    full_once = pl.BlockSpec((tokens, width), lambda i, _: (0, 0), **once)
    line = pl.BlockSpec((1, width), lambda i, _: (0, 0))
    across = pl.BlockSpec((width, tokens), lambda i, _: (0, 0))
    across_once = pl.BlockSpec((width, tokens), lambda i, _: (0, 0), **once)
    columns = pl.BlockSpec((chips, size, step), lambda i, _: (0, 0, i))
    tall = pl.BlockSpec((step // (2 * sub), sub, width), lambda i, _: (i, 0, 0))
    packed = pl.BlockSpec(memory_space=pl.ANY)
    if folded:
        down = [first[0], first[1], second[0], second[1]]
        down_specs = [pl.BlockSpec((1, size, half_ff), lambda i, _: (i, 0, 2))] * 4
    else:
        down = [
            jnp.concatenate([x[..., ff:], y[..., ff:]], axis=-1).reshape(-1, sub, width)
            for x, y in zip(first, second)
        ]
        down_specs = [tall, tall]
    packed_shape = jax.ShapeDtypeStruct((chips, size, ff + half_ff), low)
    tall_shape = jax.ShapeDtypeStruct((ff // (2 * sub), sub, width), low)
    extra = 0 if folded else 2
    out = pl.pallas_call(
        functools.partial(ffn_kernel, rows, sub, folded),
        name="feed_forward",
        grid_spec=pltpu.PrefetchScalarGridSpec(
            num_scalar_prefetch=1,
            grid=(ff // step,),
            in_specs=[
                full_once,
                across_once,
                pl.BlockSpec((width, width), lambda i, _: (0, 0), **once),
                line,
                full_once,
                columns,
                columns,
                columns,
                columns,
            ]
            + down_specs,
            out_specs=[full, full, full, across, line] + [packed] * 4 + [tall] * extra,
            scratch_shapes=[
                pltpu.VMEM((tokens, width), f32),
                pltpu.VMEM((tokens, LANES), f32),
                pltpu.VMEM((tokens, width), low),
                pltpu.VMEM((width, tokens), low),
                pltpu.VMEM((tokens, width), f32),
                pltpu.VMEM((tokens, width), f32),
            ]
            + [pltpu.VMEM((chips, size, ff + half_ff), low)] * 4
            + [pltpu.SemaphoreType.DMA((ff // step, 4, 2 if folded else 1))],
        ),
        out_shape=[
            jax.ShapeDtypeStruct((tokens, width), low),
            jax.ShapeDtypeStruct((tokens, width), f32),
            jax.ShapeDtypeStruct((tokens, width), low),
            jax.ShapeDtypeStruct((width, tokens), low),
            jax.ShapeDtypeStruct((1, width), f32),
        ]
        + [packed_shape] * 4
        + [tall_shape] * extra,
        compiler_params=pltpu.CompilerParams(vmem_limit_bytes=60 << 20),
    )(core, hidden, attended_t, w_out, gain, seed, *first, *second, *down)
    if folded:
        return out
    out = list(out)
    for part in range(2):
        rest = out[9 + part].reshape(chips, size, ff)
        for side in range(2):
            number = 5 + 2 * part + side
            half = rest[..., side * half_ff : (side + 1) * half_ff]
            out[number] = out[number].at[:, :, ff:].set(half)
    return out[:9]


def square_gradient_kernel(
    core_ref,
    normed_ref,
    att_ref,
    dq_ref,
    dk_ref,
    dv_ref,
    do_ref,
    qk_leave_ref,
    vo_leave_ref,
    qk_stay_ref,
    vo_stay_ref,
    normed_t_ref,
):
    core = core_ref[0]
    tokens = att_ref.shape[1]

    @pl.when(pl.program_id(0) == 0)
    def _():
        normed_t_ref[...] = jnp.transpose(normed_ref[...])

    normed_t = normed_t_ref[...]
    own = normed_t_ref[:, pl.ds(pl.multiple_of(core * tokens, tokens), tokens)]
    grads = (
        mm_nt(own, dq_ref[...]),
        mm(normed_t, dk_ref[...]),
        mm(normed_t, dv_ref[...]),
        mm(att_ref[...], do_ref[...]),
    )
    for number, grad in enumerate(grads):
        leave_ref, stay_ref = (
            (qk_leave_ref, qk_stay_ref) if number < 2 else (vo_leave_ref, vo_stay_ref)
        )
        leave, stay = part_rows(grad, core, leave_ref.shape[2])
        leave_ref[number % 2] = leave.astype(jnp.bfloat16)
        stay_ref[number % 2] = stay.astype(jnp.bfloat16)


def square_gradients(core, normed_all, attended_t, grad_q_t, grad_k, grad_v, grad_out, rows):
    keys, width = normed_all.shape
    tokens = attended_t.shape[1]
    step = 256
    chips = width // (2 * rows)
    low = jnp.bfloat16
    block = pl.BlockSpec((2, chips, rows, step), lambda i, _: (0, 0, 0, i))
    shape = jax.ShapeDtypeStruct((2, chips, rows, width), low)
    return pl.pallas_call(
        square_gradient_kernel,
        name="square_gradients",
        grid_spec=pltpu.PrefetchScalarGridSpec(
            num_scalar_prefetch=1,
            grid=(width // step,),
            in_specs=[
                pl.BlockSpec((keys, width), lambda i, _: (0, 0)),
                pl.BlockSpec((width, tokens), lambda i, _: (0, 0)),
                pl.BlockSpec((step, tokens), lambda i, _: (i, 0)),
                pl.BlockSpec((keys, step), lambda i, _: (0, i)),
                pl.BlockSpec((keys, step), lambda i, _: (0, i)),
                pl.BlockSpec((tokens, step), lambda i, _: (0, i)),
            ],
            out_specs=[block] * 4,
            scratch_shapes=[pltpu.VMEM((width, keys), low)],
        ),
        out_shape=[shape] * 4,
        compiler_params=pltpu.CompilerParams(vmem_limit_bytes=18 << 20),
    )(core, normed_all, attended_t, grad_q_t, grad_k, grad_v, grad_out)


def shards(
    embeddings,
    lengths,
    cotangent,
    conv_weight,
    scorer,
    gain_attn,
    w_query,
    w_key,
    w_value,
    w_out,
    rel_bias,
    gain_ffn,
    w_gate,
    w_up,
    w_down,
):
    num_micro, num_seqs, local_bytes, model_width = embeddings.shape
    piece_tokens = local_bytes // 2
    count = num_micro * num_seqs
    seq_count = lax.axis_size("seq")
    assert seq_count == 2 * count
    seq_index = lax.axis_index("seq")
    core = lax.axis_index("dp") % 2
    device = lax.axis_index("dp") * seq_count + seq_index
    local_tokens = count * piece_tokens
    key_count = 2 * local_tokens
    low, f32 = (jnp.bfloat16, jnp.float32)
    phases_a, phases_b = stage_phases()
    along, across_a, across_b = (phases_a[:2], phases_a[2:], phases_b[2:])
    rows = w_query.shape[0]
    vec_rows = KERNEL + 3
    half = 2 * model_width
    ff = w_gate.shape[1]
    chain = Chain()

    groups = exchange_groups()
    lines = [[step] for group in groups for step in group]
    pieces = embeddings.reshape(count, local_bytes, model_width)
    piece_lengths = lengths.reshape(count)
    down_rows = w_down.shape[0]
    folded = rows % 24 == 0 and 2 * down_rows * seq_count == 512 and 3 * ff == 8 * model_width
    down_block = w_down if folded else w_down.reshape(rows, ff)
    square, wide = pack_weights(w_query, w_key, w_value, w_out, w_gate, w_up, down_block)
    digits = jnp.concatenate([piece_lengths // 64, piece_lengths % 64]).astype(low)
    vectors = jnp.concatenate(
        [
            conv_weight,
            scorer[None],
            gain_attn[None],
            gain_ffn[None],
            jnp.broadcast_to(digits[:, None], (2 * count, rows)),
        ],
        axis=0,
    )
    vectors = exchange(vectors, lines[0])
    digits = vectors[1][vec_rows:, 0].astype(jnp.int32)
    other_lengths = 64 * digits[:count] + digits[count:]
    vectors = [vector[:vec_rows] for vector in vectors]
    square = Gathering(chain, square, along)
    bytes_before, bytes_after = neighbour_edges(pieces, 2 * EDGE)
    for number, group in enumerate(lines[1:]):
        vectors = chain.note(jnp.concatenate(chain.after(*vectors), axis=1))
        vectors = exchange(vectors, group)
        if number == 1:
            square.finish()
            wide = Gathering(chain, chain.after(wide), along)
    vectors = chain.note(jnp.concatenate(chain.after(*vectors), axis=1))
    steps = [step for group in groups for step in group]
    source = jnp.arange(model_width, dtype=jnp.int32)
    partner = device ^ sum(
        ((source // rows >> number) & 1) * (1 << bit if axis == "seq" else seq_count << bit)
        for number, (axis, bit) in enumerate(steps)
    )
    target = partner * rows + source % rows
    place = target[:, None] == jnp.arange(model_width, dtype=jnp.int32)[None, :]
    vectors = chain.note(mm(vectors, place.astype(low)))
    gain_one, gain_two = (vectors[KERNEL + 1], vectors[KERNEL + 2])
    token_start = seq_index * piece_tokens
    info = jnp.concatenate([token_start.reshape(1).astype(jnp.int32), piece_lengths])
    square.finish()
    first = Gathering(chain, chain.note(square.whole[..., :half]), across_a, square.held)
    second = Gathering(chain, chain.note(square.whole[..., half:]), across_b, square.held)
    sent = chain.note(
        pool_forward(info, bytes_before, chain.after(pieces), bytes_after, vectors)
    )
    arrived = to_chips(sent)
    chain_lengths = jnp.where(core == seq_index // count, piece_lengths, other_lengths)
    seq_length = lax.dynamic_index_in_dim(chain_lengths, seq_index % count, 0, keepdims=False)
    first_tile = core * (local_tokens // TILE)
    first_ref = first_tile.astype(jnp.int32).reshape(1)
    wide.finish()
    first.finish()
    second.finish()
    seq_length, rel_late = chain.after(seq_length, rel_bias)
    key_aug, block_rows, far = attn_tables(
        first_tile, local_tokens, key_count, seq_length, rel_late
    )
    bias = chain.note(near_bias(rel_late.T))
    wide.finish()
    ff_side = 3 * ff // 2
    gate_full = Gathering(chain, chain.note(wide.whole[..., :ff_side]), across_a, wide.held)
    up_full = Gathering(chain, chain.note(wide.whole[..., ff_side:]), across_b, wide.held)
    arrived = in_token_order(chain.after(*arrived))
    normed_low = chain.note(arrived[:, :piece_tokens].reshape(local_tokens, model_width))
    normed_other = swap_bit(normed_low, "dp", 0)
    scale = arrived[:, piece_tokens : piece_tokens + 2, :piece_tokens].astype(f32)
    scale = jnp.sum(scale, axis=1).reshape(local_tokens, 1)
    unit = normed_low.astype(f32) / gain_one
    hidden_in = unit / scale
    first.finish()
    second.finish()
    normed_other = chain.after(normed_other)
    normed_all = chain.note(
        jnp.concatenate(
            [
                jnp.where(core == 0, normed_low, normed_other),
                jnp.where(core == 0, normed_other, normed_low),
            ],
            axis=0,
        )
    )
    first = first.finish().reshape(model_width, half)
    second = second.finish().reshape(model_width, half)
    query_full, key_full = (first[:, :model_width], first[:, model_width:])
    value_full, out_full = (second[:, :model_width], second[:, model_width:])

    def project_t(weight, tokens):
        return lax.dot_general(
            weight, tokens, (((0,), (1,)), ((), ())), preferred_element_type=f32
        ).astype(low)

    q_t = project_t(query_full, chain.after(normed_low))
    v_t = project_t(value_full, normed_all)
    keys_all = chain.note(mm(normed_all, key_full).astype(low))
    gate_full.finish()
    up_full.finish()
    seed_pieces = cotangent.reshape(count, piece_tokens, model_width)
    seed_arrived = to_chips(chain.after(seed_pieces))
    attended_t, lse = attn_forward(
        first_ref, chain.after(q_t), keys_all, key_aug, v_t, far, bias
    )
    chain.note(attended_t)
    seed_low = in_token_order(chain.after(*seed_arrived)).reshape(local_tokens, model_width)
    chain.note(seed_low)
    gate_full.finish()
    up_full.finish()
    k_t = chain.note(project_t(key_full, chain.after(normed_all)))
    halves = [gather.last() for gather in (gate_full, up_full)]
    waiting = chain.after(*[half[1] for half in halves])
    halves = [(half[0], other) for half, other in zip(halves, waiting)]

    core_ref = core.astype(jnp.int32).reshape(1)
    (
        block_out,
        grad_after,
        grad_after_low,
        grad_attended_t,
        gain_ffn_grad,
        gate_leave,
        up_leave,
        gate_stay,
        up_stay,
    ) = feed_forward(
        core_ref,
        hidden_in,
        attended_t,
        out_full,
        gain_two[None],
        seed_low,
        *halves,
        rows,
        down_rows,
    )
    chain.note(grad_after_low)
    gate_arrived = swap_bit(gate_leave, "dp", 0)
    up_arrived = swap_bit(up_leave, "dp", 0)
    values_all = chain.note(mm(chain.after(normed_all), value_full).astype(low))
    gate_sum = Reduction(chain, gate_stay[None], gate_arrived[None], rows, phases_a)
    up_sum = Reduction(chain, up_stay[None], up_arrived[None], rows, phases_b)
    gate_sum.finish()
    up_sum.finish()
    grad_queries_t, key_terms, value_terms, near, sums, leaving, staying = attn_backward(
        first_ref,
        q_t,
        chain.after(grad_attended_t),
        attended_t,
        lse,
        keys_all,
        values_all,
        k_t,
        key_aug,
        block_rows,
        far,
        bias,
        query_full,
        key_full,
        value_full,
    )
    arrived = swap_bit(chain.note(leaving), "dp", 0)
    blocks_arrived = from_chips(block_out, count)
    blocks_arrived = chain.after(*blocks_arrived)
    chain.note(blocks_arrived[0])
    blocks_out = in_piece_order(blocks_arrived)
    gate_sum.finish()
    up_sum.finish()
    grad_normed = staying + chain.after(arrived).astype(f32)
    gained = grad_normed * gain_one
    grad_hidden = grad_after + scale * (
        gained - unit * jnp.mean(gained * unit, axis=-1, keepdims=True)
    )
    arrived = from_chips(chain.note(grad_hidden.astype(low)), count)
    first_leave, second_leave, first_stay, second_stay = square_gradients(
        core_ref,
        normed_all,
        attended_t,
        grad_queries_t,
        chain.after(key_terms),
        value_terms,
        grad_after_low,
        rows * seq_count,
    )
    chain.note(first_leave)
    grad_pieces = in_piece_order(chain.after(*arrived))
    chain.note(grad_pieces)
    first_arrived = swap_bit(first_leave, "dp", 0)
    second_arrived = swap_bit(second_leave, "dp", 0)
    grad_before, grad_after_edge = neighbour_edges(grad_pieces, EDGE)
    bias_terms = chain.note(bias_gradient(first_ref, chain.after(near), sums))
    first_sum = Reduction(chain, first_stay, first_arrived, rows, phases_a)
    second_sum = Reduction(chain, second_stay, second_arrived, rows, phases_b)
    first_sum.finish()
    second_sum.finish()
    gate_sum.finish()
    up_sum.finish()
    pooled = ()
    for part in range(2):
        pooled = pool_backward(
            info,
            bytes_before,
            pieces,
            bytes_after,
            grad_before,
            chain.after(grad_pieces),
            grad_after_edge,
            vectors,
            part * count // 2,
            (part + 1) * count // 2,
            tuple(pooled),
        )
        chain.note(pooled[1])
        gate_side = gate_sum.finish()
        up_side = up_sum.finish()
        first_sum.finish()
        second_sum.finish()
    gain_attn_grad = chain.note(jnp.sum(chain.after(grad_normed) * unit, axis=0))
    embed_grad, pool_small = pooled
    embed_out = embed_grad.reshape(num_micro, num_seqs, local_bytes, model_width)
    pool_small = jnp.sum(pool_small, axis=0)[: KERNEL + 1]
    bias_row = jnp.pad(bias_terms.reshape(-1), (0, model_width - bias_terms.size))
    small = jnp.concatenate(
        [pool_small, gain_attn_grad[None], gain_ffn_grad, bias_row[None]],
        axis=0,
    )
    small = exchange(chain.note(small), groups[0])
    for group in groups[1:]:
        small = exchange(chain.note(tree_sum(chain.after(*small))), group)
        if group is groups[1]:
            first_sum.finish()
            second_sum.finish()
    small = chain.note(tree_sum(chain.after(*small)))
    gate_side, up_side = (gate_side[0], up_side[0])
    gate_grad, up_grad = (gate_side[:, :ff], up_side[:, :ff])
    down_grad = jnp.concatenate([gate_side[:, ff:], up_side[:, ff:]], axis=1)
    down_grad = (
        unfold_rows(down_grad, model_width) if folded else down_grad.reshape(down_rows, model_width)
    )
    blocks_out = blocks_out.reshape(num_micro, num_seqs, piece_tokens, model_width)
    second_grad = second_sum.finish()
    first_grad = first_sum.finish()
    query_grad, key_grad = (first_grad[0], first_grad[1])
    value_grad, out_grad = (second_grad[0], second_grad[1])
    bias_total = small[vec_rows, : bias_terms.size].reshape(bias_terms.shape).T
    own = lax.dynamic_slice_in_dim(small[:vec_rows], device * rows, rows, axis=1)
    return (
        blocks_out,
        embed_out,
        own[:KERNEL],
        own[KERNEL],
        own[KERNEL + 1],
        query_grad,
        key_grad,
        value_grad,
        out_grad,
        bias_total,
        own[KERNEL + 2],
        gate_grad,
        up_grad,
        down_grad,
    )


def solution(mesh):
    return jax.shard_map(
        shards,
        mesh=mesh,
        in_specs=(
            P(None, "dp", "seq", None),
            P(None, "dp"),
            P(None, "dp", "seq", None),
            P(None, ("dp", "seq")),
            P(("dp", "seq")),
            P(("dp", "seq")),
            P(("dp", "seq"), None),
            P(("dp", "seq"), None),
            P(("dp", "seq"), None),
            P(("dp", "seq"), None),
            P(),
            P(("dp", "seq")),
            P(("dp", "seq"), None),
            P(("dp", "seq"), None),
            P(("dp", "seq"), None),
        ),
        out_specs=(
            P(None, "dp", "seq", None),
            P(None, "dp", "seq", None),
            P(None, ("dp", "seq")),
            P(("dp", "seq")),
            P(("dp", "seq")),
            P(("dp", "seq"), None),
            P(("dp", "seq"), None),
            P(("dp", "seq"), None),
            P(("dp", "seq"), None),
            P(),
            P(("dp", "seq")),
            P(("dp", "seq"), None),
            P(("dp", "seq"), None),
            P(("dp", "seq"), None),
        ),
        check_vma=False,
    )
```

```python
import functools

import jax
import jax.numpy as jnp
from jax import lax
from jax.experimental import pallas as pl
from jax.experimental.layout import Layout, with_layout_constraint
from jax.experimental.pallas import tpu as pltpu
from jax.sharding import PartitionSpec as P

HEADS = 12
HEAD = 64
BUCKETS = 32
KERNEL = 5


norm_eps = 1e-06
highest = lax.Precision.HIGHEST
cut_points = (12, 16, 23, 32, 46, 64, 91)


def neighbour_edges(x, width):
    devices, length = (lax.axis_size("seq"), x.shape[1])
    up = [(i, i + 1) for i in range(devices - 1)]
    down = [(j, i) for i, j in up]
    before = lax.ppermute(x[:, length - width :], "seq", up)
    after = lax.ppermute(x[:, :width], "seq", down)
    return before, after


def bucket_of(offset):
    distance = jnp.abs(offset)
    far_bucket = 8 + sum(((distance >= cut_point).astype(jnp.int32) for cut_point in cut_points))
    return jnp.where(distance < 8, distance, far_bucket) + jnp.where(offset > 0, 16, 0)


EDGE = 8
LANES = 128


def shifted(x, step):
    return pltpu.roll(x, (-step) % x.shape[0], 0)


def byte_facts(token_start, length, rows):
    token = token_start - EDGE + lax.broadcasted_iota(jnp.int32, (rows, LANES), 0)
    first = 2 * token
    even_live = jnp.where((first >= 0) & (first < length), 1.0, 0.0)
    odd_live = jnp.where((first + 1 >= 0) & (first + 1 < length), 1.0, 0.0)
    remainder = lax.rem(first + 6 * EDGE, 3)
    odd_token = lax.rem(token + 2 * EDGE, 2) == 1
    return even_live, odd_live, remainder, odd_token


def pooled_scalars(six, remainder, odd_token):
    even_b, odd_b, even, odd, even_a, odd_a = six
    pair = even + odd
    quad = pair + jnp.where(odd_token, even_b + odd_b, even_a + odd_a)
    shared = pair + jnp.where(remainder == 0, even_a, odd_b)
    split = remainder == 2
    triple_even = jnp.where(split, even_b + odd_b + even, shared)
    triple_odd = jnp.where(split, odd + even_a + odd_a, shared)
    third = 1.0 / 3.0
    return (
        (even, 0.5 * pair, third * triple_even, 0.25 * quad),
        (odd, 0.5 * pair, third * triple_odd, 0.25 * quad),
    )


def spread_scalars(even, odd, remainder, odd_token):
    third = 1.0 / 3.0
    pair = 0.5 * (even[1] + odd[1])
    quad = 0.25 * (even[3] + odd[3])
    both = third * (even[2] + odd[2])
    only_even = third * even[2]
    only_odd = third * odd[2]
    split = remainder == 2
    zero = jnp.zeros_like(pair)
    quad_b = jnp.where(odd_token, quad, zero)
    quad_a = jnp.where(odd_token, zero, quad)
    even_here = even[0] + pair + quad + jnp.where(split, only_even, both)
    odd_here = odd[0] + pair + quad + jnp.where(split, only_odd, both)
    even_b = quad_b + jnp.where(split, only_even, zero)
    odd_b = quad_b + jnp.where(split, only_even, jnp.where(remainder == 1, both, zero))
    even_a = quad_a + jnp.where(split, only_odd, jnp.where(remainder == 0, both, zero))
    odd_a = quad_a + jnp.where(split, only_odd, zero)
    return even_b, odd_b, even_here, odd_here, even_a, odd_a


def softmax_of(logits):
    top = jnp.maximum(jnp.maximum(logits[0], logits[1]), jnp.maximum(logits[2], logits[3]))
    parts = [jnp.exp(logit - top) for logit in logits]
    total = (parts[0] + parts[1]) + (parts[2] + parts[3])
    return [part / total for part in parts]


def lane_sum(x):
    return jnp.broadcast_to(jnp.sum(x, axis=1, keepdims=True), x.shape)


def byte_windows(ref, rows, lanes):
    return [ref[EDGE + step : EDGE + step + rows, lanes] for step in (-1, 0, 1)]


def load_bytes(before_ref, body_ref, after_ref, wide_ref):
    edge = 2 * EDGE
    size = body_ref.shape[1]
    for number in range(body_ref.shape[2] // LANES):
        lanes = slice(number * LANES, (number + 1) * LANES)
        wide_ref[number, :edge] = before_ref[0, :, lanes].astype(jnp.float32)
        wide_ref[number, edge : edge + size] = body_ref[0, :, lanes].astype(jnp.float32)
        wide_ref[number, edge + size :] = after_ref[0, :, lanes].astype(jnp.float32)


def conv_chunk(wide_ref, xe_ref, xo_ref, ce_ref, co_ref, vec_ref, facts, number):
    lanes = chunk_lanes(number)
    rows = facts[0].shape[0]
    main = slice(EDGE, EDGE + rows)
    xe_ref[main, lanes] = wide_ref[number, pl.ds(0, rows, stride=2)] * facts[0]
    xo_ref[main, lanes] = wide_ref[number, pl.ds(1, rows, stride=2)] * facts[1]
    even_b, even, even_a = byte_windows(xe_ref, rows, lanes)
    odd_b, odd, odd_a = byte_windows(xo_ref, rows, lanes)
    taps = [vec_ref[j : j + 1, lanes] for j in range(KERNEL)]
    conv_even = (
        taps[0] * even_b + taps[1] * odd_b + taps[2] * even + taps[3] * odd + taps[4] * even_a
    )
    conv_odd = (
        taps[0] * odd_b + taps[1] * even + taps[2] * odd + taps[3] * even_a + taps[4] * odd_a
    )
    ce_ref[main, lanes] = conv_even * facts[0]
    co_ref[main, lanes] = conv_odd * facts[1]


def clear_edges(refs, rows):
    for ref in refs:
        zeros = jnp.zeros((EDGE, ref.shape[1]), jnp.float32)
        ref[:EDGE] = zeros
        ref[EDGE + rows :] = zeros


def chunk_lanes(number):
    return pl.ds(pl.multiple_of(number * LANES, LANES), LANES)


def size_weights(logit_ref, remainder, odd_token):
    even = lane_sum(logit_ref[0])
    odd = lane_sum(logit_ref[1])
    six = (shifted(even, -1), shifted(odd, -1), even, odd, shifted(even, 1), shifted(odd, 1))
    logits_even, logits_odd = pooled_scalars(six, remainder, odd_token)
    return softmax_of(logits_even), softmax_of(logits_odd)


def pool_forward_kernel(
    info_ref,
    before_ref,
    body_ref,
    after_ref,
    vec_ref,
    out_ref,
    wide_ref,
    xe_ref,
    xo_ref,
    ce_ref,
    co_ref,
    logit_ref,
    coef_ref,
    square_ref,
):
    piece = pl.program_id(0)
    width = body_ref.shape[2]
    tokens = body_ref.shape[1] // 2
    rows = tokens + 2 * EDGE
    chunks = width // LANES
    facts = byte_facts(info_ref[0], info_ref[1 + piece], rows)
    load_bytes(before_ref, body_ref, after_ref, wide_ref)
    clear_edges((xe_ref, xo_ref, ce_ref, co_ref), rows)
    logit_ref[...] = jnp.zeros_like(logit_ref)
    main = slice(EDGE, EDGE + rows)

    def first_pass(number, carry):
        lanes = chunk_lanes(number)
        conv_chunk(wide_ref, xe_ref, xo_ref, ce_ref, co_ref, vec_ref, facts, number)
        scorer = vec_ref[KERNEL : KERNEL + 1, lanes]
        logit_ref[0] = logit_ref[0] + ce_ref[main, lanes] * scorer
        logit_ref[1] = logit_ref[1] + co_ref[main, lanes] * scorer
        return carry

    lax.fori_loop(0, chunks, first_pass, 0)
    remainder, odd_token = facts[2:]
    even, odd = size_weights(logit_ref, remainder, odd_token)
    spread = spread_scalars(even, odd, remainder, odd_token)
    for k in range(6):
        coef_ref[k] = 0.5 * spread[k][EDGE : EDGE + tokens]
    square_ref[...] = jnp.zeros_like(square_ref)

    def second_pass(number, carry):
        lanes = chunk_lanes(number)
        total = None
        for step in range(3):
            start = 2 * EDGE + step - 1
            for parity, ref in ((0, ce_ref), (1, co_ref)):
                term = coef_ref[2 * step + parity] * ref[start : start + tokens, lanes]
                total = term if total is None else total + term
        xe_ref[:tokens, lanes] = total
        square_ref[...] = square_ref[...] + total * total
        return carry

    lax.fori_loop(0, chunks, second_pass, 0)
    scale = lax.rsqrt(lane_sum(square_ref[...]) * (1.0 / width) + norm_eps)
    square_ref[...] = scale

    def third_pass(number, carry):
        lanes = chunk_lanes(number)
        gain = vec_ref[KERNEL + 1 : KERNEL + 2, lanes]
        out_ref[0, :tokens, lanes] = (
            xe_ref[:tokens, lanes] * square_ref[...] * gain
        ).astype(jnp.bfloat16)
        return carry

    lax.fori_loop(0, chunks, third_pass, 0)
    row = jnp.transpose(scale)[: 2 * EDGE]
    top = row.astype(jnp.bfloat16).astype(jnp.float32)
    line = lax.broadcasted_iota(jnp.int32, row.shape, 0)
    tail = jnp.where(line == 0, top, jnp.where(line == 1, row - top, 0.0)).astype(jnp.bfloat16)
    rest = jnp.zeros((2 * EDGE, width - tokens), jnp.bfloat16)
    out_ref[0, tokens:] = jnp.concatenate([tail, rest], axis=1)


def pool_forward(info, before, body, after, vectors):
    count, size, width = body.shape
    tokens = size // 2
    rows = tokens + 2 * EDGE
    assert tokens % LANES == 0 and tokens < width
    wide = pltpu.VMEM((width // LANES, size + 4 * EDGE, LANES), jnp.float32)
    tall = pltpu.VMEM((rows + 2 * EDGE, width), jnp.float32)
    edge = pl.BlockSpec((1, 2 * EDGE, width), lambda p, _: (p, 0, 0))
    return pl.pallas_call(
        pool_forward_kernel,
        name="pool_forward",
        grid_spec=pltpu.PrefetchScalarGridSpec(
            num_scalar_prefetch=1,
            grid=(count,),
            in_specs=[
                edge,
                pl.BlockSpec((1, size, width), lambda p, _: (p, 0, 0)),
                edge,
                pl.BlockSpec((8, width), lambda p, _: (0, 0)),
            ],
            out_specs=pl.BlockSpec((1, tokens + 2 * EDGE, width), lambda p, _: (p, 0, 0)),
            scratch_shapes=[
                wide,
                tall,
                tall,
                tall,
                tall,
                pltpu.VMEM((2, rows, LANES), jnp.float32),
                pltpu.VMEM((6, tokens, LANES), jnp.float32),
                pltpu.VMEM((tokens, LANES), jnp.float32),
            ],
        ),
        out_shape=jax.ShapeDtypeStruct((count, tokens + 2 * EDGE, width), jnp.bfloat16),
        compiler_params=pltpu.CompilerParams(vmem_limit_bytes=14 << 20),
    )(info, before, body, after, vectors)


def pool_backward_kernel(
    base,
    skipped,
    info_ref,
    before_ref,
    body_ref,
    after_ref,
    grad_before_ref,
    grad_ref,
    grad_after_ref,
    vec_ref,
    *rest,
):
    (
        embed_ref,
        small_ref,
        wide_ref,
        xe_ref,
        xo_ref,
        ce_ref,
        co_ref,
        dh_ref,
        de_ref,
        do_ref,
        logit_ref,
        dots_ref,
        coef_ref,
        pair_ref,
    ) = rest[skipped:]
    piece = pl.program_id(0) + base
    width = body_ref.shape[2]
    tokens = body_ref.shape[1] // 2
    rows = tokens + 2 * EDGE
    chunks = width // LANES
    f32 = jnp.float32
    facts = byte_facts(info_ref[0], info_ref[1 + piece], rows)
    load_bytes(before_ref, body_ref, after_ref, wide_ref)
    clear_edges((xe_ref, xo_ref, ce_ref, co_ref, dh_ref, de_ref, do_ref), rows)
    dh_ref[EDGE : 2 * EDGE] = grad_before_ref[0].astype(f32)
    dh_ref[2 * EDGE : 2 * EDGE + tokens] = grad_ref[0].astype(f32)
    dh_ref[2 * EDGE + tokens : 3 * EDGE + tokens] = grad_after_ref[0].astype(f32)
    logit_ref[...] = jnp.zeros_like(logit_ref)
    dots_ref[...] = jnp.zeros_like(dots_ref)
    main = slice(EDGE, EDGE + rows)

    def first_pass(number, carry):
        lanes = chunk_lanes(number)
        conv_chunk(wide_ref, xe_ref, xo_ref, ce_ref, co_ref, vec_ref, facts, number)
        scorer = vec_ref[KERNEL : KERNEL + 1, lanes]
        logit_ref[0] = logit_ref[0] + ce_ref[main, lanes] * scorer
        logit_ref[1] = logit_ref[1] + co_ref[main, lanes] * scorer
        grad = dh_ref[main, lanes]
        for step in range(3):
            start = EDGE + step - 1
            for parity, ref in ((0, ce_ref), (1, co_ref)):
                k = 2 * step + parity
                dots_ref[k] = dots_ref[k] + grad * ref[start : start + rows, lanes]
        return carry

    lax.fori_loop(0, chunks, first_pass, 0)
    remainder, odd_token = facts[2:]
    even, odd = size_weights(logit_ref, remainder, odd_token)
    six = [0.5 * lane_sum(dots_ref[k]) for k in range(6)]
    grads_even, grads_odd = pooled_scalars(six, remainder, odd_token)

    def logit_grads(weights, grads):
        mean = (weights[0] * grads[0] + weights[1] * grads[1]) + (
            weights[2] * grads[2] + weights[3] * grads[3]
        )
        return [weight * (grad - mean) for weight, grad in zip(weights, grads)]

    spread = spread_scalars(even, odd, remainder, odd_token)
    steer = spread_scalars(
        logit_grads(even, grads_even), logit_grads(odd, grads_odd), remainder, odd_token
    )
    for k in range(6):
        step = k // 2 - 1
        coef_ref[k] = 0.5 * shifted(spread[k], -step)
    coef_ref[6] = steer[2] + shifted(steer[4], -1) + shifted(steer[0], 1)
    coef_ref[7] = steer[3] + shifted(steer[5], -1) + shifted(steer[1], 1)

    def second_pass(number, carry):
        lanes = chunk_lanes(number)
        scorer = vec_ref[KERNEL : KERNEL + 1, lanes]
        grad_b, grad, grad_a = byte_windows(dh_ref, rows, lanes)
        for parity, live, ref in ((0, facts[0], de_ref), (1, facts[1], do_ref)):
            total = (
                coef_ref[parity] * grad_a
                + coef_ref[2 + parity] * grad
                + coef_ref[4 + parity] * grad_b
                + coef_ref[6 + parity] * scorer
            )
            ref[main, lanes] = total * live
        own = slice(2 * EDGE, 2 * EDGE + tokens)
        before = slice(2 * EDGE - 1, 2 * EDGE - 1 + tokens)
        after = slice(2 * EDGE + 1, 2 * EDGE + 1 + tokens)
        taps = [vec_ref[j : j + 1, lanes] for j in range(KERNEL)]
        even_b, even, even_a = [de_ref[part, lanes] for part in (before, own, after)]
        odd_b, odd, odd_a = [do_ref[part, lanes] for part in (before, own, after)]
        inner = slice(EDGE, EDGE + tokens)
        pair_ref[pl.ds(0, tokens, stride=2)] = facts[0][inner] * (
            taps[0] * even_a + taps[1] * odd + taps[2] * even + taps[3] * odd_b + taps[4] * even_b
        )
        pair_ref[pl.ds(1, tokens, stride=2)] = facts[1][inner] * (
            taps[0] * odd_a + taps[1] * even_a + taps[2] * odd + taps[3] * even + taps[4] * odd_b
        )
        embed_ref[0, :, lanes] = pair_ref[...]
        x_even = [xe_ref[part, lanes] for part in (before, own, after)]
        x_odd = [xo_ref[part, lanes] for part in (before, own, after)]
        terms = [
            even * x_even[0] + odd * x_odd[0],
            even * x_odd[0] + odd * x_even[1],
            even * x_even[1] + odd * x_odd[1],
            even * x_odd[1] + odd * x_even[2],
            even * x_even[2] + odd * x_odd[2],
            coef_ref[6, inner] * ce_ref[own, lanes] + coef_ref[7, inner] * co_ref[own, lanes],
        ]
        sums = [jnp.sum(term, axis=0, keepdims=True) for term in terms]
        sums = sums + [jnp.zeros_like(sums[0])] * (8 - len(sums))
        small_ref[0, :, lanes] = jnp.concatenate(sums, axis=0)
        return carry

    lax.fori_loop(0, chunks, second_pass, 0)


def pool_backward(
    info, before, body, after, grad_before, grad, grad_after, vectors, base, stop, earlier
):
    count, size, width = body.shape
    tokens = size // 2
    rows = tokens + 2 * EDGE
    wide = pltpu.VMEM((width // LANES, size + 4 * EDGE, LANES), jnp.float32)
    tall = pltpu.VMEM((rows + 2 * EDGE, width), jnp.float32)
    edge = pl.BlockSpec((1, 2 * EDGE, width), lambda p, _: (p + base, 0, 0))
    grad_edge = pl.BlockSpec((1, EDGE, width), lambda p, _: (p + base, 0, 0))
    return pl.pallas_call(
        functools.partial(pool_backward_kernel, base, len(earlier)),
        name="pool_backward",
        grid_spec=pltpu.PrefetchScalarGridSpec(
            num_scalar_prefetch=1,
            grid=(stop - base,),
            in_specs=[
                edge,
                pl.BlockSpec((1, size, width), lambda p, _: (p + base, 0, 0)),
                edge,
                grad_edge,
                pl.BlockSpec((1, tokens, width), lambda p, _: (p + base, 0, 0)),
                grad_edge,
                pl.BlockSpec((8, width), lambda p, _: (0, 0)),
            ]
            + [pl.BlockSpec(memory_space=pl.ANY)] * len(earlier),
            out_specs=[
                pl.BlockSpec((1, size, width), lambda p, _: (p + base, 0, 0)),
                pl.BlockSpec((1, 8, width), lambda p, _: (p + base, 0, 0)),
            ],
            scratch_shapes=[wide]
            + [tall] * 7
            + [
                pltpu.VMEM((2, rows, LANES), jnp.float32),
                pltpu.VMEM((6, rows, LANES), jnp.float32),
                pltpu.VMEM((8, rows, LANES), jnp.float32),
                pltpu.VMEM((size, LANES), jnp.float32),
            ],
        ),
        out_shape=[
            jax.ShapeDtypeStruct((count, size, width), jnp.float32),
            jax.ShapeDtypeStruct((count, 8, width), jnp.float32),
        ],
        input_output_aliases={8 + i: i for i in range(len(earlier))},
        compiler_params=pltpu.CompilerParams(vmem_limit_bytes=20 << 20),
    )(info, before, body, after, grad_before, grad, grad_after, vectors, *earlier)


def bits_of(axis):
    size = lax.axis_size(axis)
    count = size.bit_length() - 1
    assert 1 << count == size
    return count


def stage_phases():
    dp_bits, seq_bits = (bits_of("dp"), bits_of("seq"))
    along = [("seq", bit) for bit in reversed(range(seq_bits))]
    low_half = [("dp", bit) for bit in range(1, 1 + (dp_bits - 1) // 2)]
    high_half = [("dp", bit) for bit in range(1 + (dp_bits - 1) // 2, dp_bits)]
    ends = ([along[:1], along[1:]], [[("dp", 0)]])
    return (ends[0] + [high_half, low_half] + ends[1], ends[0] + [low_half, high_half] + ends[1])


def place_of(axis, bit):
    dp_bits, seq_bits = (bits_of("dp"), bits_of("seq"))
    return dp_bits - 1 - bit if axis == "dp" else dp_bits + seq_bits - 1 - bit


def swap_bit(x, axis, bit):
    size = lax.axis_size(axis)
    return lax.ppermute(x, axis, [(i, i ^ (1 << bit)) for i in range(size)])


def own_bit(axis, bit):
    return (lax.axis_index(axis) >> bit) & 1


def in_order(x):
    return with_layout_constraint(x, Layout(major_to_minor=tuple(range(x.ndim))))


class Chain:
    def __init__(self):
        self.noted = None

    def after(self, *values):
        if self.noted is not None:
            values = lax.optimization_barrier(values + (self.noted,))[:-1]
        return values if len(values) > 1 else values[0]

    def note(self, value):
        self.noted = value
        return value


class Gathering:
    def __init__(self, chain, block, phases, held=()):
        self.chain, self.whole, self.held = (chain, block, list(held))
        self.phases = [list(phase) for phase in phases]
        self.start()

    def start(self):
        if self.phases:
            self.arrived = swap_bit(self.whole, *self.phases[0][0])

    def finish(self):
        for axis, bit in self.phases.pop(0):
            if self.arrived is None:
                self.arrived = swap_bit(self.whole, axis, bit)
            place = place_of(axis, bit)
            dim = sum(other < place for other in self.held)
            arrived, whole = self.chain.after(self.arrived, self.whole)
            upper = own_bit(axis, bit) == 1
            self.whole = self.chain.note(
                in_order(
                    jnp.stack(
                        [jnp.where(upper, arrived, whole), jnp.where(upper, whole, arrived)],
                        axis=dim,
                    )
                )
            )
            self.held.append(place)
            self.arrived = None
        self.start()
        return self.whole


    def last(self):
        assert len(self.phases) == 1
        return self.whole, self.arrived


class Reduction:
    def __init__(self, chain, staying, arriving, rows, phases):
        self.chain = chain
        phases = phases[::-1]
        assert phases[0] == [("dp", 0)]
        self.steps = [step for phase in phases[1:] for step in phase[::-1]]
        self.counts = [len(phase) for phase in phases]
        self.held = list(range(1 + len(self.steps)))
        self.held.remove(place_of("dp", 0))
        shape = staying.shape[:1] + (2,) * len(self.steps) + (rows, staying.shape[-1])
        self.staying = staying.reshape(shape)
        self.arriving = arriving.reshape(shape)

    def halves(self, x):
        axis, bit = self.steps[0]
        dim = 1 + self.held.index(place_of(axis, bit))
        own = own_bit(axis, bit)
        return [
            lax.dynamic_index_in_dim(x, which, dim, keepdims=False) for which in (1 - own, own)
        ]

    def finish(self):
        f32 = jnp.float32
        for _ in range(self.counts.pop(0)):
            arrived, staying = self.chain.after(self.arriving, self.staying)
            if not self.steps:
                self.chain.note(arrived)
                return staying.astype(f32) + arrived.astype(f32)
            parts = zip(self.halves(staying), self.halves(arrived))
            leaving, staying = [
                (x.astype(f32) + y.astype(f32)).astype(jnp.bfloat16) for x, y in parts
            ]
            self.chain.note(leaving)
            self.staying = staying
            axis, bit = self.steps.pop(0)
            self.held.remove(place_of(axis, bit))
            self.arriving = swap_bit(leaving, axis, bit)


def group_masks(group):
    axis = group[0][0]
    size = lax.axis_size(axis)
    masks = [0]
    for _, bit in group:
        masks = masks + [mask | 1 << bit for mask in masks]
    return [(axis, [(i, i ^ mask) for i in range(size)]) for mask in masks[1:]]


def exchange(x, group):
    return [x] + [lax.ppermute(x, axis, pairs) for axis, pairs in group_masks(group)]


def tree_sum(values):
    while len(values) > 1:
        values = [a + b for a, b in zip(values[::2], values[1::2])]
    return values[0]


def exchange_groups():
    groups = [[("dp", 0)]]
    for axis, first in (("dp", 1), ("seq", 0)):
        left = [(axis, bit) for bit in range(first, bits_of(axis))]
        groups += [left[i : i + 2] for i in range(0, len(left), 2)]
    return groups


def fold_rows(x, rows):
    width, third, side = (x.shape[1], rows // 3, x.shape[1] // 3)
    rest = x[2 * rows :]
    corner = jnp.concatenate([rest[:third, 2 * side :], rest[third:, 2 * side :]], axis=1)
    tail = jnp.concatenate([rest[:, : 2 * side], corner], axis=0)
    return jnp.concatenate([x[:rows], x[rows : 2 * rows], tail], axis=1)


def unfold_rows(x, width):
    rows, third, side = (x.shape[0], x.shape[0] // 3, width // 3)
    tail = x[:, 2 * width :]
    corner = tail[2 * third :]
    right = jnp.concatenate([corner[:, :side], corner[:, side:]], axis=0)
    rest = jnp.concatenate([tail[: 2 * third], right], axis=1)
    return jnp.concatenate([x[:, :width], x[:, width : 2 * width], rest], axis=0)


def each_block(fold, x, size, *rest):
    parts = [fold(x[i : i + size], *rest) for i in range(0, x.shape[0], size)]
    return parts[0] if len(parts) == 1 else jnp.concatenate(parts, axis=0)


def pack_kernel(*refs):
    *square, gate_ref, up_ref, down_ref, square_ref, wide_ref = refs
    rows, ff = gate_ref.shape
    place = 0
    for ref in square:
        width = ref.shape[1]
        square_ref[:, place : place + width] = ref[...]
        place += width
    half = ff // 2
    down = down_ref[...]
    if down.shape[0] != rows:
        down = fold_rows(down.astype(jnp.float32), rows).astype(jnp.bfloat16)
    wide_ref[:, :ff] = gate_ref[...]
    wide_ref[:, ff : ff + half] = down[:, :half]
    wide_ref[:, ff + half : 2 * ff + half] = up_ref[...]
    wide_ref[:, 2 * ff + half :] = down[:, half:]


def pack_weights(w_query, w_key, w_value, w_out, w_gate, w_up, w_down):
    rows = w_query.shape[0]
    parts = (w_query, w_key, w_value, w_out, w_gate, w_up, w_down)
    widths = (4 * w_query.shape[1], 3 * w_gate.shape[1])
    return pl.pallas_call(
        pack_kernel,
        name="pack_weights",
        out_shape=[jax.ShapeDtypeStruct((rows, width), w_query.dtype) for width in widths],
    )(*parts)


def to_chips(pieces):
    count = pieces.shape[0]
    dp_size, seq_size = (lax.axis_size("dp"), lax.axis_size("seq"))
    seq_index = lax.axis_index("seq")
    arrived = []
    for phase in range(count):
        pairs = chip_pairs(dp_size, seq_size, count, phase)
        leaving = lax.dynamic_index_in_dim(pieces, (seq_index + phase) % count, 0, keepdims=False)
        arrived.append(lax.ppermute(leaving, ("dp", "seq"), pairs))
    return arrived


def in_token_order(arrived):
    count = len(arrived)
    number = lax.axis_index("seq") % count
    stacked = jnp.stack(arrived)
    return jnp.stack(
        [
            lax.dynamic_index_in_dim(stacked, (number - r) % count, 0, keepdims=False)
            for r in range(count)
        ]
    )


def from_chips(tokens, count):
    dp_size, seq_size = (lax.axis_size("dp"), lax.axis_size("seq"))
    number = lax.axis_index("seq") % count
    split = tokens.reshape((count, tokens.shape[0] // count) + tokens.shape[1:])
    arrived = []
    for phase in range(count):
        pairs = [(j, i) for i, j in chip_pairs(dp_size, seq_size, count, phase)]
        leaving = lax.dynamic_index_in_dim(split, (number - phase) % count, 0, keepdims=False)
        arrived.append(lax.ppermute(leaving, ("dp", "seq"), pairs))
    return arrived


def in_piece_order(arrived):
    count = len(arrived)
    seq_index = lax.axis_index("seq")
    stacked = jnp.stack(arrived)
    return jnp.stack(
        [
            lax.dynamic_index_in_dim(stacked, (j - seq_index) % count, 0, keepdims=False)
            for j in range(count)
        ]
    )


def chip_pairs(dp_size, seq_size, count, phase):
    pairs = []
    for dp in range(dp_size):
        for seq in range(seq_size):
            core_to = seq // count
            seq_to = dp % 2 * count + (seq + phase) % count
            pairs.append((dp * seq_size + seq, (dp // 2 * 2 + core_to) * seq_size + seq_to))
    return pairs


TILE = 128
AUG = 16


def mm(a, b):
    return jnp.dot(a, b, preferred_element_type=jnp.float32)


def mm_nt(a, b):
    return lax.dot_general(a, b, (((1,), (1,)), ((), ())), preferred_element_type=jnp.float32)


def mm_tn(a, b):
    return lax.dot_general(a, b, (((0,), (0,)), ((), ())), preferred_element_type=jnp.float32)


def one_head(pair_rows, a):
    zeros = jnp.zeros((HEAD, pair_rows.shape[1]), pair_rows.dtype)
    half = pair_rows[a * HEAD : (a + 1) * HEAD]
    return jnp.concatenate([half, zeros] if a == 0 else [zeros, half], axis=0)


def near_rows(first_tile, i, d):
    return pl.ds(pl.multiple_of((first_tile + (i + d)) * TILE, TILE), TILE)


def split_rows(base, row):
    low, f32 = (jnp.bfloat16, jnp.float32)
    top = row.astype(low).astype(f32)
    middle = (row - top).astype(low).astype(f32)
    bottom = row - top - middle
    line = lax.broadcasted_iota(jnp.int32, base.shape, 0)
    return jnp.where(
        line == 9, -top, jnp.where(line == 10, -middle, jnp.where(line == 11, -bottom, base))
    ).astype(low)


def attn_forward_kernel(
    first_ref, q_ref, k_ref, ka_ref, v_ref, far_ref, bias_ref, out_ref, lse_ref, s_ref
):
    keys = k_ref.shape[0]
    tokens = q_ref.shape[1]
    lhs = jnp.concatenate([k_ref[...], ka_ref[...]], axis=1)
    pad = jnp.zeros((TILE - AUG, tokens), jnp.bfloat16)
    first = first_ref[0]
    for a in range(2):
        rhs = jnp.concatenate([one_head(q_ref[...], a), far_ref[a], pad], axis=0)
        s_ref[TILE : TILE + keys] = mm(lhs, rhs)
        for i in range(tokens // TILE):
            for d in range(3):
                rows = near_rows(first, i, d)
                lanes = slice(i * TILE, (i + 1) * TILE)
                s_ref[rows, lanes] = s_ref[rows, lanes] + bias_ref[a, d]
        s = s_ref[TILE : TILE + keys]
        row_max = jnp.max(s, axis=0, keepdims=True)
        probs = jnp.exp(s - row_max).astype(jnp.bfloat16)
        v_rows = jnp.concatenate(
            [v_ref[a * HEAD : (a + 1) * HEAD], jnp.ones((AUG, keys), jnp.bfloat16)], axis=0
        )
        both = mm(v_rows, probs)
        total = both[HEAD : HEAD + 1]
        out_ref[a * HEAD : (a + 1) * HEAD] = (both[:HEAD] / total).astype(jnp.bfloat16)
        lse_ref[0, a : a + 1] = row_max + jnp.log(total)


def attn_forward(first, q_t, keys, key_aug, v_t, far, bias):
    width, tokens = q_t.shape
    key_count = keys.shape[0]
    pairs = width // TILE
    return pl.pallas_call(
        attn_forward_kernel,
        name="attn_forward",
        grid_spec=pltpu.PrefetchScalarGridSpec(
            num_scalar_prefetch=1,
            grid=(pairs,),
            in_specs=[
                pl.BlockSpec((TILE, tokens), lambda h, _: (h, 0)),
                pl.BlockSpec((key_count, TILE), lambda h, _: (0, h)),
                pl.BlockSpec((key_count, TILE), lambda h, _: (0, 0)),
                pl.BlockSpec((TILE, key_count), lambda h, _: (h, 0)),
                pl.BlockSpec((2, AUG, tokens), lambda h, _: (h, 0, 0)),
                pl.BlockSpec((2, 3, TILE, TILE), lambda h, _: (h, 0, 0, 0)),
            ],
            out_specs=[
                pl.BlockSpec((TILE, tokens), lambda h, _: (h, 0)),
                pl.BlockSpec((1, 2, tokens), lambda h, _: (h, 0, 0)),
            ],
            scratch_shapes=[pltpu.VMEM((key_count + 2 * TILE, tokens), jnp.float32)],
        ),
        out_shape=[
            jax.ShapeDtypeStruct((width, tokens), jnp.bfloat16),
            jax.ShapeDtypeStruct((pairs, 2, tokens), jnp.float32),
        ],
        compiler_params=pltpu.CompilerParams(vmem_limit_bytes=14 << 20),
    )(first, q_t, keys, key_aug, v_t, far, bias)


def attn_backward_kernel(
    first_ref,
    q_ref,
    do_ref,
    out_ref,
    lse_ref,
    k_ref,
    v_ref,
    kt_ref,
    ka_ref,
    block_ref,
    far_ref,
    bias_ref,
    wq_ref,
    wk_ref,
    wv_ref,
    dq_ref,
    dk_ref,
    dv_ref,
    near_ref,
    sums_ref,
    leave_ref,
    stay_ref,
    s_ref,
    ds_ref,
    p_ref,
    dq_all_ref,
    dk_all_ref,
    dv_all_ref,
):
    keys = k_ref.shape[0]
    tokens = q_ref.shape[1]
    f32, low = (jnp.float32, jnp.bfloat16)
    first = first_ref[0]
    main = slice(TILE, TILE + keys)
    k_lhs = jnp.concatenate([k_ref[...], ka_ref[...]], axis=1)
    v_lhs = jnp.concatenate([v_ref[...], ka_ref[...]], axis=1)
    pad = jnp.zeros((TILE - AUG, tokens), low)
    edge = jnp.zeros((TILE, tokens), low)
    q_heads = [one_head(q_ref[...], a) for a in range(2)]
    do_heads = [one_head(do_ref[...], a) for a in range(2)]
    for a in range(2):
        head = slice(a * HEAD, (a + 1) * HEAD)
        aug = split_rows(far_ref[a].astype(f32), lse_ref[0, a : a + 1])
        s_ref[main] = mm(k_lhs, jnp.concatenate([q_heads[a], aug, pad], axis=0))
        for i in range(tokens // TILE):
            for d in range(3):
                rows = near_rows(first, i, d)
                lanes = slice(i * TILE, (i + 1) * TILE)
                s_ref[rows, lanes] = s_ref[rows, lanes] + bias_ref[a, d]
        probs = jnp.exp(s_ref[main])
        p_ref[a] = probs.astype(low)
        row_dot = jnp.sum(
            do_ref[head].astype(f32) * out_ref[head].astype(f32), axis=0, keepdims=True
        )
        aug = split_rows(jnp.zeros((AUG, tokens), f32), row_dot)
        grad_probs = mm(v_lhs, jnp.concatenate([do_heads[a], aug, pad], axis=0))
        ds_ref[a, main] = (probs * grad_probs).astype(low)
        ds_ref[a, :TILE] = edge
        ds_ref[a, TILE + keys :] = edge
        left = jnp.concatenate([kt_ref[head], block_ref[...]], axis=0)
        both = mm(left, ds_ref[a, main])
        dq_ref[head] = both[:HEAD].astype(low)
        sums_ref[0, a] = both[HEAD:]
        for d in range(3):
            total = None
            for i in range(tokens // TILE):
                rows = near_rows(first, i, d)
                term = ds_ref[a, rows, i * TILE : (i + 1) * TILE].astype(f32)
                total = term if total is None else total + term
            near_ref[a, d] = total
    dk_ref[...] = mm_nt(
        jnp.concatenate([ds_ref[0, main], ds_ref[1, main]], axis=1),
        jnp.concatenate(q_heads, axis=1),
    ).astype(low)
    dv_ref[...] = mm_nt(
        jnp.concatenate([p_ref[0], p_ref[1]], axis=1), jnp.concatenate(do_heads, axis=1)
    ).astype(low)
    pair = pl.program_id(0)
    place = pl.ds(pl.multiple_of(pair * TILE, TILE), TILE)
    dq_all_ref[place] = dq_ref[...]
    dk_all_ref[:, place] = dk_ref[...]
    dv_all_ref[:, place] = dv_ref[...]

    @pl.when(pair == pl.num_programs(0) - 1)
    def _():
        core = jnp.where(first == 0, 0, 1)

        def shared(number):
            rows = pl.ds(pl.multiple_of(number * tokens, tokens), tokens)
            return mm_nt(dk_all_ref[rows], wk_ref[...]) + mm_nt(dv_all_ref[rows], wv_ref[...])

        leave_ref[...] = shared(1 - core).astype(low)
        stay_ref[...] = shared(core) + lax.dot_general(
            dq_all_ref[...], wq_ref[...], (((0,), (1,)), ((), ())), preferred_element_type=f32
        )


def attn_backward(
    first,
    q_t,
    do_t,
    out_t,
    lse,
    keys,
    values,
    k_t,
    key_aug,
    block_rows,
    far,
    bias,
    w_query,
    w_key,
    w_value,
):
    width, tokens = q_t.shape
    key_count = keys.shape[0]
    pairs = width // TILE
    weight = pl.BlockSpec((width, width), lambda h, _: (0, 0), pipeline_mode=pl.Buffered(1))
    whole = pl.BlockSpec((tokens, width), lambda h, _: (0, 0))
    across = pl.BlockSpec((TILE, tokens), lambda h, _: (h, 0))
    along = pl.BlockSpec((key_count, TILE), lambda h, _: (0, h))
    return pl.pallas_call(
        attn_backward_kernel,
        name="attn_backward",
        grid_spec=pltpu.PrefetchScalarGridSpec(
            num_scalar_prefetch=1,
            grid=(pairs,),
            in_specs=[
                across,
                across,
                across,
                pl.BlockSpec((1, 2, tokens), lambda h, _: (h, 0, 0)),
                along,
                along,
                pl.BlockSpec((TILE, key_count), lambda h, _: (h, 0)),
                pl.BlockSpec((key_count, TILE), lambda h, _: (0, 0)),
                pl.BlockSpec((AUG, key_count), lambda h, _: (0, 0)),
                pl.BlockSpec((2, AUG, tokens), lambda h, _: (h, 0, 0)),
                pl.BlockSpec((2, 3, TILE, TILE), lambda h, _: (h, 0, 0, 0)),
                weight,
                weight,
                weight,
            ],
            out_specs=[
                across,
                along,
                along,
                pl.BlockSpec((2, 3, TILE, TILE), lambda h, _: (h, 0, 0, 0)),
                pl.BlockSpec((1, 2, AUG, tokens), lambda h, _: (h, 0, 0, 0)),
                whole,
                whole,
            ],
            scratch_shapes=[
                pltpu.VMEM((key_count + 2 * TILE, tokens), jnp.float32),
                pltpu.VMEM((2, key_count + 2 * TILE, tokens), jnp.bfloat16),
                pltpu.VMEM((2, key_count, tokens), jnp.bfloat16),
                pltpu.VMEM((width, tokens), jnp.bfloat16),
                pltpu.VMEM((key_count, width), jnp.bfloat16),
                pltpu.VMEM((key_count, width), jnp.bfloat16),
            ],
        ),
        out_shape=[
            jax.ShapeDtypeStruct((width, tokens), jnp.bfloat16),
            jax.ShapeDtypeStruct((key_count, width), jnp.bfloat16),
            jax.ShapeDtypeStruct((key_count, width), jnp.bfloat16),
            jax.ShapeDtypeStruct((2 * pairs, 3, TILE, TILE), jnp.float32),
            jax.ShapeDtypeStruct((pairs, 2, AUG, tokens), jnp.float32),
            jax.ShapeDtypeStruct((tokens, width), jnp.bfloat16),
            jax.ShapeDtypeStruct((tokens, width), jnp.float32),
        ],
        compiler_params=pltpu.CompilerParams(vmem_limit_bytes=26 << 20),
    )(
        first,
        q_t,
        do_t,
        out_t,
        lse,
        keys,
        values,
        k_t,
        key_aug,
        block_rows,
        far,
        bias,
        w_query,
        w_key,
        w_value,
    )


def attn_tables(first, tokens, key_count, length, rel_bias):
    low, f32 = (jnp.bfloat16, jnp.float32)
    blocks = key_count // TILE
    assert blocks <= 8
    key_pos = jnp.arange(key_count, dtype=jnp.int32)
    column = jnp.arange(TILE, dtype=jnp.int32)[None, :]
    key_aug = jnp.where(column == (key_pos // TILE)[:, None], 1.0, 0.0)
    dead = jnp.where(2 * key_pos < length, 0.0, -1000000000.0)[:, None]
    key_aug = jnp.where(column == 8, dead, key_aug)
    key_aug = jnp.where((column >= 9) & (column < 12), 1.0, key_aug).astype(low)
    line = jnp.arange(AUG, dtype=jnp.int32)
    block_rows = jnp.where(line[:, None] == (key_pos // TILE)[None, :], 1.0, 0.0).astype(low)
    tile = first + jnp.arange(tokens, dtype=jnp.int32) // TILE
    apart = (line[:, None] - tile[None, :])[None]
    rel_t = rel_bias.astype(f32).T
    before = rel_t[:, BUCKETS // 2 - 1][:, None, None]
    after = rel_t[:, BUCKETS - 1][:, None, None]
    far = jnp.where(apart <= -2, before, jnp.where(apart >= 2, after, 0.0))
    in_use = (line < blocks)[None, :, None]
    far = jnp.where(in_use, far, jnp.where((line == 8)[None, :, None], 1.0, 0.0)).astype(low)
    return key_aug, block_rows, far


def near_bias_kernel(rel_ref, out_ref):
    width = 4 * TILE
    heads = rel_ref.shape[0]
    lane = lax.broadcasted_iota(jnp.int32, (BUCKETS, width), 1)
    bucket = bucket_of(2 * TILE - 1 - lane)
    line = lax.broadcasted_iota(jnp.int32, (BUCKETS, width), 0)
    table = mm(rel_ref[...], jnp.where(bucket == line, 1.0, 0.0).astype(jnp.bfloat16))
    for h in range(heads):
        rows = jnp.broadcast_to(table[h : h + 1], (TILE, width))
        rows = pltpu.roll(rows, 3 * TILE + 1, 1, stride=1, stride_axis=0)
        for d in range(3):
            out_ref[h, d] = rows[:, (2 - d) * TILE : (3 - d) * TILE]


def near_bias(rel_t):
    return pl.pallas_call(
        near_bias_kernel,
        name="near_bias",
        out_shape=jax.ShapeDtypeStruct((rel_t.shape[0], 3, TILE, TILE), jnp.float32),
    )(rel_t)


def bias_gradient_kernel(first_ref, near_ref, sums_ref, out_ref, line_ref):
    width = 4 * TILE
    heads = near_ref.shape[0]
    tokens = sums_ref.shape[3]
    f32 = jnp.float32
    line = lax.broadcasted_iota(jnp.int32, (AUG, tokens), 0)
    tile = first_ref[0] + lax.broadcasted_iota(jnp.int32, (AUG, tokens), 1) // TILE
    apart = line - tile
    column = lax.broadcasted_iota(jnp.int32, (1, BUCKETS), 1)
    far_rows = []
    for h in range(heads):
        tiles = [near_ref[h, 2 - k] for k in range(3)]
        rows = jnp.concatenate(tiles + [jnp.zeros((TILE, TILE), f32)], axis=1)
        eight = rows[:8]
        for start in range(8, TILE, 8):
            eight = eight + pltpu.roll(rows[start : start + 8], width - start, 1)
        total = eight[:1]
        for step in range(1, 8):
            total = total + pltpu.roll(eight[step : step + 1], width - step, 1)
        line_ref[h : h + 1] = total
        sums = sums_ref[h // 2, h % 2]
        before = jnp.sum(jnp.where(apart <= -2, sums, 0.0), axis=1, keepdims=True)
        after = jnp.sum(jnp.where(apart >= 2, sums, 0.0), axis=1, keepdims=True)
        before = jnp.sum(before, axis=0, keepdims=True)
        after = jnp.sum(after, axis=0, keepdims=True)
        far_rows.append(
            jnp.where(column == BUCKETS // 2 - 1, before, 0.0)
            + jnp.where(column == BUCKETS - 1, after, 0.0)
        )
    lane = lax.broadcasted_iota(jnp.int32, (BUCKETS, width), 1)
    offset = jnp.where(lane < 3 * TILE, TILE - lane, 5 * TILE - lane)
    bucket = bucket_of(offset)
    pick = jnp.where(bucket == lax.broadcasted_iota(jnp.int32, (BUCKETS, width), 0), 1.0, 0.0)
    close = lax.dot_general(
        line_ref[...], pick, (((1,), (1,)), ((), ())), precision=highest, preferred_element_type=f32
    )
    out_ref[...] = close + jnp.concatenate(far_rows, axis=0)


def bias_gradient(first_ref, near, sums):
    heads = near.shape[0]
    return pl.pallas_call(
        bias_gradient_kernel,
        name="bias_gradient",
        in_specs=[
            pl.BlockSpec(memory_space=pltpu.SMEM),
            pl.BlockSpec(memory_space=pltpu.VMEM),
            pl.BlockSpec(memory_space=pltpu.VMEM),
        ],
        out_shape=jax.ShapeDtypeStruct((heads, BUCKETS), jnp.float32),
        scratch_shapes=[pltpu.VMEM((heads, 4 * TILE), jnp.float32)],
    )(first_ref, near, sums)


def part_rows(blocks, mine, size):
    width = blocks.shape[-1]
    split = blocks.reshape(blocks.shape[0] // (2 * size), 2, size, width)
    other, own = (split[:, 0], split[:, 1])
    first = mine == 1
    return jnp.where(first, other, own), jnp.where(first, own, other)


def join_rows(own, other, core):
    kind = own.dtype
    chips, size, width = own.shape
    if size % 16:
        own, other = (own.astype(jnp.float32), other.astype(jnp.float32))
    first = core == 0
    blocks = jnp.stack([jnp.where(first, own, other), jnp.where(first, other, own)], axis=1)
    return blocks.reshape(2 * chips * size, width).astype(kind)


def ffn_kernel(
    rows,
    sub,
    folded,
    core_ref,
    hidden_ref,
    att_ref,
    w_out_ref,
    gain_ref,
    seed_ref,
    gate_own_ref,
    gate_other_ref,
    up_own_ref,
    up_other_ref,
    *rest,
):
    f32, low = (jnp.float32, jnp.bfloat16)
    count = 4 if folded else 2
    down_refs, rest = (rest[:count], rest[count:])
    block_ref, grad_ref, grad_low_ref, grad_att_ref, gain_grad_ref = rest[:5]
    out_refs = rest[5:9]
    rest = rest[9:]
    if not folded:
        down_leave_ref, down_stay_ref = rest[:2]
        rest = rest[2:]
    after_ref, unit_ref, normed_ref, normed_t_ref, out_ref, back_ref, *held_refs, sems = rest
    leave_refs, stay_refs = (held_refs[:2], held_refs[2:])
    number = pl.program_id(0)
    core = core_ref[0]
    step = gate_own_ref.shape[2]
    chips, size, packed = held_refs[0].shape
    half_ff = packed // 3
    ff = 2 * half_ff
    width = hidden_ref.shape[1]

    @pl.when(number == 0)
    def _():
        after = hidden_ref[...] + mm_tn(att_ref[...], w_out_ref[...])
        scale = lax.rsqrt(jnp.mean(after * after, axis=1, keepdims=True) + norm_eps)
        normed = (after * scale * gain_ref[...]).astype(low)
        after_ref[...] = after
        unit_ref[...] = jnp.broadcast_to(scale, unit_ref.shape)
        normed_ref[...] = normed
        normed_t_ref[...] = jnp.transpose(normed)
        out_ref[...] = after
        back_ref[...] = jnp.zeros_like(back_ref)

    normed = normed_ref[...]
    seed = seed_ref[...]
    w_gate = join_rows(gate_own_ref[...], gate_other_ref[...], core)
    w_up = join_rows(up_own_ref[...], up_other_ref[...], core)
    if folded:
        own, other = [
            jnp.concatenate([down_refs[i][0], down_refs[i + 2][0]], axis=1).astype(f32)
            for i in range(2)
        ]
        own, other = [
            each_block(unfold_rows, x, rows, width).astype(low)[None] for x in (own, other)
        ]
        w_down = join_rows(own, other, core)
    else:
        w_down = join_rows(down_refs[0][...], down_refs[1][...], core)
    gate = mm(normed, w_gate)
    up = mm(normed, w_up)
    cube = 0.044715 * gate * gate
    bend = jnp.tanh(0.7978845608028654 * (gate + cube * gate))
    half = 0.5 * (1.0 + bend)
    act = gate * half
    slope = half + (0.5 * 0.7978845608028654) * gate * (1.0 - bend * bend) * (1.0 + 3.0 * cube)
    inner = (act * up).astype(low)
    out_ref[...] += mm(inner, w_down)
    grad_inner = mm_nt(seed, w_down)
    grad_gate = (grad_inner * up * slope).astype(low)
    grad_up = (grad_inner * act).astype(low)
    back_ref[...] += mm_nt(grad_gate, w_gate) + mm_nt(grad_up, w_up)
    lanes = pl.ds(pl.multiple_of(number * step, step), step)
    for side, grad in enumerate((grad_gate, grad_up)):
        leave, stay = part_rows(mm(normed_t_ref[...], grad), core, size)
        leave_refs[side][:, :, lanes] = leave.astype(low)
        stay_refs[side][:, :, lanes] = stay.astype(low)
    leave, stay = part_rows(mm_tn(inner, seed), core, sub)
    if folded:
        for refs, part in ((leave_refs, leave), (stay_refs, stay)):
            part = each_block(fold_rows, part[0], 8 * rows // 3, rows).astype(low)
            refs[0][number, :, ff:] = part[:, :half_ff]
            refs[1][number, :, ff:] = part[:, half_ff:]
    else:
        down_leave_ref[...] = leave.astype(low)
        down_stay_ref[...] = stay.astype(low)

    def copies(at):
        lanes = pl.ds(pl.multiple_of(at * step, step), step)
        moves = []
        for i, (held_ref, moved_ref) in enumerate(zip(held_refs, out_refs)):
            moves.append(
                pltpu.make_async_copy(
                    held_ref.at[:, :, lanes], moved_ref.at[:, :, lanes], sems.at[at, i, 0]
                )
            )
            if folded:
                moves.append(
                    pltpu.make_async_copy(
                        held_ref.at[at, :, pl.ds(ff, half_ff)],
                        moved_ref.at[at, :, pl.ds(ff, half_ff)],
                        sems.at[at, i, 1],
                    )
                )
        return moves

    for move in copies(number):
        move.start()

    @pl.when(number == pl.num_programs(0) - 1)
    def _():
        block_ref[...] = out_ref[...].astype(low)
        back = back_ref[...]
        scale = unit_ref[:, :1]
        unit = after_ref[...] * scale
        gained = back * gain_ref[...]
        mean = jnp.mean(gained * unit, axis=1, keepdims=True)
        grad = seed_ref[...].astype(f32) + scale * (gained - unit * mean)
        grad_ref[...] = grad
        grad_low_ref[...] = grad.astype(low)
        grad_att_ref[...] = mm_nt(w_out_ref[...], grad.astype(low)).astype(low)
        gain_grad_ref[...] = jnp.sum(back * unit, axis=0, keepdims=True)
        for at in range(ff // step):
            for move in copies(at):
                move.wait()


def feed_forward(core, hidden, attended_t, w_out, gain, seed, first, second, rows, down_rows):
    tokens, width = hidden.shape
    step = 512
    f32, low = (jnp.float32, jnp.bfloat16)
    ff = 2 * first[0].shape[-1] // 3
    half_ff = ff // 2
    size = rows * lax.axis_size("seq")
    sub = down_rows * lax.axis_size("seq")
    chips = width // (2 * size)
    folded = down_rows != rows and 2 * sub == step
    first, second = [[x.reshape(chips, size, ff + half_ff) for x in pair] for pair in (first, second)]
    once = dict(pipeline_mode=pl.Buffered(1))
    full = pl.BlockSpec((tokens, width), lambda i, _: (0, 0))
    full_once = pl.BlockSpec((tokens, width), lambda i, _: (0, 0), **once)
    line = pl.BlockSpec((1, width), lambda i, _: (0, 0))
    across = pl.BlockSpec((width, tokens), lambda i, _: (0, 0))
    across_once = pl.BlockSpec((width, tokens), lambda i, _: (0, 0), **once)
    columns = pl.BlockSpec((chips, size, step), lambda i, _: (0, 0, i))
    tall = pl.BlockSpec((step // (2 * sub), sub, width), lambda i, _: (i, 0, 0))
    packed = pl.BlockSpec(memory_space=pl.ANY)
    if folded:
        down = [first[0], first[1], second[0], second[1]]
        down_specs = [pl.BlockSpec((1, size, half_ff), lambda i, _: (i, 0, 2))] * 4
    else:
        down = [
            jnp.concatenate([x[..., ff:], y[..., ff:]], axis=-1).reshape(-1, sub, width)
            for x, y in zip(first, second)
        ]
        down_specs = [tall, tall]
    packed_shape = jax.ShapeDtypeStruct((chips, size, ff + half_ff), low)
    tall_shape = jax.ShapeDtypeStruct((ff // (2 * sub), sub, width), low)
    extra = 0 if folded else 2
    out = pl.pallas_call(
        functools.partial(ffn_kernel, rows, sub, folded),
        name="feed_forward",
        grid_spec=pltpu.PrefetchScalarGridSpec(
            num_scalar_prefetch=1,
            grid=(ff // step,),
            in_specs=[
                full_once,
                across_once,
                pl.BlockSpec((width, width), lambda i, _: (0, 0), **once),
                line,
                full_once,
                columns,
                columns,
                columns,
                columns,
            ]
            + down_specs,
            out_specs=[full, full, full, across, line] + [packed] * 4 + [tall] * extra,
            scratch_shapes=[
                pltpu.VMEM((tokens, width), f32),
                pltpu.VMEM((tokens, LANES), f32),
                pltpu.VMEM((tokens, width), low),
                pltpu.VMEM((width, tokens), low),
                pltpu.VMEM((tokens, width), f32),
                pltpu.VMEM((tokens, width), f32),
            ]
            + [pltpu.VMEM((chips, size, ff + half_ff), low)] * 4
            + [pltpu.SemaphoreType.DMA((ff // step, 4, 2 if folded else 1))],
        ),
        out_shape=[
            jax.ShapeDtypeStruct((tokens, width), low),
            jax.ShapeDtypeStruct((tokens, width), f32),
            jax.ShapeDtypeStruct((tokens, width), low),
            jax.ShapeDtypeStruct((width, tokens), low),
            jax.ShapeDtypeStruct((1, width), f32),
        ]
        + [packed_shape] * 4
        + [tall_shape] * extra,
        compiler_params=pltpu.CompilerParams(vmem_limit_bytes=60 << 20),
    )(core, hidden, attended_t, w_out, gain, seed, *first, *second, *down)
    if folded:
        return out
    out = list(out)
    for part in range(2):
        rest = out[9 + part].reshape(chips, size, ff)
        for side in range(2):
            number = 5 + 2 * part + side
            half = rest[..., side * half_ff : (side + 1) * half_ff]
            out[number] = out[number].at[:, :, ff:].set(half)
    return out[:9]


def square_gradient_kernel(
    core_ref,
    normed_ref,
    att_ref,
    dq_ref,
    dk_ref,
    dv_ref,
    do_ref,
    qk_leave_ref,
    vo_leave_ref,
    qk_stay_ref,
    vo_stay_ref,
    normed_t_ref,
):
    core = core_ref[0]
    tokens = att_ref.shape[1]

    @pl.when(pl.program_id(0) == 0)
    def _():
        normed_t_ref[...] = jnp.transpose(normed_ref[...])

    normed_t = normed_t_ref[...]
    own = normed_t_ref[:, pl.ds(pl.multiple_of(core * tokens, tokens), tokens)]
    grads = (
        mm_nt(own, dq_ref[...]),
        mm(normed_t, dk_ref[...]),
        mm(normed_t, dv_ref[...]),
        mm(att_ref[...], do_ref[...]),
    )
    for number, grad in enumerate(grads):
        leave_ref, stay_ref = (
            (qk_leave_ref, qk_stay_ref) if number < 2 else (vo_leave_ref, vo_stay_ref)
        )
        leave, stay = part_rows(grad, core, leave_ref.shape[2])
        leave_ref[number % 2] = leave.astype(jnp.bfloat16)
        stay_ref[number % 2] = stay.astype(jnp.bfloat16)


def square_gradients(core, normed_all, attended_t, grad_q_t, grad_k, grad_v, grad_out, rows):
    keys, width = normed_all.shape
    tokens = attended_t.shape[1]
    step = 256
    chips = width // (2 * rows)
    low = jnp.bfloat16
    block = pl.BlockSpec((2, chips, rows, step), lambda i, _: (0, 0, 0, i))
    shape = jax.ShapeDtypeStruct((2, chips, rows, width), low)
    return pl.pallas_call(
        square_gradient_kernel,
        name="square_gradients",
        grid_spec=pltpu.PrefetchScalarGridSpec(
            num_scalar_prefetch=1,
            grid=(width // step,),
            in_specs=[
                pl.BlockSpec((keys, width), lambda i, _: (0, 0)),
                pl.BlockSpec((width, tokens), lambda i, _: (0, 0)),
                pl.BlockSpec((step, tokens), lambda i, _: (i, 0)),
                pl.BlockSpec((keys, step), lambda i, _: (0, i)),
                pl.BlockSpec((keys, step), lambda i, _: (0, i)),
                pl.BlockSpec((tokens, step), lambda i, _: (0, i)),
            ],
            out_specs=[block] * 4,
            scratch_shapes=[pltpu.VMEM((width, keys), low)],
        ),
        out_shape=[shape] * 4,
        compiler_params=pltpu.CompilerParams(vmem_limit_bytes=18 << 20),
    )(core, normed_all, attended_t, grad_q_t, grad_k, grad_v, grad_out)


def shards(
    embeddings,
    lengths,
    cotangent,
    conv_weight,
    scorer,
    gain_attn,
    w_query,
    w_key,
    w_value,
    w_out,
    rel_bias,
    gain_ffn,
    w_gate,
    w_up,
    w_down,
):
    num_micro, num_seqs, local_bytes, model_width = embeddings.shape
    piece_tokens = local_bytes // 2
    count = num_micro * num_seqs
    seq_count = lax.axis_size("seq")
    assert seq_count == 2 * count
    seq_index = lax.axis_index("seq")
    core = lax.axis_index("dp") % 2
    device = lax.axis_index("dp") * seq_count + seq_index
    local_tokens = count * piece_tokens
    key_count = 2 * local_tokens
    low, f32 = (jnp.bfloat16, jnp.float32)
    phases_a, phases_b = stage_phases()
    along, across_a, across_b = (phases_a[:2], phases_a[2:], phases_b[2:])
    rows = w_query.shape[0]
    vec_rows = KERNEL + 3
    half = 2 * model_width
    ff = w_gate.shape[1]
    chain = Chain()

    groups = exchange_groups()
    lines = [[step] for group in groups for step in group]
    pieces = embeddings.reshape(count, local_bytes, model_width)
    piece_lengths = lengths.reshape(count)
    down_rows = w_down.shape[0]
    folded = rows % 24 == 0 and 2 * down_rows * seq_count == 512 and 3 * ff == 8 * model_width
    down_block = w_down if folded else w_down.reshape(rows, ff)
    square, wide = pack_weights(w_query, w_key, w_value, w_out, w_gate, w_up, down_block)
    digits = jnp.concatenate([piece_lengths // 64, piece_lengths % 64]).astype(low)
    vectors = jnp.concatenate(
        [
            conv_weight,
            scorer[None],
            gain_attn[None],
            gain_ffn[None],
            jnp.broadcast_to(digits[:, None], (2 * count, rows)),
        ],
        axis=0,
    )
    vectors = exchange(vectors, lines[0])
    digits = vectors[1][vec_rows:, 0].astype(jnp.int32)
    other_lengths = 64 * digits[:count] + digits[count:]
    vectors = [vector[:vec_rows] for vector in vectors]
    square = Gathering(chain, square, along)
    bytes_before, bytes_after = neighbour_edges(pieces, 2 * EDGE)
    for number, group in enumerate(lines[1:]):
        vectors = chain.note(jnp.concatenate(chain.after(*vectors), axis=1))
        vectors = exchange(vectors, group)
        if number == 1:
            square.finish()
            wide = Gathering(chain, chain.after(wide), along)
    vectors = chain.note(jnp.concatenate(chain.after(*vectors), axis=1))
    steps = [step for group in groups for step in group]
    source = jnp.arange(model_width, dtype=jnp.int32)
    partner = device ^ sum(
        ((source // rows >> number) & 1) * (1 << bit if axis == "seq" else seq_count << bit)
        for number, (axis, bit) in enumerate(steps)
    )
    target = partner * rows + source % rows
    place = target[:, None] == jnp.arange(model_width, dtype=jnp.int32)[None, :]
    vectors = chain.note(mm(vectors, place.astype(low)))
    gain_one, gain_two = (vectors[KERNEL + 1], vectors[KERNEL + 2])
    token_start = seq_index * piece_tokens
    info = jnp.concatenate([token_start.reshape(1).astype(jnp.int32), piece_lengths])
    square.finish()
    first = Gathering(chain, chain.note(square.whole[..., :half]), across_a, square.held)
    second = Gathering(chain, chain.note(square.whole[..., half:]), across_b, square.held)
    sent = chain.note(
        pool_forward(info, bytes_before, chain.after(pieces), bytes_after, vectors)
    )
    arrived = to_chips(sent)
    chain_lengths = jnp.where(core == seq_index // count, piece_lengths, other_lengths)
    seq_length = lax.dynamic_index_in_dim(chain_lengths, seq_index % count, 0, keepdims=False)
    first_tile = core * (local_tokens // TILE)
    first_ref = first_tile.astype(jnp.int32).reshape(1)
    wide.finish()
    first.finish()
    second.finish()
    seq_length, rel_late = chain.after(seq_length, rel_bias)
    key_aug, block_rows, far = attn_tables(
        first_tile, local_tokens, key_count, seq_length, rel_late
    )
    bias = chain.note(near_bias(rel_late.T))
    wide.finish()
    ff_side = 3 * ff // 2
    gate_full = Gathering(chain, chain.note(wide.whole[..., :ff_side]), across_a, wide.held)
    up_full = Gathering(chain, chain.note(wide.whole[..., ff_side:]), across_b, wide.held)
    arrived = in_token_order(chain.after(*arrived))
    normed_low = chain.note(arrived[:, :piece_tokens].reshape(local_tokens, model_width))
    normed_other = swap_bit(normed_low, "dp", 0)
    scale = arrived[:, piece_tokens : piece_tokens + 2, :piece_tokens].astype(f32)
    scale = jnp.sum(scale, axis=1).reshape(local_tokens, 1)
    unit = normed_low.astype(f32) / gain_one
    hidden_in = unit / scale
    first.finish()
    second.finish()
    normed_other = chain.after(normed_other)
    normed_all = chain.note(
        jnp.concatenate(
            [
                jnp.where(core == 0, normed_low, normed_other),
                jnp.where(core == 0, normed_other, normed_low),
            ],
            axis=0,
        )
    )
    first = first.finish().reshape(model_width, half)
    second = second.finish().reshape(model_width, half)
    query_full, key_full = (first[:, :model_width], first[:, model_width:])
    value_full, out_full = (second[:, :model_width], second[:, model_width:])

    def project_t(weight, tokens):
        return lax.dot_general(
            weight, tokens, (((0,), (1,)), ((), ())), preferred_element_type=f32
        ).astype(low)

    q_t = project_t(query_full, chain.after(normed_low))
    v_t = project_t(value_full, normed_all)
    keys_all = chain.note(mm(normed_all, key_full).astype(low))
    gate_full.finish()
    up_full.finish()
    seed_pieces = cotangent.reshape(count, piece_tokens, model_width)
    seed_arrived = to_chips(chain.after(seed_pieces))
    attended_t, lse = attn_forward(
        first_ref, chain.after(q_t), keys_all, key_aug, v_t, far, bias
    )
    chain.note(attended_t)
    seed_low = in_token_order(chain.after(*seed_arrived)).reshape(local_tokens, model_width)
    chain.note(seed_low)
    gate_full.finish()
    up_full.finish()
    k_t = chain.note(project_t(key_full, chain.after(normed_all)))
    halves = [gather.last() for gather in (gate_full, up_full)]
    waiting = chain.after(*[half[1] for half in halves])
    halves = [(half[0], other) for half, other in zip(halves, waiting)]

    core_ref = core.astype(jnp.int32).reshape(1)
    (
        block_out,
        grad_after,
        grad_after_low,
        grad_attended_t,
        gain_ffn_grad,
        gate_leave,
        up_leave,
        gate_stay,
        up_stay,
    ) = feed_forward(
        core_ref,
        hidden_in,
        attended_t,
        out_full,
        gain_two[None],
        seed_low,
        *halves,
        rows,
        down_rows,
    )
    chain.note(grad_after_low)
    gate_arrived = swap_bit(gate_leave, "dp", 0)
    up_arrived = swap_bit(up_leave, "dp", 0)
    values_all = chain.note(mm(chain.after(normed_all), value_full).astype(low))
    gate_sum = Reduction(chain, gate_stay[None], gate_arrived[None], rows, phases_a)
    up_sum = Reduction(chain, up_stay[None], up_arrived[None], rows, phases_b)
    gate_sum.finish()
    up_sum.finish()
    grad_queries_t, key_terms, value_terms, near, sums, leaving, staying = attn_backward(
        first_ref,
        q_t,
        chain.after(grad_attended_t),
        attended_t,
        lse,
        keys_all,
        values_all,
        k_t,
        key_aug,
        block_rows,
        far,
        bias,
        query_full,
        key_full,
        value_full,
    )
    arrived = swap_bit(chain.note(leaving), "dp", 0)
    gate_sum.finish()
    up_sum.finish()
    grad_normed = staying + chain.after(arrived).astype(f32)
    gained = grad_normed * gain_one
    grad_hidden = grad_after + scale * (
        gained - unit * jnp.mean(gained * unit, axis=-1, keepdims=True)
    )
    arrived = from_chips(chain.note(grad_hidden.astype(low)), count)
    first_leave, second_leave, first_stay, second_stay = square_gradients(
        core_ref,
        normed_all,
        attended_t,
        grad_queries_t,
        chain.after(key_terms),
        value_terms,
        grad_after_low,
        rows * seq_count,
    )
    chain.note(first_leave)
    grad_pieces = in_piece_order(chain.after(*arrived))
    chain.note(grad_pieces)
    first_arrived = swap_bit(first_leave, "dp", 0)
    second_arrived = swap_bit(second_leave, "dp", 0)
    grad_before, grad_after_edge = neighbour_edges(grad_pieces, EDGE)
    bias_terms = chain.note(bias_gradient(first_ref, chain.after(near), sums))
    first_sum = Reduction(chain, first_stay, first_arrived, rows, phases_a)
    second_sum = Reduction(chain, second_stay, second_arrived, rows, phases_b)
    first_sum.finish()
    second_sum.finish()
    gate_sum.finish()
    up_sum.finish()
    pooled = ()
    for part in range(2):
        pooled = pool_backward(
            info,
            bytes_before,
            pieces,
            bytes_after,
            grad_before,
            chain.after(grad_pieces),
            grad_after_edge,
            vectors,
            part * count // 2,
            (part + 1) * count // 2,
            tuple(pooled),
        )
        chain.note(pooled[1])
        if part == 1:
            blocks_arrived = from_chips(chain.after(block_out), count)
        gate_side = gate_sum.finish()
        up_side = up_sum.finish()
        first_sum.finish()
        second_sum.finish()
    gain_attn_grad = chain.note(jnp.sum(chain.after(grad_normed) * unit, axis=0))
    embed_grad, pool_small = pooled
    embed_out = embed_grad.reshape(num_micro, num_seqs, local_bytes, model_width)
    pool_small = jnp.sum(pool_small, axis=0)[: KERNEL + 1]
    bias_row = jnp.pad(bias_terms.reshape(-1), (0, model_width - bias_terms.size))
    small = jnp.concatenate(
        [pool_small, gain_attn_grad[None], gain_ffn_grad, bias_row[None]],
        axis=0,
    )
    small = exchange(chain.note(small), groups[0])
    for group in groups[1:]:
        small = exchange(chain.note(tree_sum(chain.after(*small))), group)
        if group is groups[1]:
            first_sum.finish()
            second_sum.finish()
    small = chain.note(tree_sum(chain.after(*small)))
    blocks_out = in_piece_order(chain.after(*blocks_arrived))
    gate_side, up_side = (gate_side[0], up_side[0])
    gate_grad, up_grad = (gate_side[:, :ff], up_side[:, :ff])
    down_grad = jnp.concatenate([gate_side[:, ff:], up_side[:, ff:]], axis=1)
    down_grad = (
        unfold_rows(down_grad, model_width) if folded else down_grad.reshape(down_rows, model_width)
    )
    blocks_out = blocks_out.reshape(num_micro, num_seqs, piece_tokens, model_width)
    second_grad = second_sum.finish()
    first_grad = first_sum.finish()
    query_grad, key_grad = (first_grad[0], first_grad[1])
    value_grad, out_grad = (second_grad[0], second_grad[1])
    bias_total = small[vec_rows, : bias_terms.size].reshape(bias_terms.shape).T
    own = lax.dynamic_slice_in_dim(small[:vec_rows], device * rows, rows, axis=1)
    return (
        blocks_out,
        embed_out,
        own[:KERNEL],
        own[KERNEL],
        own[KERNEL + 1],
        query_grad,
        key_grad,
        value_grad,
        out_grad,
        bias_total,
        own[KERNEL + 2],
        gate_grad,
        up_grad,
        down_grad,
    )


def solution(mesh):
    return jax.shard_map(
        shards,
        mesh=mesh,
        in_specs=(
            P(None, "dp", "seq", None),
            P(None, "dp"),
            P(None, "dp", "seq", None),
            P(None, ("dp", "seq")),
            P(("dp", "seq")),
            P(("dp", "seq")),
            P(("dp", "seq"), None),
            P(("dp", "seq"), None),
            P(("dp", "seq"), None),
            P(("dp", "seq"), None),
            P(),
            P(("dp", "seq")),
            P(("dp", "seq"), None),
            P(("dp", "seq"), None),
            P(("dp", "seq"), None),
        ),
        out_specs=(
            P(None, "dp", "seq", None),
            P(None, "dp", "seq", None),
            P(None, ("dp", "seq")),
            P(("dp", "seq")),
            P(("dp", "seq")),
            P(("dp", "seq"), None),
            P(("dp", "seq"), None),
            P(("dp", "seq"), None),
            P(("dp", "seq"), None),
            P(),
            P(("dp", "seq")),
            P(("dp", "seq"), None),
            P(("dp", "seq"), None),
            P(("dp", "seq"), None),
        ),
        check_vma=False,
    )
```

```python
import functools

import jax
import jax.numpy as jnp
from jax import lax
from jax.experimental import pallas as pl
from jax.experimental.layout import Layout, with_layout_constraint
from jax.experimental.pallas import tpu as pltpu
from jax.sharding import PartitionSpec as P

HEADS = 12
HEAD = 64
BUCKETS = 32
KERNEL = 5


norm_eps = 1e-06
highest = lax.Precision.HIGHEST
cut_points = (12, 16, 23, 32, 46, 64, 91)


def neighbour_edges(x, width):
    devices, length = (lax.axis_size("seq"), x.shape[1])
    up = [(i, i + 1) for i in range(devices - 1)]
    down = [(j, i) for i, j in up]
    before = lax.ppermute(x[:, length - width :], "seq", up)
    after = lax.ppermute(x[:, :width], "seq", down)
    return before, after


def bucket_of(offset):
    distance = jnp.abs(offset)
    far_bucket = 8 + sum(((distance >= cut_point).astype(jnp.int32) for cut_point in cut_points))
    return jnp.where(distance < 8, distance, far_bucket) + jnp.where(offset > 0, 16, 0)


EDGE = 8
LANES = 128


def shifted(x, step):
    return pltpu.roll(x, (-step) % x.shape[0], 0)


def byte_facts(token_start, length, rows):
    token = token_start - EDGE + lax.broadcasted_iota(jnp.int32, (rows, LANES), 0)
    first = 2 * token
    even_live = jnp.where((first >= 0) & (first < length), 1.0, 0.0)
    odd_live = jnp.where((first + 1 >= 0) & (first + 1 < length), 1.0, 0.0)
    remainder = lax.rem(first + 6 * EDGE, 3)
    odd_token = lax.rem(token + 2 * EDGE, 2) == 1
    return even_live, odd_live, remainder, odd_token


def pooled_scalars(six, remainder, odd_token):
    even_b, odd_b, even, odd, even_a, odd_a = six
    pair = even + odd
    quad = pair + jnp.where(odd_token, even_b + odd_b, even_a + odd_a)
    shared = pair + jnp.where(remainder == 0, even_a, odd_b)
    split = remainder == 2
    triple_even = jnp.where(split, even_b + odd_b + even, shared)
    triple_odd = jnp.where(split, odd + even_a + odd_a, shared)
    third = 1.0 / 3.0
    return (
        (even, 0.5 * pair, third * triple_even, 0.25 * quad),
        (odd, 0.5 * pair, third * triple_odd, 0.25 * quad),
    )


def spread_scalars(even, odd, remainder, odd_token):
    third = 1.0 / 3.0
    pair = 0.5 * (even[1] + odd[1])
    quad = 0.25 * (even[3] + odd[3])
    both = third * (even[2] + odd[2])
    only_even = third * even[2]
    only_odd = third * odd[2]
    split = remainder == 2
    zero = jnp.zeros_like(pair)
    quad_b = jnp.where(odd_token, quad, zero)
    quad_a = jnp.where(odd_token, zero, quad)
    even_here = even[0] + pair + quad + jnp.where(split, only_even, both)
    odd_here = odd[0] + pair + quad + jnp.where(split, only_odd, both)
    even_b = quad_b + jnp.where(split, only_even, zero)
    odd_b = quad_b + jnp.where(split, only_even, jnp.where(remainder == 1, both, zero))
    even_a = quad_a + jnp.where(split, only_odd, jnp.where(remainder == 0, both, zero))
    odd_a = quad_a + jnp.where(split, only_odd, zero)
    return even_b, odd_b, even_here, odd_here, even_a, odd_a


def softmax_of(logits):
    top = jnp.maximum(jnp.maximum(logits[0], logits[1]), jnp.maximum(logits[2], logits[3]))
    parts = [jnp.exp(logit - top) for logit in logits]
    total = (parts[0] + parts[1]) + (parts[2] + parts[3])
    return [part / total for part in parts]


def lane_sum(x):
    return jnp.broadcast_to(jnp.sum(x, axis=1, keepdims=True), x.shape)


def byte_windows(ref, rows, lanes):
    return [ref[EDGE + step : EDGE + step + rows, lanes] for step in (-1, 0, 1)]


def load_bytes(before_ref, body_ref, after_ref, wide_ref):
    edge = 2 * EDGE
    size = body_ref.shape[1]
    for number in range(body_ref.shape[2] // LANES):
        lanes = slice(number * LANES, (number + 1) * LANES)
        wide_ref[number, :edge] = before_ref[0, :, lanes].astype(jnp.float32)
        wide_ref[number, edge : edge + size] = body_ref[0, :, lanes].astype(jnp.float32)
        wide_ref[number, edge + size :] = after_ref[0, :, lanes].astype(jnp.float32)


def conv_chunk(wide_ref, xe_ref, xo_ref, ce_ref, co_ref, vec_ref, facts, number):
    lanes = chunk_lanes(number)
    rows = facts[0].shape[0]
    main = slice(EDGE, EDGE + rows)
    xe_ref[main, lanes] = wide_ref[number, pl.ds(0, rows, stride=2)] * facts[0]
    xo_ref[main, lanes] = wide_ref[number, pl.ds(1, rows, stride=2)] * facts[1]
    even_b, even, even_a = byte_windows(xe_ref, rows, lanes)
    odd_b, odd, odd_a = byte_windows(xo_ref, rows, lanes)
    taps = [vec_ref[j : j + 1, lanes] for j in range(KERNEL)]
    conv_even = (
        taps[0] * even_b + taps[1] * odd_b + taps[2] * even + taps[3] * odd + taps[4] * even_a
    )
    conv_odd = (
        taps[0] * odd_b + taps[1] * even + taps[2] * odd + taps[3] * even_a + taps[4] * odd_a
    )
    ce_ref[main, lanes] = conv_even * facts[0]
    co_ref[main, lanes] = conv_odd * facts[1]


def clear_edges(refs, rows):
    for ref in refs:
        zeros = jnp.zeros((EDGE, ref.shape[1]), jnp.float32)
        ref[:EDGE] = zeros
        ref[EDGE + rows :] = zeros


def chunk_lanes(number):
    return pl.ds(pl.multiple_of(number * LANES, LANES), LANES)


def size_weights(logit_ref, remainder, odd_token):
    even = lane_sum(logit_ref[0])
    odd = lane_sum(logit_ref[1])
    six = (shifted(even, -1), shifted(odd, -1), even, odd, shifted(even, 1), shifted(odd, 1))
    logits_even, logits_odd = pooled_scalars(six, remainder, odd_token)
    return softmax_of(logits_even), softmax_of(logits_odd)


def pool_forward_kernel(
    info_ref,
    before_ref,
    body_ref,
    after_ref,
    vec_ref,
    out_ref,
    wide_ref,
    xe_ref,
    xo_ref,
    ce_ref,
    co_ref,
    logit_ref,
    coef_ref,
    square_ref,
):
    piece = pl.program_id(0)
    width = body_ref.shape[2]
    tokens = body_ref.shape[1] // 2
    rows = tokens + 2 * EDGE
    chunks = width // LANES
    facts = byte_facts(info_ref[0], info_ref[1 + piece], rows)
    load_bytes(before_ref, body_ref, after_ref, wide_ref)
    clear_edges((xe_ref, xo_ref, ce_ref, co_ref), rows)
    logit_ref[...] = jnp.zeros_like(logit_ref)
    main = slice(EDGE, EDGE + rows)

    def first_pass(number, carry):
        lanes = chunk_lanes(number)
        conv_chunk(wide_ref, xe_ref, xo_ref, ce_ref, co_ref, vec_ref, facts, number)
        scorer = vec_ref[KERNEL : KERNEL + 1, lanes]
        logit_ref[0] = logit_ref[0] + ce_ref[main, lanes] * scorer
        logit_ref[1] = logit_ref[1] + co_ref[main, lanes] * scorer
        return carry

    lax.fori_loop(0, chunks, first_pass, 0)
    remainder, odd_token = facts[2:]
    even, odd = size_weights(logit_ref, remainder, odd_token)
    spread = spread_scalars(even, odd, remainder, odd_token)
    for k in range(6):
        coef_ref[k] = 0.5 * spread[k][EDGE : EDGE + tokens]
    square_ref[...] = jnp.zeros_like(square_ref)

    def second_pass(number, carry):
        lanes = chunk_lanes(number)
        total = None
        for step in range(3):
            start = 2 * EDGE + step - 1
            for parity, ref in ((0, ce_ref), (1, co_ref)):
                term = coef_ref[2 * step + parity] * ref[start : start + tokens, lanes]
                total = term if total is None else total + term
        xe_ref[:tokens, lanes] = total
        square_ref[...] = square_ref[...] + total * total
        return carry

    lax.fori_loop(0, chunks, second_pass, 0)
    scale = lax.rsqrt(lane_sum(square_ref[...]) * (1.0 / width) + norm_eps)
    square_ref[...] = scale

    def third_pass(number, carry):
        lanes = chunk_lanes(number)
        gain = vec_ref[KERNEL + 1 : KERNEL + 2, lanes]
        out_ref[0, :tokens, lanes] = (
            xe_ref[:tokens, lanes] * square_ref[...] * gain
        ).astype(jnp.bfloat16)
        return carry

    lax.fori_loop(0, chunks, third_pass, 0)
    row = jnp.transpose(scale)[: 2 * EDGE]
    top = row.astype(jnp.bfloat16).astype(jnp.float32)
    line = lax.broadcasted_iota(jnp.int32, row.shape, 0)
    tail = jnp.where(line == 0, top, jnp.where(line == 1, row - top, 0.0)).astype(jnp.bfloat16)
    rest = jnp.zeros((2 * EDGE, width - tokens), jnp.bfloat16)
    out_ref[0, tokens:] = jnp.concatenate([tail, rest], axis=1)


def pool_forward(info, before, body, after, vectors):
    count, size, width = body.shape
    tokens = size // 2
    rows = tokens + 2 * EDGE
    assert tokens % LANES == 0 and tokens < width
    wide = pltpu.VMEM((width // LANES, size + 4 * EDGE, LANES), jnp.float32)
    tall = pltpu.VMEM((rows + 2 * EDGE, width), jnp.float32)
    edge = pl.BlockSpec((1, 2 * EDGE, width), lambda p, _: (p, 0, 0))
    return pl.pallas_call(
        pool_forward_kernel,
        name="pool_forward",
        grid_spec=pltpu.PrefetchScalarGridSpec(
            num_scalar_prefetch=1,
            grid=(count,),
            in_specs=[
                edge,
                pl.BlockSpec((1, size, width), lambda p, _: (p, 0, 0)),
                edge,
                pl.BlockSpec((8, width), lambda p, _: (0, 0)),
            ],
            out_specs=pl.BlockSpec((1, tokens + 2 * EDGE, width), lambda p, _: (p, 0, 0)),
            scratch_shapes=[
                wide,
                tall,
                tall,
                tall,
                tall,
                pltpu.VMEM((2, rows, LANES), jnp.float32),
                pltpu.VMEM((6, tokens, LANES), jnp.float32),
                pltpu.VMEM((tokens, LANES), jnp.float32),
            ],
        ),
        out_shape=jax.ShapeDtypeStruct((count, tokens + 2 * EDGE, width), jnp.bfloat16),
        compiler_params=pltpu.CompilerParams(vmem_limit_bytes=14 << 20),
    )(info, before, body, after, vectors)


def pool_backward_kernel(
    base,
    skipped,
    info_ref,
    before_ref,
    body_ref,
    after_ref,
    grad_before_ref,
    grad_ref,
    grad_after_ref,
    vec_ref,
    *rest,
):
    (
        embed_ref,
        small_ref,
        wide_ref,
        xe_ref,
        xo_ref,
        ce_ref,
        co_ref,
        dh_ref,
        de_ref,
        do_ref,
        logit_ref,
        dots_ref,
        coef_ref,
        pair_ref,
    ) = rest[skipped:]
    piece = pl.program_id(0) + base
    width = body_ref.shape[2]
    tokens = body_ref.shape[1] // 2
    rows = tokens + 2 * EDGE
    chunks = width // LANES
    f32 = jnp.float32
    facts = byte_facts(info_ref[0], info_ref[1 + piece], rows)
    load_bytes(before_ref, body_ref, after_ref, wide_ref)
    clear_edges((xe_ref, xo_ref, ce_ref, co_ref, dh_ref, de_ref, do_ref), rows)
    dh_ref[EDGE : 2 * EDGE] = grad_before_ref[0].astype(f32)
    dh_ref[2 * EDGE : 2 * EDGE + tokens] = grad_ref[0].astype(f32)
    dh_ref[2 * EDGE + tokens : 3 * EDGE + tokens] = grad_after_ref[0].astype(f32)
    logit_ref[...] = jnp.zeros_like(logit_ref)
    dots_ref[...] = jnp.zeros_like(dots_ref)
    main = slice(EDGE, EDGE + rows)

    def first_pass(number, carry):
        lanes = chunk_lanes(number)
        conv_chunk(wide_ref, xe_ref, xo_ref, ce_ref, co_ref, vec_ref, facts, number)
        scorer = vec_ref[KERNEL : KERNEL + 1, lanes]
        logit_ref[0] = logit_ref[0] + ce_ref[main, lanes] * scorer
        logit_ref[1] = logit_ref[1] + co_ref[main, lanes] * scorer
        grad = dh_ref[main, lanes]
        for step in range(3):
            start = EDGE + step - 1
            for parity, ref in ((0, ce_ref), (1, co_ref)):
                k = 2 * step + parity
                dots_ref[k] = dots_ref[k] + grad * ref[start : start + rows, lanes]
        return carry

    lax.fori_loop(0, chunks, first_pass, 0)
    remainder, odd_token = facts[2:]
    even, odd = size_weights(logit_ref, remainder, odd_token)
    six = [0.5 * lane_sum(dots_ref[k]) for k in range(6)]
    grads_even, grads_odd = pooled_scalars(six, remainder, odd_token)

    def logit_grads(weights, grads):
        mean = (weights[0] * grads[0] + weights[1] * grads[1]) + (
            weights[2] * grads[2] + weights[3] * grads[3]
        )
        return [weight * (grad - mean) for weight, grad in zip(weights, grads)]

    spread = spread_scalars(even, odd, remainder, odd_token)
    steer = spread_scalars(
        logit_grads(even, grads_even), logit_grads(odd, grads_odd), remainder, odd_token
    )
    for k in range(6):
        step = k // 2 - 1
        coef_ref[k] = 0.5 * shifted(spread[k], -step)
    coef_ref[6] = steer[2] + shifted(steer[4], -1) + shifted(steer[0], 1)
    coef_ref[7] = steer[3] + shifted(steer[5], -1) + shifted(steer[1], 1)

    def second_pass(number, carry):
        lanes = chunk_lanes(number)
        scorer = vec_ref[KERNEL : KERNEL + 1, lanes]
        grad_b, grad, grad_a = byte_windows(dh_ref, rows, lanes)
        for parity, live, ref in ((0, facts[0], de_ref), (1, facts[1], do_ref)):
            total = (
                coef_ref[parity] * grad_a
                + coef_ref[2 + parity] * grad
                + coef_ref[4 + parity] * grad_b
                + coef_ref[6 + parity] * scorer
            )
            ref[main, lanes] = total * live
        own = slice(2 * EDGE, 2 * EDGE + tokens)
        before = slice(2 * EDGE - 1, 2 * EDGE - 1 + tokens)
        after = slice(2 * EDGE + 1, 2 * EDGE + 1 + tokens)
        taps = [vec_ref[j : j + 1, lanes] for j in range(KERNEL)]
        even_b, even, even_a = [de_ref[part, lanes] for part in (before, own, after)]
        odd_b, odd, odd_a = [do_ref[part, lanes] for part in (before, own, after)]
        inner = slice(EDGE, EDGE + tokens)
        pair_ref[pl.ds(0, tokens, stride=2)] = facts[0][inner] * (
            taps[0] * even_a + taps[1] * odd + taps[2] * even + taps[3] * odd_b + taps[4] * even_b
        )
        pair_ref[pl.ds(1, tokens, stride=2)] = facts[1][inner] * (
            taps[0] * odd_a + taps[1] * even_a + taps[2] * odd + taps[3] * even + taps[4] * odd_b
        )
        embed_ref[0, :, lanes] = pair_ref[...]
        x_even = [xe_ref[part, lanes] for part in (before, own, after)]
        x_odd = [xo_ref[part, lanes] for part in (before, own, after)]
        terms = [
            even * x_even[0] + odd * x_odd[0],
            even * x_odd[0] + odd * x_even[1],
            even * x_even[1] + odd * x_odd[1],
            even * x_odd[1] + odd * x_even[2],
            even * x_even[2] + odd * x_odd[2],
            coef_ref[6, inner] * ce_ref[own, lanes] + coef_ref[7, inner] * co_ref[own, lanes],
        ]
        sums = [jnp.sum(term, axis=0, keepdims=True) for term in terms]
        sums = sums + [jnp.zeros_like(sums[0])] * (8 - len(sums))
        small_ref[0, :, lanes] = jnp.concatenate(sums, axis=0)
        return carry

    lax.fori_loop(0, chunks, second_pass, 0)


def pool_backward(
    info, before, body, after, grad_before, grad, grad_after, vectors, base, stop, earlier
):
    count, size, width = body.shape
    tokens = size // 2
    rows = tokens + 2 * EDGE
    wide = pltpu.VMEM((width // LANES, size + 4 * EDGE, LANES), jnp.float32)
    tall = pltpu.VMEM((rows + 2 * EDGE, width), jnp.float32)
    edge = pl.BlockSpec((1, 2 * EDGE, width), lambda p, _: (p + base, 0, 0))
    grad_edge = pl.BlockSpec((1, EDGE, width), lambda p, _: (p + base, 0, 0))
    return pl.pallas_call(
        functools.partial(pool_backward_kernel, base, len(earlier)),
        name="pool_backward",
        grid_spec=pltpu.PrefetchScalarGridSpec(
            num_scalar_prefetch=1,
            grid=(stop - base,),
            in_specs=[
                edge,
                pl.BlockSpec((1, size, width), lambda p, _: (p + base, 0, 0)),
                edge,
                grad_edge,
                pl.BlockSpec((1, tokens, width), lambda p, _: (p + base, 0, 0)),
                grad_edge,
                pl.BlockSpec((8, width), lambda p, _: (0, 0)),
            ]
            + [pl.BlockSpec(memory_space=pl.ANY)] * len(earlier),
            out_specs=[
                pl.BlockSpec((1, size, width), lambda p, _: (p + base, 0, 0)),
                pl.BlockSpec((1, 8, width), lambda p, _: (p + base, 0, 0)),
            ],
            scratch_shapes=[wide]
            + [tall] * 7
            + [
                pltpu.VMEM((2, rows, LANES), jnp.float32),
                pltpu.VMEM((6, rows, LANES), jnp.float32),
                pltpu.VMEM((8, rows, LANES), jnp.float32),
                pltpu.VMEM((size, LANES), jnp.float32),
            ],
        ),
        out_shape=[
            jax.ShapeDtypeStruct((count, size, width), jnp.float32),
            jax.ShapeDtypeStruct((count, 8, width), jnp.float32),
        ],
        input_output_aliases={8 + i: i for i in range(len(earlier))},
        compiler_params=pltpu.CompilerParams(vmem_limit_bytes=20 << 20),
    )(info, before, body, after, grad_before, grad, grad_after, vectors, *earlier)


def bits_of(axis):
    size = lax.axis_size(axis)
    count = size.bit_length() - 1
    assert 1 << count == size
    return count


def stage_phases():
    dp_bits, seq_bits = (bits_of("dp"), bits_of("seq"))
    along = [("seq", bit) for bit in reversed(range(seq_bits))]
    low_half = [("dp", bit) for bit in range(1, 1 + (dp_bits - 1) // 2)]
    high_half = [("dp", bit) for bit in range(1 + (dp_bits - 1) // 2, dp_bits)]
    ends = ([along[:1], along[1:]], [[("dp", 0)]])
    return (ends[0] + [high_half, low_half] + ends[1], ends[0] + [low_half, high_half] + ends[1])


def place_of(axis, bit):
    dp_bits, seq_bits = (bits_of("dp"), bits_of("seq"))
    return dp_bits - 1 - bit if axis == "dp" else dp_bits + seq_bits - 1 - bit


def swap_bit(x, axis, bit):
    size = lax.axis_size(axis)
    return lax.ppermute(x, axis, [(i, i ^ (1 << bit)) for i in range(size)])


def own_bit(axis, bit):
    return (lax.axis_index(axis) >> bit) & 1


def in_order(x):
    return with_layout_constraint(x, Layout(major_to_minor=tuple(range(x.ndim))))


class Chain:
    def __init__(self):
        self.noted = None

    def after(self, *values):
        if self.noted is not None:
            values = lax.optimization_barrier(values + (self.noted,))[:-1]
        return values if len(values) > 1 else values[0]

    def note(self, value):
        self.noted = value
        return value


class Gathering:
    def __init__(self, chain, block, phases, held=()):
        self.chain, self.whole, self.held = (chain, block, list(held))
        self.phases = [list(phase) for phase in phases]
        self.start()

    def start(self):
        if self.phases:
            self.arrived = swap_bit(self.whole, *self.phases[0][0])

    def finish(self):
        for axis, bit in self.phases.pop(0):
            if self.arrived is None:
                self.arrived = swap_bit(self.whole, axis, bit)
            place = place_of(axis, bit)
            dim = sum(other < place for other in self.held)
            arrived, whole = self.chain.after(self.arrived, self.whole)
            upper = own_bit(axis, bit) == 1
            self.whole = self.chain.note(
                in_order(
                    jnp.stack(
                        [jnp.where(upper, arrived, whole), jnp.where(upper, whole, arrived)],
                        axis=dim,
                    )
                )
            )
            self.held.append(place)
            self.arrived = None
        self.start()
        return self.whole


    def last(self):
        assert len(self.phases) == 1
        return self.whole, self.arrived


class Reduction:
    def __init__(self, chain, staying, arriving, rows, phases):
        self.chain = chain
        phases = phases[::-1]
        assert phases[0] == [("dp", 0)]
        self.steps = [step for phase in phases[1:] for step in phase[::-1]]
        self.counts = [len(phase) for phase in phases]
        self.held = list(range(1 + len(self.steps)))
        self.held.remove(place_of("dp", 0))
        shape = staying.shape[:1] + (2,) * len(self.steps) + (rows, staying.shape[-1])
        self.staying = staying.reshape(shape)
        self.arriving = arriving.reshape(shape)

    def halves(self, x):
        axis, bit = self.steps[0]
        dim = 1 + self.held.index(place_of(axis, bit))
        own = own_bit(axis, bit)
        return [
            lax.dynamic_index_in_dim(x, which, dim, keepdims=False) for which in (1 - own, own)
        ]

    def finish(self):
        f32 = jnp.float32
        for _ in range(self.counts.pop(0)):
            arrived, staying = self.chain.after(self.arriving, self.staying)
            if not self.steps:
                self.chain.note(arrived)
                return staying.astype(f32) + arrived.astype(f32)
            parts = zip(self.halves(staying), self.halves(arrived))
            leaving, staying = [
                (x.astype(f32) + y.astype(f32)).astype(jnp.bfloat16) for x, y in parts
            ]
            self.chain.note(leaving)
            self.staying = staying
            axis, bit = self.steps.pop(0)
            self.held.remove(place_of(axis, bit))
            self.arriving = swap_bit(leaving, axis, bit)


def group_masks(group):
    axis = group[0][0]
    size = lax.axis_size(axis)
    masks = [0]
    for _, bit in group:
        masks = masks + [mask | 1 << bit for mask in masks]
    return [(axis, [(i, i ^ mask) for i in range(size)]) for mask in masks[1:]]


def exchange(x, group):
    return [x] + [lax.ppermute(x, axis, pairs) for axis, pairs in group_masks(group)]


def tree_sum(values):
    while len(values) > 1:
        values = [a + b for a, b in zip(values[::2], values[1::2])]
    return values[0]


def exchange_groups():
    groups = [[("dp", 0)]]
    for axis, first in (("dp", 1), ("seq", 0)):
        left = [(axis, bit) for bit in range(first, bits_of(axis))]
        groups += [left[i : i + 2] for i in range(0, len(left), 2)]
    return groups


def fold_rows(x, rows):
    width, third, side = (x.shape[1], rows // 3, x.shape[1] // 3)
    rest = x[2 * rows :]
    corner = jnp.concatenate([rest[:third, 2 * side :], rest[third:, 2 * side :]], axis=1)
    tail = jnp.concatenate([rest[:, : 2 * side], corner], axis=0)
    return jnp.concatenate([x[:rows], x[rows : 2 * rows], tail], axis=1)


def unfold_rows(x, width):
    rows, third, side = (x.shape[0], x.shape[0] // 3, width // 3)
    tail = x[:, 2 * width :]
    corner = tail[2 * third :]
    right = jnp.concatenate([corner[:, :side], corner[:, side:]], axis=0)
    rest = jnp.concatenate([tail[: 2 * third], right], axis=1)
    return jnp.concatenate([x[:, :width], x[:, width : 2 * width], rest], axis=0)


def each_block(fold, x, size, *rest):
    parts = [fold(x[i : i + size], *rest) for i in range(0, x.shape[0], size)]
    return parts[0] if len(parts) == 1 else jnp.concatenate(parts, axis=0)


def pack_kernel(*refs):
    *square, gate_ref, up_ref, down_ref, square_ref, wide_ref = refs
    rows, ff = gate_ref.shape
    place = 0
    for ref in square:
        width = ref.shape[1]
        square_ref[:, place : place + width] = ref[...]
        place += width
    half = ff // 2
    down = down_ref[...]
    if down.shape[0] != rows:
        down = fold_rows(down.astype(jnp.float32), rows).astype(jnp.bfloat16)
    wide_ref[:, :ff] = gate_ref[...]
    wide_ref[:, ff : ff + half] = down[:, :half]
    wide_ref[:, ff + half : 2 * ff + half] = up_ref[...]
    wide_ref[:, 2 * ff + half :] = down[:, half:]


def pack_weights(w_query, w_key, w_value, w_out, w_gate, w_up, w_down):
    rows = w_query.shape[0]
    parts = (w_query, w_key, w_value, w_out, w_gate, w_up, w_down)
    widths = (4 * w_query.shape[1], 3 * w_gate.shape[1])
    return pl.pallas_call(
        pack_kernel,
        name="pack_weights",
        out_shape=[jax.ShapeDtypeStruct((rows, width), w_query.dtype) for width in widths],
    )(*parts)


def to_chips(pieces):
    count = pieces.shape[0]
    dp_size, seq_size = (lax.axis_size("dp"), lax.axis_size("seq"))
    seq_index = lax.axis_index("seq")
    arrived = []
    for phase in range(count):
        pairs = chip_pairs(dp_size, seq_size, count, phase)
        leaving = lax.dynamic_index_in_dim(pieces, (seq_index + phase) % count, 0, keepdims=False)
        arrived.append(lax.ppermute(leaving, ("dp", "seq"), pairs))
    return arrived


def in_token_order(arrived):
    count = len(arrived)
    number = lax.axis_index("seq") % count
    stacked = jnp.stack(arrived)
    return jnp.stack(
        [
            lax.dynamic_index_in_dim(stacked, (number - r) % count, 0, keepdims=False)
            for r in range(count)
        ]
    )


def from_chips(tokens, count):
    dp_size, seq_size = (lax.axis_size("dp"), lax.axis_size("seq"))
    number = lax.axis_index("seq") % count
    split = tokens.reshape((count, tokens.shape[0] // count) + tokens.shape[1:])
    arrived = []
    for phase in range(count):
        pairs = [(j, i) for i, j in chip_pairs(dp_size, seq_size, count, phase)]
        leaving = lax.dynamic_index_in_dim(split, (number - phase) % count, 0, keepdims=False)
        arrived.append(lax.ppermute(leaving, ("dp", "seq"), pairs))
    return arrived


def in_piece_order(arrived):
    count = len(arrived)
    seq_index = lax.axis_index("seq")
    stacked = jnp.stack(arrived)
    return jnp.stack(
        [
            lax.dynamic_index_in_dim(stacked, (j - seq_index) % count, 0, keepdims=False)
            for j in range(count)
        ]
    )


def chip_pairs(dp_size, seq_size, count, phase):
    pairs = []
    for dp in range(dp_size):
        for seq in range(seq_size):
            core_to = seq // count
            seq_to = dp % 2 * count + (seq + phase) % count
            pairs.append((dp * seq_size + seq, (dp // 2 * 2 + core_to) * seq_size + seq_to))
    return pairs


TILE = 128
AUG = 16


def mm(a, b):
    return jnp.dot(a, b, preferred_element_type=jnp.float32)


def mm_nt(a, b):
    return lax.dot_general(a, b, (((1,), (1,)), ((), ())), preferred_element_type=jnp.float32)


def mm_tn(a, b):
    return lax.dot_general(a, b, (((0,), (0,)), ((), ())), preferred_element_type=jnp.float32)


def one_head(pair_rows, a):
    zeros = jnp.zeros((HEAD, pair_rows.shape[1]), pair_rows.dtype)
    half = pair_rows[a * HEAD : (a + 1) * HEAD]
    return jnp.concatenate([half, zeros] if a == 0 else [zeros, half], axis=0)


def near_rows(first_tile, i, d):
    return pl.ds(pl.multiple_of((first_tile + (i + d)) * TILE, TILE), TILE)


def split_rows(base, row):
    low, f32 = (jnp.bfloat16, jnp.float32)
    top = row.astype(low).astype(f32)
    middle = (row - top).astype(low).astype(f32)
    bottom = row - top - middle
    line = lax.broadcasted_iota(jnp.int32, base.shape, 0)
    return jnp.where(
        line == 9, -top, jnp.where(line == 10, -middle, jnp.where(line == 11, -bottom, base))
    ).astype(low)


def attn_forward_kernel(
    first_ref, q_ref, k_ref, ka_ref, v_ref, far_ref, bias_ref, out_ref, lse_ref, s_ref
):
    keys = k_ref.shape[0]
    tokens = q_ref.shape[1]
    lhs = jnp.concatenate([k_ref[...], ka_ref[...]], axis=1)
    pad = jnp.zeros((TILE - AUG, tokens), jnp.bfloat16)
    first = first_ref[0]
    for a in range(2):
        rhs = jnp.concatenate([one_head(q_ref[...], a), far_ref[a], pad], axis=0)
        s_ref[TILE : TILE + keys] = mm(lhs, rhs)
        for i in range(tokens // TILE):
            for d in range(3):
                rows = near_rows(first, i, d)
                lanes = slice(i * TILE, (i + 1) * TILE)
                s_ref[rows, lanes] = s_ref[rows, lanes] + bias_ref[a, d]
        s = s_ref[TILE : TILE + keys]
        row_max = jnp.max(s, axis=0, keepdims=True)
        probs = jnp.exp(s - row_max).astype(jnp.bfloat16)
        v_rows = jnp.concatenate(
            [v_ref[a * HEAD : (a + 1) * HEAD], jnp.ones((AUG, keys), jnp.bfloat16)], axis=0
        )
        both = mm(v_rows, probs)
        total = both[HEAD : HEAD + 1]
        out_ref[a * HEAD : (a + 1) * HEAD] = (both[:HEAD] / total).astype(jnp.bfloat16)
        lse_ref[0, a : a + 1] = row_max + jnp.log(total)


def attn_forward(first, q_t, keys, key_aug, v_t, far, bias):
    width, tokens = q_t.shape
    key_count = keys.shape[0]
    pairs = width // TILE
    return pl.pallas_call(
        attn_forward_kernel,
        name="attn_forward",
        grid_spec=pltpu.PrefetchScalarGridSpec(
            num_scalar_prefetch=1,
            grid=(pairs,),
            in_specs=[
                pl.BlockSpec((TILE, tokens), lambda h, _: (h, 0)),
                pl.BlockSpec((key_count, TILE), lambda h, _: (0, h)),
                pl.BlockSpec((key_count, TILE), lambda h, _: (0, 0)),
                pl.BlockSpec((TILE, key_count), lambda h, _: (h, 0)),
                pl.BlockSpec((2, AUG, tokens), lambda h, _: (h, 0, 0)),
                pl.BlockSpec((2, 3, TILE, TILE), lambda h, _: (h, 0, 0, 0)),
            ],
            out_specs=[
                pl.BlockSpec((TILE, tokens), lambda h, _: (h, 0)),
                pl.BlockSpec((1, 2, tokens), lambda h, _: (h, 0, 0)),
            ],
            scratch_shapes=[pltpu.VMEM((key_count + 2 * TILE, tokens), jnp.float32)],
        ),
        out_shape=[
            jax.ShapeDtypeStruct((width, tokens), jnp.bfloat16),
            jax.ShapeDtypeStruct((pairs, 2, tokens), jnp.float32),
        ],
        compiler_params=pltpu.CompilerParams(vmem_limit_bytes=14 << 20),
    )(first, q_t, keys, key_aug, v_t, far, bias)


def attn_backward_kernel(
    first_ref,
    q_ref,
    do_ref,
    out_ref,
    lse_ref,
    k_ref,
    v_ref,
    kt_ref,
    ka_ref,
    block_ref,
    far_ref,
    bias_ref,
    wq_ref,
    wk_ref,
    wv_ref,
    dq_ref,
    dk_ref,
    dv_ref,
    near_ref,
    sums_ref,
    leave_ref,
    stay_ref,
    s_ref,
    ds_ref,
    p_ref,
    dq_all_ref,
    dk_all_ref,
    dv_all_ref,
):
    keys = k_ref.shape[0]
    tokens = q_ref.shape[1]
    f32, low = (jnp.float32, jnp.bfloat16)
    first = first_ref[0]
    main = slice(TILE, TILE + keys)
    k_lhs = jnp.concatenate([k_ref[...], ka_ref[...]], axis=1)
    v_lhs = jnp.concatenate([v_ref[...], ka_ref[...]], axis=1)
    pad = jnp.zeros((TILE - AUG, tokens), low)
    edge = jnp.zeros((TILE, tokens), low)
    q_heads = [one_head(q_ref[...], a) for a in range(2)]
    do_heads = [one_head(do_ref[...], a) for a in range(2)]
    for a in range(2):
        head = slice(a * HEAD, (a + 1) * HEAD)
        aug = split_rows(far_ref[a].astype(f32), lse_ref[0, a : a + 1])
        s_ref[main] = mm(k_lhs, jnp.concatenate([q_heads[a], aug, pad], axis=0))
        for i in range(tokens // TILE):
            for d in range(3):
                rows = near_rows(first, i, d)
                lanes = slice(i * TILE, (i + 1) * TILE)
                s_ref[rows, lanes] = s_ref[rows, lanes] + bias_ref[a, d]
        probs = jnp.exp(s_ref[main])
        p_ref[a] = probs.astype(low)
        row_dot = jnp.sum(
            do_ref[head].astype(f32) * out_ref[head].astype(f32), axis=0, keepdims=True
        )
        aug = split_rows(jnp.zeros((AUG, tokens), f32), row_dot)
        grad_probs = mm(v_lhs, jnp.concatenate([do_heads[a], aug, pad], axis=0))
        ds_ref[a, main] = (probs * grad_probs).astype(low)
        ds_ref[a, :TILE] = edge
        ds_ref[a, TILE + keys :] = edge
        left = jnp.concatenate([kt_ref[head], block_ref[...]], axis=0)
        both = mm(left, ds_ref[a, main])
        dq_ref[head] = both[:HEAD].astype(low)
        sums_ref[0, a] = both[HEAD:]
        for d in range(3):
            total = None
            for i in range(tokens // TILE):
                rows = near_rows(first, i, d)
                term = ds_ref[a, rows, i * TILE : (i + 1) * TILE].astype(f32)
                total = term if total is None else total + term
            near_ref[a, d] = total
    dk_ref[...] = mm_nt(
        jnp.concatenate([ds_ref[0, main], ds_ref[1, main]], axis=1),
        jnp.concatenate(q_heads, axis=1),
    ).astype(low)
    dv_ref[...] = mm_nt(
        jnp.concatenate([p_ref[0], p_ref[1]], axis=1), jnp.concatenate(do_heads, axis=1)
    ).astype(low)
    pair = pl.program_id(0)
    place = pl.ds(pl.multiple_of(pair * TILE, TILE), TILE)
    dq_all_ref[place] = dq_ref[...]
    dk_all_ref[:, place] = dk_ref[...]
    dv_all_ref[:, place] = dv_ref[...]

    @pl.when(pair == pl.num_programs(0) - 1)
    def _():
        core = jnp.where(first == 0, 0, 1)

        def shared(number):
            rows = pl.ds(pl.multiple_of(number * tokens, tokens), tokens)
            return mm_nt(dk_all_ref[rows], wk_ref[...]) + mm_nt(dv_all_ref[rows], wv_ref[...])

        leave_ref[...] = shared(1 - core).astype(low)
        stay_ref[...] = shared(core) + lax.dot_general(
            dq_all_ref[...], wq_ref[...], (((0,), (1,)), ((), ())), preferred_element_type=f32
        )


def attn_backward(
    first,
    q_t,
    do_t,
    out_t,
    lse,
    keys,
    values,
    k_t,
    key_aug,
    block_rows,
    far,
    bias,
    w_query,
    w_key,
    w_value,
):
    width, tokens = q_t.shape
    key_count = keys.shape[0]
    pairs = width // TILE
    weight = pl.BlockSpec((width, width), lambda h, _: (0, 0), pipeline_mode=pl.Buffered(1))
    whole = pl.BlockSpec((tokens, width), lambda h, _: (0, 0))
    across = pl.BlockSpec((TILE, tokens), lambda h, _: (h, 0))
    along = pl.BlockSpec((key_count, TILE), lambda h, _: (0, h))
    return pl.pallas_call(
        attn_backward_kernel,
        name="attn_backward",
        grid_spec=pltpu.PrefetchScalarGridSpec(
            num_scalar_prefetch=1,
            grid=(pairs,),
            in_specs=[
                across,
                across,
                across,
                pl.BlockSpec((1, 2, tokens), lambda h, _: (h, 0, 0)),
                along,
                along,
                pl.BlockSpec((TILE, key_count), lambda h, _: (h, 0)),
                pl.BlockSpec((key_count, TILE), lambda h, _: (0, 0)),
                pl.BlockSpec((AUG, key_count), lambda h, _: (0, 0)),
                pl.BlockSpec((2, AUG, tokens), lambda h, _: (h, 0, 0)),
                pl.BlockSpec((2, 3, TILE, TILE), lambda h, _: (h, 0, 0, 0)),
                weight,
                weight,
                weight,
            ],
            out_specs=[
                across,
                along,
                along,
                pl.BlockSpec((2, 3, TILE, TILE), lambda h, _: (h, 0, 0, 0)),
                pl.BlockSpec((1, 2, AUG, tokens), lambda h, _: (h, 0, 0, 0)),
                whole,
                whole,
            ],
            scratch_shapes=[
                pltpu.VMEM((key_count + 2 * TILE, tokens), jnp.float32),
                pltpu.VMEM((2, key_count + 2 * TILE, tokens), jnp.bfloat16),
                pltpu.VMEM((2, key_count, tokens), jnp.bfloat16),
                pltpu.VMEM((width, tokens), jnp.bfloat16),
                pltpu.VMEM((key_count, width), jnp.bfloat16),
                pltpu.VMEM((key_count, width), jnp.bfloat16),
            ],
        ),
        out_shape=[
            jax.ShapeDtypeStruct((width, tokens), jnp.bfloat16),
            jax.ShapeDtypeStruct((key_count, width), jnp.bfloat16),
            jax.ShapeDtypeStruct((key_count, width), jnp.bfloat16),
            jax.ShapeDtypeStruct((2 * pairs, 3, TILE, TILE), jnp.float32),
            jax.ShapeDtypeStruct((pairs, 2, AUG, tokens), jnp.float32),
            jax.ShapeDtypeStruct((tokens, width), jnp.bfloat16),
            jax.ShapeDtypeStruct((tokens, width), jnp.float32),
        ],
        compiler_params=pltpu.CompilerParams(vmem_limit_bytes=26 << 20),
    )(
        first,
        q_t,
        do_t,
        out_t,
        lse,
        keys,
        values,
        k_t,
        key_aug,
        block_rows,
        far,
        bias,
        w_query,
        w_key,
        w_value,
    )


def attn_tables(first, tokens, key_count, length, rel_bias):
    low, f32 = (jnp.bfloat16, jnp.float32)
    blocks = key_count // TILE
    assert blocks <= 8
    key_pos = jnp.arange(key_count, dtype=jnp.int32)
    column = jnp.arange(TILE, dtype=jnp.int32)[None, :]
    key_aug = jnp.where(column == (key_pos // TILE)[:, None], 1.0, 0.0)
    dead = jnp.where(2 * key_pos < length, 0.0, -1000000000.0)[:, None]
    key_aug = jnp.where(column == 8, dead, key_aug)
    key_aug = jnp.where((column >= 9) & (column < 12), 1.0, key_aug).astype(low)
    line = jnp.arange(AUG, dtype=jnp.int32)
    block_rows = jnp.where(line[:, None] == (key_pos // TILE)[None, :], 1.0, 0.0).astype(low)
    tile = first + jnp.arange(tokens, dtype=jnp.int32) // TILE
    apart = (line[:, None] - tile[None, :])[None]
    rel_t = rel_bias.astype(f32).T
    before = rel_t[:, BUCKETS // 2 - 1][:, None, None]
    after = rel_t[:, BUCKETS - 1][:, None, None]
    far = jnp.where(apart <= -2, before, jnp.where(apart >= 2, after, 0.0))
    in_use = (line < blocks)[None, :, None]
    far = jnp.where(in_use, far, jnp.where((line == 8)[None, :, None], 1.0, 0.0)).astype(low)
    return key_aug, block_rows, far


def near_bias_kernel(rel_ref, out_ref):
    width = 4 * TILE
    heads = rel_ref.shape[0]
    lane = lax.broadcasted_iota(jnp.int32, (BUCKETS, width), 1)
    bucket = bucket_of(2 * TILE - 1 - lane)
    line = lax.broadcasted_iota(jnp.int32, (BUCKETS, width), 0)
    table = mm(rel_ref[...], jnp.where(bucket == line, 1.0, 0.0).astype(jnp.bfloat16))
    for h in range(heads):
        rows = jnp.broadcast_to(table[h : h + 1], (TILE, width))
        rows = pltpu.roll(rows, 3 * TILE + 1, 1, stride=1, stride_axis=0)
        for d in range(3):
            out_ref[h, d] = rows[:, (2 - d) * TILE : (3 - d) * TILE]


def near_bias(rel_t):
    return pl.pallas_call(
        near_bias_kernel,
        name="near_bias",
        out_shape=jax.ShapeDtypeStruct((rel_t.shape[0], 3, TILE, TILE), jnp.float32),
    )(rel_t)


def bias_gradient_kernel(first_ref, near_ref, sums_ref, out_ref, line_ref):
    width = 4 * TILE
    heads = near_ref.shape[0]
    tokens = sums_ref.shape[3]
    f32 = jnp.float32
    line = lax.broadcasted_iota(jnp.int32, (AUG, tokens), 0)
    tile = first_ref[0] + lax.broadcasted_iota(jnp.int32, (AUG, tokens), 1) // TILE
    apart = line - tile
    column = lax.broadcasted_iota(jnp.int32, (1, BUCKETS), 1)
    far_rows = []
    for h in range(heads):
        tiles = [near_ref[h, 2 - k] for k in range(3)]
        rows = jnp.concatenate(tiles + [jnp.zeros((TILE, TILE), f32)], axis=1)
        eight = rows[:8]
        for start in range(8, TILE, 8):
            eight = eight + pltpu.roll(rows[start : start + 8], width - start, 1)
        total = eight[:1]
        for step in range(1, 8):
            total = total + pltpu.roll(eight[step : step + 1], width - step, 1)
        line_ref[h : h + 1] = total
        sums = sums_ref[h // 2, h % 2]
        before = jnp.sum(jnp.where(apart <= -2, sums, 0.0), axis=1, keepdims=True)
        after = jnp.sum(jnp.where(apart >= 2, sums, 0.0), axis=1, keepdims=True)
        before = jnp.sum(before, axis=0, keepdims=True)
        after = jnp.sum(after, axis=0, keepdims=True)
        far_rows.append(
            jnp.where(column == BUCKETS // 2 - 1, before, 0.0)
            + jnp.where(column == BUCKETS - 1, after, 0.0)
        )
    lane = lax.broadcasted_iota(jnp.int32, (BUCKETS, width), 1)
    offset = jnp.where(lane < 3 * TILE, TILE - lane, 5 * TILE - lane)
    bucket = bucket_of(offset)
    pick = jnp.where(bucket == lax.broadcasted_iota(jnp.int32, (BUCKETS, width), 0), 1.0, 0.0)
    close = lax.dot_general(
        line_ref[...], pick, (((1,), (1,)), ((), ())), precision=highest, preferred_element_type=f32
    )
    out_ref[...] = close + jnp.concatenate(far_rows, axis=0)


def bias_gradient(first_ref, near, sums):
    heads = near.shape[0]
    return pl.pallas_call(
        bias_gradient_kernel,
        name="bias_gradient",
        in_specs=[
            pl.BlockSpec(memory_space=pltpu.SMEM),
            pl.BlockSpec(memory_space=pltpu.VMEM),
            pl.BlockSpec(memory_space=pltpu.VMEM),
        ],
        out_shape=jax.ShapeDtypeStruct((heads, BUCKETS), jnp.float32),
        scratch_shapes=[pltpu.VMEM((heads, 4 * TILE), jnp.float32)],
    )(first_ref, near, sums)


def part_rows(blocks, mine, size):
    width = blocks.shape[-1]
    split = blocks.reshape(blocks.shape[0] // (2 * size), 2, size, width)
    other, own = (split[:, 0], split[:, 1])
    first = mine == 1
    return jnp.where(first, other, own), jnp.where(first, own, other)


def join_rows(own, other, core):
    kind = own.dtype
    chips, size, width = own.shape
    if size % 16:
        own, other = (own.astype(jnp.float32), other.astype(jnp.float32))
    first = core == 0
    blocks = jnp.stack([jnp.where(first, own, other), jnp.where(first, other, own)], axis=1)
    return blocks.reshape(2 * chips * size, width).astype(kind)


def ffn_kernel(
    rows,
    sub,
    folded,
    core_ref,
    hidden_ref,
    att_ref,
    w_out_ref,
    gain_ref,
    seed_ref,
    gate_own_ref,
    gate_other_ref,
    up_own_ref,
    up_other_ref,
    *rest,
):
    f32, low = (jnp.float32, jnp.bfloat16)
    count = 4 if folded else 2
    down_refs, rest = (rest[:count], rest[count:])
    block_ref, grad_ref, grad_low_ref, grad_att_ref, gain_grad_ref = rest[:5]
    out_refs = rest[5:9]
    rest = rest[9:]
    if not folded:
        down_leave_ref, down_stay_ref = rest[:2]
        rest = rest[2:]
    after_ref, unit_ref, normed_ref, normed_t_ref, out_ref, back_ref, *held_refs, sems = rest
    leave_refs, stay_refs = (held_refs[:2], held_refs[2:])
    number = pl.program_id(0)
    core = core_ref[0]
    step = gate_own_ref.shape[2]
    chips, size, packed = held_refs[0].shape
    half_ff = packed // 3
    ff = 2 * half_ff
    width = hidden_ref.shape[1]

    @pl.when(number == 0)
    def _():
        after = hidden_ref[...] + mm_tn(att_ref[...], w_out_ref[...])
        scale = lax.rsqrt(jnp.mean(after * after, axis=1, keepdims=True) + norm_eps)
        normed = (after * scale * gain_ref[...]).astype(low)
        after_ref[...] = after
        unit_ref[...] = jnp.broadcast_to(scale, unit_ref.shape)
        normed_ref[...] = normed
        normed_t_ref[...] = jnp.transpose(normed)
        out_ref[...] = after
        back_ref[...] = jnp.zeros_like(back_ref)

    normed = normed_ref[...]
    seed = seed_ref[...]
    w_gate = join_rows(gate_own_ref[...], gate_other_ref[...], core)
    w_up = join_rows(up_own_ref[...], up_other_ref[...], core)
    if folded:
        own, other = [
            jnp.concatenate([down_refs[i][0], down_refs[i + 2][0]], axis=1).astype(f32)
            for i in range(2)
        ]
        own, other = [
            each_block(unfold_rows, x, rows, width).astype(low)[None] for x in (own, other)
        ]
        w_down = join_rows(own, other, core)
    else:
        w_down = join_rows(down_refs[0][...], down_refs[1][...], core)
    gate = mm(normed, w_gate)
    up = mm(normed, w_up)
    cube = 0.044715 * gate * gate
    bend = jnp.tanh(0.7978845608028654 * (gate + cube * gate))
    half = 0.5 * (1.0 + bend)
    act = gate * half
    slope = half + (0.5 * 0.7978845608028654) * gate * (1.0 - bend * bend) * (1.0 + 3.0 * cube)
    inner = (act * up).astype(low)
    out_ref[...] += mm(inner, w_down)
    grad_inner = mm_nt(seed, w_down)
    grad_gate = (grad_inner * up * slope).astype(low)
    grad_up = (grad_inner * act).astype(low)
    back_ref[...] += mm_nt(grad_gate, w_gate) + mm_nt(grad_up, w_up)
    lanes = pl.ds(pl.multiple_of(number * step, step), step)
    for side, grad in enumerate((grad_gate, grad_up)):
        leave, stay = part_rows(mm(normed_t_ref[...], grad), core, size)
        leave_refs[side][:, :, lanes] = leave.astype(low)
        stay_refs[side][:, :, lanes] = stay.astype(low)
    leave, stay = part_rows(mm_tn(inner, seed), core, sub)
    if folded:
        for refs, part in ((leave_refs, leave), (stay_refs, stay)):
            part = each_block(fold_rows, part[0], 8 * rows // 3, rows).astype(low)
            refs[0][number, :, ff:] = part[:, :half_ff]
            refs[1][number, :, ff:] = part[:, half_ff:]
    else:
        down_leave_ref[...] = leave.astype(low)
        down_stay_ref[...] = stay.astype(low)

    def copies(at):
        lanes = pl.ds(pl.multiple_of(at * step, step), step)
        moves = []
        for i, (held_ref, moved_ref) in enumerate(zip(held_refs, out_refs)):
            moves.append(
                pltpu.make_async_copy(
                    held_ref.at[:, :, lanes], moved_ref.at[:, :, lanes], sems.at[at, i, 0]
                )
            )
            if folded:
                moves.append(
                    pltpu.make_async_copy(
                        held_ref.at[at, :, pl.ds(ff, half_ff)],
                        moved_ref.at[at, :, pl.ds(ff, half_ff)],
                        sems.at[at, i, 1],
                    )
                )
        return moves

    for move in copies(number):
        move.start()

    @pl.when(number == pl.num_programs(0) - 1)
    def _():
        block_ref[...] = out_ref[...].astype(low)
        back = back_ref[...]
        scale = unit_ref[:, :1]
        unit = after_ref[...] * scale
        gained = back * gain_ref[...]
        mean = jnp.mean(gained * unit, axis=1, keepdims=True)
        grad = seed_ref[...].astype(f32) + scale * (gained - unit * mean)
        grad_ref[...] = grad
        grad_low_ref[...] = grad.astype(low)
        grad_att_ref[...] = mm_nt(w_out_ref[...], grad.astype(low)).astype(low)
        gain_grad_ref[...] = jnp.sum(back * unit, axis=0, keepdims=True)
        for at in range(ff // step):
            for move in copies(at):
                move.wait()


def feed_forward(core, hidden, attended_t, w_out, gain, seed, first, second, rows, down_rows):
    tokens, width = hidden.shape
    step = 512
    f32, low = (jnp.float32, jnp.bfloat16)
    ff = 2 * first[0].shape[-1] // 3
    half_ff = ff // 2
    size = rows * lax.axis_size("seq")
    sub = down_rows * lax.axis_size("seq")
    chips = width // (2 * size)
    folded = down_rows != rows and 2 * sub == step
    first, second = [[x.reshape(chips, size, ff + half_ff) for x in pair] for pair in (first, second)]
    once = dict(pipeline_mode=pl.Buffered(1))
    full = pl.BlockSpec((tokens, width), lambda i, _: (0, 0))
    full_once = pl.BlockSpec((tokens, width), lambda i, _: (0, 0), **once)
    line = pl.BlockSpec((1, width), lambda i, _: (0, 0))
    across = pl.BlockSpec((width, tokens), lambda i, _: (0, 0))
    across_once = pl.BlockSpec((width, tokens), lambda i, _: (0, 0), **once)
    columns = pl.BlockSpec((chips, size, step), lambda i, _: (0, 0, i))
    tall = pl.BlockSpec((step // (2 * sub), sub, width), lambda i, _: (i, 0, 0))
    packed = pl.BlockSpec(memory_space=pl.ANY)
    if folded:
        down = [first[0], first[1], second[0], second[1]]
        down_specs = [pl.BlockSpec((1, size, half_ff), lambda i, _: (i, 0, 2))] * 4
    else:
        down = [
            jnp.concatenate([x[..., ff:], y[..., ff:]], axis=-1).reshape(-1, sub, width)
            for x, y in zip(first, second)
        ]
        down_specs = [tall, tall]
    packed_shape = jax.ShapeDtypeStruct((chips, size, ff + half_ff), low)
    tall_shape = jax.ShapeDtypeStruct((ff // (2 * sub), sub, width), low)
    extra = 0 if folded else 2
    out = pl.pallas_call(
        functools.partial(ffn_kernel, rows, sub, folded),
        name="feed_forward",
        grid_spec=pltpu.PrefetchScalarGridSpec(
            num_scalar_prefetch=1,
            grid=(ff // step,),
            in_specs=[
                full_once,
                across_once,
                pl.BlockSpec((width, width), lambda i, _: (0, 0), **once),
                line,
                full_once,
                columns,
                columns,
                columns,
                columns,
            ]
            + down_specs,
            out_specs=[full, full, full, across, line] + [packed] * 4 + [tall] * extra,
            scratch_shapes=[
                pltpu.VMEM((tokens, width), f32),
                pltpu.VMEM((tokens, LANES), f32),
                pltpu.VMEM((tokens, width), low),
                pltpu.VMEM((width, tokens), low),
                pltpu.VMEM((tokens, width), f32),
                pltpu.VMEM((tokens, width), f32),
            ]
            + [pltpu.VMEM((chips, size, ff + half_ff), low)] * 4
            + [pltpu.SemaphoreType.DMA((ff // step, 4, 2 if folded else 1))],
        ),
        out_shape=[
            jax.ShapeDtypeStruct((tokens, width), low),
            jax.ShapeDtypeStruct((tokens, width), f32),
            jax.ShapeDtypeStruct((tokens, width), low),
            jax.ShapeDtypeStruct((width, tokens), low),
            jax.ShapeDtypeStruct((1, width), f32),
        ]
        + [packed_shape] * 4
        + [tall_shape] * extra,
        compiler_params=pltpu.CompilerParams(vmem_limit_bytes=60 << 20),
    )(core, hidden, attended_t, w_out, gain, seed, *first, *second, *down)
    if folded:
        return out
    out = list(out)
    for part in range(2):
        rest = out[9 + part].reshape(chips, size, ff)
        for side in range(2):
            number = 5 + 2 * part + side
            half = rest[..., side * half_ff : (side + 1) * half_ff]
            out[number] = out[number].at[:, :, ff:].set(half)
    return out[:9]


def square_gradient_kernel(
    core_ref,
    normed_ref,
    att_ref,
    dq_ref,
    dk_ref,
    dv_ref,
    do_ref,
    qk_leave_ref,
    vo_leave_ref,
    qk_stay_ref,
    vo_stay_ref,
    normed_t_ref,
):
    core = core_ref[0]
    tokens = att_ref.shape[1]

    @pl.when(pl.program_id(0) == 0)
    def _():
        normed_t_ref[...] = jnp.transpose(normed_ref[...])

    normed_t = normed_t_ref[...]
    own = normed_t_ref[:, pl.ds(pl.multiple_of(core * tokens, tokens), tokens)]
    grads = (
        mm_nt(own, dq_ref[...]),
        mm(normed_t, dk_ref[...]),
        mm(normed_t, dv_ref[...]),
        mm(att_ref[...], do_ref[...]),
    )
    for number, grad in enumerate(grads):
        leave_ref, stay_ref = (
            (qk_leave_ref, qk_stay_ref) if number < 2 else (vo_leave_ref, vo_stay_ref)
        )
        leave, stay = part_rows(grad, core, leave_ref.shape[2])
        leave_ref[number % 2] = leave.astype(jnp.bfloat16)
        stay_ref[number % 2] = stay.astype(jnp.bfloat16)


def square_gradients(core, normed_all, attended_t, grad_q_t, grad_k, grad_v, grad_out, rows):
    keys, width = normed_all.shape
    tokens = attended_t.shape[1]
    step = 256
    chips = width // (2 * rows)
    low = jnp.bfloat16
    block = pl.BlockSpec((2, chips, rows, step), lambda i, _: (0, 0, 0, i))
    shape = jax.ShapeDtypeStruct((2, chips, rows, width), low)
    return pl.pallas_call(
        square_gradient_kernel,
        name="square_gradients",
        grid_spec=pltpu.PrefetchScalarGridSpec(
            num_scalar_prefetch=1,
            grid=(width // step,),
            in_specs=[
                pl.BlockSpec((keys, width), lambda i, _: (0, 0)),
                pl.BlockSpec((width, tokens), lambda i, _: (0, 0)),
                pl.BlockSpec((step, tokens), lambda i, _: (i, 0)),
                pl.BlockSpec((keys, step), lambda i, _: (0, i)),
                pl.BlockSpec((keys, step), lambda i, _: (0, i)),
                pl.BlockSpec((tokens, step), lambda i, _: (0, i)),
            ],
            out_specs=[block] * 4,
            scratch_shapes=[pltpu.VMEM((width, keys), low)],
        ),
        out_shape=[shape] * 4,
        compiler_params=pltpu.CompilerParams(vmem_limit_bytes=18 << 20),
    )(core, normed_all, attended_t, grad_q_t, grad_k, grad_v, grad_out)


def shards(
    embeddings,
    lengths,
    cotangent,
    conv_weight,
    scorer,
    gain_attn,
    w_query,
    w_key,
    w_value,
    w_out,
    rel_bias,
    gain_ffn,
    w_gate,
    w_up,
    w_down,
):
    num_micro, num_seqs, local_bytes, model_width = embeddings.shape
    piece_tokens = local_bytes // 2
    count = num_micro * num_seqs
    seq_count = lax.axis_size("seq")
    assert seq_count == 2 * count
    seq_index = lax.axis_index("seq")
    core = lax.axis_index("dp") % 2
    device = lax.axis_index("dp") * seq_count + seq_index
    local_tokens = count * piece_tokens
    key_count = 2 * local_tokens
    low, f32 = (jnp.bfloat16, jnp.float32)
    phases_a, phases_b = stage_phases()
    along, across_a, across_b = (phases_a[:2], phases_a[2:], phases_b[2:])
    rows = w_query.shape[0]
    vec_rows = KERNEL + 3
    half = 2 * model_width
    ff = w_gate.shape[1]
    chain = Chain()

    groups = exchange_groups()
    lines = [[step] for group in groups for step in group]
    pieces = embeddings.reshape(count, local_bytes, model_width)
    piece_lengths = lengths.reshape(count)
    down_rows = w_down.shape[0]
    folded = rows % 24 == 0 and 2 * down_rows * seq_count == 512 and 3 * ff == 8 * model_width
    down_block = w_down if folded else w_down.reshape(rows, ff)
    square, wide = pack_weights(w_query, w_key, w_value, w_out, w_gate, w_up, down_block)
    digits = jnp.concatenate([piece_lengths // 64, piece_lengths % 64]).astype(low)
    vectors = jnp.concatenate(
        [
            conv_weight,
            scorer[None],
            gain_attn[None],
            gain_ffn[None],
            jnp.broadcast_to(digits[:, None], (2 * count, rows)),
        ],
        axis=0,
    )
    vectors = exchange(vectors, lines[0])
    digits = vectors[1][vec_rows:, 0].astype(jnp.int32)
    other_lengths = 64 * digits[:count] + digits[count:]
    vectors = [vector[:vec_rows] for vector in vectors]
    square = Gathering(chain, square, along)
    bytes_before, bytes_after = neighbour_edges(pieces, 2 * EDGE)
    for number, group in enumerate(lines[1:]):
        vectors = chain.note(jnp.concatenate(chain.after(*vectors), axis=1))
        vectors = exchange(vectors, group)
        if number == 1:
            square.finish()
            wide = Gathering(chain, chain.after(wide), along)
    vectors = chain.note(jnp.concatenate(chain.after(*vectors), axis=1))
    steps = [step for group in groups for step in group]
    source = jnp.arange(model_width, dtype=jnp.int32)
    partner = device ^ sum(
        ((source // rows >> number) & 1) * (1 << bit if axis == "seq" else seq_count << bit)
        for number, (axis, bit) in enumerate(steps)
    )
    target = partner * rows + source % rows
    place = target[:, None] == jnp.arange(model_width, dtype=jnp.int32)[None, :]
    vectors = chain.note(mm(vectors, place.astype(low)))
    gain_one, gain_two = (vectors[KERNEL + 1], vectors[KERNEL + 2])
    token_start = seq_index * piece_tokens
    info = jnp.concatenate([token_start.reshape(1).astype(jnp.int32), piece_lengths])
    square.finish()
    first = Gathering(chain, chain.note(square.whole[..., :half]), across_a, square.held)
    second = Gathering(chain, chain.note(square.whole[..., half:]), across_b, square.held)
    sent = chain.note(
        pool_forward(info, bytes_before, chain.after(pieces), bytes_after, vectors)
    )
    arrived = to_chips(sent)
    chain_lengths = jnp.where(core == seq_index // count, piece_lengths, other_lengths)
    seq_length = lax.dynamic_index_in_dim(chain_lengths, seq_index % count, 0, keepdims=False)
    first_tile = core * (local_tokens // TILE)
    first_ref = first_tile.astype(jnp.int32).reshape(1)
    wide.finish()
    first.finish()
    second.finish()
    seq_length, rel_late = chain.after(seq_length, rel_bias)
    key_aug, block_rows, far = attn_tables(
        first_tile, local_tokens, key_count, seq_length, rel_late
    )
    bias = chain.note(near_bias(rel_late.T))
    wide.finish()
    ff_side = 3 * ff // 2
    gate_full = Gathering(chain, chain.note(wide.whole[..., :ff_side]), across_a, wide.held)
    up_full = Gathering(chain, chain.note(wide.whole[..., ff_side:]), across_b, wide.held)
    arrived = in_token_order(chain.after(*arrived))
    normed_low = chain.note(arrived[:, :piece_tokens].reshape(local_tokens, model_width))
    normed_other = swap_bit(normed_low, "dp", 0)
    scale = arrived[:, piece_tokens : piece_tokens + 2, :piece_tokens].astype(f32)
    scale = jnp.sum(scale, axis=1).reshape(local_tokens, 1)
    unit = normed_low.astype(f32) / gain_one
    hidden_in = unit / scale
    first.finish()
    second.finish()
    normed_other = chain.after(normed_other)
    normed_all = chain.note(
        jnp.concatenate(
            [
                jnp.where(core == 0, normed_low, normed_other),
                jnp.where(core == 0, normed_other, normed_low),
            ],
            axis=0,
        )
    )
    first = first.finish().reshape(model_width, half)
    second = second.finish().reshape(model_width, half)
    query_full, key_full = (first[:, :model_width], first[:, model_width:])
    value_full, out_full = (second[:, :model_width], second[:, model_width:])

    def project_t(weight, tokens):
        return lax.dot_general(
            weight, tokens, (((0,), (1,)), ((), ())), preferred_element_type=f32
        ).astype(low)

    q_t = project_t(query_full, chain.after(normed_low))
    v_t = project_t(value_full, normed_all)
    keys_all = chain.note(mm(normed_all, key_full).astype(low))
    gate_full.finish()
    up_full.finish()
    seed_pieces = cotangent.reshape(count, piece_tokens, model_width)
    seed_arrived = to_chips(chain.after(seed_pieces))
    attended_t, lse = attn_forward(
        first_ref, chain.after(q_t), keys_all, key_aug, v_t, far, bias
    )
    chain.note(attended_t)
    seed_low = in_token_order(chain.after(*seed_arrived)).reshape(local_tokens, model_width)
    chain.note(seed_low)
    gate_full.finish()
    up_full.finish()
    k_t = chain.note(project_t(key_full, chain.after(normed_all)))
    halves = [gather.last() for gather in (gate_full, up_full)]
    waiting = chain.after(*[half[1] for half in halves])
    halves = [(half[0], other) for half, other in zip(halves, waiting)]

    core_ref = core.astype(jnp.int32).reshape(1)
    (
        block_out,
        grad_after,
        grad_after_low,
        grad_attended_t,
        gain_ffn_grad,
        gate_leave,
        up_leave,
        gate_stay,
        up_stay,
    ) = feed_forward(
        core_ref,
        hidden_in,
        attended_t,
        out_full,
        gain_two[None],
        seed_low,
        *halves,
        rows,
        down_rows,
    )
    chain.note(grad_after_low)
    gate_arrived = swap_bit(gate_leave, "dp", 0)
    up_arrived = swap_bit(up_leave, "dp", 0)
    values_all = chain.note(mm(chain.after(normed_all), value_full).astype(low))
    gate_sum = Reduction(chain, gate_stay[None], gate_arrived[None], rows, phases_a)
    up_sum = Reduction(chain, up_stay[None], up_arrived[None], rows, phases_b)
    gate_sum.finish()
    up_sum.finish()
    grad_queries_t, key_terms, value_terms, near, sums, leaving, staying = attn_backward(
        first_ref,
        q_t,
        chain.after(grad_attended_t),
        attended_t,
        lse,
        keys_all,
        values_all,
        k_t,
        key_aug,
        block_rows,
        far,
        bias,
        query_full,
        key_full,
        value_full,
    )
    arrived = swap_bit(chain.note(leaving), "dp", 0)
    gate_sum.finish()
    up_sum.finish()
    grad_normed = staying + chain.after(arrived).astype(f32)
    gained = grad_normed * gain_one
    grad_hidden = grad_after + scale * (
        gained - unit * jnp.mean(gained * unit, axis=-1, keepdims=True)
    )
    arrived = from_chips(chain.note(grad_hidden.astype(low)), count)
    first_leave, second_leave, first_stay, second_stay = square_gradients(
        core_ref,
        normed_all,
        attended_t,
        grad_queries_t,
        chain.after(key_terms),
        value_terms,
        grad_after_low,
        rows * seq_count,
    )
    chain.note(first_leave)
    grad_pieces = in_piece_order(chain.after(*arrived))
    chain.note(grad_pieces)
    first_arrived = swap_bit(first_leave, "dp", 0)
    second_arrived = swap_bit(second_leave, "dp", 0)
    grad_before, grad_after_edge = neighbour_edges(grad_pieces, EDGE)
    bias_terms = chain.note(bias_gradient(first_ref, chain.after(near), sums))
    first_sum = Reduction(chain, first_stay, first_arrived, rows, phases_a)
    second_sum = Reduction(chain, second_stay, second_arrived, rows, phases_b)
    first_sum.finish()
    second_sum.finish()
    gate_sum.finish()
    up_sum.finish()
    pooled = ()
    for part in range(2):
        pooled = pool_backward(
            info,
            bytes_before,
            pieces,
            bytes_after,
            grad_before,
            chain.after(grad_pieces),
            grad_after_edge,
            vectors,
            part * count // 2,
            (part + 1) * count // 2,
            tuple(pooled),
        )
        chain.note(pooled[1])
        gate_side = gate_sum.finish()
        up_side = up_sum.finish()
        first_sum.finish()
        second_sum.finish()
        if part == 1:
            blocks_arrived = from_chips(chain.after(block_out), count)
    gain_attn_grad = chain.note(jnp.sum(chain.after(grad_normed) * unit, axis=0))
    embed_grad, pool_small = pooled
    embed_out = embed_grad.reshape(num_micro, num_seqs, local_bytes, model_width)
    pool_small = jnp.sum(pool_small, axis=0)[: KERNEL + 1]
    bias_row = jnp.pad(bias_terms.reshape(-1), (0, model_width - bias_terms.size))
    small = jnp.concatenate(
        [pool_small, gain_attn_grad[None], gain_ffn_grad, bias_row[None]],
        axis=0,
    )
    small = exchange(chain.note(small), groups[0])
    for group in groups[1:]:
        small = exchange(chain.note(tree_sum(chain.after(*small))), group)
        if group is groups[1]:
            first_sum.finish()
            second_sum.finish()
    small = chain.note(tree_sum(chain.after(*small)))
    blocks_out = in_piece_order(chain.after(*blocks_arrived))
    gate_side, up_side = (gate_side[0], up_side[0])
    gate_grad, up_grad = (gate_side[:, :ff], up_side[:, :ff])
    down_grad = jnp.concatenate([gate_side[:, ff:], up_side[:, ff:]], axis=1)
    down_grad = (
        unfold_rows(down_grad, model_width) if folded else down_grad.reshape(down_rows, model_width)
    )
    blocks_out = blocks_out.reshape(num_micro, num_seqs, piece_tokens, model_width)
    second_grad = second_sum.finish()
    first_grad = first_sum.finish()
    query_grad, key_grad = (first_grad[0], first_grad[1])
    value_grad, out_grad = (second_grad[0], second_grad[1])
    bias_total = small[vec_rows, : bias_terms.size].reshape(bias_terms.shape).T
    own = lax.dynamic_slice_in_dim(small[:vec_rows], device * rows, rows, axis=1)
    return (
        blocks_out,
        embed_out,
        own[:KERNEL],
        own[KERNEL],
        own[KERNEL + 1],
        query_grad,
        key_grad,
        value_grad,
        out_grad,
        bias_total,
        own[KERNEL + 2],
        gate_grad,
        up_grad,
        down_grad,
    )


def solution(mesh):
    return jax.shard_map(
        shards,
        mesh=mesh,
        in_specs=(
            P(None, "dp", "seq", None),
            P(None, "dp"),
            P(None, "dp", "seq", None),
            P(None, ("dp", "seq")),
            P(("dp", "seq")),
            P(("dp", "seq")),
            P(("dp", "seq"), None),
            P(("dp", "seq"), None),
            P(("dp", "seq"), None),
            P(("dp", "seq"), None),
            P(),
            P(("dp", "seq")),
            P(("dp", "seq"), None),
            P(("dp", "seq"), None),
            P(("dp", "seq"), None),
        ),
        out_specs=(
            P(None, "dp", "seq", None),
            P(None, "dp", "seq", None),
            P(None, ("dp", "seq")),
            P(("dp", "seq")),
            P(("dp", "seq")),
            P(("dp", "seq"), None),
            P(("dp", "seq"), None),
            P(("dp", "seq"), None),
            P(("dp", "seq"), None),
            P(),
            P(("dp", "seq")),
            P(("dp", "seq"), None),
            P(("dp", "seq"), None),
            P(("dp", "seq"), None),
        ),
        check_vma=False,
    )
```
